32 devices in a mesh: row: 8 (over z, y), col: 4 (over x, core).
Axes of the slice: x: 2, y: 2, z: 4, core: 2. Of those that a mesh axis runs over, the one named last changes fastest.
Arguments:
- corrupted_letters: int32 [2, 64, 64], P(None, 'col', 'row'), may hold values from 0 to 22
- truth_categories: int32 [2, 64, 64], P(None, 'col', 'row'), may hold values from 0 to 22
- concealed_sites: int32 [2, 64, 64], P(None, 'col', 'row'), may hold values 0 or 1
- existing_aligned: int32 [2, 64], replicated, may hold values 0 or 1
- chain_ordinals: int32 [2, 64], replicated, may hold values from 1 to 96, as said below
- observed_sites: int32 [2, 64], replicated, may hold values 0 or 1
- distance_bucket_truth: int32 [2, 64, 64], P(None, 'row', 'col'), may hold values from 0 to 63
- letter_lookup: float32 [23, 256], replicated, may hold values from -6 to 6
- alignment_projection: float32 [256, 2135], replicated, may hold values from -0.375 to 0.375
- contracting_projection: float32 [1280, 256], replicated, may hold values from -0.75 to 0.75
- relative_projection: float32 [1089, 128], replicated, may hold values from -0.875 to 0.875
- pairwise_projection: float32 [128, 840], replicated, may hold values from -0.5 to 0.5
- scalar_params: float32 [1367], replicated
- running_mean_lookup: float32 [23, 256], replicated, may hold values from -1.335144e-05 to 1.335144e-05
- running_mean_alignment: float32 [256, 2135], replicated, may hold values from -1.335144e-05 to 1.335144e-05
- running_mean_contracting: float32 [1280, 256], replicated, may hold values from -1.335144e-05 to 1.335144e-05
- running_mean_relative: float32 [1089, 128], replicated, may hold values from -1.335144e-05 to 1.335144e-05
- running_mean_pairwise: float32 [128, 840], replicated, may hold values from -1.335144e-05 to 1.335144e-05
- running_mean_scalars: float32 [1367], replicated, may hold values from -1.335144e-05 to 1.335144e-05
- running_square_lookup: float32 [23, 256], replicated, may hold values from 3.5e-13 to 1.4e-12
- running_square_alignment: float32 [256, 2135], replicated, may hold values from 3.5e-13 to 1.4e-12
- running_square_contracting: float32 [1280, 256], replicated, may hold values from 3.5e-13 to 1.4e-12
- running_square_relative: float32 [1089, 128], replicated, may hold values from 3.5e-13 to 1.4e-12
- running_square_pairwise: float32 [128, 840], replicated, may hold values from 3.5e-13 to 1.4e-12
- running_square_scalars: float32 [1367], replicated, may hold values from 3.5e-13 to 1.4e-12
Outputs:
- loss: float32 [], replicated
- grad_norm: float32 [], replicated
- new_embed: float32 [23, 256], replicated
- new_moment_embed: float32 [23, 256], replicated
- new_square_embed: float32 [23, 256], replicated
- new_msa: float32 [256, 2135], replicated
- new_moment_msa: float32 [256, 2135], replicated
- new_square_msa: float32 [256, 2135], replicated
- new_down: float32 [1280, 256], replicated
- new_moment_down: float32 [1280, 256], replicated
- new_square_down: float32 [1280, 256], replicated
- new_in: float32 [1089, 128], replicated
- new_moment_in: float32 [1089, 128], replicated
- new_square_in: float32 [1089, 128], replicated
- new_pair: float32 [128, 840], replicated
- new_moment_pair: float32 [128, 840], replicated
- new_square_pair: float32 [128, 840], replicated
- new_small: float32 [1367], replicated
- new_moment_small: float32 [1367], replicated
- new_square_small: float32 [1367], replicated
The draws below stay inside these ranges and needn't reach their ends.
Inputs may be any that keep to these rules, and one draw needn't show every extreme that they name: `chain_ordinals`: in each protein, starts at 1 and rises strictly; consecutive entries differ by 1 or 2, by 2 at exactly 32 places.
All inputs are finite; a program needn't handle non-finite values. No bound on the sum of `concealed_sites` on one device may be relied on, other than what follows from the above.
Results may differ from the reference program's by a relative error of at most 0.0022.
The reference program's roundings to bfloat16 on the way count: a program that leaves them out, or rounds other values in their place, can miss the bound.
Values may be sent and summed in bfloat16 or wider, within the bound.
A program may use at most 192 MiB of HBM per device.

```python
import math
import jax
import jax.numpy as jnp
from jax import lax

ALIGNMENT_WIDTH = 256
PAIRWISE_WIDTH = 128
PRODUCT_WIDTH = 32
CTRI = 128
EXPANSION_WIDTH = 1024
ALPHABET_SIZE = 23
DISTANCE_BUCKETS = 64
REACH = 32
MHEADS = 8
HEAD = 32
ADAM_STEP = 4
CHAIN_TOTAL_NUM = 2
ALIGNED_SEQS = 64
CROP_LENGTH = 64


def draw_scalar_params(key, part):
    normaliser_scales = 1.0 + 0.15 * jax.random.normal(jax.random.fold_in(key, 1), (3 * ALIGNMENT_WIDTH + 3 * PAIRWISE_WIDTH,), jnp.float32)
    biases = 0.5 * jax.random.normal(jax.random.fold_in(key, 2), (PAIRWISE_WIDTH + DISTANCE_BUCKETS + ALPHABET_SIZE,), jnp.float32)
    return jnp.concatenate([normaliser_scales, biases])


def draw_chain_ordinals(key, part):

    def single(index):
        order = jax.random.permutation(jax.random.fold_in(key, 3 + index), CROP_LENGTH - 1)
        later = jnp.where(order < CROP_LENGTH // 2, 2, 1).astype(jnp.int32)
        steps = jnp.concatenate([jnp.ones((1,), jnp.int32), later])
        return jnp.cumsum(steps).astype(jnp.int32)
    return jnp.stack([single(index) for index in range(CHAIN_TOTAL_NUM)])


def set_ends(values, rng, low, high):
    longest = values.shape.index(max(values.shape))
    spots = []
    for shift in (0, 1):
        where = [jax.random.randint(jax.random.fold_in(rng, axis), (), 0, length) for axis, length in enumerate(values.shape)]
        where[longest] = (where[longest] + shift) % values.shape[longest]
        spots.append(tuple(where))
    return values.at[spots[0]].set(low).at[spots[1]].set(high)


def scatter_about(key, dims, scale, limit, kind=jnp.bfloat16):
    values = jax.random.normal(key, dims, jnp.float32) * scale
    return jnp.minimum(jnp.maximum(values, -limit), limit).astype(kind)


def setup_inputs(seed: int = 0) -> dict:
    key_list = jax.random.split(jax.random.key(seed), 26)
    corrupted_letters = set_ends(jax.random.randint(key_list[0], (CHAIN_TOTAL_NUM, ALIGNED_SEQS, CROP_LENGTH), 0, ALPHABET_SIZE), jax.random.fold_in(key_list[0], 1), 0, ALPHABET_SIZE - 1).astype(jnp.int32)
    truth_categories = set_ends(jax.random.randint(key_list[1], (CHAIN_TOTAL_NUM, ALIGNED_SEQS, CROP_LENGTH), 0, ALPHABET_SIZE), jax.random.fold_in(key_list[1], 1), 0, ALPHABET_SIZE - 1).astype(jnp.int32)
    concealed_sites = set_ends((jax.random.randint(key_list[2], (CHAIN_TOTAL_NUM, ALIGNED_SEQS, CROP_LENGTH), 0, 20) < 3).astype(jnp.int32), jax.random.fold_in(key_list[2], 1), 0, 1)
    existing_aligned = set_ends((jax.random.randint(key_list[3], (CHAIN_TOTAL_NUM, ALIGNED_SEQS), 0, 4) < 3).astype(jnp.int32), jax.random.fold_in(key_list[3], 1), 0, 1)
    chain_ordinals = draw_chain_ordinals(jax.random.fold_in(key_list[25], 71), 0)
    observed_sites = set_ends((jax.random.randint(key_list[5], (CHAIN_TOTAL_NUM, CROP_LENGTH), 0, 8) < 7).astype(jnp.int32), jax.random.fold_in(key_list[5], 1), 0, 1)
    distance_bucket_truth = set_ends(jax.random.randint(key_list[6], (CHAIN_TOTAL_NUM, CROP_LENGTH, CROP_LENGTH), 0, DISTANCE_BUCKETS), jax.random.fold_in(key_list[6], 1), 0, DISTANCE_BUCKETS - 1).astype(jnp.int32)
    letter_lookup = scatter_about(key_list[7], (ALPHABET_SIZE, ALIGNMENT_WIDTH), 1.0, 6.0, jnp.float32)
    alignment_projection = scatter_about(key_list[8], (ALIGNMENT_WIDTH, 4 * ALIGNMENT_WIDTH + EXPANSION_WIDTH + 2 * PRODUCT_WIDTH + ALPHABET_SIZE), ALIGNMENT_WIDTH ** -0.5, 0.375, jnp.float32)
    contracting_projection = scatter_about(key_list[9], (ALIGNMENT_WIDTH + EXPANSION_WIDTH, ALIGNMENT_WIDTH), (EXPANSION_WIDTH // 16) ** -0.5, 0.75, jnp.float32)
    relative_projection = scatter_about(key_list[10], (PRODUCT_WIDTH * PRODUCT_WIDTH + 2 * REACH + 1, PAIRWISE_WIDTH), 0.15, 0.875, jnp.float32)
    pairwise_projection = scatter_about(key_list[11], (PAIRWISE_WIDTH, 5 * CTRI + PAIRWISE_WIDTH + MHEADS + DISTANCE_BUCKETS), PAIRWISE_WIDTH ** -0.5, 0.5, jnp.float32)
    scalar_params = draw_scalar_params(jax.random.fold_in(key_list[25], 71), 0)
    running_mean_lookup = scatter_about(key_list[13], (ALPHABET_SIZE, ALIGNMENT_WIDTH), (2.1e-6), 1.33514404296875e-05, jnp.float32)
    running_mean_alignment = scatter_about(key_list[14], (ALIGNMENT_WIDTH, 4 * ALIGNMENT_WIDTH + EXPANSION_WIDTH + 2 * PRODUCT_WIDTH + ALPHABET_SIZE), (2.1e-6), 1.33514404296875e-05, jnp.float32)
    running_mean_contracting = scatter_about(key_list[15], (ALIGNMENT_WIDTH + EXPANSION_WIDTH, ALIGNMENT_WIDTH), (2.1e-6), 1.33514404296875e-05, jnp.float32)
    running_mean_relative = scatter_about(key_list[16], (PRODUCT_WIDTH * PRODUCT_WIDTH + 2 * REACH + 1, PAIRWISE_WIDTH), (2.1e-6), 1.33514404296875e-05, jnp.float32)
    running_mean_pairwise = scatter_about(key_list[17], (PAIRWISE_WIDTH, 5 * CTRI + PAIRWISE_WIDTH + MHEADS + DISTANCE_BUCKETS), (2.1e-6), 1.33514404296875e-05, jnp.float32)
    running_mean_scalars = scatter_about(key_list[18], (3 * ALIGNMENT_WIDTH + 4 * PAIRWISE_WIDTH + DISTANCE_BUCKETS + ALPHABET_SIZE,), (2.1e-6), 1.33514404296875e-05, jnp.float32)
    running_square_lookup = jnp.clip(jnp.exp(jax.random.uniform(key_list[19], (ALPHABET_SIZE, ALIGNMENT_WIDTH), jnp.float32, math.log(3.500000040224799e-13), math.log(1.4000000160899195e-12))), 3.500000040224799e-13, 1.4000000160899195e-12)
    running_square_alignment = jnp.clip(jnp.exp(jax.random.uniform(key_list[20], (ALIGNMENT_WIDTH, 4 * ALIGNMENT_WIDTH + EXPANSION_WIDTH + 2 * PRODUCT_WIDTH + ALPHABET_SIZE), jnp.float32, math.log(3.500000040224799e-13), math.log(1.4000000160899195e-12))), 3.500000040224799e-13, 1.4000000160899195e-12)
    running_square_contracting = jnp.clip(jnp.exp(jax.random.uniform(key_list[21], (ALIGNMENT_WIDTH + EXPANSION_WIDTH, ALIGNMENT_WIDTH), jnp.float32, math.log(3.500000040224799e-13), math.log(1.4000000160899195e-12))), 3.500000040224799e-13, 1.4000000160899195e-12)
    running_square_relative = jnp.clip(jnp.exp(jax.random.uniform(key_list[22], (PRODUCT_WIDTH * PRODUCT_WIDTH + 2 * REACH + 1, PAIRWISE_WIDTH), jnp.float32, math.log(3.500000040224799e-13), math.log(1.4000000160899195e-12))), 3.500000040224799e-13, 1.4000000160899195e-12)
    running_square_pairwise = jnp.clip(jnp.exp(jax.random.uniform(key_list[23], (PAIRWISE_WIDTH, 5 * CTRI + PAIRWISE_WIDTH + MHEADS + DISTANCE_BUCKETS), jnp.float32, math.log(3.500000040224799e-13), math.log(1.4000000160899195e-12))), 3.500000040224799e-13, 1.4000000160899195e-12)
    running_square_scalars = jnp.clip(jnp.exp(jax.random.uniform(key_list[24], (3 * ALIGNMENT_WIDTH + 4 * PAIRWISE_WIDTH + DISTANCE_BUCKETS + ALPHABET_SIZE,), jnp.float32, math.log(3.500000040224799e-13), math.log(1.4000000160899195e-12))), 3.500000040224799e-13, 1.4000000160899195e-12)
    return dict(corrupted_letters=corrupted_letters, truth_categories=truth_categories, concealed_sites=concealed_sites, existing_aligned=existing_aligned, chain_ordinals=chain_ordinals, observed_sites=observed_sites, distance_bucket_truth=distance_bucket_truth, letter_lookup=letter_lookup, alignment_projection=alignment_projection, contracting_projection=contracting_projection, relative_projection=relative_projection, pairwise_projection=pairwise_projection, scalar_params=scalar_params, running_mean_lookup=running_mean_lookup, running_mean_alignment=running_mean_alignment, running_mean_contracting=running_mean_contracting, running_mean_relative=running_mean_relative, running_mean_pairwise=running_mean_pairwise, running_mean_scalars=running_mean_scalars, running_square_lookup=running_square_lookup, running_square_alignment=running_square_alignment, running_square_contracting=running_square_contracting, running_square_relative=running_square_relative, running_square_pairwise=running_square_pairwise, running_square_scalars=running_square_scalars)


EPS_NORM = 1e-05
CLIP_NORM = 0.02
LEARN_RATE = 0.05
BETA_ONE = 0.9
BETA_TWO = 0.999
ADAM_EPS = 1e-08
DECAY_RATE = 0.01
EXACT_ARITHMETIC = lax.Precision.HIGHEST

@jax.custom_vjp
def low(v):
    return lax.optimization_barrier(v.astype(jnp.bfloat16)).astype(jnp.float32)

@jax.custom_vjp
def low_back(v):
    return v

def low_keep(v):
    return (low(v), None)

def low_pass(kept, grad):
    return (grad,)

def back_keep(v):
    return (v, None)

def back_low(kept, grad):
    return (low(grad),)
low.defvjp(low_keep, low_pass)
low_back.defvjp(back_keep, back_low)

def normalise_features(value, gain):
    centred = value - lax.optimization_barrier(jnp.mean(value, axis=-1, keepdims=True))
    spread = lax.optimization_barrier(jnp.mean(centred * centred, axis=-1, keepdims=True))
    return centred * lax.rsqrt(spread + EPS_NORM) * gain

def split_small(scalar_params):
    extents = (ALIGNMENT_WIDTH, ALIGNMENT_WIDTH, ALIGNMENT_WIDTH, PAIRWISE_WIDTH, PAIRWISE_WIDTH, PAIRWISE_WIDTH, PAIRWISE_WIDTH, DISTANCE_BUCKETS, ALPHABET_SIZE)
    pieces = []
    begin = 0
    for width in extents:
        pieces.append(scalar_params[begin:begin + width])
        begin += width
    return pieces

def cross_sum(category_scores, target, weight):
    top = lax.optimization_barrier(jnp.max(category_scores, axis=-1, keepdims=True))
    total = jnp.log(lax.optimization_barrier(jnp.sum(jnp.exp(category_scores - top), axis=-1))) + top[..., 0]
    category_truth = lax.broadcasted_iota(jnp.int32, category_scores.shape, category_scores.ndim - 1)
    picked = lax.optimization_barrier(jnp.sum(jnp.where(category_truth == target[..., None], category_scores, 0.0), axis=-1))
    return jnp.sum((total - picked) * weight)

def relative_table(offset, relative_projection):
    codes = lax.broadcasted_iota(jnp.int32, offset.shape + (2 * REACH + 1,), 2)
    return jnp.einsum('ijr,rc->ijc', (codes == offset[..., None]).astype(jnp.float32), relative_projection[PRODUCT_WIDTH * PRODUCT_WIDTH:], precision=EXACT_ARITHMETIC)

def pair_bias(offset, relative_projection, pairwise_projection, scalar_params):
    normaliser_scales = split_small(scalar_params)
    relative = relative_table(offset, relative_projection)
    opening_piece = 5 * CTRI + PAIRWISE_WIDTH
    return jnp.einsum('ijc,ch->ijh', normalise_features(relative, normaliser_scales[3]), pairwise_projection[:, opening_piece:opening_piece + MHEADS], precision=EXACT_ARITHMETIC)

def alignment_front(letter_lookup, alignment_projection, scalar_params, letter_entries):
    normaliser_scales = split_small(scalar_params)
    category_truth = lax.broadcasted_iota(jnp.int32, letter_entries.shape + (ALPHABET_SIZE,), 2)
    onehot = (category_truth == letter_entries[..., None]).astype(jnp.float32)
    initial_entry = jnp.einsum('src,cd->srd', onehot, letter_lookup, precision=EXACT_ARITHMETIC)
    mapped_features = jnp.einsum('uop,ph->uoh', normalise_features(initial_entry, normaliser_scales[0]), alignment_projection[:, :4 * ALIGNMENT_WIDTH], precision=EXACT_ARITHMETIC)
    return (mapped_features[..., :ALIGNMENT_WIDTH], mapped_features[..., ALIGNMENT_WIDTH:2 * ALIGNMENT_WIDTH], mapped_features[..., 2 * ALIGNMENT_WIDTH:3 * ALIGNMENT_WIDTH], mapped_features[..., 3 * ALIGNMENT_WIDTH:], initial_entry)

def row_attention(asking_vectors, lookup_vectors, content_vectors, additive_shift, key_mask):
    seqs, line_entries = (asking_vectors.shape[0], asking_vectors.shape[1])
    q_heads = asking_vectors.reshape(seqs, line_entries, MHEADS, HEAD) * HEAD ** (-0.5)
    k_heads = lookup_vectors.reshape(seqs, lookup_vectors.shape[1], MHEADS, HEAD)
    v_heads = content_vectors.reshape(seqs, lookup_vectors.shape[1], MHEADS, HEAD)
    shifted = jnp.transpose(additive_shift, (2, 0, 1))

    def single(items):
        q_one, k_one, values_single = items
        scores = jnp.einsum('ihd,jhd->hij', q_one, k_one, precision=EXACT_ARITHMETIC) + shifted
        scores = jnp.where(key_mask[None, None, :] > 0, scores, -1000000000.0)
        coefficients = jax.nn.softmax(scores, axis=-1)
        return jnp.einsum('alo,oak->lak', coefficients, values_single, precision=EXACT_ARITHMETIC).reshape(line_entries, ALIGNMENT_WIDTH)
    return lax.map(jax.checkpoint(single), (q_heads, k_heads, v_heads))

def alignment_rest(initial_entry, attended_result, sigmoid_factors, alignment_projection, contracting_projection, scalar_params, truth_categories, objective_filter, aligned_factor):
    normaliser_scales = split_small(scalar_params)
    central_entry = initial_entry + jnp.einsum('uop,ph->uoh', jax.nn.sigmoid(sigmoid_factors) * attended_result, contracting_projection[:ALIGNMENT_WIDTH], precision=EXACT_ARITHMETIC)
    expanded_features = jax.nn.relu(jnp.einsum('vhg,gz->vhz', normalise_features(central_entry, normaliser_scales[1]), alignment_projection[:, 4 * ALIGNMENT_WIDTH:4 * ALIGNMENT_WIDTH + EXPANSION_WIDTH], precision=EXACT_ARITHMETIC))
    feature_tensor = central_entry + jnp.einsum('png,gq->pnq', expanded_features, contracting_projection[ALIGNMENT_WIDTH:], precision=EXACT_ARITHMETIC)
    opening_piece = 4 * ALIGNMENT_WIDTH + EXPANSION_WIDTH
    pairwise_entries = jnp.einsum('uop,ph->uoh', normalise_features(feature_tensor, normaliser_scales[2]), alignment_projection[:, opening_piece:opening_piece + 2 * PRODUCT_WIDTH], precision=EXACT_ARITHMETIC) * aligned_factor[:, None, None]
    category_scores = jnp.einsum('ocu,uy->ocy', feature_tensor, alignment_projection[:, opening_piece + 2 * PRODUCT_WIDTH:], precision=EXACT_ARITHMETIC) + normaliser_scales[8]
    return (pairwise_entries, cross_sum(category_scores, truth_categories, objective_filter))

def outer_piece(left, right, relative_projection, count):
    size = min(left.shape[1], 8)
    outer_w = relative_projection[:PRODUCT_WIDTH * PRODUCT_WIDTH].reshape(PRODUCT_WIDTH, PRODUCT_WIDTH, PAIRWISE_WIDTH)

    def block(piece):
        outer = jnp.einsum('sic,sjd->ijcd', piece, right, precision=EXACT_ARITHMETIC)
        return jnp.einsum('ijcd,cdo->ijo', outer, outer_w, precision=EXACT_ARITHMETIC)
    blocks = jnp.moveaxis(left.reshape(left.shape[0], left.shape[1] // size, size, PRODUCT_WIDTH), 1, 0)
    result = lax.map(jax.checkpoint(block), blocks)
    return result.reshape(left.shape[1], right.shape[1], PAIRWISE_WIDTH) / count

def pair_front(offset, outer, relative_projection, pairwise_projection, scalar_params, pair_mask):
    normaliser_scales = split_small(scalar_params)
    pair_rep = relative_table(offset, relative_projection) + outer + normaliser_scales[6]
    mapped_features = jnp.einsum('ijc,ce->ije', normalise_features(pair_rep, normaliser_scales[4]), pairwise_projection[:, :5 * CTRI], precision=EXACT_ARITHMETIC)
    weight = pair_mask[..., None]
    left_edge = jax.nn.sigmoid(mapped_features[..., CTRI:2 * CTRI]) * mapped_features[..., :CTRI] * weight
    right_edge = jax.nn.sigmoid(mapped_features[..., 3 * CTRI:4 * CTRI]) * mapped_features[..., 2 * CTRI:3 * CTRI] * weight
    return (pair_rep, left_edge, right_edge, mapped_features[..., 4 * CTRI:])

def pair_tail(pairwise_projection, scalar_params, pair_rep, mixed, gate_pre, distance_bucket_truth, pair_mask):
    normaliser_scales = split_small(scalar_params)
    update = jax.nn.sigmoid(gate_pre) * jnp.einsum('ijc,cd->ijd', normalise_features(mixed, normaliser_scales[5]), pairwise_projection[:, 5 * CTRI:5 * CTRI + PAIRWISE_WIDTH], precision=EXACT_ARITHMETIC)
    category_scores = jnp.einsum('ijc,cb->ijb', pair_rep + update, pairwise_projection[:, 5 * CTRI + PAIRWISE_WIDTH + MHEADS:], precision=EXACT_ARITHMETIC) + normaliser_scales[7]
    return cross_sum(category_scores, distance_bucket_truth, pair_mask)

def adam(weight, moment, squared_value, grad, scale):
    clipped = grad * scale
    new_moment = BETA_ONE * moment + (1.0 - BETA_ONE) * clipped
    new_square = BETA_TWO * squared_value + (1.0 - BETA_TWO) * clipped * clipped
    fixed_moment = new_moment / (1.0 - BETA_ONE ** ADAM_STEP)
    fixed_square = new_square / (1.0 - BETA_TWO ** ADAM_STEP)
    new_weight = weight - LEARN_RATE * (fixed_moment / (jnp.sqrt(fixed_square) + ADAM_EPS) + DECAY_RATE * weight)
    return (new_weight, new_moment, new_square)

def protein_totals(network_parameters, letter_entries, category_truth, bmask, smask, rindex, rmask, bins):
    letter_lookup, alignment_projection, contracting_projection, relative_projection, pairwise_projection, scalar_params = network_parameters
    aligned_factor = smask.astype(jnp.float32)
    objective_filter = bmask.astype(jnp.float32) * aligned_factor[:, None]
    res_weight = rmask.astype(jnp.float32)
    pair_mask = res_weight[:, None] * res_weight[None, :]
    count = jnp.sum(aligned_factor) + 1.0
    offset = jnp.clip(rindex[:, None] - rindex[None, :], -REACH, REACH) + REACH
    asking_vectors, lookup_vectors, content_vectors, sigmoid_factors, initial_entry = alignment_front(letter_lookup, alignment_projection, scalar_params, letter_entries)
    additive_shift = pair_bias(offset, relative_projection, pairwise_projection, scalar_params)
    attended_result = row_attention(asking_vectors, low(lookup_vectors), low(content_vectors), additive_shift, res_weight)
    pairwise_entries, hidden_letter_penalty = alignment_rest(initial_entry, attended_result, sigmoid_factors, alignment_projection, contracting_projection, scalar_params, category_truth, objective_filter, aligned_factor)
    outer = outer_piece(pairwise_entries[..., :PRODUCT_WIDTH], low(pairwise_entries[..., PRODUCT_WIDTH:]), relative_projection, count)
    pair_rep, left_edge, right_edge, gate_pre = pair_front(offset, outer, relative_projection, pairwise_projection, scalar_params, pair_mask)
    mixed = jnp.einsum('ikc,jkc->ijc', left_edge, low(right_edge), precision=EXACT_ARITHMETIC)
    distogram_sum = pair_tail(pairwise_projection, scalar_params, pair_rep, mixed, gate_pre, bins, pair_mask)
    return (hidden_letter_penalty, distogram_sum)

def reference(corrupted_letters, truth_categories, concealed_sites, existing_aligned, chain_ordinals, observed_sites, distance_bucket_truth, letter_lookup, alignment_projection, contracting_projection, relative_projection, pairwise_projection, scalar_params, running_mean_lookup, running_mean_alignment, running_mean_contracting, running_mean_relative, running_mean_pairwise, running_mean_scalars, running_square_lookup, running_square_alignment, running_square_contracting, running_square_relative, running_square_pairwise, running_square_scalars):
    aligned_factor = existing_aligned.astype(jnp.float32)
    masked_count = jnp.maximum(jnp.sum(concealed_sites.astype(jnp.float32) * aligned_factor[:, :, None]), 1.0)
    res_weight = observed_sites.astype(jnp.float32)
    distogram_count = jnp.maximum(jnp.sum(lax.optimization_barrier(jnp.sum(res_weight, axis=1)) ** 2), 1.0)

    def total(*network_parameters):
        masked_total = jnp.zeros((), jnp.float32)
        distogram_total = jnp.zeros((), jnp.float32)
        for protein_item in range(CHAIN_TOTAL_NUM):
            hidden_letter_penalty, distogram_sum = protein_totals(network_parameters, corrupted_letters[protein_item], truth_categories[protein_item], concealed_sites[protein_item], existing_aligned[protein_item], chain_ordinals[protein_item], observed_sites[protein_item], distance_bucket_truth[protein_item])
            masked_total = masked_total + hidden_letter_penalty
            distogram_total = distogram_total + distogram_sum
        return masked_total / masked_count + distogram_total / distogram_count
    network_parameters = (letter_lookup, alignment_projection, contracting_projection, relative_projection, pairwise_projection, scalar_params)
    running_means = (running_mean_lookup, running_mean_alignment, running_mean_contracting, running_mean_relative, running_mean_pairwise, running_mean_scalars)
    running_squares = (running_square_lookup, running_square_alignment, running_square_contracting, running_square_relative, running_square_pairwise, running_square_scalars)
    loss, pull = jax.vjp(total, *network_parameters)
    gradient_tree = pull(jnp.ones_like(loss))
    grad_norm = jnp.sqrt(sum((jnp.sum(item * item) for item in gradient_tree)))
    scale = jnp.minimum(1.0, CLIP_NORM / grad_norm)
    result = [loss, grad_norm]
    for index in range(6):
        result.extend(adam(network_parameters[index], running_means[index], running_squares[index], gradient_tree[index], scale))
    return tuple(result)
```

```python
import functools
from types import SimpleNamespace

import jax
import jax.numpy as jnp
from jax import lax
from jax.experimental import pallas as pl
from jax.experimental.pallas import tpu as pltpu
from jax.sharding import PartitionSpec as P

F32, BF16 = jnp.float32, jnp.bfloat16
MESH = pl.DeviceIdType.MESH
ROW, COL = "row", "col"
WA, WP, WO, LETTERS, BINS, REACH, HEADS, HEAD = 256, 128, 32, 23, 64, 32, 8, 32
UP = 1024
NREL = 2 * REACH + 1
AP = 32
RP = 128
EPS = 1e-05
NB, NS, NI, NJ = 2, 16, 8, 16
NM = NB * NS * NI
NP = NB * NI * NJ
BS = NB * NS
BI = NB * NI
DS = WO * NS
CLIP, RATE, B1, B2, STEP, ADAM_EPS, DECAY = 0.02, 0.05, 0.9, 0.999, 4, 1e-08, 0.01

NN = (((1,), (0,)), ((), ()))
NT = (((1,), (1,)), ((), ()))
TN = (((0,), (0,)), ((), ()))

ROWS = dict(
    up=8 * WA,
    back=2 * UP,
    o=2 * WA,
    eh=WA,
    tabs=8 * AP,
    outer=WO * WO,
    tri=5 * WP,
    out=WP,
    bd=WP,
    rel=72,
    bias=8,
    small=16,
)
TOTAL = 0
for name, count in ROWS.items():
    ROWS[name] = TOTAL
    TOTAL += count
ROWS = SimpleNamespace(**ROWS)
TOTAL = -(-TOTAL // 1024) * 1024


def mm(a, b, dims=NN):
    return lax.dot_general(a, b, dims, preferred_element_type=F32)


def split2(x):
    high = x.astype(BF16)
    return high, (x - high.astype(F32)).astype(BF16)


def split3(x):
    high = x.astype(BF16)
    rest = x - high.astype(F32)
    middle = rest.astype(BF16)
    return high, middle, (rest - middle.astype(F32)).astype(BF16)


def mm3(a, b, dims=NN):
    ah, al = split2(a)
    bh, bl = split2(b)
    return mm(ah, bh, dims) + (mm(al, bh, dims) + mm(ah, bl, dims))


def mm6(a, b, dims=NN):
    ah, am, al = split3(a)
    bh, bm, bl = split3(b)
    low = mm(al, bh, dims) + (mm(am, bm, dims) + mm(ah, bl, dims))
    return mm(ah, bh, dims) + ((mm(am, bh, dims) + mm(ah, bm, dims)) + low)


def mm2(a, exact, dims=NN):
    ah, al = split2(a)
    return mm(ah, exact, dims) + mm(al, exact, dims)


def mm2r(exact, b, dims=NN):
    bh, bl = split2(b)
    return mm(exact, bh, dims) + mm(exact, bl, dims)


def mm3r(exact, b, dims=NN):
    bh, bm, bl = split3(b)
    return mm(exact, bh, dims) + (mm(exact, bm, dims) + mm(exact, bl, dims))


def norm(x):
    centred = x - jnp.mean(x, axis=-1, keepdims=True)
    scale = lax.rsqrt(jnp.mean(centred * centred, axis=-1, keepdims=True) + EPS)
    return centred * scale, scale


def norm_back(grad, unit, scale):
    return scale * (
        grad
        - jnp.mean(grad, axis=-1, keepdims=True)
        - unit * jnp.mean(grad * unit, axis=-1, keepdims=True)
    )


def iota(shape, axis):
    return lax.broadcasted_iota(jnp.int32, shape, axis)


def head_mask(rows, per_row):
    shape = (rows, WA)
    return iota(shape, 0) // per_row == iota(shape, 1) // HEAD


def colsum(x):
    return jnp.sum(x, axis=0, keepdims=True)


def total_of(x):
    return jnp.sum(jnp.sum(x, axis=1, keepdims=True), axis=0, keepdims=True)


def scratch_plan(rows, cols):
    length = rows * NI
    shard = TOTAL // cols
    return dict(
        lk=((AP, WA), F32),
        weh=((WA, 128), F32),
        wbd=((WP, 128), F32),
        wrel=((RP, WP), F32),
        tail=((8, 128), F32),
        kb=((WA, WA), BF16),
        vb=((WA, WA), BF16),
        amat=((BS, NI, WA), F32),
        pam=((BS, NI, WA), F32),
        hm=((64, WA), F32),
        letx=((128, length), F32),
        bias=((BI, HEADS, length), F32),
        biash=((NB, 64, length), F32),
        prob=((BS, 64, length), F32),
        sg=((NM, WA), F32),
        att=((NM, WA), F32),
        xh1=((NM, WA), F32),
        r1=((NM, 1), F32),
        hid=((NM, UP), F32),
        rep=((NM, WA), F32),
        xh2=((NM, WA), F32),
        r2=((NM, 1), F32),
        dlog=((NM, 128), F32),
        left3=((NM, 96), BF16),
        mhi=((BI, DS, WP), BF16),
        mlo=((BI, DS, WP), BF16),
        rall=((NB, length, DS), BF16),
        prep=((NP, WP), F32),
        xh3=((NP, WP), F32),
        r3=((NP, 1), F32),
        proj=((NP, 5 * WP), F32),
        le=((BI * NJ, WP), F32),
        re=((NB * length * NJ, WP), F32),
        dm=((BI * length, WP), F32),
        gl=((BI, NJ, WP), F32),
        dr=((length, DS), F32),
        dmid=((NM, WA), F32),
        dbias=((NB, 64, length), F32),
        da=((BS, NI, WA), F32),
        dpam=((BS, NI, WA), F32),
        dtab=((BI, 16, RP), F32),
        dn=((NM, WA), F32),
        sum8=((8, WA), F32),
        grad=((TOTAL, 128), F32),
        lets=((8, 128), F32),
        letr=((rows, 8, 128), F32),
        cnts=((8, 128), F32),
        cntr=((cols, 8, 128), F32),
        rs=((NB, NI, DS), BF16),
        rr=((rows, NB, NI, DS), BF16),
        os=((cols, BI, NJ, WP), BF16),
        orr=((cols, BI, NJ, WP), BF16),
        es=((NB, NI, NJ, WP), BF16),
        er=((rows, NB, NI, NJ, WP), BF16),
        ts=((cols, BI, NJ, WP), BF16),
        tr=((cols, BI, NJ, WP), BF16),
        ds=((BI, NJ, WP), BF16),
        dsr=((cols, BI, NJ, WP), BF16),
        gs=((rows, NB, NI, NJ, WP), BF16),
        gr=((rows, NB, NI, NJ, WP), BF16),
        qs=((BI, NJ, WP), BF16),
        qr=((cols, BI, NJ, WP), BF16),
        us=((rows, NB, NI, DS), BF16),
        ur=((rows, NB, NI, DS), BF16),
        arc=((cols, shard, 128), F32),
        arr=((rows, shard // rows, 128), F32),
    )


LET, RIGHT, EDGE, GEDGE, GRIGHT, SUM_ROW, SHARE_ROW = range(7)
CNT, OUTER, TRI, GMIX, GOUTER, SUM_COL, SHARE_COL = range(7)
PHASES = 7


def main_kernel(rows, cols, names, *refs):
    (ints, lett, lines, lookup, w_a, w_c, w_r, w_p, scal) = refs[:9]
    gout, tout, aux = refs[9:12]
    s = SimpleNamespace(**dict(zip(names, refs[12:-4])))
    row_send, row_recv, col_send, col_recv = refs[-4:]
    length = rows * NI
    me_r, me_c = lax.axis_index(ROW), lax.axis_index(COL)

    barrier = pltpu.get_barrier_semaphore()
    for step in range(1, rows):
        pl.semaphore_signal(
            barrier,
            inc=1,
            device_id={ROW: lax.rem(me_r + step, rows), COL: me_c},
            device_id_type=MESH,
        )
    for step in range(1, cols):
        pl.semaphore_signal(
            barrier,
            inc=1,
            device_id={ROW: me_r, COL: lax.rem(me_c + step, cols)},
            device_id_type=MESH,
        )
    pl.semaphore_wait(barrier, rows + cols - 2)

    def exchange(along, phase, source, target):
        if along == ROW:
            count, me, number = rows, me_r, phase
            send, recv = row_send, row_recv
        else:
            count, me, number = cols, me_c, phase
            send, recv = col_send, col_recv
        copies = []
        for step in range(1, count):
            peer = lax.rem(me + step, count)
            origin = lax.rem(me + (count - step), count)
            where = (
                {ROW: peer, COL: me_c} if along == ROW else {ROW: me_r, COL: peer}
            )
            out = pltpu.make_async_remote_copy(
                src_ref=source(peer),
                dst_ref=target(me),
                send_sem=send.at[number, step],
                recv_sem=recv.at[number, step],
                device_id=where,
                device_id_type=MESH,
            )
            out.start()
            arriving = pltpu.make_async_remote_copy(
                src_ref=source(peer),
                dst_ref=target(origin),
                send_sem=send.at[number, step],
                recv_sem=recv.at[number, step],
                device_id=where,
                device_id_type=MESH,
            )
            copies.append((out, arriving))
        return copies

    def finish(copies):
        for out, arriving in copies:
            out.wait_send()
            arriving.wait_recv()

    s.lets[...] = lett[...]
    s.letr[me_r] = lett[...]
    flight = exchange(ROW, LET, lambda p: s.lets, lambda p: s.letr.at[p])

    def gain(begin, width):
        return scal[0:1, begin : begin + width]

    gain_row, gain_trans, gain_outer = gain(0, WA), gain(256, WA), gain(512, WA)
    gain_rel, gain_pair, gain_mixed = gain(768, WP), gain(896, WP), gain(1024, WP)
    bias_outer = gain(1152, WP)
    s.lk[...] = jnp.zeros((AP, WA), F32)
    s.lk[0:LETTERS, :] = lookup[...]
    s.weh[...] = jnp.zeros((WA, 128), F32)
    s.weh[:, 0:87] = w_a[:, 2048:2135]
    s.wbd[...] = jnp.zeros((WP, 128), F32)
    s.wbd[:, 0:72] = w_p[:, 768:840]
    s.wrel[...] = jnp.zeros((RP, WP), F32)
    s.wrel[0:NREL, :] = w_r[UP : UP + NREL, :]
    s.tail[...] = jnp.zeros((8, 128), F32)
    s.tail[0:1, 0:87] = scal[0:1, 1280:1367]

    table = s.lk[...]
    unit0, _ = norm(table)
    mapped = mm6(unit0 * gain_row, w_a[:, 0 : 4 * WA])
    tout[...] = mapped
    t_q = mapped[:, 0:WA] * HEAD ** (-0.5)
    t_k = mapped[:, WA : 2 * WA].astype(BF16).astype(F32)
    t_v = mapped[:, 2 * WA : 3 * WA].astype(BF16).astype(F32)
    t_g = jax.nn.sigmoid(mapped[:, 3 * WA :])
    square = head_mask(WA, AP)
    key_block = jnp.where(square, jnp.concatenate([t_k] * HEADS, axis=0), 0.0).astype(BF16)
    s.vb[...] = jnp.where(square, jnp.concatenate([t_v] * HEADS, axis=0), 0.0).astype(BF16)
    stacked = mm(jnp.concatenate(split3(t_q), axis=0), key_block, NT)
    score_table = stacked[0:AP] + (stacked[AP : 2 * AP] + stacked[2 * AP :])
    s.hm[...] = jnp.where(head_mask(64, NI), 1.0, 0.0)

    letter = ints[:, 0:1].astype(jnp.int32)
    triple = jnp.where(
        (iota((NM, 3 * AP), 1) % AP) == letter, 1.0, 0.0
    ).astype(BF16)

    def chosen(values):
        return mm(triple, jnp.concatenate(split3(values), axis=0))

    s.amat[...] = chosen(score_table).reshape(BS, NI, WA)
    start = chosen(table)
    s.sg[...] = chosen(t_g)

    unit_r, _ = norm(s.wrel[...])
    bias_table = mm3(unit_r * gain_rel, s.wbd[...]).T
    bias_parts = jnp.concatenate(split3(bias_table[0:8].astype(F32)), axis=0)

    def codes(index):
        return jnp.where(
            iota((RP, length), 0) == lines[index : index + 1, :].astype(jnp.int32), 1.0, 0.0
        ).astype(BF16)

    for b in range(NB):
        for i in range(NI):
            part = mm(bias_parts, codes(b * NI + i))
            part = part[0:8] + (part[8:16] + part[16:24])
            for h in range(HEADS):
                s.biash[b, h * NI + i : h * NI + i + 1, :] = part[h : h + 1, :]

    finish(flight)
    letters_all = s.letr[...].reshape(length, 128).T
    s.letx[...] = letters_all
    s.cnts[...] = jnp.broadcast_to(
        jnp.sum(letters_all[BS : BS + 1, :], axis=1, keepdims=True), (8, 128)
    )
    s.cntr[me_c] = s.cnts[...]
    count_flight = exchange(COL, CNT, lambda p: s.cnts, lambda p: s.cntr.at[p])

    def letter_codes(bs):
        row = s.letx[pl.ds(bs, 1), :].astype(jnp.int32)
        one = jnp.where(iota((AP, length), 0) == row, 1.0, 0.0)
        return jnp.concatenate([one] * HEADS, axis=0).astype(BF16)

    def spread(value):
        wide = jnp.broadcast_to(value[None], (HEADS, NI, WA)).reshape(64, WA)
        return wide * s.hm[...]

    def gather_heads(value):
        return jnp.sum((value * s.hm[...]).reshape(HEADS, NI, WA), axis=0)

    for b in range(NB):
        key_mask = lines[BI + b : BI + b + 1, :]

        @pl.loop(0, NS)
        def _(q):
            bs = b * NS + q
            code = letter_codes(bs)
            parts = split3(s.amat[bs])
            wide = jnp.concatenate([spread(p.astype(F32)).astype(BF16) for p in parts], axis=0)
            raw = mm(wide, code)
            scores = (raw[0:64] + (raw[64:128] + raw[128:192])) + s.biash[b]
            scores = jnp.where(key_mask > 0, scores, -1000000000.0)
            power = jnp.exp(scores - jnp.max(scores, axis=-1, keepdims=True))
            weight = power / jnp.sum(power, axis=-1, keepdims=True)
            s.prob[bs] = weight
            picked = mm(jnp.concatenate(split2(weight), axis=0), code, NT)
            s.pam[bs] = gather_heads(picked[0:64] + picked[64:128])

    att = mm2(s.pam[...].reshape(NM, WA), s.vb[...])
    s.att[...] = att
    mid = start + mm3(s.sg[...] * att, w_c[0:WA, :])
    unit1, scale1 = norm(mid)
    s.xh1[...] = unit1
    s.r1[...] = scale1
    hidden = jnp.maximum(mm3(unit1 * gain_trans, w_a[:, 4 * WA : 4 * WA + UP]), 0.0)
    s.hid[...] = hidden
    rep = mid + mm3(hidden, w_c[WA:, :])
    s.rep[...] = rep
    unit2, scale2 = norm(rep)
    s.xh2[...] = unit2
    s.r2[...] = scale2
    seq_weight = ints[:, 3:4]
    lane = iota((NM, 128), 1)
    edges = mm3(unit2 * gain_outer, s.weh[...]) * seq_weight

    right = jnp.where((lane >= 32) & (lane < 64), edges, 0.0).astype(BF16)
    spot = iota((128, DS), 0)
    repeat = jnp.where(spot - 32 == iota((128, DS), 1) // NS, 1.0, 0.0)
    repeat = jnp.where((spot >= 32) & (spot < 64), repeat, 0.0).astype(BF16)
    wide = mm(right, repeat)
    own_seq = (iota((NM, DS), 0) // NI) % NS == iota((NM, DS), 1) % NS
    wide = jnp.sum(jnp.where(own_seq, wide, 0.0).reshape(NB, NS, NI, DS), axis=1)
    s.rs[...] = wide.astype(BF16)
    s.rr[me_r] = s.rs[...]
    flight = exchange(ROW, RIGHT, lambda p: s.rs, lambda p: s.rr.at[p])

    finish(count_flight)
    masked = jnp.maximum(jnp.sum(s.cntr[...], axis=0)[0:1, 0:1], 1.0)
    logits = mm3(rep, s.weh[...]) + s.tail[0:1, :]
    valid = (lane >= 64) & (lane < 64 + LETTERS)
    top = jnp.max(jnp.where(valid, logits, -3e38), axis=-1, keepdims=True)
    power = jnp.where(valid, jnp.exp(jnp.where(valid, logits, top) - top), 0.0)
    whole = jnp.sum(power, axis=-1, keepdims=True)
    truth = lane - 64 == ints[:, 1:2].astype(jnp.int32)
    truth = truth & valid
    picked = jnp.sum(jnp.where(truth, logits, 0.0), axis=-1, keepdims=True)
    loss_mask = ints[:, 2:3]
    msa_sum = colsum((jnp.log(whole) + top - picked) * loss_mask)
    s.dlog[...] = (power / whole - jnp.where(truth, 1.0, 0.0)) * (loss_mask / masked)

    order_to = (iota((NM, NM), 0) // (NI * NS) == iota((NM, NM), 1) // (NI * NS)) & (
        (iota((NM, NM), 0) // NS) % NI == iota((NM, NM), 1) % NI
    )
    order_to = order_to & (iota((NM, NM), 0) % NS == (iota((NM, NM), 1) // NI) % NS)
    order = jnp.where(order_to, 1.0, 0.0).astype(BF16)
    left = mm3r(order, jnp.where(lane < 32, edges, 0.0))
    high, low = split2(left)
    high32, low32 = high.astype(F32), low.astype(F32)
    left3 = high32 + pltpu.roll(low32, 32, 1) + pltpu.roll(high32, 64, 1)
    s.left3[...] = left3[:, 0:96].astype(BF16)

    def outer_weight(d):
        return w_r[pl.ds(d, WO, stride=WO), :]

    for d in range(WO):
        wh, wl = split2(outer_weight(d))
        made = mm(s.left3[...], jnp.concatenate([wh, wh, wl], axis=0))
        mh, ml = split2(made.reshape(BI, NS, WP))
        s.mhi[:, d * NS : (d + 1) * NS, :] = mh
        s.mlo[:, d * NS : (d + 1) * NS, :] = ml

    finish(flight)
    for b in range(NB):
        s.rall[b] = s.rr[:, b].astype(F32).reshape(length, DS).astype(BF16)
    inv_count = [ints[b * NI * NJ : b * NI * NJ + 1, 7:8] for b in range(NB)]
    for b in range(NB):

        @pl.loop(0, NI)
        def _(i):
            bi = b * NI + i
            block = mm(s.rall[b], s.mhi[bi]) + mm(s.rall[b], s.mlo[bi])
            block = block * inv_count[b]
            for c in range(cols):
                s.os[c, bi] = block[c * NJ : (c + 1) * NJ].astype(BF16)

    s.orr[me_c] = s.os[me_c]
    finish(exchange(COL, OUTER, lambda p: s.os.at[p], lambda p: s.orr.at[p]))

    pair_lane = iota((NP, 128), 1)
    offset = ints[:, 6:7].astype(jnp.int32)
    pair_codes = jnp.where(pair_lane == offset, 1.0, 0.0).astype(BF16)
    outer = s.orr[0].astype(F32)
    for c in range(1, cols):
        outer = outer + s.orr[c].astype(F32)
    pair_rep = (mm3r(pair_codes, s.wrel[...]) + outer.reshape(NP, WP)) + bias_outer
    s.prep[...] = pair_rep
    unit3, scale3 = norm(pair_rep)
    s.xh3[...] = unit3
    s.r3[...] = scale3
    proj = mm3(unit3 * gain_pair, w_p[:, 0 : 5 * WP])
    pair_mask = ints[:, 5:6]
    sig1 = jax.nn.sigmoid(proj[:, WP : 2 * WP])
    sig2 = jax.nn.sigmoid(proj[:, 3 * WP : 4 * WP])
    sig3 = jax.nn.sigmoid(proj[:, 4 * WP :])
    s.proj[:, 0 : WP] = proj[:, 0:WP]
    s.proj[:, WP : 2 * WP] = sig1
    s.proj[:, 2 * WP : 3 * WP] = proj[:, 2 * WP : 3 * WP]
    s.proj[:, 3 * WP : 4 * WP] = sig2
    s.proj[:, 4 * WP :] = sig3
    s.le[...] = sig1 * proj[:, 0:WP] * pair_mask
    right_edge = (sig2 * proj[:, 2 * WP : 3 * WP] * pair_mask).astype(BF16)
    s.es[...] = right_edge.reshape(NB, NI, NJ, WP)
    s.er[me_r] = s.es[...]
    finish(exchange(ROW, EDGE, lambda p: s.es, lambda p: s.er.at[p]))
    for b in range(NB):
        for r in range(rows):
            begin = (b * length + r * NI) * NJ
            s.re[begin : begin + NI * NJ, :] = (
                s.er[r, b].astype(F32).reshape(NI * NJ, WP)
            )

    for b in range(NB):

        @pl.loop(0, NI)
        def _(i):
            bi = b * NI + i
            for c in range(cols):
                block = jnp.zeros((NJ, WP), F32)
                for k in range(NJ):
                    other = s.re[pl.ds((b * length + c * NJ) * NJ + k, NJ, stride=NJ), :]
                    block = block + s.le[pl.ds(bi * NJ + k, 1), :] * other
                s.ts[c, bi] = block.astype(BF16)

    s.tr[me_c] = s.ts[me_c]
    finish(exchange(COL, TRI, lambda p: s.ts.at[p], lambda p: s.tr.at[p]))

    mixed = s.tr[0].astype(F32)
    for c in range(1, cols):
        mixed = mixed + s.tr[c].astype(F32)
    unit4, scale4 = norm(mixed.reshape(NP, WP))
    w_out = w_p[:, 5 * WP : 6 * WP]
    moved = mm3(unit4 * gain_mixed, w_out)
    sig3 = s.proj[:, 4 * WP :]
    pair_out = s.prep[...] + sig3 * moved
    bins = mm3(pair_out, s.wbd[...]) + pltpu.roll(
        jnp.where(iota((8, 128), 1) < BINS, s.tail[...], 0.0), 8, 1
    )[0:1]
    valid = (pair_lane >= 8) & (pair_lane < 8 + BINS)
    top = jnp.max(jnp.where(valid, bins, -3e38), axis=-1, keepdims=True)
    power = jnp.where(valid, jnp.exp(jnp.where(valid, bins, top) - top), 0.0)
    whole = jnp.sum(power, axis=-1, keepdims=True)
    truth = (pair_lane - 8 == ints[:, 4:5].astype(jnp.int32)) & valid
    picked = jnp.sum(jnp.where(truth, bins, 0.0), axis=-1, keepdims=True)
    dist_sum = colsum((jnp.log(whole) + top - picked) * pair_mask)
    inv_dist = lines[BI + NB : BI + NB + 1, 0:1]
    dbins = (power / whole - jnp.where(truth, 1.0, 0.0)) * (pair_mask * inv_dist)

    def put(place, value, skip=0):
        base = place + skip
        height, width = value.shape
        for w in range(width // 128):
            s.grad[base + w * height : base + (w + 1) * height, :] = value[
                :, w * 128 : (w + 1) * 128
            ]

    def column_products(name, place):
        s.sum8[...] = jnp.zeros((8, WA), F32)

        @pl.loop(0, NM // 32)
        def _(q):
            some = pl.ds(pl.multiple_of(q * 32, 32), 32)
            product = s.dn[some, :] * name[some, :]
            s.sum8[...] += jnp.sum(product.reshape(4, 8, WA), axis=0)

        whole = colsum(s.sum8[...])
        for half in range(2):
            s.grad[small + place + half : small + place + half + 1, :] = whole[
                :, 128 * half : 128 * half + 128
            ]

    s.grad[ROWS.small :, :] = jnp.zeros((TOTAL - ROWS.small, 128), F32)
    small = ROWS.small
    put(ROWS.bd, mm3(pair_out, dbins, TN))
    dbias_dist = pltpu.roll(jnp.broadcast_to(colsum(dbins), (8, 128)), 120, 1)[0:1]
    dout = mm3(dbins, s.wbd[...], NT)
    dgate = dout * moved * (sig3 * (1.0 - sig3))
    dmoved = dout * sig3
    put(ROWS.out, mm3(unit4 * gain_mixed, dmoved, TN))
    dnormed = mm3(dmoved, w_out, NT)
    s.grad[small + 5 : small + 6, :] = colsum(dnormed * unit4)
    dmixed = norm_back(dnormed * gain_mixed, unit4, scale4)
    s.ds[...] = dmixed.astype(BF16).reshape(BI, NJ, WP)
    s.dsr[me_c] = s.ds[...]
    finish(exchange(COL, GMIX, lambda p: s.ds, lambda p: s.dsr.at[p]))
    for bi in range(BI):
        for c in range(cols):
            begin = bi * length + c * NJ
            s.dm[begin : begin + NJ, :] = s.dsr[c, bi].astype(F32)

    for b in range(NB):

        @pl.loop(0, rows)
        def _(r):
            for q in range(NI):
                block = jnp.zeros((NJ, WP), F32)
                for i in range(NI):
                    bi = b * NI + i
                    block = block + (
                        s.dm[pl.ds(bi * length + r * NI + q, 1), :]
                        * s.le[bi * NJ : (bi + 1) * NJ, :]
                    )
                s.gs[r, b, q] = block.astype(BF16)

    s.gr[me_r] = s.gs[me_r]
    flight = exchange(ROW, GEDGE, lambda p: s.gs.at[p], lambda p: s.gr.at[p])
    for b in range(NB):

        @pl.loop(0, NI)
        def _(i):
            bi = b * NI + i
            block = jnp.zeros((NJ, WP), F32)
            for j in range(length):
                begin = (b * length + j) * NJ
                block = block + (
                    s.dm[pl.ds(bi * length + j, 1), :] * s.re[begin : begin + NJ, :]
                )
            s.gl[bi] = block

    finish(flight)
    dright = s.gr[0].astype(F32)
    for r in range(1, rows):
        dright = dright + s.gr[r].astype(F32)
    dright = dright.reshape(NP, WP) * pair_mask
    dleft = s.gl[...].reshape(NP, WP) * pair_mask
    p1, sig1 = s.proj[:, 0:WP], s.proj[:, WP : 2 * WP]
    p2, sig2 = s.proj[:, 2 * WP : 3 * WP], s.proj[:, 3 * WP : 4 * WP]
    dproj = jnp.concatenate(
        [
            dleft * sig1,
            dleft * p1 * (sig1 * (1.0 - sig1)),
            dright * sig2,
            dright * p2 * (sig2 * (1.0 - sig2)),
            dgate,
        ],
        axis=1,
    )
    unit3 = s.xh3[...]
    put(ROWS.tri, mm3(unit3 * gain_pair, dproj, TN))
    dnormed = mm3(dproj, w_p[:, 0 : 5 * WP], NT)
    s.grad[small + 4 : small + 5, :] = colsum(dnormed * unit3)
    drep = dout + norm_back(dnormed * gain_pair, unit3, s.r3[...])
    s.grad[small + 6 : small + 7, :] = colsum(drep)
    s.grad[ROWS.rel : ROWS.rel + 72, :] = mm2r(pair_codes, drep, TN)[0:72]
    s.qs[...] = drep.astype(BF16).reshape(BI, NJ, WP)
    s.qr[me_c] = s.qs[...]
    finish(exchange(COL, GOUTER, lambda p: s.qs, lambda p: s.qr.at[p]))

    for b in range(NB):
        turned = s.rall[b].astype(F32).T.astype(BF16)
        s.dr[...] = jnp.zeros((length, DS), F32)

        @pl.loop(0, NI)
        def _(i):
            bi = b * NI + i
            block = jnp.concatenate([s.qr[c, bi] for c in range(cols)], axis=0)
            s.dr[...] += mm(block, s.mhi[bi], NT) + mm(block, s.mlo[bi], NT)
            mh, ml = split2(mm(turned, block) * inv_count[b])
            s.mhi[bi] = mh
            s.mlo[bi] = ml

        for r in range(rows):
            s.us[r, b] = (s.dr[r * NI : (r + 1) * NI, :] * inv_count[b]).astype(BF16)
    s.ur[me_r] = s.us[me_r]
    flight = exchange(ROW, GRIGHT, lambda p: s.us.at[p], lambda p: s.ur.at[p])

    left3 = s.left3[...].astype(F32).T.astype(BF16)
    left_both, left_high = left3[0:64], left3[0:32]
    dleft = jnp.zeros((NM, WO), F32)
    for d in range(WO):
        wh, wl = split2(outer_weight(d))
        mh = s.mhi[:, d * NS : (d + 1) * NS, :].reshape(NM, WP)
        ml = s.mlo[:, d * NS : (d + 1) * NS, :].reshape(NM, WP)
        dleft = dleft + (mm(mh, wh, NT) + (mm(ml, wh, NT) + mm(mh, wl, NT)))
        made = mm(left_both, mh)
        s.grad[pl.ds(ROWS.outer + d, WO, stride=WO), :] = (
            made[0:32] + made[32:64] + mm(left_high, ml)
        )
    dleft = mm3r(order, dleft, TN)

    finish(flight)
    dright = s.ur[0].astype(F32)
    for r in range(1, rows):
        dright = dright + s.ur[r].astype(F32)
    wide = jnp.broadcast_to(dright[:, None], (NB, NS, NI, DS)).reshape(NM, DS)
    dedges = mm2(jnp.where(own_seq, wide, 0.0), repeat, NT)
    dedges = (dedges + jnp.concatenate([dleft, jnp.zeros((NM, 96), F32)], axis=1)) * seq_weight
    unit2, rep = s.xh2[...], s.rep[...]
    dlog = s.dlog[...]
    put(ROWS.eh, mm3(unit2 * gain_outer, dedges, TN) + mm3(rep, dlog, TN))
    s.dn[...] = mm3(dedges, s.weh[...], NT)
    dnormed = s.dn[...]
    column_products(s.xh2, 2)
    drep = mm3(dlog, s.weh[...], NT) + norm_back(dnormed * gain_outer, unit2, s.r2[...])
    hidden = s.hid[...]
    put(ROWS.back, mm3(hidden, drep, TN))
    dhidden = jnp.where(hidden > 0, mm3(drep, w_c[WA:, :], NT), 0.0)
    unit1 = s.xh1[...]
    put(ROWS.up, mm3(unit1 * gain_trans, dhidden, TN))
    s.dn[...] = mm3(dhidden, w_a[:, 4 * WA : 4 * WA + UP], NT)
    dnormed = s.dn[...]
    column_products(s.xh1, 0)
    dmid = drep + norm_back(dnormed * gain_trans, unit1, s.r1[...])
    sg, att = s.sg[...], s.att[...]
    put(ROWS.o, mm3(sg * att, dmid, TN))
    dgated = mm3(dmid, w_c[0:WA, :], NT)
    single = triple[:, 0:AP]
    put(ROWS.tabs, mm2r(single, dmid, TN), 6 * AP)
    put(ROWS.tabs, mm2r(single, dgated * att, TN), 4 * AP)
    datt = dgated * sg

    pam = s.pam[...].reshape(NM, WA)
    blocks = jnp.where(head_mask(WA, AP), mm3(pam, datt, TN), 0.0)
    put(ROWS.tabs, jnp.sum(blocks.reshape(HEADS, AP, WA), axis=0), 2 * AP)
    s.dpam[...] = mm2(datt, s.vb[...], NT).reshape(BS, NI, WA)
    for b in range(NB):
        key_mask = lines[BI + b : BI + b + 1, :]
        s.dbias[b] = jnp.zeros((64, length), F32)

        @pl.loop(0, NS)
        def _(q):
            bs = b * NS + q
            code = letter_codes(bs)
            parts = split2(s.dpam[bs])
            wide = jnp.concatenate([spread(p.astype(F32)).astype(BF16) for p in parts], axis=0)
            raw = mm(wide, code)
            dweight = raw[0:64] + raw[64:128]
            weight = s.prob[bs]
            inner = jnp.sum(weight * dweight, axis=-1, keepdims=True)
            dscore = jnp.where(key_mask > 0, weight * (dweight - inner), 0.0)
            s.dbias[b] += dscore
            back = mm(jnp.concatenate(split2(dscore), axis=0), code, NT)
            s.da[bs] = gather_heads(back[0:64] + back[64:128])

    put(ROWS.tabs, mm2r(single, s.da[...].reshape(NM, WA), TN))
    for b in range(NB):
        for i in range(NI):
            part = jnp.concatenate(
                [s.dbias[b, h * NI + i : h * NI + i + 1, :] for h in range(HEADS)], axis=0
            )
            s.dtab[b * NI + i] = mm(
                jnp.concatenate(split2(part), axis=0), codes(b * NI + i), NT
            )
    s.grad[ROWS.bias : ROWS.bias + 8, :] = jnp.sum(
        s.dtab[...].reshape(2 * BI, 8, RP), axis=0
    )

    lane1 = iota((1, 128), 1)
    s.grad[small + 7 : small + 8, :] = jnp.where(lane1 < BINS, dbias_dist, colsum(dlog))
    s.grad[small + 8 : small + 9, :] = jnp.where(
        lane1 == 0, msa_sum, jnp.where(lane1 == 1, dist_sum, 0.0)
    )
    aux[...] = jnp.broadcast_to(masked, (8, 128))

    shard = TOTAL // cols
    piece = shard // rows
    s.arc[me_c] = s.grad[pl.ds(pl.multiple_of(me_c * shard, 8), shard), :]
    finish(
        exchange(
            COL,
            SUM_COL,
            lambda p: s.grad.at[pl.ds(pl.multiple_of(p * shard, 8), shard)],
            lambda p: s.arc.at[p],
        )
    )
    summed = s.arc[0]
    for c in range(1, cols):
        summed = summed + s.arc[c]
    s.arc[0] = summed
    s.arr[me_r] = s.arc[0, pl.ds(pl.multiple_of(me_r * piece, 8), piece), :]
    finish(
        exchange(
            ROW,
            SUM_ROW,
            lambda p: s.arc.at[0, pl.ds(pl.multiple_of(p * piece, 8), piece)],
            lambda p: s.arr.at[p],
        )
    )
    summed = s.arr[0]
    for r in range(1, rows):
        summed = summed + s.arr[r]
    mine = pl.ds(pl.multiple_of(me_c * shard + me_r * piece, 8), piece)
    gout[mine, :] = summed

    def spot_row(p):
        return gout.at[pl.ds(pl.multiple_of(me_c * shard + p * piece, 8), piece)]

    def spot_col(p):
        return gout.at[pl.ds(pl.multiple_of(p * shard, 8), shard)]

    finish(exchange(ROW, SHARE_ROW, lambda p: spot_row(me_r), spot_row))
    finish(exchange(COL, SHARE_COL, lambda p: spot_col(me_c), spot_col))


def post_kernel(*refs):
    gout, tout, aux = refs[:3]
    weights, means, squares = refs[3:9], refs[9:15], refs[15:21]
    w_lines, new = refs[21], refs[22:40]
    report = refs[40]
    lk, wrel, wbd, g_a, g_small, g_rel, g_bd = refs[41:]
    lookup, w_a, w_c, w_r, w_p, scal = weights

    lk[...] = jnp.zeros((AP, WA), F32)
    lk[0:LETTERS, :] = lookup[...]
    wrel[...] = jnp.zeros((RP, WP), F32)
    wrel[0:NREL, :] = w_r[UP : UP + NREL, :]
    wbd[...] = jnp.zeros((WP, 128), F32)
    wbd[:, 0:72] = w_p[:, 768:840]

    def table(number):
        base = ROWS.tabs + 2 * number * AP
        return jnp.concatenate(
            [gout[base : base + AP, :], gout[base + AP : base + 2 * AP, :]], axis=1
        )

    dscore, dvalue, dgate, dstart = table(0), table(1), table(2), table(3)
    mapped = tout[...]
    t_q = mapped[:, 0:WA] * HEAD ** (-0.5)
    t_k = mapped[:, WA : 2 * WA].astype(BF16).astype(F32)
    t_g = jax.nn.sigmoid(mapped[:, 3 * WA :])
    square = head_mask(WA, AP)
    key_block = jnp.where(square, jnp.concatenate([t_k] * HEADS, axis=0), 0.0).astype(BF16)
    dq = mm2(dscore, key_block) * HEAD ** (-0.5)
    dk = jnp.where(square, mm3(dscore, t_q, TN), 0.0)
    dk = jnp.sum(dk.reshape(HEADS, AP, WA), axis=0)
    dg = dgate * (t_g * (1.0 - t_g))
    dmapped = jnp.concatenate([dq, dk, dvalue, dg], axis=1)
    unit0, scale0 = norm(lk[...])
    gain_row = scal[0:1, 0:WA]
    g_a[...] = mm3(unit0 * gain_row, dmapped, TN)
    dnormed = mm3(dmapped, w_a[:, 0 : 4 * WA], NT)
    dgain_row = colsum(dnormed * unit0)
    g_lookup = dstart + norm_back(dnormed * gain_row, unit0, scale0)

    unit_r, scale_r = norm(wrel[...])
    gain_rel = scal[0:1, 768:896]
    dtable = jnp.concatenate(
        [gout[ROWS.bias : ROWS.bias + 8, :], jnp.zeros((120, 128), F32)], axis=0
    ).T
    lane = iota((WP, 128), 1)
    d_bias = mm3(unit_r * gain_rel, dtable, TN)
    g_bd[...] = jnp.where(lane < 8, d_bias, gout[ROWS.bd : ROWS.bd + WP, :])
    dnormed = mm3(dtable, wbd[...], NT)
    dgain_rel = colsum(dnormed * unit_r)
    g_rel[...] = gout[ROWS.rel : ROWS.rel + 72, :] + norm_back(
        dnormed * gain_rel, unit_r, scale_r
    )[0:72]

    base = ROWS.small
    g_small[...] = jnp.zeros_like(g_small)
    g_small[0:1, 0:WA] = dgain_row
    for place, row in enumerate((0, 1, 2, 3)):
        g_small[0:1, 256 + 128 * place : 384 + 128 * place] = gout[base + row : base + row + 1, :]
    g_small[0:1, 768:896] = dgain_rel
    g_small[0:1, 896:1024] = gout[base + 4 : base + 5, :]
    g_small[0:1, 1024:1152] = gout[base + 5 : base + 6, :]
    g_small[0:1, 1152:1280] = gout[base + 6 : base + 7, :]
    tail_lane = iota((1, 128), 1)
    g_small[0:1, 1280:1408] = jnp.where(tail_lane < 87, gout[base + 7 : base + 8, :], 0.0)

    rel_row = iota((72, 128), 0)
    direct = gout[0 : ROWS.tabs, :]
    squares_sum = total_of(direct * direct)
    direct = gout[ROWS.outer : ROWS.bd, :]
    squares_sum = squares_sum + total_of(direct * direct)
    for part in (
        g_a[...],
        g_lookup[0:LETTERS],
        jnp.where(rel_row < NREL, g_rel[...], 0.0),
        g_bd[...],
        g_small[...],
    ):
        squares_sum = squares_sum + total_of(part * part)
    size = jnp.sqrt(squares_sum)
    scale = jnp.minimum(1.0, CLIP / size)

    def adam(which, where, grad):
        clipped = grad * scale
        weight = weights[which][where]
        moment = B1 * means[which][where] + (1.0 - B1) * clipped
        second = B2 * squares[which][where] + (1.0 - B2) * clipped * clipped
        step = (moment / (1.0 - B1**STEP)) / (jnp.sqrt(second / (1.0 - B2**STEP)) + ADAM_EPS)
        new[3 * which][where] = weight - RATE * (step + DECAY * weight)
        new[3 * which + 1][where] = moment
        new[3 * which + 2][where] = second

    every = slice(None)
    adam(0, (every, every), g_lookup[0:LETTERS])
    adam(1, (every, slice(0, 4 * WA)), g_a[...])
    for w in range(8):
        begin = ROWS.up + w * WA
        adam(1, (every, slice(1024 + 128 * w, 1152 + 128 * w)), gout[begin : begin + WA, :])
    adam(1, (every, slice(2048, 2135)), gout[ROWS.eh : ROWS.eh + WA, 0:87])
    for w in range(2):
        half = slice(128 * w, 128 * w + 128)
        begin = ROWS.o + w * WA
        adam(2, (slice(0, WA), half), gout[begin : begin + WA, :])
        begin = ROWS.back + w * UP
        adam(2, (slice(WA, WA + UP), half), gout[begin : begin + UP, :])
    adam(3, (slice(0, UP), every), gout[ROWS.outer : ROWS.outer + UP, :])
    adam(3, (slice(UP, UP + NREL), every), g_rel[0:NREL, :])
    for w in range(5):
        begin = ROWS.tri + w * WP
        adam(4, (every, slice(128 * w, 128 * w + 128)), gout[begin : begin + WP, :])
    adam(4, (every, slice(640, 768)), gout[ROWS.out : ROWS.out + WP, :])
    adam(4, (every, slice(768, 840)), g_bd[:, 0:72])
    adam(5, (every, every), g_small[0:1, 0:1367])

    sums = gout[base + 8 : base + 9, :]
    inv_dist = w_lines[BI + NB : BI + NB + 1, 0:1]
    loss = sums[:, 0:1] / aux[0:1, 0:1] + sums[:, 1:2] * inv_dist
    report[...] = jnp.where(iota((8, 128), 1) == 0, loss, size)


def vmem():
    return pl.BlockSpec(memory_space=pltpu.VMEM)


def per_device(rows, cols, *arrays):
    (letters, truth, concealed, existing, ordinals, observed, bins) = arrays[:7]
    weights, means, squares = arrays[7:13], arrays[13:19], arrays[19:25]
    length = rows * NI
    row_id, col_id = lax.axis_index(ROW), lax.axis_index(COL)
    seq_all = existing.astype(F32)
    seq_here = lax.dynamic_slice_in_dim(seq_all, col_id * NS, NS, 1)
    loss_mask = concealed.astype(F32) * seq_here[:, :, None]
    sites = observed.astype(F32)
    index_rows = lax.dynamic_slice_in_dim(ordinals, row_id * NI, NI, 1)
    index_cols = lax.dynamic_slice_in_dim(ordinals, col_id * NJ, NJ, 1)
    mask_rows = lax.dynamic_slice_in_dim(sites, row_id * NI, NI, 1)
    mask_cols = lax.dynamic_slice_in_dim(sites, col_id * NJ, NJ, 1)

    def offsets(left, right):
        return jnp.clip(left[:, :, None] - right[:, None, :], -REACH, REACH) + REACH

    inverse = 1.0 / (jnp.sum(seq_all, axis=1) + 1.0)
    dist_count = jnp.maximum(jnp.sum(jnp.sum(sites, axis=1) ** 2), 1.0)
    shape = (NB, NS, NI)
    pair_shape = (NB, NI, NJ)
    columns = (
        letters.astype(F32),
        truth.astype(F32),
        loss_mask,
        jnp.broadcast_to(seq_here[:, :, None], shape),
        bins.astype(F32),
        mask_rows[:, :, None] * mask_cols[:, None, :],
        offsets(index_rows, index_cols).astype(F32),
        jnp.broadcast_to(inverse[:, None, None], pair_shape),
    )
    ints = jnp.stack([c.reshape(NM) for c in columns], axis=1)
    lett = jnp.concatenate(
        [
            jnp.transpose(letters.astype(F32), (2, 0, 1)).reshape(NI, BS),
            jnp.sum(loss_mask, axis=(0, 1))[:, None],
            jnp.zeros((NI, 127 - BS), F32),
        ],
        axis=1,
    )
    lines = jnp.concatenate(
        [
            offsets(index_rows, ordinals).astype(F32).reshape(BI, length),
            sites,
            jnp.broadcast_to(1.0 / dist_count, (8 - NB, length)),
        ],
        axis=0,
    )
    flat = [w if w.ndim == 2 else w[None] for w in weights]
    plan = scratch_plan(rows, cols)
    names = tuple(plan)
    gout, tout, aux = pl.pallas_call(
        functools.partial(main_kernel, rows, cols, names),
                out_shape=(
            jax.ShapeDtypeStruct((TOTAL, 128), F32),
            jax.ShapeDtypeStruct((AP, 4 * WA), F32),
            jax.ShapeDtypeStruct((8, 128), F32),
        ),
        in_specs=[vmem()] * 9,
        out_specs=(vmem(), vmem(), vmem()),
        scratch_shapes=[pltpu.VMEM(dims, kind) for dims, kind in plan.values()]
        + [
            pltpu.SemaphoreType.DMA((PHASES, rows)),
            pltpu.SemaphoreType.DMA((PHASES, rows)),
            pltpu.SemaphoreType.DMA((PHASES, cols)),
            pltpu.SemaphoreType.DMA((PHASES, cols)),
        ],
        compiler_params=pltpu.CompilerParams(
            collective_id=0, has_side_effects=True, vmem_limit_bytes=60 * 2**20
        ),
    )(ints, lett, lines, *flat)

    flat_means = [w if w.ndim == 2 else w[None] for w in means]
    flat_squares = [w if w.ndim == 2 else w[None] for w in squares]
    shapes = []
    for w in flat:
        shapes += [jax.ShapeDtypeStruct(w.shape, F32)] * 3
    result = pl.pallas_call(
        post_kernel,
                out_shape=tuple(shapes) + (jax.ShapeDtypeStruct((8, 128), F32),),
        in_specs=[vmem()] * 22,
        out_specs=tuple([vmem()] * 19),
        scratch_shapes=[
            pltpu.VMEM((AP, WA), F32),
            pltpu.VMEM((RP, WP), F32),
            pltpu.VMEM((WP, 128), F32),
            pltpu.VMEM((WA, 4 * WA), F32),
            pltpu.VMEM((8, 1408), F32),
            pltpu.VMEM((72, 128), F32),
            pltpu.VMEM((WP, 128), F32),
        ],
        compiler_params=pltpu.CompilerParams(vmem_limit_bytes=60 * 2**20),
    )(gout, tout, aux, *flat, *flat_means, *flat_squares, lines)
    report = result[18]
    outs = [report[0, 0], report[0, 1]]
    for value in result[:15]:
        outs.append(value)
    for value in result[15:18]:
        outs.append(value[0])
    return tuple(outs)


def solution(mesh):
    rows, cols = mesh.shape[ROW], mesh.shape[COL]
    placed = (
        (P(None, COL, ROW),) * 3 + (P(),) * 3 + (P(None, ROW, COL),) + (P(),) * 18
    )
    return jax.shard_map(
        functools.partial(per_device, rows, cols),
        mesh=mesh,
        in_specs=placed,
        out_specs=(P(),) * 20,
        check_vma=False,
    )
```

```python
import functools
from types import SimpleNamespace

import jax
import jax.numpy as jnp
from jax import lax
from jax.experimental import pallas as pl
from jax.experimental.pallas import tpu as pltpu
from jax.sharding import PartitionSpec as P

F32, BF16 = jnp.float32, jnp.bfloat16
MESH = pl.DeviceIdType.MESH
ROW, COL = "row", "col"
WA, WP, WO, LETTERS, BINS, REACH, HEADS, HEAD = 256, 128, 32, 23, 64, 32, 8, 32
UP = 1024
NREL = 2 * REACH + 1
AP = 32
RP = 128
EPS = 1e-05
NB, NS, NI, NJ = 2, 16, 8, 16
NM = NB * NS * NI
NP = NB * NI * NJ
BS = NB * NS
BI = NB * NI
DS = WO * NS
CLIP, RATE, B1, B2, STEP, ADAM_EPS, DECAY = 0.02, 0.05, 0.9, 0.999, 4, 1e-08, 0.01

MAIN_VMEM, POST_VMEM = 44 * 2**20, 44 * 2**20

NN = (((1,), (0,)), ((), ()))
NT = (((1,), (1,)), ((), ()))
TN = (((0,), (0,)), ((), ()))

ROWS = dict(
    up=2 * UP,
    back=2 * UP,
    o=2 * WA,
    eh=WA,
    tabs=8 * AP,
    outer=WO * WO,
    tri=5 * WP,
    out=WP,
    bd=WP,
    rel=72,
    bias=8,
    small=16,
)
TOTAL = 0
for name, count in ROWS.items():
    ROWS[name] = TOTAL
    TOTAL += count
ROWS = SimpleNamespace(**ROWS)
TOTAL = -(-TOTAL // 1024) * 1024


def mm(a, b, dims=NN):
    return lax.dot_general(a, b, dims, preferred_element_type=F32)


def split2(x):
    high = x.astype(BF16)
    return high, (x - high.astype(F32)).astype(BF16)


def split3(x):
    high = x.astype(BF16)
    rest = x - high.astype(F32)
    middle = rest.astype(BF16)
    return high, middle, (rest - middle.astype(F32)).astype(BF16)


def mm3(a, b, dims=NN):
    ah, al = split2(a)
    bh, bl = split2(b)
    return mm(ah, bh, dims) + (mm(al, bh, dims) + mm(ah, bl, dims))


def mm6(a, b, dims=NN):
    ah, am, al = split3(a)
    bh, bm, bl = split3(b)
    low = mm(al, bh, dims) + (mm(am, bm, dims) + mm(ah, bl, dims))
    return mm(ah, bh, dims) + ((mm(am, bh, dims) + mm(ah, bm, dims)) + low)


def mm2(a, exact, dims=NN):
    ah, al = split2(a)
    return mm(ah, exact, dims) + mm(al, exact, dims)


def mm2r(exact, b, dims=NN):
    bh, bl = split2(b)
    return mm(exact, bh, dims) + mm(exact, bl, dims)


def mm3r(exact, b, dims=NN):
    bh, bm, bl = split3(b)
    return mm(exact, bh, dims) + (mm(exact, bm, dims) + mm(exact, bl, dims))


def norm(x):
    centred = x - jnp.mean(x, axis=-1, keepdims=True)
    scale = lax.rsqrt(jnp.mean(centred * centred, axis=-1, keepdims=True) + EPS)
    return centred * scale, scale


def norm_back(grad, unit, scale):
    return scale * (
        grad
        - jnp.mean(grad, axis=-1, keepdims=True)
        - unit * jnp.mean(grad * unit, axis=-1, keepdims=True)
    )


def iota(shape, axis):
    return lax.broadcasted_iota(jnp.int32, shape, axis)


def head_mask(rows, per_row):
    shape = (rows, WA)
    return iota(shape, 0) // per_row == iota(shape, 1) // HEAD


def colsum(x):
    return jnp.sum(x, axis=0, keepdims=True)


def total_of(x):
    return jnp.sum(jnp.sum(x, axis=1, keepdims=True), axis=0, keepdims=True)


def scratch_plan(rows, cols):
    length = rows * NI
    shard = TOTAL // cols
    return dict(
        lk=((AP, WA), F32),
        weh=((128, WA), F32),
        wbd=((128, WP), F32),
        seqw=((NM, 1), F32),
        lmask=((NM, 1), F32),
        truth=((NM, 1), F32),
        target=((NP, 1), F32),
        pmask=((NP, 1), F32),
        offset=((NP, 1), F32),
        codes=((BI, length), F32),
        sites=((8, length), F32),
        wrel=((RP, WP), F32),
        tail=((8, 128), F32),
        kb=((WA, WA), BF16),
        vb=((WA, WA), BF16),
        amat=((BS, NI, WA), F32),
        pam=((BS, NI, WA), F32),
        hm=((64, WA), F32),
        letx=((128, length), F32),
        biash=((NB, 64, length), F32),
        prob=((BS, 64, length), F32),
        sg=((NM, WA), F32),
        att=((NM, WA), F32),
        xh1=((NM, WA), F32),
        r1=((NM, 1), F32),
        hid=((NM, UP), F32),
        rep=((NM, WA), F32),
        xh2=((NM, WA), F32),
        r2=((NM, 1), F32),
        dlog=((NM, 128), F32),
        left3=((NM, 96), BF16),
        mhi=((BI, DS, WP), BF16),
        mlo=((BI, DS, WP), BF16),
        rall=((NB, length, DS), BF16),
        prep=((NP, WP), F32),
        xh3=((NP, WP), F32),
        r3=((NP, 1), F32),
        proj=((NP, 5 * WP), F32),
        le=((BI * NJ, WP), F32),
        re=((NB * length * NJ, WP), F32),
        dm=((BI * length, WP), F32),
        gl=((BI, NJ, WP), F32),
        dr=((length, DS), F32),
        dmid=((NM, WA), F32),
        dbias=((NB, 64, length), F32),
        da=((BS, NI, WA), F32),
        dpam=((BS, NI, WA), F32),
        dtab=((BI, 16, RP), F32),
        dn=((NM, WA), F32),
        sum8=((8, WA), F32),
        grad=((TOTAL, 128), F32),
        lets=((8, 128), F32),
        letr=((rows, 8, 128), F32),
        cnts=((8, 128), F32),
        cntr=((cols, 8, 128), F32),
        rs=((NB, NI, DS), BF16),
        rr=((rows, NB, NI, DS), BF16),
        os=((cols, BI, NJ, WP), BF16),
        orr=((cols, BI, NJ, WP), BF16),
        es=((NB, NI, NJ, WP), BF16),
        er=((rows, NB, NI, NJ, WP), BF16),
        ts=((cols, BI, NJ, WP), BF16),
        tr=((cols, BI, NJ, WP), BF16),
        ds=((BI, NJ, WP), BF16),
        dsr=((cols, BI, NJ, WP), BF16),
        gs=((rows, NB, NI, NJ, WP), BF16),
        gr=((rows, NB, NI, NJ, WP), BF16),
        qs=((BI, NJ, WP), BF16),
        qr=((cols, BI, NJ, WP), BF16),
        us=((rows, NB, NI, DS), BF16),
        ur=((rows, NB, NI, DS), BF16),
        arc=((cols, shard, 128), F32),
        arr=((rows, shard // rows, 128), F32),
    )


LET, RIGHT, EDGE, GEDGE, GRIGHT, SUM_ROW, SHARE_ROW = range(7)
CNT, OUTER, TRI, GMIX, GOUTER, SUM_COL, SHARE_COL = range(7)
PHASES = 7


def main_kernel(rows, cols, names, *refs):
    (letters, truths, hidden_sites, existing, ordinals, observed, targets) = refs[:7]
    (lookup, w_a, w_c, w_r, w_p, scal) = refs[7:13]
    gout, tout, aux = refs[13:16]
    s = SimpleNamespace(**dict(zip(names, refs[16:-4])))
    row_send, row_recv, col_send, col_recv = refs[-4:]
    length = rows * NI
    me_r, me_c = lax.axis_index(ROW), lax.axis_index(COL)

    barrier = pltpu.get_barrier_semaphore()
    for step in range(1, rows):
        pl.semaphore_signal(
            barrier,
            inc=1,
            device_id={ROW: lax.rem(me_r + step, rows), COL: me_c},
            device_id_type=MESH,
        )
    for step in range(1, cols):
        pl.semaphore_signal(
            barrier,
            inc=1,
            device_id={ROW: me_r, COL: lax.rem(me_c + step, cols)},
            device_id_type=MESH,
        )
    pl.semaphore_wait(barrier, rows + cols - 2)

    def exchange(along, phase, source, target):
        if along == ROW:
            count, me, number = rows, me_r, phase
            send, recv = row_send, row_recv
        else:
            count, me, number = cols, me_c, phase
            send, recv = col_send, col_recv
        copies = []
        for step in range(1, count):
            peer = lax.rem(me + step, count)
            origin = lax.rem(me + (count - step), count)
            where = (
                {ROW: peer, COL: me_c} if along == ROW else {ROW: me_r, COL: peer}
            )
            out = pltpu.make_async_remote_copy(
                src_ref=source(peer),
                dst_ref=target(me),
                send_sem=send.at[number, step],
                recv_sem=recv.at[number, step],
                device_id=where,
                device_id_type=MESH,
            )
            out.start()
            arriving = pltpu.make_async_remote_copy(
                src_ref=source(peer),
                dst_ref=target(origin),
                send_sem=send.at[number, step],
                recv_sem=recv.at[number, step],
                device_id=where,
                device_id_type=MESH,
            )
            copies.append((out, arriving))
        return copies

    def finish(copies):
        for out, arriving in copies:
            out.wait_send()
            arriving.wait_recv()

    here = existing[...].astype(F32)
    sites = observed[...].astype(F32)
    numbers = ordinals[...].astype(F32)

    def by_protein(values, count, each):
        wide = (count, values.shape[1])
        return jnp.where(iota(wide, 0) // each == 0, values[0:1], values[1:2])

    def at_lane(values, lanes):
        return jnp.sum(jnp.where(iota(values.shape, 1) == lanes, values, 0.0), axis=1, keepdims=True)

    row_m, row_p = iota((NM, 1), 0), iota((NP, 1), 0)
    seq_m, res_m = (row_m // NI) % NS, row_m % NI
    spread_m = jnp.where(
        iota((NM, BI), 1) == (iota((NM, BI), 0) // (NI * NS)) * NI + iota((NM, BI), 0) % NI, 1.0, 0.0
    ).astype(BF16)
    spread_p = jnp.where(iota((NP, BI), 1) == iota((NP, BI), 0) // NJ, 1.0, 0.0).astype(BF16)

    def column_m(values):
        wide = mm(spread_m, values[...].reshape(BI, NS).astype(F32).astype(BF16))
        return at_lane(wide, seq_m)

    seq_weight = at_lane(by_protein(here, NM, NI * NS), me_c * NS + seq_m)
    letter = column_m(letters)
    loss_mask = column_m(hidden_sites) * seq_weight
    s.seqw[...] = seq_weight
    s.lmask[...] = loss_mask
    s.truth[...] = column_m(truths)
    s.target[...] = at_lane(
        mm(spread_p, targets[...].reshape(BI, NJ).astype(F32).astype(BF16)), row_p % NJ
    )

    s.lets[...] = jnp.where(
        (iota((NI, 128), 0) == 0) & (iota((NI, 128), 1) == BS), total_of(loss_mask), 0.0
    )
    for b in range(NB):
        s.lets[:, b * NS : (b + 1) * NS] = letters[b].astype(F32)
    s.letr[me_r] = s.lets[...]
    flight = exchange(ROW, LET, lambda p: s.lets, lambda p: s.letr.at[p])

    first, second = me_r * NI + (row_p // NJ) % NI, me_c * NJ + row_p % NJ
    sites_p = by_protein(sites, NP, NI * NJ)
    numbers_p = by_protein(numbers, NP, NI * NJ)
    s.pmask[...] = at_lane(sites_p, first) * at_lane(sites_p, second)
    s.offset[...] = (
        jnp.clip(at_lane(numbers_p, first) - at_lane(numbers_p, second), -REACH, REACH) + REACH
    )
    numbers_b = by_protein(numbers, BI, NI)
    own = at_lane(numbers_b, me_r * NI + iota((BI, 1), 0) % NI)
    s.codes[...] = jnp.clip(own - numbers_b, -REACH, REACH) + REACH
    s.sites[...] = jnp.zeros((8, length), F32)
    s.sites[0:NB, :] = sites
    inv_all = 1.0 / (jnp.sum(here, axis=1, keepdims=True) + 1.0)
    inv_count = [inv_all[b : b + 1] for b in range(NB)]
    per_protein = jnp.sum(sites, axis=1, keepdims=True)
    inv_dist = 1.0 / jnp.maximum(colsum(per_protein * per_protein), 1.0)

    def gain(begin, width):
        return scal[begin : begin + width].reshape(1, width)

    gain_row, gain_trans, gain_outer = gain(0, WA), gain(256, WA), gain(512, WA)
    gain_rel, gain_pair, gain_mixed = gain(768, WP), gain(896, WP), gain(1024, WP)
    bias_outer = gain(1152, WP)
    s.lk[...] = jnp.zeros((AP, WA), F32)
    s.lk[0:LETTERS, :] = lookup[...]
    s.weh[...] = jnp.zeros((128, WA), F32)
    s.weh[0:87, :] = w_a[2048:2135, :]
    s.wbd[...] = jnp.zeros((128, WP), F32)
    s.wbd[0:72, :] = w_p[768:840, :]
    s.wrel[...] = jnp.zeros((RP, WP), F32)
    s.wrel[0:NREL, :] = w_r[UP : UP + NREL, :]
    s.tail[...] = jnp.zeros((8, 128), F32)
    s.tail[0:1, 0:87] = scal[1280:1367].reshape(1, 87)

    table = s.lk[...]
    unit0, _ = norm(table)
    mapped = mm6(unit0 * gain_row, w_a[0 : 4 * WA, :], NT)
    tout[...] = mapped
    t_q = mapped[:, 0:WA] * HEAD ** (-0.5)
    t_k = mapped[:, WA : 2 * WA].astype(BF16).astype(F32)
    t_v = mapped[:, 2 * WA : 3 * WA].astype(BF16).astype(F32)
    t_g = jax.nn.sigmoid(mapped[:, 3 * WA :])
    square = head_mask(WA, AP)
    key_block = jnp.where(square, jnp.concatenate([t_k] * HEADS, axis=0), 0.0).astype(BF16)
    s.vb[...] = jnp.where(square, jnp.concatenate([t_v] * HEADS, axis=0), 0.0).astype(BF16)
    stacked = mm(jnp.concatenate(split3(t_q), axis=0), key_block, NT)
    score_table = stacked[0:AP] + (stacked[AP : 2 * AP] + stacked[2 * AP :])
    s.hm[...] = jnp.where(head_mask(64, NI), 1.0, 0.0)

    letter = letter.astype(jnp.int32)
    triple = jnp.where(
        (iota((NM, 3 * AP), 1) % AP) == letter, 1.0, 0.0
    ).astype(BF16)

    def chosen(values):
        return mm(triple, jnp.concatenate(split3(values), axis=0))

    s.amat[...] = chosen(score_table).reshape(BS, NI, WA)
    start = chosen(table)
    s.sg[...] = chosen(t_g)

    unit_r, _ = norm(s.wrel[...])
    bias_table = mm3(s.wbd[0:8, :], unit_r * gain_rel, NT)
    bias_parts = jnp.concatenate(split3(bias_table), axis=0)

    def codes(index):
        return jnp.where(
            iota((RP, length), 0) == s.codes[index : index + 1, :].astype(jnp.int32), 1.0, 0.0
        ).astype(BF16)

    for b in range(NB):
        for i in range(NI):
            part = mm(bias_parts, codes(b * NI + i))
            part = part[0:8] + (part[8:16] + part[16:24])
            for h in range(HEADS):
                s.biash[b, h * NI + i : h * NI + i + 1, :] = part[h : h + 1, :]

    finish(flight)
    letters_all = s.letr[...].reshape(length, 128).T
    s.letx[...] = letters_all
    s.cnts[...] = jnp.broadcast_to(
        jnp.sum(letters_all[BS : BS + 1, :], axis=1, keepdims=True), (8, 128)
    )
    s.cntr[me_c] = s.cnts[...]
    count_flight = exchange(COL, CNT, lambda p: s.cnts, lambda p: s.cntr.at[p])

    def letter_codes(bs):
        row = s.letx[pl.ds(bs, 1), :].astype(jnp.int32)
        one = jnp.where(iota((AP, length), 0) == row, 1.0, 0.0)
        return jnp.concatenate([one] * HEADS, axis=0).astype(BF16)

    def spread(value):
        wide = jnp.broadcast_to(value[None], (HEADS, NI, WA)).reshape(64, WA)
        return wide * s.hm[...]

    def gather_heads(value):
        return jnp.sum((value * s.hm[...]).reshape(HEADS, NI, WA), axis=0)

    for b in range(NB):
        key_mask = s.sites[b : b + 1, :]

        @pl.loop(0, NS)
        def _(q):
            bs = b * NS + q
            code = letter_codes(bs)
            parts = split3(s.amat[bs])
            wide = jnp.concatenate([spread(p.astype(F32)).astype(BF16) for p in parts], axis=0)
            raw = mm(wide, code)
            scores = (raw[0:64] + (raw[64:128] + raw[128:192])) + s.biash[b]
            scores = jnp.where(key_mask > 0, scores, -1000000000.0)
            power = jnp.exp(scores - jnp.max(scores, axis=-1, keepdims=True))
            weight = power / jnp.sum(power, axis=-1, keepdims=True)
            s.prob[bs] = weight
            picked = mm(jnp.concatenate(split2(weight), axis=0), code, NT)
            s.pam[bs] = gather_heads(picked[0:64] + picked[64:128])

    att = mm2(s.pam[...].reshape(NM, WA), s.vb[...])
    s.att[...] = att
    mid = start + mm3(s.sg[...] * att, w_c[0:WA, :])
    unit1, scale1 = norm(mid)
    s.xh1[...] = unit1
    s.r1[...] = scale1
    hidden = jnp.maximum(mm3(unit1 * gain_trans, w_a[4 * WA : 4 * WA + UP, :], NT), 0.0)
    s.hid[...] = hidden
    rep = mid + mm3(hidden, w_c[WA:, :])
    s.rep[...] = rep
    unit2, scale2 = norm(rep)
    s.xh2[...] = unit2
    s.r2[...] = scale2
    seq_weight = s.seqw[...]
    lane = iota((NM, 128), 1)
    edges = mm3(unit2 * gain_outer, s.weh[...], NT) * seq_weight

    right = jnp.where((lane >= 32) & (lane < 64), edges, 0.0).astype(BF16)
    spot = iota((128, DS), 0)
    repeat = jnp.where(spot - 32 == iota((128, DS), 1) // NS, 1.0, 0.0)
    repeat = jnp.where((spot >= 32) & (spot < 64), repeat, 0.0).astype(BF16)
    wide = mm(right, repeat)
    own_seq = (iota((NM, DS), 0) // NI) % NS == iota((NM, DS), 1) % NS
    wide = jnp.sum(jnp.where(own_seq, wide, 0.0).reshape(NB, NS, NI, DS), axis=1)
    s.rs[...] = wide.astype(BF16)
    s.rr[me_r] = s.rs[...]
    flight = exchange(ROW, RIGHT, lambda p: s.rs, lambda p: s.rr.at[p])

    finish(count_flight)
    masked = jnp.maximum(jnp.sum(s.cntr[...], axis=0)[0:1, 0:1], 1.0)
    logits = mm3(rep, s.weh[...], NT) + s.tail[0:1, :]
    valid = (lane >= 64) & (lane < 64 + LETTERS)
    top = jnp.max(jnp.where(valid, logits, -3e38), axis=-1, keepdims=True)
    power = jnp.where(valid, jnp.exp(jnp.where(valid, logits, top) - top), 0.0)
    whole = jnp.sum(power, axis=-1, keepdims=True)
    truth = lane - 64 == s.truth[...].astype(jnp.int32)
    truth = truth & valid
    picked = jnp.sum(jnp.where(truth, logits, 0.0), axis=-1, keepdims=True)
    loss_mask = s.lmask[...]
    msa_sum = colsum((jnp.log(whole) + top - picked) * loss_mask)
    s.dlog[...] = (power / whole - jnp.where(truth, 1.0, 0.0)) * (loss_mask / masked)

    order_to = (iota((NM, NM), 0) // (NI * NS) == iota((NM, NM), 1) // (NI * NS)) & (
        (iota((NM, NM), 0) // NS) % NI == iota((NM, NM), 1) % NI
    )
    order_to = order_to & (iota((NM, NM), 0) % NS == (iota((NM, NM), 1) // NI) % NS)
    order = jnp.where(order_to, 1.0, 0.0).astype(BF16)
    left = mm3r(order, jnp.where(lane < 32, edges, 0.0))
    high, low = split2(left)
    high32, low32 = high.astype(F32), low.astype(F32)
    left3 = high32 + pltpu.roll(low32, 32, 1) + pltpu.roll(high32, 64, 1)
    s.left3[...] = left3[:, 0:96].astype(BF16)

    def outer_weight(d):
        return w_r[pl.ds(d, WO, stride=WO), :]

    for d in range(WO):
        wh, wl = split2(outer_weight(d))
        made = mm(s.left3[...], jnp.concatenate([wh, wh, wl], axis=0))
        mh, ml = split2(made.reshape(BI, NS, WP))
        s.mhi[:, d * NS : (d + 1) * NS, :] = mh
        s.mlo[:, d * NS : (d + 1) * NS, :] = ml

    finish(flight)
    for b in range(NB):
        s.rall[b] = s.rr[:, b].astype(F32).reshape(length, DS).astype(BF16)
    for b in range(NB):

        @pl.loop(0, NI)
        def _(i):
            bi = b * NI + i
            block = mm(s.rall[b], s.mhi[bi]) + mm(s.rall[b], s.mlo[bi])
            block = block * inv_count[b]
            for c in range(cols):
                s.os[c, bi] = block[c * NJ : (c + 1) * NJ].astype(BF16)

    s.orr[me_c] = s.os[me_c]
    finish(exchange(COL, OUTER, lambda p: s.os.at[p], lambda p: s.orr.at[p]))

    pair_lane = iota((NP, 128), 1)
    offset = s.offset[...].astype(jnp.int32)
    pair_codes = jnp.where(pair_lane == offset, 1.0, 0.0).astype(BF16)
    outer = s.orr[0].astype(F32)
    for c in range(1, cols):
        outer = outer + s.orr[c].astype(F32)
    pair_rep = (mm3r(pair_codes, s.wrel[...]) + outer.reshape(NP, WP)) + bias_outer
    s.prep[...] = pair_rep
    unit3, scale3 = norm(pair_rep)
    s.xh3[...] = unit3
    s.r3[...] = scale3
    proj = mm3(unit3 * gain_pair, w_p[0 : 5 * WP, :], NT)
    pair_mask = s.pmask[...]
    sig1 = jax.nn.sigmoid(proj[:, WP : 2 * WP])
    sig2 = jax.nn.sigmoid(proj[:, 3 * WP : 4 * WP])
    sig3 = jax.nn.sigmoid(proj[:, 4 * WP :])
    s.proj[:, 0 : WP] = proj[:, 0:WP]
    s.proj[:, WP : 2 * WP] = sig1
    s.proj[:, 2 * WP : 3 * WP] = proj[:, 2 * WP : 3 * WP]
    s.proj[:, 3 * WP : 4 * WP] = sig2
    s.proj[:, 4 * WP :] = sig3
    s.le[...] = sig1 * proj[:, 0:WP] * pair_mask
    right_edge = (sig2 * proj[:, 2 * WP : 3 * WP] * pair_mask).astype(BF16)
    s.es[...] = right_edge.reshape(NB, NI, NJ, WP)
    s.er[me_r] = s.es[...]
    finish(exchange(ROW, EDGE, lambda p: s.es, lambda p: s.er.at[p]))
    for b in range(NB):
        for r in range(rows):
            begin = (b * length + r * NI) * NJ
            s.re[begin : begin + NI * NJ, :] = (
                s.er[r, b].astype(F32).reshape(NI * NJ, WP)
            )

    for b in range(NB):

        @pl.loop(0, NI)
        def _(i):
            bi = b * NI + i
            for c in range(cols):
                block = jnp.zeros((NJ, WP), F32)
                for k in range(NJ):
                    other = s.re[pl.ds((b * length + c * NJ) * NJ + k, NJ, stride=NJ), :]
                    block = block + s.le[pl.ds(bi * NJ + k, 1), :] * other
                s.ts[c, bi] = block.astype(BF16)

    s.tr[me_c] = s.ts[me_c]
    finish(exchange(COL, TRI, lambda p: s.ts.at[p], lambda p: s.tr.at[p]))

    mixed = s.tr[0].astype(F32)
    for c in range(1, cols):
        mixed = mixed + s.tr[c].astype(F32)
    unit4, scale4 = norm(mixed.reshape(NP, WP))
    w_out = w_p[5 * WP : 6 * WP, :]
    moved = mm3(unit4 * gain_mixed, w_out, NT)
    sig3 = s.proj[:, 4 * WP :]
    pair_out = s.prep[...] + sig3 * moved
    bins = mm3(pair_out, s.wbd[...], NT) + pltpu.roll(
        jnp.where(iota((8, 128), 1) < BINS, s.tail[...], 0.0), 8, 1
    )[0:1]
    valid = (pair_lane >= 8) & (pair_lane < 8 + BINS)
    top = jnp.max(jnp.where(valid, bins, -3e38), axis=-1, keepdims=True)
    power = jnp.where(valid, jnp.exp(jnp.where(valid, bins, top) - top), 0.0)
    whole = jnp.sum(power, axis=-1, keepdims=True)
    truth = (pair_lane - 8 == s.target[...].astype(jnp.int32)) & valid
    picked = jnp.sum(jnp.where(truth, bins, 0.0), axis=-1, keepdims=True)
    dist_sum = colsum((jnp.log(whole) + top - picked) * pair_mask)
    dbins = (power / whole - jnp.where(truth, 1.0, 0.0)) * (pair_mask * inv_dist)

    def put(place, value, skip=0):
        base = place + skip
        height, width = value.shape
        for w in range(width // 128):
            s.grad[base + w * height : base + (w + 1) * height, :] = value[
                :, w * 128 : (w + 1) * 128
            ]

    def column_products(name, place):
        s.sum8[...] = jnp.zeros((8, WA), F32)

        @pl.loop(0, NM // 32)
        def _(q):
            some = pl.ds(pl.multiple_of(q * 32, 32), 32)
            product = s.dn[some, :] * name[some, :]
            s.sum8[...] += jnp.sum(product.reshape(4, 8, WA), axis=0)

        whole = colsum(s.sum8[...])
        for half in range(2):
            s.grad[small + place + half : small + place + half + 1, :] = whole[
                :, 128 * half : 128 * half + 128
            ]

    s.grad[ROWS.small :, :] = jnp.zeros((TOTAL - ROWS.small, 128), F32)
    small = ROWS.small
    put(ROWS.bd, mm3(dbins, pair_out, TN))
    dbias_dist = pltpu.roll(jnp.broadcast_to(colsum(dbins), (8, 128)), 120, 1)[0:1]
    dout = mm3(dbins, s.wbd[...])
    dgate = dout * moved * (sig3 * (1.0 - sig3))
    dmoved = dout * sig3
    put(ROWS.out, mm3(dmoved, unit4 * gain_mixed, TN))
    dnormed = mm3(dmoved, w_out)
    s.grad[small + 5 : small + 6, :] = colsum(dnormed * unit4)
    dmixed = norm_back(dnormed * gain_mixed, unit4, scale4)
    s.ds[...] = dmixed.astype(BF16).reshape(BI, NJ, WP)
    s.dsr[me_c] = s.ds[...]
    finish(exchange(COL, GMIX, lambda p: s.ds, lambda p: s.dsr.at[p]))
    for bi in range(BI):
        for c in range(cols):
            begin = bi * length + c * NJ
            s.dm[begin : begin + NJ, :] = s.dsr[c, bi].astype(F32)

    for b in range(NB):

        @pl.loop(0, rows)
        def _(r):
            for q in range(NI):
                block = jnp.zeros((NJ, WP), F32)
                for i in range(NI):
                    bi = b * NI + i
                    block = block + (
                        s.dm[pl.ds(bi * length + r * NI + q, 1), :]
                        * s.le[bi * NJ : (bi + 1) * NJ, :]
                    )
                s.gs[r, b, q] = block.astype(BF16)

    s.gr[me_r] = s.gs[me_r]
    flight = exchange(ROW, GEDGE, lambda p: s.gs.at[p], lambda p: s.gr.at[p])
    for b in range(NB):

        @pl.loop(0, NI)
        def _(i):
            bi = b * NI + i
            block = jnp.zeros((NJ, WP), F32)
            for j in range(length):
                begin = (b * length + j) * NJ
                block = block + (
                    s.dm[pl.ds(bi * length + j, 1), :] * s.re[begin : begin + NJ, :]
                )
            s.gl[bi] = block

    finish(flight)
    dright = s.gr[0].astype(F32)
    for r in range(1, rows):
        dright = dright + s.gr[r].astype(F32)
    dright = dright.reshape(NP, WP) * pair_mask
    dleft = s.gl[...].reshape(NP, WP) * pair_mask
    p1, sig1 = s.proj[:, 0:WP], s.proj[:, WP : 2 * WP]
    p2, sig2 = s.proj[:, 2 * WP : 3 * WP], s.proj[:, 3 * WP : 4 * WP]
    dproj = jnp.concatenate(
        [
            dleft * sig1,
            dleft * p1 * (sig1 * (1.0 - sig1)),
            dright * sig2,
            dright * p2 * (sig2 * (1.0 - sig2)),
            dgate,
        ],
        axis=1,
    )
    unit3 = s.xh3[...]
    put(ROWS.tri, mm3(dproj, unit3 * gain_pair, TN))
    dnormed = mm3(dproj, w_p[0 : 5 * WP, :])
    s.grad[small + 4 : small + 5, :] = colsum(dnormed * unit3)
    drep = dout + norm_back(dnormed * gain_pair, unit3, s.r3[...])
    s.grad[small + 6 : small + 7, :] = colsum(drep)
    s.grad[ROWS.rel : ROWS.rel + 72, :] = mm2r(pair_codes, drep, TN)[0:72]
    s.qs[...] = drep.astype(BF16).reshape(BI, NJ, WP)
    s.qr[me_c] = s.qs[...]
    finish(exchange(COL, GOUTER, lambda p: s.qs, lambda p: s.qr.at[p]))

    for b in range(NB):
        turned = s.rall[b].astype(F32).T.astype(BF16)
        s.dr[...] = jnp.zeros((length, DS), F32)

        @pl.loop(0, NI)
        def _(i):
            bi = b * NI + i
            block = jnp.concatenate([s.qr[c, bi] for c in range(cols)], axis=0)
            s.dr[...] += mm(block, s.mhi[bi], NT) + mm(block, s.mlo[bi], NT)
            mh, ml = split2(mm(turned, block) * inv_count[b])
            s.mhi[bi] = mh
            s.mlo[bi] = ml

        for r in range(rows):
            s.us[r, b] = (s.dr[r * NI : (r + 1) * NI, :] * inv_count[b]).astype(BF16)
    s.ur[me_r] = s.us[me_r]
    flight = exchange(ROW, GRIGHT, lambda p: s.us.at[p], lambda p: s.ur.at[p])

    left3 = s.left3[...].astype(F32).T.astype(BF16)
    left_both, left_high = left3[0:64], left3[0:32]
    dleft = jnp.zeros((NM, WO), F32)
    for d in range(WO):
        wh, wl = split2(outer_weight(d))
        mh = s.mhi[:, d * NS : (d + 1) * NS, :].reshape(NM, WP)
        ml = s.mlo[:, d * NS : (d + 1) * NS, :].reshape(NM, WP)
        dleft = dleft + (mm(mh, wh, NT) + (mm(ml, wh, NT) + mm(mh, wl, NT)))
        made = mm(left_both, mh)
        s.grad[pl.ds(ROWS.outer + d, WO, stride=WO), :] = (
            made[0:32] + made[32:64] + mm(left_high, ml)
        )
    dleft = mm3r(order, dleft, TN)

    finish(flight)
    dright = s.ur[0].astype(F32)
    for r in range(1, rows):
        dright = dright + s.ur[r].astype(F32)
    wide = jnp.broadcast_to(dright[:, None], (NB, NS, NI, DS)).reshape(NM, DS)
    dedges = mm2(jnp.where(own_seq, wide, 0.0), repeat, NT)
    dedges = (dedges + jnp.concatenate([dleft, jnp.zeros((NM, 96), F32)], axis=1)) * seq_weight
    unit2, rep = s.xh2[...], s.rep[...]
    dlog = s.dlog[...]
    put(ROWS.eh, mm3(dedges, unit2 * gain_outer, TN) + mm3(dlog, rep, TN))
    s.dn[...] = mm3(dedges, s.weh[...])
    dnormed = s.dn[...]
    column_products(s.xh2, 2)
    drep = mm3(dlog, s.weh[...]) + norm_back(dnormed * gain_outer, unit2, s.r2[...])
    hidden = s.hid[...]
    put(ROWS.back, mm3(hidden, drep, TN))
    dhidden = jnp.where(hidden > 0, mm3(drep, w_c[WA:, :], NT), 0.0)
    unit1 = s.xh1[...]
    put(ROWS.up, mm3(dhidden, unit1 * gain_trans, TN))
    s.dn[...] = mm3(dhidden, w_a[4 * WA : 4 * WA + UP, :])
    dnormed = s.dn[...]
    column_products(s.xh1, 0)
    dmid = drep + norm_back(dnormed * gain_trans, unit1, s.r1[...])
    sg, att = s.sg[...], s.att[...]
    put(ROWS.o, mm3(sg * att, dmid, TN))
    dgated = mm3(dmid, w_c[0:WA, :], NT)
    single = triple[:, 0:AP]
    put(ROWS.tabs, mm2r(single, dmid, TN), 6 * AP)
    put(ROWS.tabs, mm2r(single, dgated * att, TN), 4 * AP)
    datt = dgated * sg

    pam = s.pam[...].reshape(NM, WA)
    blocks = jnp.where(head_mask(WA, AP), mm3(pam, datt, TN), 0.0)
    put(ROWS.tabs, jnp.sum(blocks.reshape(HEADS, AP, WA), axis=0), 2 * AP)
    s.dpam[...] = mm2(datt, s.vb[...], NT).reshape(BS, NI, WA)
    for b in range(NB):
        key_mask = s.sites[b : b + 1, :]
        s.dbias[b] = jnp.zeros((64, length), F32)

        @pl.loop(0, NS)
        def _(q):
            bs = b * NS + q
            code = letter_codes(bs)
            parts = split2(s.dpam[bs])
            wide = jnp.concatenate([spread(p.astype(F32)).astype(BF16) for p in parts], axis=0)
            raw = mm(wide, code)
            dweight = raw[0:64] + raw[64:128]
            weight = s.prob[bs]
            inner = jnp.sum(weight * dweight, axis=-1, keepdims=True)
            dscore = jnp.where(key_mask > 0, weight * (dweight - inner), 0.0)
            s.dbias[b] += dscore
            back = mm(jnp.concatenate(split2(dscore), axis=0), code, NT)
            s.da[bs] = gather_heads(back[0:64] + back[64:128])

    put(ROWS.tabs, mm2r(single, s.da[...].reshape(NM, WA), TN))
    for b in range(NB):
        for i in range(NI):
            part = jnp.concatenate(
                [s.dbias[b, h * NI + i : h * NI + i + 1, :] for h in range(HEADS)], axis=0
            )
            s.dtab[b * NI + i] = mm(
                jnp.concatenate(split2(part), axis=0), codes(b * NI + i), NT
            )
    s.grad[ROWS.bias : ROWS.bias + 8, :] = jnp.sum(
        s.dtab[...].reshape(2 * BI, 8, RP), axis=0
    )

    lane1 = iota((1, 128), 1)
    s.grad[small + 7 : small + 8, :] = jnp.where(lane1 < BINS, dbias_dist, colsum(dlog))
    s.grad[small + 8 : small + 9, :] = jnp.where(
        lane1 == 0, msa_sum, jnp.where(lane1 == 1, dist_sum, 0.0)
    )
    aux[...] = jnp.where(iota((8, 128), 1) == 0, masked, inv_dist)

    shard = TOTAL // cols
    piece = shard // rows
    s.arc[me_c] = s.grad[pl.ds(pl.multiple_of(me_c * shard, 8), shard), :]
    finish(
        exchange(
            COL,
            SUM_COL,
            lambda p: s.grad.at[pl.ds(pl.multiple_of(p * shard, 8), shard)],
            lambda p: s.arc.at[p],
        )
    )
    summed = s.arc[0]
    for c in range(1, cols):
        summed = summed + s.arc[c]
    s.arc[0] = summed
    s.arr[me_r] = s.arc[0, pl.ds(pl.multiple_of(me_r * piece, 8), piece), :]
    finish(
        exchange(
            ROW,
            SUM_ROW,
            lambda p: s.arc.at[0, pl.ds(pl.multiple_of(p * piece, 8), piece)],
            lambda p: s.arr.at[p],
        )
    )
    summed = s.arr[0]
    for r in range(1, rows):
        summed = summed + s.arr[r]
    mine = pl.ds(pl.multiple_of(me_c * shard + me_r * piece, 8), piece)
    gout[mine, :] = summed

    def spot_row(p):
        return gout.at[pl.ds(pl.multiple_of(me_c * shard + p * piece, 8), piece)]

    def spot_col(p):
        return gout.at[pl.ds(pl.multiple_of(p * shard, 8), shard)]

    finish(exchange(ROW, SHARE_ROW, lambda p: spot_row(me_r), spot_row))
    finish(exchange(COL, SHARE_COL, lambda p: spot_col(me_c), spot_col))


def post_kernel(*refs):
    gout, tout, aux = refs[:3]
    weights, means, squares = refs[3:9], refs[9:15], refs[15:21]
    new, loss_out, size_out = refs[21:39], refs[39], refs[40]
    lk, wrel, g_a, g_small, g_rel = refs[41:]
    lookup, w_a, w_c, w_r, w_p, scal = weights

    lk[...] = jnp.zeros((AP, WA), F32)
    lk[0:LETTERS, :] = lookup[...]
    wrel[...] = jnp.zeros((RP, WP), F32)
    wrel[0:NREL, :] = w_r[UP : UP + NREL, :]

    def table(number):
        base = ROWS.tabs + 2 * number * AP
        return jnp.concatenate(
            [gout[base : base + AP, :], gout[base + AP : base + 2 * AP, :]], axis=1
        )

    dscore, dvalue, dgate, dstart = table(0), table(1), table(2), table(3)
    mapped = tout[...]
    t_q = mapped[:, 0:WA] * HEAD ** (-0.5)
    t_k = mapped[:, WA : 2 * WA].astype(BF16).astype(F32)
    t_g = jax.nn.sigmoid(mapped[:, 3 * WA :])
    square = head_mask(WA, AP)
    key_block = jnp.where(square, jnp.concatenate([t_k] * HEADS, axis=0), 0.0).astype(BF16)
    dq = mm2(dscore, key_block) * HEAD ** (-0.5)
    dk = jnp.where(square, mm3(dscore, t_q, TN), 0.0)
    dk = jnp.sum(dk.reshape(HEADS, AP, WA), axis=0)
    dg = dgate * (t_g * (1.0 - t_g))
    dmapped = jnp.concatenate([dq, dk, dvalue, dg], axis=1)
    unit0, scale0 = norm(lk[...])
    gain_row = scal[0:WA].reshape(1, WA)
    g_a[...] = mm3(dmapped, unit0 * gain_row, TN)
    dnormed = mm3(dmapped, w_a[0 : 4 * WA, :])
    dgain_row = colsum(dnormed * unit0)
    g_lookup = dstart + norm_back(dnormed * gain_row, unit0, scale0)

    unit_r, scale_r = norm(wrel[...])
    gain_rel = scal[768:896].reshape(1, WP)
    dtable = gout[ROWS.bias : ROWS.bias + 8, :]
    g_bias = mm3(dtable, unit_r * gain_rel)
    dnormed = mm3(dtable, w_p[768:776, :], TN)
    dgain_rel = colsum(dnormed * unit_r)
    g_rel[...] = gout[ROWS.rel : ROWS.rel + 72, :] + norm_back(
        dnormed * gain_rel, unit_r, scale_r
    )[0:72]

    base = ROWS.small
    g_small[0:WA] = dgain_row.reshape(WA)
    for place, row in ((256, 0), (384, 1), (512, 2), (640, 3), (896, 4), (1024, 5), (1152, 6)):
        g_small[place : place + 128] = gout[base + row : base + row + 1, :].reshape(128)
    g_small[768:896] = dgain_rel.reshape(128)
    lane = iota((1, 128), 1)
    tail = jnp.where(lane < 87, gout[base + 7 : base + 8, :], 0.0)
    g_small[1280:1408] = tail.reshape(128)

    rel_row = iota((72, 128), 0)
    direct = gout[0 : ROWS.tabs, :]
    squares_sum = total_of(direct * direct)
    direct = gout[ROWS.outer : ROWS.rel, :]
    squares_sum = squares_sum + total_of(direct * direct)
    for part in (
        g_a[...],
        g_lookup[0:LETTERS],
        jnp.where(rel_row < NREL, g_rel[...], 0.0),
        g_bias,
        dgain_row,
        gout[base : base + 7, :],
        dgain_rel,
        tail,
    ):
        squares_sum = squares_sum + total_of(part * part)
    size = jnp.sqrt(squares_sum)
    scale = jnp.minimum(1.0, CLIP / size)

    def adam(which, where, grad, factor=scale):
        clipped = grad * factor
        weight = weights[which][where]
        moment = B1 * means[which][where] + (1.0 - B1) * clipped
        second = B2 * squares[which][where] + (1.0 - B2) * clipped * clipped
        step = (moment / (1.0 - B1**STEP)) / (jnp.sqrt(second / (1.0 - B2**STEP)) + ADAM_EPS)
        new[3 * which][where] = weight - RATE * (step + DECAY * weight)
        new[3 * which + 1][where] = moment
        new[3 * which + 2][where] = second

    every = slice(None)
    adam(0, (every, every), g_lookup[0:LETTERS])
    adam(1, (slice(0, 4 * WA), every), g_a[...])
    for w in range(2):
        half = slice(128 * w, 128 * w + 128)
        begin = ROWS.up + w * UP
        adam(1, (slice(1024, 2048), half), gout[begin : begin + UP, :])
        begin = ROWS.eh + w * 128
        adam(1, (slice(2048, 2135), half), gout[begin : begin + 87, :])
        begin = ROWS.o + w * WA
        adam(2, (slice(0, WA), half), gout[begin : begin + WA, :])
        begin = ROWS.back + w * UP
        adam(2, (slice(WA, WA + UP), half), gout[begin : begin + UP, :])
    adam(3, (slice(0, UP), every), gout[ROWS.outer : ROWS.outer + UP, :])
    adam(3, (slice(UP, UP + NREL), every), g_rel[0:NREL, :])
    adam(4, (slice(0, 768), every), gout[ROWS.tri : ROWS.tri + 768, :])
    adam(4, (slice(768, 776), every), g_bias)
    adam(4, (slice(776, 840), every), gout[ROWS.bd + 8 : ROWS.bd + 72, :])
    adam(5, (slice(0, 1367),), g_small[0:1367], scale.reshape(1))

    sums = gout[base + 8 : base + 9, :]
    loss = sums[:, 0:1] / aux[0:1, 0:1] + sums[:, 1:2] * aux[0:1, 1:2]
    loss_out[0] = loss[0, 0]
    size_out[0] = size[0, 0]


def vmem():
    return pl.BlockSpec(memory_space=pltpu.VMEM)


def per_device(rows, cols, *arrays):
    letters, truth, concealed, existing, ordinals, observed, bins = arrays[:7]

    def turned(group):
        return [w.T if place in (1, 4) else w for place, w in enumerate(group)]

    weights, means, squares = turned(arrays[7:13]), turned(arrays[13:19]), turned(arrays[19:25])
    plan = scratch_plan(rows, cols)
    gout, tout, aux = pl.pallas_call(
        functools.partial(main_kernel, rows, cols, tuple(plan)),
        out_shape=(
            jax.ShapeDtypeStruct((TOTAL, 128), F32),
            jax.ShapeDtypeStruct((AP, 4 * WA), F32),
            jax.ShapeDtypeStruct((8, 128), F32),
        ),
        in_specs=[vmem()] * 13,
        out_specs=(vmem(), vmem(), vmem()),
        scratch_shapes=[pltpu.VMEM(dims, kind) for dims, kind in plan.values()]
        + [
            pltpu.SemaphoreType.DMA((PHASES, rows)),
            pltpu.SemaphoreType.DMA((PHASES, rows)),
            pltpu.SemaphoreType.DMA((PHASES, cols)),
            pltpu.SemaphoreType.DMA((PHASES, cols)),
        ],
        compiler_params=pltpu.CompilerParams(
            collective_id=0, has_side_effects=True, vmem_limit_bytes=MAIN_VMEM
        ),
    )(
        jnp.swapaxes(letters, 1, 2),
        jnp.swapaxes(truth, 1, 2),
        jnp.swapaxes(concealed, 1, 2),
        existing,
        ordinals,
        observed,
        bins,
        *weights,
    )

    shapes = []
    for w in weights:
        shapes += [jax.ShapeDtypeStruct(w.shape, F32)] * 3
    one = jax.ShapeDtypeStruct((1,), F32)
    scalar = pl.BlockSpec(memory_space=pltpu.SMEM)
    result = pl.pallas_call(
        post_kernel,
        out_shape=tuple(shapes) + (one, one),
        in_specs=[vmem()] * 21,
        out_specs=tuple([vmem()] * 18) + (scalar, scalar),
        scratch_shapes=[
            pltpu.VMEM((AP, WA), F32),
            pltpu.VMEM((RP, WP), F32),
            pltpu.VMEM((4 * WA, WA), F32),
            pltpu.VMEM((1408,), F32),
            pltpu.VMEM((72, 128), F32),
        ],
        compiler_params=pltpu.CompilerParams(vmem_limit_bytes=POST_VMEM),
    )(gout, tout, aux, *weights, *means, *squares)
    outs = [result[18].reshape(()), result[19].reshape(())]
    for place, value in enumerate(result[:18]):
        outs.append(value.T if place // 3 in (1, 4) else value)
    return tuple(outs)


def solution(mesh):
    rows, cols = mesh.shape[ROW], mesh.shape[COL]
    placed = (
        (P(None, COL, ROW),) * 3 + (P(),) * 3 + (P(None, ROW, COL),) + (P(),) * 18
    )
    return jax.shard_map(
        functools.partial(per_device, rows, cols),
        mesh=mesh,
        in_specs=placed,
        out_specs=(P(),) * 20,
        check_vma=False,
    )
```

```python
import functools
from types import SimpleNamespace

import jax
import jax.numpy as jnp
from jax import lax
from jax.experimental import pallas as pl
from jax.experimental.pallas import tpu as pltpu
from jax.sharding import PartitionSpec as P

F32, BF16 = jnp.float32, jnp.bfloat16
MESH = pl.DeviceIdType.MESH
ROW, COL = "row", "col"
CORE, X, Y, Z = "core", "x", "y", "z"
WA, WP, WO, LETTERS, BINS, REACH, HEADS, HEAD = 256, 128, 32, 23, 64, 32, 8, 32
UP = 1024
NREL = 2 * REACH + 1
AP = 32
RP = 128
EPS = 1e-05
NB, NS, NI, NJ = 2, 16, 8, 16
NM = NB * NS * NI
NP = NB * NI * NJ
BS = NB * NS
BI = NB * NI
DS = WO * NS
CLIP, RATE, B1, B2, STEP, ADAM_EPS, DECAY = 0.02, 0.05, 0.9, 0.999, 4, 1e-08, 0.01

MAIN_VMEM, POST_VMEM = 44 * 2**20, 30 * 2**20

NN = (((1,), (0,)), ((), ()))
NT = (((1,), (1,)), ((), ()))
TN = (((0,), (0,)), ((), ()))

GROUPS = (
    dict(outer=WO * WO, tri=5 * WP, out=WP),
    dict(back=2 * UP),
    dict(up=2 * UP, o=2 * WA),
    dict(eh=176, tabs=6 * AP, dist=BINS, rel=72),
    dict(score=2 * AP, bias=8, small=16),
)
BF16_GROUPS = 3


def layout(rows, cols):
    places, bases, begin = {}, [], 0
    for number, group in enumerate(GROUPS):
        bases.append(begin)
        for name, count in group.items():
            places[name] = begin
            begin += count
        size = 16 * rows if number + 1 == len(GROUPS) else 16 * rows * cols
        begin = bases[-1] - (bases[-1] - begin) // size * size
    return SimpleNamespace(**places), bases + [begin]


def mm(a, b, dims=NN):
    return lax.dot_general(a, b, dims, preferred_element_type=F32)


def split2(x):
    high = x.astype(BF16)
    return high, (x - high.astype(F32)).astype(BF16)


def split3(x):
    high = x.astype(BF16)
    rest = x - high.astype(F32)
    middle = rest.astype(BF16)
    return high, middle, (rest - middle.astype(F32)).astype(BF16)


def mm3(a, b, dims=NN):
    ah, al = split2(a)
    bh, bl = split2(b)
    return mm(ah, bh, dims) + (mm(al, bh, dims) + mm(ah, bl, dims))


def mm6(a, b, dims=NN):
    ah, am, al = split3(a)
    bh, bm, bl = split3(b)
    low = mm(al, bh, dims) + (mm(am, bm, dims) + mm(ah, bl, dims))
    return mm(ah, bh, dims) + ((mm(am, bh, dims) + mm(ah, bm, dims)) + low)


def mm2(a, exact, dims=NN):
    ah, al = split2(a)
    return mm(ah, exact, dims) + mm(al, exact, dims)


def mm2r(exact, b, dims=NN):
    bh, bl = split2(b)
    return mm(exact, bh, dims) + mm(exact, bl, dims)


def mm3r(exact, b, dims=NN):
    bh, bm, bl = split3(b)
    return mm(exact, bh, dims) + (mm(exact, bm, dims) + mm(exact, bl, dims))


def norm(x):
    centred = x - jnp.mean(x, axis=-1, keepdims=True)
    scale = lax.rsqrt(jnp.mean(centred * centred, axis=-1, keepdims=True) + EPS)
    return centred * scale, scale


def norm_back(grad, unit, scale):
    return scale * (
        grad
        - jnp.mean(grad, axis=-1, keepdims=True)
        - unit * jnp.mean(grad * unit, axis=-1, keepdims=True)
    )


def iota(shape, axis):
    return lax.broadcasted_iota(jnp.int32, shape, axis)


def head_mask(rows, per_row):
    shape = (rows, WA)
    return iota(shape, 0) // per_row == iota(shape, 1) // HEAD


def colsum(x):
    return jnp.sum(x, axis=0, keepdims=True)


def total_of(x):
    return jnp.sum(jnp.sum(x, axis=1, keepdims=True), axis=0, keepdims=True)


def scratch_plan(rows, cols):
    length = rows * NI
    bases = layout(rows, cols)[1]
    final = bases[5] - bases[4]
    return dict(
        lk=((AP, WA), F32),
        weh=((128, WA), F32),
        wbd=((128, WP), F32),
        seqw=((NM, 1), F32),
        lmask=((NM, 1), F32),
        truth=((NM, 1), F32),
        target=((NP, 1), F32),
        pmask=((NP, 1), F32),
        offset=((NP, 1), F32),
        codes=((BI, length), F32),
        sites=((8, length), F32),
        wrel=((RP, WP), F32),
        tail=((8, 128), F32),
        kb=((WA, WA), BF16),
        vb=((WA, WA), BF16),
        amat=((BS, NI, WA), F32),
        pam=((BS, NI, WA), F32),
        hm=((64, WA), F32),
        letx=((128, length), F32),
        biash=((NB, 64, length), F32),
        prob=((BS, 64, length), F32),
        sg=((NM, WA), F32),
        att=((NM, WA), F32),
        xh1=((NM, WA), F32),
        r1=((NM, 1), F32),
        hid=((NM, UP), F32),
        rep=((NM, WA), F32),
        xh2=((NM, WA), F32),
        r2=((NM, 1), F32),
        dlog=((NM, 128), F32),
        left3=((NM, 96), BF16),
        mhi=((BI, DS, WP), BF16),
        mlo=((BI, DS, WP), BF16),
        rall=((NB, length, DS), BF16),
        prep=((NP, WP), F32),
        xh3=((NP, WP), F32),
        r3=((NP, 1), F32),
        proj=((NP, 5 * WP), F32),
        le=((BI * NJ, WP), F32),
        re=((NB * length * NJ, WP), F32),
        dm=((BI * length, WP), F32),
        gl=((BI, NJ, WP), F32),
        dr=((length, DS), F32),
        dmid=((NM, WA), F32),
        dbias=((NB, 64, length), F32),
        da=((BS, NI, WA), F32),
        dpam=((BS, NI, WA), F32),
        dtab=((BI, 16, RP), F32),
        dn=((NM, WA), F32),
        sum8=((8, WA), F32),
        grad=((bases[5], 128), F32),
        lets=((8, 128), F32),
        letr=((rows, 8, 128), F32),
        cnts=((8, 128), F32),
        cntr=((cols, 8, 128), F32),
        rs=((NB, NI, DS), BF16),
        rr=((rows, NB, NI, DS), BF16),
        os=((cols, BI, NJ, WP), BF16),
        orr=((cols, BI, NJ, WP), BF16),
        es=((NB, NI, NJ, WP), BF16),
        er=((rows, NB, NI, NJ, WP), BF16),
        ts=((cols, BI, NJ, WP), BF16),
        tr=((cols, BI, NJ, WP), BF16),
        ds=((BI, NJ, WP), BF16),
        dsr=((cols, BI, NJ, WP), BF16),
        gs=((rows, NB, NI, NJ, WP), BF16),
        gr=((rows, NB, NI, NJ, WP), BF16),
        qs=((BI, NJ, WP), BF16),
        qr=((cols, BI, NJ, WP), BF16),
        us=((rows, NB, NI, DS), BF16),
        ur=((rows, NB, NI, DS), BF16),
        arx=((bases[4], 128), F32),
        fr=((rows, final // rows, 128), F32),
        fp=((final // rows, 128), F32),
        fc=((cols, final // rows, 128), F32),
        letters=((NB, NI, NS), jnp.int32),
        truths=((NB, NI, NS), jnp.int32),
        concealed=((NB, NI, NS), jnp.int32),
        existing=((NB, cols * NS), jnp.int32),
        ordinals=((NB, length), jnp.int32),
        observed=((NB, length), jnp.int32),
        targets=((NB, NI, NJ), jnp.int32),
        lookup=((LETTERS, WA), F32),
        w_a=((2135, WA), F32),
        w_c=((WA + UP, WA), F32),
        w_r=((UP + NREL, WP), F32),
        w_p=((840, WP), F32),
        scal=((1367,), F32),
    )


OPERANDS = 13


LET, RIGHT, EDGE, GEDGE, GRIGHT, SUM_ROW, SHARE_ROW = range(7)
CNT, OUTER, TRI, GMIX, GOUTER, SHARE_COL = range(6)
PHASES = 7


def main_kernel(rows, cols, names, *refs):
    operands = refs[:OPERANDS]
    gbig, grest, gfin, tout, aux = refs[OPERANDS : OPERANDS + 5]
    s = SimpleNamespace(**dict(zip(names, refs[OPERANDS + 5 : -7])))
    row_send, row_recv, col_send, col_recv, sum_send, sum_recv, load_sem = refs[-7:]
    held = refs[OPERANDS + 5 : -7][-OPERANDS:]
    loads = [
        pltpu.make_async_copy(far, near, load_sem.at[place])
        for place, (far, near) in enumerate(zip(operands, held))
    ]
    for load in loads:
        load.start()
    letters, truths, hidden_sites, existing, ordinals, observed, targets = held[:7]
    lookup, w_a, w_c, w_r, w_p, scal = held[7:]
    ROWS, bases = layout(rows, cols)
    length = rows * NI
    me_r, me_c = lax.axis_index(ROW), lax.axis_index(COL)

    barrier = pltpu.get_barrier_semaphore()
    for step in range(1, rows):
        pl.semaphore_signal(
            barrier,
            inc=1,
            device_id={ROW: lax.rem(me_r + step, rows), COL: me_c},
            device_id_type=MESH,
        )
    for step in range(1, cols):
        pl.semaphore_signal(
            barrier,
            inc=1,
            device_id={ROW: me_r, COL: lax.rem(me_c + step, cols)},
            device_id_type=MESH,
        )
    pl.semaphore_wait(barrier, rows + cols - 2)

    def exchange(along, phase, source, target):
        if along == ROW:
            count, me, number = rows, me_r, phase
            send, recv = row_send, row_recv
        else:
            count, me, number = cols, me_c, phase
            send, recv = col_send, col_recv
        copies = []
        for step in range(1, count):
            peer = lax.rem(me + step, count)
            origin = lax.rem(me + (count - step), count)
            where = (
                {ROW: peer, COL: me_c} if along == ROW else {ROW: me_r, COL: peer}
            )
            out = pltpu.make_async_remote_copy(
                src_ref=source(peer),
                dst_ref=target(me),
                send_sem=send.at[number, step],
                recv_sem=recv.at[number, step],
                device_id=where,
                device_id_type=MESH,
            )
            out.start()
            arriving = pltpu.make_async_remote_copy(
                src_ref=source(peer),
                dst_ref=target(origin),
                send_sem=send.at[number, step],
                recv_sem=recv.at[number, step],
                device_id=where,
                device_id_type=MESH,
            )
            copies.append((out, arriving))
        return copies

    def finish(copies):
        for out, arriving in copies:
            out.wait_send()
            arriving.wait_recv()

    for load in loads[:7]:
        load.wait()
    here = existing[...].astype(F32)
    sites = observed[...].astype(F32)
    numbers = ordinals[...].astype(F32)

    def by_protein(values, count, each):
        wide = (count, values.shape[1])
        return jnp.where(iota(wide, 0) // each == 0, values[0:1], values[1:2])

    def at_lane(values, lanes):
        return jnp.sum(jnp.where(iota(values.shape, 1) == lanes, values, 0.0), axis=1, keepdims=True)

    row_m, row_p = iota((NM, 1), 0), iota((NP, 1), 0)
    seq_m, res_m = (row_m // NI) % NS, row_m % NI
    spread_m = jnp.where(
        iota((NM, BI), 1) == (iota((NM, BI), 0) // (NI * NS)) * NI + iota((NM, BI), 0) % NI, 1.0, 0.0
    ).astype(BF16)
    spread_p = jnp.where(iota((NP, BI), 1) == iota((NP, BI), 0) // NJ, 1.0, 0.0).astype(BF16)

    def column_m(values):
        wide = mm(spread_m, values[...].reshape(BI, NS).astype(F32).astype(BF16))
        return at_lane(wide, seq_m)

    seq_weight = at_lane(by_protein(here, NM, NI * NS), me_c * NS + seq_m)
    letter = column_m(letters)
    loss_mask = column_m(hidden_sites) * seq_weight
    s.seqw[...] = seq_weight
    s.lmask[...] = loss_mask
    s.truth[...] = column_m(truths)
    s.target[...] = at_lane(
        mm(spread_p, targets[...].reshape(BI, NJ).astype(F32).astype(BF16)), row_p % NJ
    )

    s.lets[...] = jnp.where(
        (iota((NI, 128), 0) == 0) & (iota((NI, 128), 1) == BS), total_of(loss_mask), 0.0
    )
    for b in range(NB):
        s.lets[:, b * NS : (b + 1) * NS] = letters[b].astype(F32)
    s.letr[me_r] = s.lets[...]
    flight = exchange(ROW, LET, lambda p: s.lets, lambda p: s.letr.at[p])

    first, second = me_r * NI + (row_p // NJ) % NI, me_c * NJ + row_p % NJ
    sites_p = by_protein(sites, NP, NI * NJ)
    numbers_p = by_protein(numbers, NP, NI * NJ)
    s.pmask[...] = at_lane(sites_p, first) * at_lane(sites_p, second)
    s.offset[...] = (
        jnp.clip(at_lane(numbers_p, first) - at_lane(numbers_p, second), -REACH, REACH) + REACH
    )
    numbers_b = by_protein(numbers, BI, NI)
    own = at_lane(numbers_b, me_r * NI + iota((BI, 1), 0) % NI)
    s.codes[...] = jnp.clip(own - numbers_b, -REACH, REACH) + REACH
    s.sites[...] = jnp.zeros((8, length), F32)
    s.sites[0:NB, :] = sites
    inv_all = 1.0 / (jnp.sum(here, axis=1, keepdims=True) + 1.0)
    inv_count = [inv_all[b : b + 1] for b in range(NB)]
    per_protein = jnp.sum(sites, axis=1, keepdims=True)
    inv_dist = 1.0 / jnp.maximum(colsum(per_protein * per_protein), 1.0)

    for load in loads[7:]:
        load.wait()

    def gain(begin, width):
        return scal[begin : begin + width].reshape(1, width)

    gain_row, gain_trans, gain_outer = gain(0, WA), gain(256, WA), gain(512, WA)
    gain_rel, gain_pair, gain_mixed = gain(768, WP), gain(896, WP), gain(1024, WP)
    bias_outer = gain(1152, WP)
    s.lk[...] = jnp.zeros((AP, WA), F32)
    s.lk[0:LETTERS, :] = lookup[...]
    s.weh[...] = jnp.zeros((128, WA), F32)
    s.weh[0:87, :] = w_a[2048:2135, :]
    s.wbd[...] = jnp.zeros((128, WP), F32)
    s.wbd[0:72, :] = w_p[768:840, :]
    s.wrel[...] = jnp.zeros((RP, WP), F32)
    s.wrel[0:NREL, :] = w_r[UP : UP + NREL, :]
    s.tail[...] = jnp.zeros((8, 128), F32)
    s.tail[0:1, 0:87] = scal[1280:1367].reshape(1, 87)

    table = s.lk[...]
    unit0, _ = norm(table)
    mapped = mm6(unit0 * gain_row, w_a[0 : 4 * WA, :], NT)
    tout[...] = mapped
    t_q = mapped[:, 0:WA] * HEAD ** (-0.5)
    t_k = mapped[:, WA : 2 * WA].astype(BF16).astype(F32)
    t_v = mapped[:, 2 * WA : 3 * WA].astype(BF16).astype(F32)
    t_g = jax.nn.sigmoid(mapped[:, 3 * WA :])
    square = head_mask(WA, AP)
    key_block = jnp.where(square, jnp.concatenate([t_k] * HEADS, axis=0), 0.0).astype(BF16)
    s.vb[...] = jnp.where(square, jnp.concatenate([t_v] * HEADS, axis=0), 0.0).astype(BF16)
    stacked = mm(jnp.concatenate(split3(t_q), axis=0), key_block, NT)
    score_table = stacked[0:AP] + (stacked[AP : 2 * AP] + stacked[2 * AP :])
    s.hm[...] = jnp.where(head_mask(64, NI), 1.0, 0.0)

    letter = letter.astype(jnp.int32)
    triple = jnp.where(
        (iota((NM, 3 * AP), 1) % AP) == letter, 1.0, 0.0
    ).astype(BF16)

    def chosen(values):
        return mm(triple, jnp.concatenate(split3(values), axis=0))

    s.amat[...] = chosen(score_table).reshape(BS, NI, WA)
    start = chosen(table)
    s.sg[...] = chosen(t_g)

    unit_r, _ = norm(s.wrel[...])
    bias_table = mm3(s.wbd[0:8, :], unit_r * gain_rel, NT)
    bias_parts = jnp.concatenate(split3(bias_table), axis=0)

    def codes(index):
        return jnp.where(
            iota((RP, length), 0) == s.codes[index : index + 1, :].astype(jnp.int32), 1.0, 0.0
        ).astype(BF16)

    for b in range(NB):
        for i in range(NI):
            part = mm(bias_parts, codes(b * NI + i))
            part = part[0:8] + (part[8:16] + part[16:24])
            for h in range(HEADS):
                s.biash[b, h * NI + i : h * NI + i + 1, :] = part[h : h + 1, :]

    finish(flight)
    letters_all = s.letr[...].reshape(length, 128).T
    s.letx[...] = letters_all
    s.cnts[...] = jnp.broadcast_to(
        jnp.sum(letters_all[BS : BS + 1, :], axis=1, keepdims=True), (8, 128)
    )
    s.cntr[me_c] = s.cnts[...]
    count_flight = exchange(COL, CNT, lambda p: s.cnts, lambda p: s.cntr.at[p])

    def letter_codes(bs):
        row = s.letx[pl.ds(bs, 1), :].astype(jnp.int32)
        one = jnp.where(iota((AP, length), 0) == row, 1.0, 0.0)
        return jnp.concatenate([one] * HEADS, axis=0).astype(BF16)

    def spread(value):
        wide = jnp.broadcast_to(value[None], (HEADS, NI, WA)).reshape(64, WA)
        return wide * s.hm[...]

    def gather_heads(value):
        return jnp.sum((value * s.hm[...]).reshape(HEADS, NI, WA), axis=0)

    for b in range(NB):
        key_mask = s.sites[b : b + 1, :]

        @pl.loop(0, NS)
        def _(q):
            bs = b * NS + q
            code = letter_codes(bs)
            parts = split3(s.amat[bs])
            wide = jnp.concatenate([spread(p.astype(F32)).astype(BF16) for p in parts], axis=0)
            raw = mm(wide, code)
            scores = (raw[0:64] + (raw[64:128] + raw[128:192])) + s.biash[b]
            scores = jnp.where(key_mask > 0, scores, -1000000000.0)
            power = jnp.exp(scores - jnp.max(scores, axis=-1, keepdims=True))
            weight = power / jnp.sum(power, axis=-1, keepdims=True)
            s.prob[bs] = weight
            picked = mm(jnp.concatenate(split2(weight), axis=0), code, NT)
            s.pam[bs] = gather_heads(picked[0:64] + picked[64:128])

    att = mm2(s.pam[...].reshape(NM, WA), s.vb[...])
    s.att[...] = att
    mid = start + mm3(s.sg[...] * att, w_c[0:WA, :])
    unit1, scale1 = norm(mid)
    s.xh1[...] = unit1
    s.r1[...] = scale1
    hidden = jnp.maximum(mm3(unit1 * gain_trans, w_a[4 * WA : 4 * WA + UP, :], NT), 0.0)
    s.hid[...] = hidden
    rep = mid + mm3(hidden, w_c[WA:, :])
    s.rep[...] = rep
    unit2, scale2 = norm(rep)
    s.xh2[...] = unit2
    s.r2[...] = scale2
    seq_weight = s.seqw[...]
    lane = iota((NM, 128), 1)
    edges = mm3(unit2 * gain_outer, s.weh[...], NT) * seq_weight

    right = jnp.where((lane >= 32) & (lane < 64), edges, 0.0).astype(BF16)
    spot = iota((128, DS), 0)
    repeat = jnp.where(spot - 32 == iota((128, DS), 1) // NS, 1.0, 0.0)
    repeat = jnp.where((spot >= 32) & (spot < 64), repeat, 0.0).astype(BF16)
    wide = mm(right, repeat)
    own_seq = (iota((NM, DS), 0) // NI) % NS == iota((NM, DS), 1) % NS
    wide = jnp.sum(jnp.where(own_seq, wide, 0.0).reshape(NB, NS, NI, DS), axis=1)
    s.rs[...] = wide.astype(BF16)
    s.rr[me_r] = s.rs[...]
    flight = exchange(ROW, RIGHT, lambda p: s.rs, lambda p: s.rr.at[p])

    finish(count_flight)
    masked = jnp.maximum(jnp.sum(s.cntr[...], axis=0)[0:1, 0:1], 1.0)
    logits = mm3(rep, s.weh[...], NT) + s.tail[0:1, :]
    valid = (lane >= 64) & (lane < 64 + LETTERS)
    top = jnp.max(jnp.where(valid, logits, -3e38), axis=-1, keepdims=True)
    power = jnp.where(valid, jnp.exp(jnp.where(valid, logits, top) - top), 0.0)
    whole = jnp.sum(power, axis=-1, keepdims=True)
    truth = lane - 64 == s.truth[...].astype(jnp.int32)
    truth = truth & valid
    picked = jnp.sum(jnp.where(truth, logits, 0.0), axis=-1, keepdims=True)
    loss_mask = s.lmask[...]
    msa_sum = colsum((jnp.log(whole) + top - picked) * loss_mask)
    s.dlog[...] = (power / whole - jnp.where(truth, 1.0, 0.0)) * (loss_mask / masked)

    order_to = (iota((NM, NM), 0) // (NI * NS) == iota((NM, NM), 1) // (NI * NS)) & (
        (iota((NM, NM), 0) // NS) % NI == iota((NM, NM), 1) % NI
    )
    order_to = order_to & (iota((NM, NM), 0) % NS == (iota((NM, NM), 1) // NI) % NS)
    order = jnp.where(order_to, 1.0, 0.0).astype(BF16)
    left = mm3r(order, jnp.where(lane < 32, edges, 0.0))
    high, low = split2(left)
    high32, low32 = high.astype(F32), low.astype(F32)
    left3 = high32 + pltpu.roll(low32, 32, 1) + pltpu.roll(high32, 64, 1)
    s.left3[...] = left3[:, 0:96].astype(BF16)

    def outer_weight(d):
        return w_r[pl.ds(d, WO, stride=WO), :]

    for d in range(WO):
        wh, wl = split2(outer_weight(d))
        made = mm(s.left3[...], jnp.concatenate([wh, wh, wl], axis=0))
        mh, ml = split2(made.reshape(BI, NS, WP))
        s.mhi[:, d * NS : (d + 1) * NS, :] = mh
        s.mlo[:, d * NS : (d + 1) * NS, :] = ml

    finish(flight)
    for b in range(NB):
        s.rall[b] = s.rr[:, b].astype(F32).reshape(length, DS).astype(BF16)
    for b in range(NB):

        @pl.loop(0, NI)
        def _(i):
            bi = b * NI + i
            block = mm(s.rall[b], s.mhi[bi]) + mm(s.rall[b], s.mlo[bi])
            block = block * inv_count[b]
            for c in range(cols):
                s.os[c, bi] = block[c * NJ : (c + 1) * NJ].astype(BF16)

    s.orr[me_c] = s.os[me_c]
    finish(exchange(COL, OUTER, lambda p: s.os.at[p], lambda p: s.orr.at[p]))

    pair_lane = iota((NP, 128), 1)
    offset = s.offset[...].astype(jnp.int32)
    pair_codes = jnp.where(pair_lane == offset, 1.0, 0.0).astype(BF16)
    outer = s.orr[0].astype(F32)
    for c in range(1, cols):
        outer = outer + s.orr[c].astype(F32)
    pair_rep = (mm3r(pair_codes, s.wrel[...]) + outer.reshape(NP, WP)) + bias_outer
    s.prep[...] = pair_rep
    unit3, scale3 = norm(pair_rep)
    s.xh3[...] = unit3
    s.r3[...] = scale3
    proj = mm3(unit3 * gain_pair, w_p[0 : 5 * WP, :], NT)
    pair_mask = s.pmask[...]
    sig1 = jax.nn.sigmoid(proj[:, WP : 2 * WP])
    sig2 = jax.nn.sigmoid(proj[:, 3 * WP : 4 * WP])
    sig3 = jax.nn.sigmoid(proj[:, 4 * WP :])
    s.proj[:, 0 : WP] = proj[:, 0:WP]
    s.proj[:, WP : 2 * WP] = sig1
    s.proj[:, 2 * WP : 3 * WP] = proj[:, 2 * WP : 3 * WP]
    s.proj[:, 3 * WP : 4 * WP] = sig2
    s.proj[:, 4 * WP :] = sig3
    s.le[...] = sig1 * proj[:, 0:WP] * pair_mask
    right_edge = (sig2 * proj[:, 2 * WP : 3 * WP] * pair_mask).astype(BF16)
    s.es[...] = right_edge.reshape(NB, NI, NJ, WP)
    s.er[me_r] = s.es[...]
    finish(exchange(ROW, EDGE, lambda p: s.es, lambda p: s.er.at[p]))
    for b in range(NB):
        for r in range(rows):
            begin = (b * length + r * NI) * NJ
            s.re[begin : begin + NI * NJ, :] = (
                s.er[r, b].astype(F32).reshape(NI * NJ, WP)
            )

    for b in range(NB):

        @pl.loop(0, NI)
        def _(i):
            bi = b * NI + i
            for c in range(cols):
                block = jnp.zeros((NJ, WP), F32)
                for k in range(NJ):
                    other = s.re[pl.ds((b * length + c * NJ) * NJ + k, NJ, stride=NJ), :]
                    block = block + s.le[pl.ds(bi * NJ + k, 1), :] * other
                s.ts[c, bi] = block.astype(BF16)

    s.tr[me_c] = s.ts[me_c]
    finish(exchange(COL, TRI, lambda p: s.ts.at[p], lambda p: s.tr.at[p]))

    mixed = s.tr[0].astype(F32)
    for c in range(1, cols):
        mixed = mixed + s.tr[c].astype(F32)
    unit4, scale4 = norm(mixed.reshape(NP, WP))
    w_out = w_p[5 * WP : 6 * WP, :]
    moved = mm3(unit4 * gain_mixed, w_out, NT)
    sig3 = s.proj[:, 4 * WP :]
    pair_out = s.prep[...] + sig3 * moved
    bins = mm3(pair_out, s.wbd[...], NT) + pltpu.roll(
        jnp.where(iota((8, 128), 1) < BINS, s.tail[...], 0.0), 8, 1
    )[0:1]
    valid = (pair_lane >= 8) & (pair_lane < 8 + BINS)
    top = jnp.max(jnp.where(valid, bins, -3e38), axis=-1, keepdims=True)
    power = jnp.where(valid, jnp.exp(jnp.where(valid, bins, top) - top), 0.0)
    whole = jnp.sum(power, axis=-1, keepdims=True)
    truth = (pair_lane - 8 == s.target[...].astype(jnp.int32)) & valid
    picked = jnp.sum(jnp.where(truth, bins, 0.0), axis=-1, keepdims=True)
    dist_sum = colsum((jnp.log(whole) + top - picked) * pair_mask)
    dbins = (power / whole - jnp.where(truth, 1.0, 0.0)) * (pair_mask * inv_dist)

    def put(place, value, skip=0):
        base = place + skip
        height, width = value.shape
        for w in range(width // 128):
            s.grad[base + w * height : base + (w + 1) * height, :] = value[
                :, w * 128 : (w + 1) * 128
            ]

    sizes = {CORE: 2, X: cols // 2, Y: 2, Z: rows // 2}
    places = {CORE: me_c % 2, X: me_c // 2, Y: me_r % 2, Z: me_r // 2}

    def line_peer(axis, place):
        if axis == CORE:
            return {ROW: me_r, COL: me_c // 2 * 2 + place}
        if axis == X:
            return {ROW: me_r, COL: place * 2 + me_c % 2}
        if axis == Y:
            return {ROW: me_r // 2 * 2 + place, COL: me_c}
        return {ROW: place * 2 + me_r % 2, COL: me_c}

    class Sum:
        def __init__(self, number):
            self.number = number
            self.stage = -1
            base, size = bases[number] // 8, (bases[number + 1] - bases[number]) // 8
            self.parts = []
            for half in range(2):
                order = (CORE, X, Y, Z) if half == 0 else (CORE, Y, X, Z)
                begin = base + half * (size // 2)
                self.parts.append(SimpleNamespace(order=order, at=begin, size=size // 2, rx=begin))
            self.flight = []

        def copies(self, part, half, axis, source, target, arrive):
            count = sizes[axis]
            for step in range(1, count):
                peer = lax.rem(places[axis] + step, count)
                origin = lax.rem(places[axis] + (count - step), count)
                slot = (self.number, half, self.stage, step)
                both = []
                for end in (target(peer, step), arrive(origin, step)):
                    both.append(
                        pltpu.make_async_remote_copy(
                            src_ref=source(peer),
                            dst_ref=end,
                            send_sem=sum_send.at[slot],
                            recv_sem=sum_recv.at[slot],
                            device_id=line_peer(axis, peer),
                            device_id_type=MESH,
                        )
                    )
                both[0].start()
                self.flight.append(both)

        def advance(self):
            finish(self.flight)
            self.flight = []
            if 0 <= self.stage < 4:
                for part in self.parts:
                    self.add(part)
            self.stage += 1
            if self.stage == 4:
                for part in self.parts:
                    self.store(part)
            if self.stage < 4:
                for half, part in enumerate(self.parts):
                    self.start_sum(part, half)
            elif self.stage < 8:
                for half, part in enumerate(self.parts):
                    self.start_share(part, half)

        def start_sum(self, part, half):
            axis = part.order[self.stage]
            small = part.size // sizes[axis]
            part.small, part.axis = small, axis

            def source(peer):
                return s.grad.at[rows_at(part.at + peer * small, small)]

            def target(place, step):
                return s.arx.at[pl.ds((part.rx + (step - 1) * small) * 8, small * 8)]

            self.copies(part, half, axis, source, target, target)

        def add(self, part):
            mine = rows_at(part.at + places[part.axis] * part.small, part.small)
            value = s.grad[mine, :]
            for step in range(1, sizes[part.axis]):
                begin = (part.rx + (step - 1) * part.small) * 8
                value = value + s.arx[begin : begin + part.small * 8, :]
            s.grad[mine, :] = value
            part.at = part.at + places[part.axis] * part.small
            part.rx += (sizes[part.axis] - 1) * part.small
            part.size = part.small

        def store(self, part):
            value = s.grad[rows_at(part.at, part.size), :]
            if self.number < BF16_GROUPS:
                gbig[pl.ds(part.at, part.size)] = value.reshape(part.size, 8, 128).astype(BF16)
            else:
                grest[rows_at(part.at - bases[3] // 8, part.size), :] = value

        def start_share(self, part, half):
            axis = part.order[7 - self.stage]
            size, here = part.size, part.at
            first = here - places[axis] * size

            def spot(place, step):
                at = first + place * size
                if self.number < BF16_GROUPS:
                    return gbig.at[pl.ds(at, size)]
                return grest.at[rows_at(at - bases[3] // 8, size)]

            self.copies(
                part,
                half,
                axis,
                lambda peer: spot(places[axis], 0),
                lambda peer, step: spot(places[axis], step),
                spot,
            )
            part.at, part.size = first, size * sizes[axis]

    def rows_at(unit, count):
        return pl.ds(pl.multiple_of(unit * 8, 8), count * 8)

    early, middle, late, rest = [Sum(number) for number in range(4)]

    def column_products(name, place):
        s.sum8[...] = jnp.zeros((8, WA), F32)

        @pl.loop(0, NM // 32)
        def _(q):
            some = pl.ds(pl.multiple_of(q * 32, 32), 32)
            product = s.dn[some, :] * name[some, :]
            s.sum8[...] += jnp.sum(product.reshape(4, 8, WA), axis=0)

        whole = colsum(s.sum8[...])
        for half in range(2):
            s.grad[small + place + half : small + place + half + 1, :] = whole[
                :, 128 * half : 128 * half + 128
            ]

    for begin, end in (
        (ROWS.out + WP, bases[1]),
        (ROWS.o + 2 * WA, bases[3]),
        (ROWS.rel + 72, bases[4]),
        (ROWS.small, bases[5]),
    ):
        if end > begin:
            s.grad[begin:end, :] = jnp.zeros((end - begin, 128), F32)
    small = ROWS.small
    put(ROWS.dist, mm3(dbins, pair_out, TN)[8 : 8 + BINS])
    dbias_dist = pltpu.roll(jnp.broadcast_to(colsum(dbins), (8, 128)), 120, 1)[0:1]
    dout = mm3(dbins, s.wbd[...])
    dgate = dout * moved * (sig3 * (1.0 - sig3))
    dmoved = dout * sig3
    put(ROWS.out, mm3(dmoved, unit4 * gain_mixed, TN))
    dnormed = mm3(dmoved, w_out)
    s.grad[small + 5 : small + 6, :] = colsum(dnormed * unit4)
    dmixed = norm_back(dnormed * gain_mixed, unit4, scale4)
    s.ds[...] = dmixed.astype(BF16).reshape(BI, NJ, WP)
    s.dsr[me_c] = s.ds[...]
    finish(exchange(COL, GMIX, lambda p: s.ds, lambda p: s.dsr.at[p]))
    for bi in range(BI):
        for c in range(cols):
            begin = bi * length + c * NJ
            s.dm[begin : begin + NJ, :] = s.dsr[c, bi].astype(F32)

    for b in range(NB):

        @pl.loop(0, rows)
        def _(r):
            for q in range(NI):
                block = jnp.zeros((NJ, WP), F32)
                for i in range(NI):
                    bi = b * NI + i
                    block = block + (
                        s.dm[pl.ds(bi * length + r * NI + q, 1), :]
                        * s.le[bi * NJ : (bi + 1) * NJ, :]
                    )
                s.gs[r, b, q] = block.astype(BF16)

    s.gr[me_r] = s.gs[me_r]
    flight = exchange(ROW, GEDGE, lambda p: s.gs.at[p], lambda p: s.gr.at[p])
    for b in range(NB):

        @pl.loop(0, NI)
        def _(i):
            bi = b * NI + i
            block = jnp.zeros((NJ, WP), F32)
            for j in range(length):
                begin = (b * length + j) * NJ
                block = block + (
                    s.dm[pl.ds(bi * length + j, 1), :] * s.re[begin : begin + NJ, :]
                )
            s.gl[bi] = block

    finish(flight)
    dright = s.gr[0].astype(F32)
    for r in range(1, rows):
        dright = dright + s.gr[r].astype(F32)
    dright = dright.reshape(NP, WP) * pair_mask
    dleft = s.gl[...].reshape(NP, WP) * pair_mask
    p1, sig1 = s.proj[:, 0:WP], s.proj[:, WP : 2 * WP]
    p2, sig2 = s.proj[:, 2 * WP : 3 * WP], s.proj[:, 3 * WP : 4 * WP]
    dproj = jnp.concatenate(
        [
            dleft * sig1,
            dleft * p1 * (sig1 * (1.0 - sig1)),
            dright * sig2,
            dright * p2 * (sig2 * (1.0 - sig2)),
            dgate,
        ],
        axis=1,
    )
    unit3 = s.xh3[...]
    put(ROWS.tri, mm3(dproj, unit3 * gain_pair, TN))
    dnormed = mm3(dproj, w_p[0 : 5 * WP, :])
    s.grad[small + 4 : small + 5, :] = colsum(dnormed * unit3)
    drep = dout + norm_back(dnormed * gain_pair, unit3, s.r3[...])
    s.grad[small + 6 : small + 7, :] = colsum(drep)
    s.grad[ROWS.rel : ROWS.rel + 72, :] = mm2r(pair_codes, drep, TN)[0:72]
    s.qs[...] = drep.astype(BF16).reshape(BI, NJ, WP)
    s.qr[me_c] = s.qs[...]
    finish(exchange(COL, GOUTER, lambda p: s.qs, lambda p: s.qr.at[p]))

    for b in range(NB):
        turned = s.rall[b].astype(F32).T.astype(BF16)
        s.dr[...] = jnp.zeros((length, DS), F32)

        @pl.loop(0, NI)
        def _(i):
            bi = b * NI + i
            block = jnp.concatenate([s.qr[c, bi] for c in range(cols)], axis=0)
            s.dr[...] += mm(block, s.mhi[bi], NT) + mm(block, s.mlo[bi], NT)
            mh, ml = split2(mm(turned, block) * inv_count[b])
            s.mhi[bi] = mh
            s.mlo[bi] = ml

        for r in range(rows):
            s.us[r, b] = (s.dr[r * NI : (r + 1) * NI, :] * inv_count[b]).astype(BF16)
    s.ur[me_r] = s.us[me_r]
    flight = exchange(ROW, GRIGHT, lambda p: s.us.at[p], lambda p: s.ur.at[p])

    left3 = s.left3[...].astype(F32).T.astype(BF16)
    left_both, left_high = left3[0:64], left3[0:32]
    dleft = jnp.zeros((NM, WO), F32)
    for d in range(WO):
        wh, wl = split2(outer_weight(d))
        mh = s.mhi[:, d * NS : (d + 1) * NS, :].reshape(NM, WP)
        ml = s.mlo[:, d * NS : (d + 1) * NS, :].reshape(NM, WP)
        dleft = dleft + (mm(mh, wh, NT) + (mm(ml, wh, NT) + mm(mh, wl, NT)))
        made = mm(left_both, mh)
        s.grad[pl.ds(ROWS.outer + d, WO, stride=WO), :] = (
            made[0:32] + made[32:64] + mm(left_high, ml)
        )
    early.advance()
    dleft = mm3r(order, dleft, TN)

    finish(flight)
    dright = s.ur[0].astype(F32)
    for r in range(1, rows):
        dright = dright + s.ur[r].astype(F32)
    wide = jnp.broadcast_to(dright[:, None], (NB, NS, NI, DS)).reshape(NM, DS)
    dedges = mm2(jnp.where(own_seq, wide, 0.0), repeat, NT)
    dedges = (dedges + jnp.concatenate([dleft, jnp.zeros((NM, 96), F32)], axis=1)) * seq_weight
    unit2, rep = s.xh2[...], s.rep[...]
    dlog = s.dlog[...]
    put(ROWS.eh, (mm3(dedges, unit2 * gain_outer, TN) + mm3(dlog, rep, TN))[0:88])
    s.dn[...] = mm3(dedges, s.weh[...])
    dnormed = s.dn[...]
    column_products(s.xh2, 2)
    drep = mm3(dlog, s.weh[...]) + norm_back(dnormed * gain_outer, unit2, s.r2[...])
    early.advance()
    hidden = s.hid[...]
    put(ROWS.back, mm3(hidden, drep, TN))
    middle.advance()
    early.advance()
    dhidden = jnp.where(hidden > 0, mm3(drep, w_c[WA:, :], NT), 0.0)
    unit1 = s.xh1[...]
    put(ROWS.up, mm3(dhidden, unit1 * gain_trans, TN))
    s.dn[...] = mm3(dhidden, w_a[4 * WA : 4 * WA + UP, :])
    dnormed = s.dn[...]
    column_products(s.xh1, 0)
    dmid = drep + norm_back(dnormed * gain_trans, unit1, s.r1[...])
    sg, att = s.sg[...], s.att[...]
    put(ROWS.o, mm3(sg * att, dmid, TN))
    dgated = mm3(dmid, w_c[0:WA, :], NT)
    late.advance()
    middle.advance()
    early.advance()
    single = triple[:, 0:AP]
    put(ROWS.tabs, mm2r(single, dmid, TN), 4 * AP)
    put(ROWS.tabs, mm2r(single, dgated * att, TN), 2 * AP)
    datt = dgated * sg

    pam = s.pam[...].reshape(NM, WA)
    blocks = jnp.where(head_mask(WA, AP), mm3(pam, datt, TN), 0.0)
    put(ROWS.tabs, jnp.sum(blocks.reshape(HEADS, AP, WA), axis=0))
    rest.advance()
    s.dpam[...] = mm2(datt, s.vb[...], NT).reshape(BS, NI, WA)
    for b in range(NB):
        key_mask = s.sites[b : b + 1, :]
        s.dbias[b] = jnp.zeros((64, length), F32)

        def attention_back(q):
            bs = b * NS + q
            code = letter_codes(bs)
            parts = split2(s.dpam[bs])
            wide = jnp.concatenate([spread(p.astype(F32)).astype(BF16) for p in parts], axis=0)
            raw = mm(wide, code)
            dweight = raw[0:64] + raw[64:128]
            weight = s.prob[bs]
            inner = jnp.sum(weight * dweight, axis=-1, keepdims=True)
            dscore = jnp.where(key_mask > 0, weight * (dweight - inner), 0.0)
            s.dbias[b] += dscore
            back = mm(jnp.concatenate(split2(dscore), axis=0), code, NT)
            s.da[bs] = gather_heads(back[0:64] + back[64:128])

        for part in range(2):
            pl.loop(part * NS // 2, (part + 1) * NS // 2)(attention_back)
            for group in (early, middle, late, rest):
                group.advance()

    put(ROWS.score, mm2r(single, s.da[...].reshape(NM, WA), TN))
    for b in range(NB):
        for i in range(NI):
            part = jnp.concatenate(
                [s.dbias[b, h * NI + i : h * NI + i + 1, :] for h in range(HEADS)], axis=0
            )
            s.dtab[b * NI + i] = mm(
                jnp.concatenate(split2(part), axis=0), codes(b * NI + i), NT
            )
    s.grad[ROWS.bias : ROWS.bias + 8, :] = jnp.sum(
        s.dtab[...].reshape(2 * BI, 8, RP), axis=0
    )

    lane1 = iota((1, 128), 1)
    s.grad[small + 7 : small + 8, :] = jnp.where(lane1 < BINS, dbias_dist, colsum(dlog))
    s.grad[small + 8 : small + 9, :] = jnp.where(
        lane1 == 0, msa_sum, jnp.where(lane1 == 1, dist_sum, 0.0)
    )
    aux[...] = jnp.where(iota((8, 128), 1) == 0, masked, inv_dist)

    last = bases[4]
    piece = (bases[5] - last) // rows

    def mine(p):
        return pl.ds(pl.multiple_of(last + p * piece, 8), piece)

    def spot(p):
        return gfin.at[pl.ds(pl.multiple_of(p * piece, 8), piece)]

    s.fr[me_r] = s.grad[mine(me_r), :]
    flight = exchange(ROW, SUM_ROW, lambda p: s.grad.at[mine(p)], lambda p: s.fr.at[p])
    for group in (middle, late, rest):
        group.advance()
    finish(flight)
    summed = s.fr[0]
    for r in range(1, rows):
        summed = summed + s.fr[r]
    s.fp[...] = summed
    s.fc[me_c] = summed
    flight = exchange(COL, SHARE_COL, lambda p: s.fp, lambda p: s.fc.at[p])
    for group in (middle, late, rest):
        group.advance()
    finish(flight)
    summed = s.fc[0]
    for c in range(1, cols):
        summed = summed + s.fc[c]
    gfin[pl.ds(pl.multiple_of(me_r * piece, 8), piece), :] = summed
    flight = exchange(ROW, SHARE_ROW, lambda p: spot(me_r), spot)
    while min(group.stage for group in (early, middle, late, rest)) < 8:
        for group in (early, middle, late, rest):
            if group.stage < 8:
                group.advance()
    finish(flight)


def post_kernel(rows, cols, *refs):
    gbig, grest, gfin, tout, aux = refs[:5]
    weights, far_moments = refs[5:11], refs[11:23]
    far, loss_out, size_out = refs[23:41], refs[41], refs[42]
    new, moments = refs[43:61], refs[61:73]
    lk, wrel, g_a, g_small, g_rel, store_sem, load_sem = refs[73:]
    loads = [
        pltpu.make_async_copy(source, near, load_sem.at[place])
        for place, (source, near) in enumerate(zip(far_moments, moments))
    ]
    for place in (2, 8, 1, 7, 3, 9, 4, 10, 0, 6, 5, 11):
        loads[place].start()
    means, squares = moments[0:6], moments[6:12]
    lookup, w_a, w_c, w_r, w_p, scal = weights
    ROWS, bases = layout(rows, cols)

    def big(begin, count):
        part = gbig[begin // 8 : (begin + count) // 8].astype(F32)
        return part.reshape(count, 128)

    def exact(begin, count):
        if begin >= bases[4]:
            return gfin[begin - bases[4] : begin - bases[4] + count, :]
        return grest[begin - bases[3] : begin - bases[3] + count, :]

    lk[...] = jnp.zeros((AP, WA), F32)
    lk[0:LETTERS, :] = lookup[...]
    wrel[...] = jnp.zeros((RP, WP), F32)
    wrel[0:NREL, :] = w_r[UP : UP + NREL, :]

    def table(begin):
        return jnp.concatenate([exact(begin, AP), exact(begin + AP, AP)], axis=1)

    dscore = table(ROWS.score)
    dvalue, dgate, dstart = [table(ROWS.tabs + 2 * AP * place) for place in range(3)]
    mapped = tout[...]
    t_q = mapped[:, 0:WA] * HEAD ** (-0.5)
    t_k = mapped[:, WA : 2 * WA].astype(BF16).astype(F32)
    t_g = jax.nn.sigmoid(mapped[:, 3 * WA :])
    square = head_mask(WA, AP)
    key_block = jnp.where(square, jnp.concatenate([t_k] * HEADS, axis=0), 0.0).astype(BF16)
    dq = mm2(dscore, key_block) * HEAD ** (-0.5)
    dk = jnp.where(square, mm3(dscore, t_q, TN), 0.0)
    dk = jnp.sum(dk.reshape(HEADS, AP, WA), axis=0)
    dg = dgate * (t_g * (1.0 - t_g))
    dmapped = jnp.concatenate([dq, dk, dvalue, dg], axis=1)
    unit0, scale0 = norm(lk[...])
    gain_row = scal[0:WA].reshape(1, WA)
    g_a[...] = mm3(dmapped, unit0 * gain_row, TN)
    dnormed = mm3(dmapped, w_a[0 : 4 * WA, :])
    dgain_row = colsum(dnormed * unit0)
    g_lookup = dstart + norm_back(dnormed * gain_row, unit0, scale0)

    unit_r, scale_r = norm(wrel[...])
    gain_rel = scal[768:896].reshape(1, WP)
    dtable = exact(ROWS.bias, 8)
    g_bias = mm3(dtable, unit_r * gain_rel)
    dnormed = mm3(dtable, w_p[768:776, :], TN)
    dgain_rel = colsum(dnormed * unit_r)
    g_rel[...] = exact(ROWS.rel, 72) + norm_back(
        dnormed * gain_rel, unit_r, scale_r
    )[0:72]

    base = ROWS.small
    g_small[0:WA] = dgain_row.reshape(WA)
    for place, row in ((256, 0), (384, 1), (512, 2), (640, 3), (896, 4), (1024, 5), (1152, 6)):
        g_small[place : place + 128] = exact(base + row, 1).reshape(128)
    g_small[768:896] = dgain_rel.reshape(128)
    lane = iota((1, 128), 1)
    tail = jnp.where(lane < 87, exact(base + 7, 1), 0.0)
    g_small[1280:1408] = tail.reshape(128)

    rel_row = iota((72, 128), 0)
    squares_sum = jnp.zeros((1, 1), F32)
    for begin, count in (
        (ROWS.outer, UP),
        (ROWS.tri, 768),
        (ROWS.back, 2 * UP),
        (ROWS.up, 2 * UP),
        (ROWS.o, 2 * WA),
    ):
        part = big(begin, count)
        squares_sum = squares_sum + total_of(part * part)
    for part in (
        g_a[...],
        g_lookup[0:LETTERS],
        jnp.where(rel_row < NREL, g_rel[...], 0.0),
        g_bias,
        dgain_row,
        exact(base, 7),
        exact(ROWS.eh, 87),
        exact(ROWS.eh + 88, 87),
        exact(ROWS.dist, BINS),
        dgain_rel,
        tail,
    ):
        squares_sum = squares_sum + total_of(part * part)
    size = jnp.sqrt(squares_sum)
    scale = jnp.minimum(1.0, CLIP / size)

    def adam(which, where, grad, factor=scale):
        clipped = grad * factor
        weight = weights[which][where]
        moment = B1 * means[which][where] + (1.0 - B1) * clipped
        second = B2 * squares[which][where] + (1.0 - B2) * clipped * clipped
        step = (moment / (1.0 - B1**STEP)) / (jnp.sqrt(second / (1.0 - B2**STEP)) + ADAM_EPS)
        new[3 * which][where] = weight - RATE * (step + DECAY * weight)
        new[3 * which + 1][where] = moment
        new[3 * which + 2][where] = second

    every = slice(None)
    stores = []

    def leave(which):
        for place in range(3 * which, 3 * which + 3):
            store = pltpu.make_async_copy(new[place], far[place], store_sem.at[place])
            store.start()
            stores.append(store)

    def ready(which):
        loads[which].wait()
        loads[6 + which].wait()

    ready(2)
    for w in range(2):
        half = slice(128 * w, 128 * w + 128)
        adam(2, (slice(0, WA), half), big(ROWS.o + w * WA, WA))
        adam(2, (slice(WA, WA + UP), half), big(ROWS.back + w * UP, UP))
    leave(2)
    ready(1)
    adam(1, (slice(0, 4 * WA), every), g_a[...])
    for w in range(2):
        half = slice(128 * w, 128 * w + 128)
        adam(1, (slice(1024, 2048), half), big(ROWS.up + w * UP, UP))
        adam(1, (slice(2048, 2135), half), exact(ROWS.eh + w * 88, 87))
    leave(1)
    ready(3)
    adam(3, (slice(0, UP), every), big(ROWS.outer, UP))
    adam(3, (slice(UP, UP + NREL), every), g_rel[0:NREL, :])
    leave(3)
    ready(4)
    adam(4, (slice(0, 768), every), big(ROWS.tri, 768))
    adam(4, (slice(768, 776), every), g_bias)
    adam(4, (slice(776, 840), every), exact(ROWS.dist, BINS))
    leave(4)
    ready(0)
    adam(0, (every, every), g_lookup[0:LETTERS])
    leave(0)
    ready(5)
    adam(5, (slice(0, 1367),), g_small[0:1367], scale.reshape(1))
    leave(5)

    sums = exact(base + 8, 1)
    loss = sums[:, 0:1] / aux[0:1, 0:1] + sums[:, 1:2] * aux[0:1, 1:2]
    loss_out[0] = loss[0, 0]
    size_out[0] = size[0, 0]
    for store in stores:
        store.wait()


def vmem():
    return pl.BlockSpec(memory_space=pltpu.VMEM)


def per_device(rows, cols, *arrays):
    letters, truth, concealed, existing, ordinals, observed, bins = arrays[:7]

    def turned(group):
        return [w.T if place in (1, 4) else w for place, w in enumerate(group)]

    weights, means, squares = turned(arrays[7:13]), turned(arrays[13:19]), turned(arrays[19:25])
    plan = scratch_plan(rows, cols)
    bases = layout(rows, cols)[1]
    far = pl.BlockSpec(memory_space=pltpu.HBM)
    summed = pl.pallas_call(
        functools.partial(main_kernel, rows, cols, tuple(plan)),
        out_shape=(
            jax.ShapeDtypeStruct((bases[3] // 8, 8, 128), BF16),
            jax.ShapeDtypeStruct((bases[4] - bases[3], 128), F32),
            jax.ShapeDtypeStruct((bases[5] - bases[4], 128), F32),
            jax.ShapeDtypeStruct((AP, 4 * WA), F32),
            jax.ShapeDtypeStruct((8, 128), F32),
        ),
        in_specs=[far] * OPERANDS,
        out_specs=tuple([vmem()] * 5),
        scratch_shapes=[pltpu.VMEM(dims, kind) for dims, kind in plan.values()]
        + [
            pltpu.SemaphoreType.DMA((PHASES, rows)),
            pltpu.SemaphoreType.DMA((PHASES, rows)),
            pltpu.SemaphoreType.DMA((PHASES, cols)),
            pltpu.SemaphoreType.DMA((PHASES, cols)),
            pltpu.SemaphoreType.DMA((4, 2, 8, rows)),
            pltpu.SemaphoreType.DMA((4, 2, 8, rows)),
            pltpu.SemaphoreType.DMA((OPERANDS,)),
        ],
        compiler_params=pltpu.CompilerParams(
            collective_id=0, has_side_effects=True, vmem_limit_bytes=MAIN_VMEM
        ),
    )(
        *[
            pltpu.with_memory_space_constraint(value, pltpu.HBM)
            for value in (
                jnp.swapaxes(letters, 1, 2),
                jnp.swapaxes(truth, 1, 2),
                jnp.swapaxes(concealed, 1, 2),
                existing,
                ordinals,
                observed,
                bins,
                *weights,
            )
        ]
    )

    shapes = []
    for w in weights:
        shapes += [jax.ShapeDtypeStruct(w.shape, F32)] * 3
    one = jax.ShapeDtypeStruct((1,), F32)
    scalar = pl.BlockSpec(memory_space=pltpu.SMEM)
    result = pl.pallas_call(
        functools.partial(post_kernel, rows, cols),
        out_shape=tuple(shapes) + (one, one),
        in_specs=[vmem()] * 11 + [far] * 12,
        out_specs=tuple([far] * 18) + (scalar, scalar),
        scratch_shapes=[pltpu.VMEM(shape.shape, F32) for shape in shapes]
        + [pltpu.VMEM(value.shape, F32) for value in (*means, *squares)]
        + [
            pltpu.VMEM((AP, WA), F32),
            pltpu.VMEM((RP, WP), F32),
            pltpu.VMEM((4 * WA, WA), F32),
            pltpu.VMEM((1408,), F32),
            pltpu.VMEM((72, 128), F32),
            pltpu.SemaphoreType.DMA((18,)),
            pltpu.SemaphoreType.DMA((12,)),
        ],
        compiler_params=pltpu.CompilerParams(vmem_limit_bytes=POST_VMEM),
    )(
        *summed,
        *weights,
        *[pltpu.with_memory_space_constraint(value, pltpu.HBM) for value in (*means, *squares)],
    )
    outs = [result[18].reshape(()), result[19].reshape(())]
    for place, value in enumerate(result[:18]):
        outs.append(value.T if place // 3 in (1, 4) else value)
    return tuple(outs)


def solution(mesh):
    rows, cols = mesh.shape[ROW], mesh.shape[COL]
    placed = (
        (P(None, COL, ROW),) * 3 + (P(),) * 3 + (P(None, ROW, COL),) + (P(),) * 18
    )
    return jax.shard_map(
        functools.partial(per_device, rows, cols),
        mesh=mesh,
        in_specs=placed,
        out_specs=(P(),) * 20,
        check_vma=False,
    )
```

```python
import functools
from types import SimpleNamespace

import jax
import jax.numpy as jnp
from jax import lax
from jax.experimental import pallas as pl
from jax.experimental.pallas import tpu as pltpu
from jax.sharding import PartitionSpec as P

F32, BF16 = jnp.float32, jnp.bfloat16
MESH = pl.DeviceIdType.MESH
ROW, COL = "row", "col"
CORE, X, Y, Z = "core", "x", "y", "z"
WA, WP, WO, LETTERS, BINS, REACH, HEADS, HEAD = 256, 128, 32, 23, 64, 32, 8, 32
UP = 1024
NREL = 2 * REACH + 1
AP = 32
RP = 128
EPS = 1e-05
NB, NS, NI, NJ = 2, 16, 8, 16
NM = NB * NS * NI
NP = NB * NI * NJ
BS = NB * NS
BI = NB * NI
DS = WO * NS
TOGETHER = 4
CLIP, RATE, B1, B2, STEP, ADAM_EPS, DECAY = 0.02, 0.05, 0.9, 0.999, 4, 1e-08, 0.01

MAIN_VMEM, POST_VMEM = 44 * 2**20, 30 * 2**20

NN = (((1,), (0,)), ((), ()))
NT = (((1,), (1,)), ((), ()))
TN = (((0,), (0,)), ((), ()))

GROUPS = (
    dict(outer=WO * WO, tri=5 * WP, out=WP),
    dict(back=2 * UP),
    dict(up=2 * UP, o=2 * WA),
    dict(eh=176, tabs=6 * AP, dist=BINS, rel=72),
    dict(score=2 * AP, bias=8, small=16),
)
BF16_GROUPS = 3


def layout(rows, cols):
    places, bases, begin = {}, [], 0
    for number, group in enumerate(GROUPS):
        bases.append(begin)
        for name, count in group.items():
            places[name] = begin
            begin += count
        size = 16 * rows if number + 1 == len(GROUPS) else 16 * rows * cols
        begin = bases[-1] - (bases[-1] - begin) // size * size
    return SimpleNamespace(**places), bases + [begin]


def mm(a, b, dims=NN):
    return lax.dot_general(a, b, dims, preferred_element_type=F32)


def split2(x):
    high = x.astype(BF16)
    return high, (x - high.astype(F32)).astype(BF16)


def split3(x):
    high = x.astype(BF16)
    rest = x - high.astype(F32)
    middle = rest.astype(BF16)
    return high, middle, (rest - middle.astype(F32)).astype(BF16)


def mm3(a, b, dims=NN):
    ah, al = split2(a)
    bh, bl = split2(b)
    return mm(ah, bh, dims) + (mm(al, bh, dims) + mm(ah, bl, dims))


def mm6(a, b, dims=NN):
    ah, am, al = split3(a)
    bh, bm, bl = split3(b)
    low = mm(al, bh, dims) + (mm(am, bm, dims) + mm(ah, bl, dims))
    return mm(ah, bh, dims) + ((mm(am, bh, dims) + mm(ah, bm, dims)) + low)


def mm2(a, exact, dims=NN):
    ah, al = split2(a)
    return mm(ah, exact, dims) + mm(al, exact, dims)


def mm2r(exact, b, dims=NN):
    bh, bl = split2(b)
    return mm(exact, bh, dims) + mm(exact, bl, dims)


def mm3r(exact, b, dims=NN):
    bh, bm, bl = split3(b)
    return mm(exact, bh, dims) + (mm(exact, bm, dims) + mm(exact, bl, dims))


def norm(x):
    centred = x - jnp.mean(x, axis=-1, keepdims=True)
    scale = lax.rsqrt(jnp.mean(centred * centred, axis=-1, keepdims=True) + EPS)
    return centred * scale, scale


def norm_back(grad, unit, scale):
    return scale * (
        grad
        - jnp.mean(grad, axis=-1, keepdims=True)
        - unit * jnp.mean(grad * unit, axis=-1, keepdims=True)
    )


def iota(shape, axis):
    return lax.broadcasted_iota(jnp.int32, shape, axis)


def head_mask(rows, per_row):
    shape = (rows, WA)
    return iota(shape, 0) // per_row == iota(shape, 1) // HEAD


def colsum(x):
    return jnp.sum(x, axis=0, keepdims=True)


def total_of(x):
    return jnp.sum(jnp.sum(x, axis=1, keepdims=True), axis=0, keepdims=True)


def scratch_plan(rows, cols):
    length = rows * NI
    bases = layout(rows, cols)[1]
    final = bases[5] - bases[4]
    return dict(
        lk=((AP, WA), F32),
        weh=((128, WA), F32),
        wbd=((128, WP), F32),
        seqw=((NM, 1), F32),
        lmask=((NM, 1), F32),
        truth=((NM, 1), F32),
        target=((NP, 1), F32),
        pmask=((NP, 1), F32),
        offset=((NP, 1), F32),
        codes=((BI, length), F32),
        sites=((8, length), F32),
        wrel=((RP, WP), F32),
        tail=((8, 128), F32),
        kb=((WA, WA), BF16),
        vb=((WA, WA), BF16),
        amat=((BS, NI, WA), F32),
        pam=((BS, NI, WA), F32),
        hm=((64, WA), F32),
        letx=((128, length), F32),
        biash=((NB, 64, length), F32),
        prob=((BS, 64, length), F32),
        sg=((NM, WA), F32),
        att=((NM, WA), F32),
        xh1=((NM, WA), F32),
        r1=((NM, 1), F32),
        hid=((NM, UP), F32),
        rep=((NM, WA), F32),
        xh2=((NM, WA), F32),
        r2=((NM, 1), F32),
        dlog=((NM, 128), F32),
        left3=((NM, 96), BF16),
        mhi=((BI, DS, WP), BF16),
        mlo=((BI, DS, WP), BF16),
        rall=((NB, length, DS), BF16),
        prep=((NP, WP), F32),
        xh3=((NP, WP), F32),
        r3=((NP, 1), F32),
        proj=((NP, 5 * WP), F32),
        le=((BI * NJ, WP), F32),
        re=((NB * length * NJ, WP), F32),
        dm=((BI * length, WP), F32),
        gl=((BI, NJ, WP), F32),
        dr=((length, DS), F32),
        dmid=((NM, WA), F32),
        dbias=((NB, 64, length), F32),
        da=((BS, NI, WA), F32),
        dpam=((BS, NI, WA), F32),
        dtab=((BI, 16, RP), F32),
        dn=((NM, WA), F32),
        sum8=((8, WA), F32),
        grad=((bases[5], 128), F32),
        lets=((8, 128), F32),
        letr=((rows, 8, 128), F32),
        cnts=((8, 128), F32),
        cntr=((cols, 8, 128), F32),
        rs=((NB, NI, DS), BF16),
        rr=((rows, NB, NI, DS), BF16),
        os=((cols, BI, NJ, WP), BF16),
        orr=((cols, BI, NJ, WP), BF16),
        er=((rows, NB, NI, NJ, WP), BF16),
        ts=((cols, BI, NJ, WP), BF16),
        tr=((cols, BI, NJ, WP), BF16),
        ds=((BI, NJ, WP), BF16),
        dsr=((cols, BI, NJ, WP), BF16),
        gs=((rows, NB, NI, NJ, WP), BF16),
        ga=((rows // 2, NB, NI, NJ, WP), BF16),
        gh=((rows // 2 - 1, NB, NI, NJ, WP), BF16),
        gz=((rows // 2 - 1, NB, NI, NJ, WP), BF16),
        qs=((BI, NJ, WP), BF16),
        qr=((cols, BI, NJ, WP), BF16),
        us=((rows, NB, NI, DS), BF16),
        ur=((rows, NB, NI, DS), BF16),
        arx=((bases[4], 128), F32),
        fr=((rows, final // rows, 128), F32),
        fp=((final // rows, 128), F32),
        fc=((cols, final // rows, 128), F32),
        letters=((NB, NI, NS), jnp.int32),
        truths=((NB, NI, NS), jnp.int32),
        concealed=((NB, NI, NS), jnp.int32),
        existing=((NB, cols * NS), jnp.int32),
        ordinals=((NB, length), jnp.int32),
        observed=((NB, length), jnp.int32),
        targets=((NB, NI, NJ), jnp.int32),
        lookup=((LETTERS, WA), F32),
        w_a=((2135, WA), F32),
        w_c=((WA + UP, WA), F32),
        w_r=((UP + NREL, WP), F32),
        w_p=((840, WP), F32),
        scal=((1367,), F32),
    )


OPERANDS = 13


LET, RIGHT, EDGE, GEDGE, GRIGHT, SUM_ROW, SHARE_ROW = range(7)
CNT, OUTER, TRI, GMIX, GOUTER, SHARE_COL = range(6)
PHASES = 7


def main_kernel(rows, cols, names, *refs):
    operands = refs[:OPERANDS]
    gbig, grest, gfin, tout, aux = refs[OPERANDS : OPERANDS + 5]
    s = SimpleNamespace(**dict(zip(names, refs[OPERANDS + 5 : -7])))
    row_send, row_recv, col_send, col_recv, sum_send, sum_recv, load_sem = refs[-7:]
    held = refs[OPERANDS + 5 : -7][-OPERANDS:]
    loads = [
        pltpu.make_async_copy(far, near, load_sem.at[place])
        for place, (far, near) in enumerate(zip(operands, held))
    ]
    for load in loads:
        load.start()
    letters, truths, hidden_sites, existing, ordinals, observed, targets = held[:7]
    lookup, w_a, w_c, w_r, w_p, scal = held[7:]
    ROWS, bases = layout(rows, cols)
    length = rows * NI
    me_r, me_c = lax.axis_index(ROW), lax.axis_index(COL)

    barrier = pltpu.get_barrier_semaphore()
    for step in range(1, rows):
        pl.semaphore_signal(
            barrier,
            inc=1,
            device_id={ROW: lax.rem(me_r + step, rows), COL: me_c},
            device_id_type=MESH,
        )
    for step in range(1, cols):
        pl.semaphore_signal(
            barrier,
            inc=1,
            device_id={ROW: me_r, COL: lax.rem(me_c + step, cols)},
            device_id_type=MESH,
        )
    def exchange(along, phase, source, target):
        if along == ROW:
            count, me, number = rows, me_r, phase
            send, recv = row_send, row_recv
        else:
            count, me, number = cols, me_c, phase
            send, recv = col_send, col_recv
        copies = []
        for step in range(1, count):
            peer = lax.rem(me + step, count)
            origin = lax.rem(me + (count - step), count)
            where = (
                {ROW: peer, COL: me_c} if along == ROW else {ROW: me_r, COL: peer}
            )
            out = pltpu.make_async_remote_copy(
                src_ref=source(peer),
                dst_ref=target(me),
                send_sem=send.at[step - 1],
                recv_sem=recv.at[number, step - 1],
                device_id=where,
                device_id_type=MESH,
            )
            out.start()
            arriving = pltpu.make_async_remote_copy(
                src_ref=source(peer),
                dst_ref=target(origin),
                send_sem=send.at[step - 1],
                recv_sem=recv.at[number, step - 1],
                device_id=where,
                device_id_type=MESH,
            )
            copies.append((out, arriving))
        return copies

    def finish(copies):
        for out, arriving in copies:
            out.wait_send()
            arriving.wait_recv()

    for load in loads[:7]:
        load.wait()
    here = existing[...].astype(F32)
    sites = observed[...].astype(F32)
    numbers = ordinals[...].astype(F32)

    def by_protein(values, count, each):
        wide = (count, values.shape[1])
        return jnp.where(iota(wide, 0) // each == 0, values[0:1], values[1:2])

    def at_lane(values, lanes):
        return jnp.sum(jnp.where(iota(values.shape, 1) == lanes, values, 0.0), axis=1, keepdims=True)

    row_m, row_p = iota((NM, 1), 0), iota((NP, 1), 0)
    seq_m, res_m = (row_m // NI) % NS, row_m % NI
    spread_m = jnp.where(
        iota((NM, BI), 1) == (iota((NM, BI), 0) // (NI * NS)) * NI + iota((NM, BI), 0) % NI, 1.0, 0.0
    ).astype(BF16)
    spread_p = jnp.where(iota((NP, BI), 1) == iota((NP, BI), 0) // NJ, 1.0, 0.0).astype(BF16)

    def column_m(values):
        wide = mm(spread_m, values[...].reshape(BI, NS).astype(F32).astype(BF16))
        return at_lane(wide, seq_m)

    seq_weight = at_lane(by_protein(here, NM, NI * NS), me_c * NS + seq_m)
    letter = column_m(letters)
    loss_mask = column_m(hidden_sites) * seq_weight
    s.seqw[...] = seq_weight
    s.lmask[...] = loss_mask
    s.truth[...] = column_m(truths)
    s.target[...] = at_lane(
        mm(spread_p, targets[...].reshape(BI, NJ).astype(F32).astype(BF16)), row_p % NJ
    )

    me_y, me_z = me_r % 2, me_r // 2
    lines = rows // 2

    def row_copy(source, target, slot, send_slot, place_z, place_y):
        return pltpu.make_async_remote_copy(
            src_ref=source,
            dst_ref=target,
            send_sem=row_send.at[send_slot],
            recv_sem=row_recv.at[slot],
            device_id={ROW: place_z * 2 + place_y, COL: me_c},
            device_id_type=MESH,
        )

    def gather_lines(phase, blocks):
        own = blocks.at[me_r]
        out = [row_copy(own, own, (phase, 0), 0, me_z, 1 - me_y)]
        arriving = []
        for step in range(1, lines):
            out.append(
                row_copy(own, own, (phase, step), step, lax.rem(me_z + step, lines), me_y)
            )
        for copy in out:
            copy.start()
        for step in range(1, lines):
            place = lax.rem(me_z + (lines - step), lines) * 2
            block = blocks.at[place + me_y]
            row_copy(own, block, (phase, step), step, me_z, me_y).wait_recv()
            slot = lines - 1 + step
            out.append(row_copy(block, block, (phase, slot), slot, me_z, 1 - me_y))
            out[-1].start()
            arriving.append((blocks.at[place + 1 - me_y], slot))
        arriving.append((blocks.at[me_z * 2 + 1 - me_y], 0))
        for block, slot in arriving:
            row_copy(own, block, (phase, slot), 0, me_z, 1 - me_y).wait_recv()
        for copy in out:
            copy.wait_send()

    def start_scatter(phase, blocks, across):
        out = []
        for step in (*range(1, lines), 0):
            place = lax.rem(me_z + step, lines)
            out.append(
                row_copy(
                    blocks.at[place * 2 + 1 - me_y],
                    across.at[place],
                    (phase, step),
                    step,
                    me_z,
                    1 - me_y,
                )
            )
            out[-1].start()
        return out

    def finish_scatter(phase, out, blocks, across, halves, along):
        for step in (*range(1, lines), 0):
            place = lax.rem(me_z + step, lines)
            here = across.at[place]
            row_copy(here, here, (phase, step), step, me_z, 1 - me_y).wait_recv()
            both = blocks[place * 2 + me_y].astype(F32) + across[place].astype(F32)
            if step == 0:
                break
            halves[step - 1] = both.astype(BF16)
            slot = lines - 1 + step
            out.append(
                row_copy(halves.at[step - 1], along.at[step - 1], (phase, slot), slot, place, me_y)
            )
            out[-1].start()
        for step in range(1, lines):
            slot = lines - 1 + step
            here = along.at[step - 1]
            row_copy(here, here, (phase, slot), slot, me_z, me_y).wait_recv()
            both = both + along[step - 1].astype(F32)
        for copy in out:
            copy.wait_send()
        return both

    s.lets[...] = jnp.where(
        (iota((NI, 128), 0) == 0) & (iota((NI, 128), 1) == BS), total_of(loss_mask), 0.0
    )
    for b in range(NB):
        s.lets[:, b * NS : (b + 1) * NS] = letters[b].astype(F32)
    s.letr[me_r] = s.lets[...]
    pl.semaphore_wait(barrier, rows + cols - 2)
    flight = exchange(ROW, LET, lambda p: s.lets, lambda p: s.letr.at[p])

    first, second = me_r * NI + (row_p // NJ) % NI, me_c * NJ + row_p % NJ
    sites_p = by_protein(sites, NP, NI * NJ)
    numbers_p = by_protein(numbers, NP, NI * NJ)
    s.pmask[...] = at_lane(sites_p, first) * at_lane(sites_p, second)
    s.offset[...] = (
        jnp.clip(at_lane(numbers_p, first) - at_lane(numbers_p, second), -REACH, REACH) + REACH
    )
    numbers_b = by_protein(numbers, BI, NI)
    own = at_lane(numbers_b, me_r * NI + iota((BI, 1), 0) % NI)
    s.codes[...] = jnp.clip(own - numbers_b, -REACH, REACH) + REACH
    s.sites[...] = jnp.zeros((8, length), F32)
    s.sites[0:NB, :] = sites
    inv_all = 1.0 / (jnp.sum(here, axis=1, keepdims=True) + 1.0)
    inv_count = [inv_all[b : b + 1] for b in range(NB)]
    per_protein = jnp.sum(sites, axis=1, keepdims=True)
    inv_dist = 1.0 / jnp.maximum(colsum(per_protein * per_protein), 1.0)

    for load in loads[7:]:
        load.wait()

    def gain(begin, width):
        return scal[begin : begin + width].reshape(1, width)

    gain_row, gain_trans, gain_outer = gain(0, WA), gain(256, WA), gain(512, WA)
    gain_rel, gain_pair, gain_mixed = gain(768, WP), gain(896, WP), gain(1024, WP)
    bias_outer = gain(1152, WP)
    s.lk[...] = jnp.zeros((AP, WA), F32)
    s.lk[0:LETTERS, :] = lookup[...]
    s.weh[...] = jnp.zeros((128, WA), F32)
    s.weh[0:87, :] = w_a[2048:2135, :]
    s.wbd[...] = jnp.zeros((128, WP), F32)
    s.wbd[0:72, :] = w_p[768:840, :]
    s.wrel[...] = jnp.zeros((RP, WP), F32)
    s.wrel[0:NREL, :] = w_r[UP : UP + NREL, :]
    s.tail[...] = jnp.zeros((8, 128), F32)
    s.tail[0:1, 0:87] = scal[1280:1367].reshape(1, 87)

    table = s.lk[...]
    unit0, _ = norm(table)
    mapped = mm6(unit0 * gain_row, w_a[0 : 4 * WA, :], NT)
    tout[...] = mapped
    t_q = mapped[:, 0:WA] * HEAD ** (-0.5)
    t_k = mapped[:, WA : 2 * WA].astype(BF16).astype(F32)
    t_v = mapped[:, 2 * WA : 3 * WA].astype(BF16).astype(F32)
    t_g = jax.nn.sigmoid(mapped[:, 3 * WA :])
    square = head_mask(WA, AP)
    key_block = jnp.where(square, jnp.concatenate([t_k] * HEADS, axis=0), 0.0).astype(BF16)
    s.vb[...] = jnp.where(square, jnp.concatenate([t_v] * HEADS, axis=0), 0.0).astype(BF16)
    stacked = mm(jnp.concatenate(split3(t_q), axis=0), key_block, NT)
    score_table = stacked[0:AP] + (stacked[AP : 2 * AP] + stacked[2 * AP :])
    s.hm[...] = jnp.where(head_mask(64, NI), 1.0, 0.0)

    letter = letter.astype(jnp.int32)
    triple = jnp.where(
        (iota((NM, 3 * AP), 1) % AP) == letter, 1.0, 0.0
    ).astype(BF16)

    def chosen(values):
        return mm(triple, jnp.concatenate(split3(values), axis=0))

    s.amat[...] = chosen(score_table).reshape(BS, NI, WA)
    start = chosen(table)
    s.sg[...] = chosen(t_g)

    unit_r, _ = norm(s.wrel[...])
    bias_table = mm3(s.wbd[0:8, :], unit_r * gain_rel, NT)
    bias_parts = jnp.concatenate(split3(bias_table), axis=0)

    def codes(index):
        return jnp.where(
            iota((RP, length), 0) == s.codes[index : index + 1, :].astype(jnp.int32), 1.0, 0.0
        ).astype(BF16)

    for b in range(NB):
        for i in range(NI):
            part = mm(bias_parts, codes(b * NI + i))
            part = part[0:8] + (part[8:16] + part[16:24])
            for h in range(HEADS):
                s.biash[b, h * NI + i : h * NI + i + 1, :] = part[h : h + 1, :]

    finish(flight)
    letters_all = s.letr[...].reshape(length, 128).T
    s.letx[...] = letters_all
    s.cnts[...] = jnp.broadcast_to(
        jnp.sum(letters_all[BS : BS + 1, :], axis=1, keepdims=True), (8, 128)
    )
    s.cntr[me_c] = s.cnts[...]
    count_flight = exchange(COL, CNT, lambda p: s.cnts, lambda p: s.cntr.at[p])

    def letter_codes(bs):
        row = s.letx[pl.ds(bs, 1), :].astype(jnp.int32)
        one = jnp.where(iota((AP, length), 0) == row, 1.0, 0.0)
        return jnp.concatenate([one] * HEADS, axis=0).astype(BF16)

    def spread(value):
        wide = jnp.broadcast_to(value[None], (HEADS, NI, WA)).reshape(64, WA)
        return wide * s.hm[...]

    def gather_heads(value):
        return jnp.sum((value * s.hm[...]).reshape(HEADS, NI, WA), axis=0)

    for b in range(NB):
        key_mask = s.sites[b : b + 1, :]

        @pl.loop(0, NS // TOGETHER)
        def _(q):
            for part in range(TOGETHER):
                bs = b * NS + q * TOGETHER + part
                code = letter_codes(bs)
                wide = [spread(p.astype(F32)).astype(BF16) for p in split2(s.amat[bs])]
                raw = mm(jnp.concatenate(wide, axis=0), code)
                scores = (raw[0:64] + raw[64:128]) + s.biash[b]
                scores = jnp.where(key_mask > 0, scores, -1000000000.0)
                power = jnp.exp(scores - jnp.max(scores, axis=-1, keepdims=True))
                weight = power / jnp.sum(power, axis=-1, keepdims=True)
                s.prob[bs] = weight
                picked = mm(jnp.concatenate(split2(weight), axis=0), code, NT)
                s.pam[bs] = gather_heads(picked[0:64] + picked[64:128])

    att = mm2(s.pam[...].reshape(NM, WA), s.vb[...])
    s.att[...] = att
    mid = start + mm3(s.sg[...] * att, w_c[0:WA, :])
    unit1, scale1 = norm(mid)
    s.xh1[...] = unit1
    s.r1[...] = scale1
    hidden = jnp.maximum(mm3(unit1 * gain_trans, w_a[4 * WA : 4 * WA + UP, :], NT), 0.0)
    s.hid[...] = hidden
    rep = mid + mm3(hidden, w_c[WA:, :])
    s.rep[...] = rep
    unit2, scale2 = norm(rep)
    s.xh2[...] = unit2
    s.r2[...] = scale2
    seq_weight = s.seqw[...]
    lane = iota((NM, 128), 1)
    edges = mm3(unit2 * gain_outer, s.weh[...], NT) * seq_weight

    right = jnp.where((lane >= 32) & (lane < 64), edges, 0.0).astype(BF16)
    spot = iota((128, DS), 0)
    repeat = jnp.where(spot - 32 == iota((128, DS), 1) // NS, 1.0, 0.0)
    repeat = jnp.where((spot >= 32) & (spot < 64), repeat, 0.0).astype(BF16)
    wide = mm(right, repeat)
    own_seq = (iota((NM, DS), 0) // NI) % NS == iota((NM, DS), 1) % NS
    wide = jnp.sum(jnp.where(own_seq, wide, 0.0).reshape(NB, NS, NI, DS), axis=1)
    s.rs[...] = wide.astype(BF16)
    s.rr[me_r] = s.rs[...]
    flight = exchange(ROW, RIGHT, lambda p: s.rs, lambda p: s.rr.at[p])

    finish(count_flight)
    masked = jnp.maximum(jnp.sum(s.cntr[...], axis=0)[0:1, 0:1], 1.0)
    logits = mm3(rep, s.weh[...], NT) + s.tail[0:1, :]
    valid = (lane >= 64) & (lane < 64 + LETTERS)
    top = jnp.max(jnp.where(valid, logits, -3e38), axis=-1, keepdims=True)
    power = jnp.where(valid, jnp.exp(jnp.where(valid, logits, top) - top), 0.0)
    whole = jnp.sum(power, axis=-1, keepdims=True)
    truth = lane - 64 == s.truth[...].astype(jnp.int32)
    truth = truth & valid
    picked = jnp.sum(jnp.where(truth, logits, 0.0), axis=-1, keepdims=True)
    loss_mask = s.lmask[...]
    msa_sum = colsum((jnp.log(whole) + top - picked) * loss_mask)
    s.dlog[...] = (power / whole - jnp.where(truth, 1.0, 0.0)) * (loss_mask / masked)

    order_to = (iota((NM, NM), 0) // (NI * NS) == iota((NM, NM), 1) // (NI * NS)) & (
        (iota((NM, NM), 0) // NS) % NI == iota((NM, NM), 1) % NI
    )
    order_to = order_to & (iota((NM, NM), 0) % NS == (iota((NM, NM), 1) // NI) % NS)
    order = jnp.where(order_to, 1.0, 0.0).astype(BF16)
    left = mm3r(order, jnp.where(lane < 32, edges, 0.0))
    high, low = split2(left)
    high32, low32 = high.astype(F32), low.astype(F32)
    left3 = high32 + pltpu.roll(low32, 32, 1) + pltpu.roll(high32, 64, 1)
    s.left3[...] = left3[:, 0:96].astype(BF16)

    def outer_weight(d):
        return w_r[pl.ds(d, WO, stride=WO), :]

    for pair in range(WO // 2):
        both = jnp.concatenate([outer_weight(2 * pair), outer_weight(2 * pair + 1)], axis=1)
        wh, wl = split2(both)
        made = mm(s.left3[...], jnp.concatenate([wh, wh, wl], axis=0))
        for half in range(2):
            d = 2 * pair + half
            mh, ml = split2(made[:, half * WP : (half + 1) * WP].reshape(BI, NS, WP))
            s.mhi[:, d * NS : (d + 1) * NS, :] = mh
            s.mlo[:, d * NS : (d + 1) * NS, :] = ml

    finish(flight)
    for b in range(NB):
        s.rall[b] = s.rr[:, b].astype(F32).reshape(length, DS).astype(BF16)
    for b in range(NB):

        @pl.loop(0, NI)
        def _(i):
            bi = b * NI + i
            block = mm(s.rall[b], s.mhi[bi]) + mm(s.rall[b], s.mlo[bi])
            block = block * inv_count[b]
            for c in range(cols):
                s.os[c, bi] = block[c * NJ : (c + 1) * NJ].astype(BF16)

    s.orr[me_c] = s.os[me_c]
    finish(exchange(COL, OUTER, lambda p: s.os.at[p], lambda p: s.orr.at[p]))

    pair_lane = iota((NP, 128), 1)
    offset = s.offset[...].astype(jnp.int32)
    pair_codes = jnp.where(pair_lane == offset, 1.0, 0.0).astype(BF16)
    outer = s.orr[0].astype(F32)
    for c in range(1, cols):
        outer = outer + s.orr[c].astype(F32)
    pair_rep = (mm3r(pair_codes, s.wrel[...]) + outer.reshape(NP, WP)) + bias_outer
    s.prep[...] = pair_rep
    unit3, scale3 = norm(pair_rep)
    s.xh3[...] = unit3
    s.r3[...] = scale3
    proj = mm3(unit3 * gain_pair, w_p[0 : 5 * WP, :], NT)
    pair_mask = s.pmask[...]
    sig1 = jax.nn.sigmoid(proj[:, WP : 2 * WP])
    sig2 = jax.nn.sigmoid(proj[:, 3 * WP : 4 * WP])
    sig3 = jax.nn.sigmoid(proj[:, 4 * WP :])
    s.proj[:, 0 : WP] = proj[:, 0:WP]
    s.proj[:, WP : 2 * WP] = sig1
    s.proj[:, 2 * WP : 3 * WP] = proj[:, 2 * WP : 3 * WP]
    s.proj[:, 3 * WP : 4 * WP] = sig2
    s.proj[:, 4 * WP :] = sig3
    s.le[...] = sig1 * proj[:, 0:WP] * pair_mask
    right_edge = (sig2 * proj[:, 2 * WP : 3 * WP] * pair_mask).astype(BF16)
    s.er[me_r] = right_edge.reshape(NB, NI, NJ, WP)
    gather_lines(EDGE, s.er)
    for b in range(NB):
        for r in range(rows):
            begin = (b * length + r * NI) * NJ
            s.re[begin : begin + NI * NJ, :] = (
                s.er[r, b].astype(F32).reshape(NI * NJ, WP)
            )

    for b in range(NB):

        @pl.loop(0, NI)
        def _(i):
            bi = b * NI + i
            for c in range(cols):
                block = jnp.zeros((NJ, WP), F32)
                for k in range(NJ):
                    other = s.re[pl.ds((b * length + c * NJ) * NJ + k, NJ, stride=NJ), :]
                    block = block + s.le[pl.ds(bi * NJ + k, 1), :] * other
                s.ts[c, bi] = block.astype(BF16)

    s.tr[me_c] = s.ts[me_c]
    finish(exchange(COL, TRI, lambda p: s.ts.at[p], lambda p: s.tr.at[p]))

    mixed = s.tr[0].astype(F32)
    for c in range(1, cols):
        mixed = mixed + s.tr[c].astype(F32)
    unit4, scale4 = norm(mixed.reshape(NP, WP))
    w_out = w_p[5 * WP : 6 * WP, :]
    moved = mm3(unit4 * gain_mixed, w_out, NT)
    sig3 = s.proj[:, 4 * WP :]
    pair_out = s.prep[...] + sig3 * moved
    bins = mm3(pair_out, s.wbd[...], NT) + pltpu.roll(
        jnp.where(iota((8, 128), 1) < BINS, s.tail[...], 0.0), 8, 1
    )[0:1]
    valid = (pair_lane >= 8) & (pair_lane < 8 + BINS)
    top = jnp.max(jnp.where(valid, bins, -3e38), axis=-1, keepdims=True)
    power = jnp.where(valid, jnp.exp(jnp.where(valid, bins, top) - top), 0.0)
    whole = jnp.sum(power, axis=-1, keepdims=True)
    truth = (pair_lane - 8 == s.target[...].astype(jnp.int32)) & valid
    picked = jnp.sum(jnp.where(truth, bins, 0.0), axis=-1, keepdims=True)
    dist_sum = colsum((jnp.log(whole) + top - picked) * pair_mask)
    dbins = (power / whole - jnp.where(truth, 1.0, 0.0)) * (pair_mask * inv_dist)

    def put(place, value, skip=0):
        base = place + skip
        height, width = value.shape
        for w in range(width // 128):
            s.grad[base + w * height : base + (w + 1) * height, :] = value[
                :, w * 128 : (w + 1) * 128
            ]

    sizes = {CORE: 2, X: cols // 2, Y: 2, Z: rows // 2}
    places = {CORE: me_c % 2, X: me_c // 2, Y: me_r % 2, Z: me_r // 2}

    def line_peer(axis, place):
        if axis == CORE:
            return {ROW: me_r, COL: me_c // 2 * 2 + place}
        if axis == X:
            return {ROW: me_r, COL: place * 2 + me_c % 2}
        if axis == Y:
            return {ROW: me_r // 2 * 2 + place, COL: me_c}
        return {ROW: place * 2 + me_r % 2, COL: me_c}

    class Sum:
        def __init__(self, number):
            self.number = number
            self.stage = -1
            self.used = [0, 0]
            base, size = bases[number] // 8, (bases[number + 1] - bases[number]) // 8
            self.parts = []
            for half in range(2):
                order = (CORE, X, Y, Z) if half == 0 else (CORE, Y, X, Z)
                begin = base + half * (size // 2)
                self.parts.append(SimpleNamespace(order=order, at=begin, size=size // 2, rx=begin))
            self.flight = []

        def copies(self, part, half, axis, source, target, arrive):
            count = sizes[axis]
            for step in range(1, count):
                peer = lax.rem(places[axis] + step, count)
                origin = lax.rem(places[axis] + (count - step), count)
                used = self.used[half]
                self.used[half] += 1
                both = []
                for end in (target(peer, step), arrive(origin, step)):
                    both.append(
                        pltpu.make_async_remote_copy(
                            src_ref=source(peer),
                            dst_ref=end,
                            send_sem=sum_send.at[self.number, half, step - 1],
                            recv_sem=sum_recv.at[self.number, half, used],
                            device_id=line_peer(axis, peer),
                            device_id_type=MESH,
                        )
                    )
                both[0].start()
                self.flight.append(both)

        def advance(self):
            finish(self.flight)
            self.flight = []
            if 0 <= self.stage < 4:
                for part in self.parts:
                    self.add(part)
            self.stage += 1
            if self.stage == 4:
                for part in self.parts:
                    self.store(part)
            if self.stage < 4:
                for half, part in enumerate(self.parts):
                    self.start_sum(part, half)
            elif self.stage < 8:
                for half, part in enumerate(self.parts):
                    self.start_share(part, half)

        def start_sum(self, part, half):
            axis = part.order[self.stage]
            small = part.size // sizes[axis]
            part.small, part.axis = small, axis

            def source(peer):
                return s.grad.at[rows_at(part.at + peer * small, small)]

            def target(place, step):
                return s.arx.at[pl.ds((part.rx + (step - 1) * small) * 8, small * 8)]

            self.copies(part, half, axis, source, target, target)

        def add(self, part):
            mine = rows_at(part.at + places[part.axis] * part.small, part.small)
            value = s.grad[mine, :]
            for step in range(1, sizes[part.axis]):
                begin = (part.rx + (step - 1) * part.small) * 8
                value = value + s.arx[begin : begin + part.small * 8, :]
            s.grad[mine, :] = value
            part.at = part.at + places[part.axis] * part.small
            part.rx += (sizes[part.axis] - 1) * part.small
            part.size = part.small

        def store(self, part):
            value = s.grad[rows_at(part.at, part.size), :]
            if self.number < BF16_GROUPS:
                gbig[pl.ds(part.at, part.size)] = value.reshape(part.size, 8, 128).astype(BF16)
            else:
                grest[rows_at(part.at - bases[3] // 8, part.size), :] = value

        def start_share(self, part, half):
            axis = part.order[7 - self.stage]
            size, here = part.size, part.at
            first = here - places[axis] * size

            def spot(place, step):
                at = first + place * size
                if self.number < BF16_GROUPS:
                    return gbig.at[pl.ds(at, size)]
                return grest.at[rows_at(at - bases[3] // 8, size)]

            self.copies(
                part,
                half,
                axis,
                lambda peer: spot(places[axis], 0),
                lambda peer, step: spot(places[axis], step),
                spot,
            )
            part.at, part.size = first, size * sizes[axis]

    def rows_at(unit, count):
        return pl.ds(pl.multiple_of(unit * 8, 8), count * 8)

    early, middle, late, rest = [Sum(number) for number in range(4)]

    def column_products(name, place):
        s.sum8[...] = jnp.zeros((8, WA), F32)

        @pl.loop(0, NM // 32)
        def _(q):
            some = pl.ds(pl.multiple_of(q * 32, 32), 32)
            product = s.dn[some, :] * name[some, :]
            s.sum8[...] += jnp.sum(product.reshape(4, 8, WA), axis=0)

        whole = colsum(s.sum8[...])
        for half in range(2):
            s.grad[small + place + half : small + place + half + 1, :] = whole[
                :, 128 * half : 128 * half + 128
            ]

    for begin, end in (
        (ROWS.out + WP, bases[1]),
        (ROWS.o + 2 * WA, bases[3]),
        (ROWS.rel + 72, bases[4]),
        (ROWS.small, bases[5]),
    ):
        if end > begin:
            s.grad[begin:end, :] = jnp.zeros((end - begin, 128), F32)
    small = ROWS.small
    put(ROWS.dist, mm3(dbins, pair_out, TN)[8 : 8 + BINS])
    dbias_dist = pltpu.roll(jnp.broadcast_to(colsum(dbins), (8, 128)), 120, 1)[0:1]
    dout = mm3(dbins, s.wbd[...])
    dgate = dout * moved * (sig3 * (1.0 - sig3))
    dmoved = dout * sig3
    put(ROWS.out, mm3(dmoved, unit4 * gain_mixed, TN))
    dnormed = mm3(dmoved, w_out)
    s.grad[small + 5 : small + 6, :] = colsum(dnormed * unit4)
    dmixed = norm_back(dnormed * gain_mixed, unit4, scale4)
    s.ds[...] = dmixed.astype(BF16).reshape(BI, NJ, WP)
    s.dsr[me_c] = s.ds[...]
    finish(exchange(COL, GMIX, lambda p: s.ds, lambda p: s.dsr.at[p]))
    for bi in range(BI):
        for c in range(cols):
            begin = bi * length + c * NJ
            s.dm[begin : begin + NJ, :] = s.dsr[c, bi].astype(F32)

    for b in range(NB):

        @pl.loop(0, rows)
        def _(r):
            for q in range(NI):
                block = jnp.zeros((NJ, WP), F32)
                for i in range(NI):
                    bi = b * NI + i
                    block = block + (
                        s.dm[pl.ds(bi * length + r * NI + q, 1), :]
                        * s.le[bi * NJ : (bi + 1) * NJ, :]
                    )
                s.gs[r, b, q] = block.astype(BF16)

    flight = start_scatter(GEDGE, s.gs, s.ga)
    for b in range(NB):

        @pl.loop(0, NI)
        def _(i):
            bi = b * NI + i
            block = jnp.zeros((NJ, WP), F32)
            for j in range(length):
                begin = (b * length + j) * NJ
                block = block + (
                    s.dm[pl.ds(bi * length + j, 1), :] * s.re[begin : begin + NJ, :]
                )
            s.gl[bi] = block

    dright = finish_scatter(GEDGE, flight, s.gs, s.ga, s.gh, s.gz)
    dright = dright.reshape(NP, WP) * pair_mask
    dleft = s.gl[...].reshape(NP, WP) * pair_mask
    p1, sig1 = s.proj[:, 0:WP], s.proj[:, WP : 2 * WP]
    p2, sig2 = s.proj[:, 2 * WP : 3 * WP], s.proj[:, 3 * WP : 4 * WP]
    dproj = jnp.concatenate(
        [
            dleft * sig1,
            dleft * p1 * (sig1 * (1.0 - sig1)),
            dright * sig2,
            dright * p2 * (sig2 * (1.0 - sig2)),
            dgate,
        ],
        axis=1,
    )
    unit3 = s.xh3[...]
    put(ROWS.tri, mm3(dproj, unit3 * gain_pair, TN))
    dnormed = mm3(dproj, w_p[0 : 5 * WP, :])
    s.grad[small + 4 : small + 5, :] = colsum(dnormed * unit3)
    drep = dout + norm_back(dnormed * gain_pair, unit3, s.r3[...])
    s.grad[small + 6 : small + 7, :] = colsum(drep)
    s.grad[ROWS.rel : ROWS.rel + 72, :] = mm2r(pair_codes, drep, TN)[0:72]
    s.qs[...] = drep.astype(BF16).reshape(BI, NJ, WP)
    s.qr[me_c] = s.qs[...]
    finish(exchange(COL, GOUTER, lambda p: s.qs, lambda p: s.qr.at[p]))

    for b in range(NB):
        turned = s.rall[b].astype(F32).T.astype(BF16)
        s.dr[...] = jnp.zeros((length, DS), F32)

        @pl.loop(0, NI)
        def _(i):
            bi = b * NI + i
            block = jnp.concatenate([s.qr[c, bi] for c in range(cols)], axis=0)
            s.dr[...] += mm(block, s.mhi[bi], NT) + mm(block, s.mlo[bi], NT)
            mh, ml = split2(mm(turned, block) * inv_count[b])
            s.mhi[bi] = mh
            s.mlo[bi] = ml

        for r in range(rows):
            s.us[r, b] = (s.dr[r * NI : (r + 1) * NI, :] * inv_count[b]).astype(BF16)
    s.ur[me_r] = s.us[me_r]
    flight = exchange(ROW, GRIGHT, lambda p: s.us.at[p], lambda p: s.ur.at[p])

    left3 = s.left3[...].astype(F32).T.astype(BF16)
    left_both, left_high = left3[0:64], left3[0:32]
    dleft = jnp.zeros((NM, WO), F32)
    for pair in range(WO // 2):
        two = (2 * pair, 2 * pair + 1)
        wh, wl = split2(jnp.concatenate([outer_weight(d) for d in two], axis=1))

        def both_of(ref):
            return jnp.concatenate(
                [ref[:, d * NS : (d + 1) * NS, :].reshape(NM, WP) for d in two], axis=1
            )

        mh, ml = both_of(s.mhi), both_of(s.mlo)
        dleft = dleft + (mm(mh, wh, NT) + (mm(ml, wh, NT) + mm(mh, wl, NT)))
        made = mm(left_both, mh)
        made = made[0:32] + made[32:64] + mm(left_high, ml)
        for half in range(2):
            s.grad[pl.ds(ROWS.outer + two[half], WO, stride=WO), :] = made[
                :, half * WP : (half + 1) * WP
            ]
    early.advance()
    dleft = mm3r(order, dleft, TN)

    finish(flight)
    dright = s.ur[0].astype(F32)
    for r in range(1, rows):
        dright = dright + s.ur[r].astype(F32)
    wide = jnp.broadcast_to(dright[:, None], (NB, NS, NI, DS)).reshape(NM, DS)
    dedges = mm2(jnp.where(own_seq, wide, 0.0), repeat, NT)
    dedges = (dedges + jnp.concatenate([dleft, jnp.zeros((NM, 96), F32)], axis=1)) * seq_weight
    unit2, rep = s.xh2[...], s.rep[...]
    dlog = s.dlog[...]
    put(ROWS.eh, (mm3(dedges, unit2 * gain_outer, TN) + mm3(dlog, rep, TN))[0:88])
    s.dn[...] = mm3(dedges, s.weh[...])
    dnormed = s.dn[...]
    column_products(s.xh2, 2)
    drep = mm3(dlog, s.weh[...]) + norm_back(dnormed * gain_outer, unit2, s.r2[...])
    early.advance()
    hidden = s.hid[...]
    put(ROWS.back, mm3(hidden, drep, TN))
    middle.advance()
    early.advance()
    dhidden = jnp.where(hidden > 0, mm3(drep, w_c[WA:, :], NT), 0.0)
    unit1 = s.xh1[...]
    put(ROWS.up, mm3(dhidden, unit1 * gain_trans, TN))
    s.dn[...] = mm3(dhidden, w_a[4 * WA : 4 * WA + UP, :])
    dnormed = s.dn[...]
    column_products(s.xh1, 0)
    dmid = drep + norm_back(dnormed * gain_trans, unit1, s.r1[...])
    sg, att = s.sg[...], s.att[...]
    put(ROWS.o, mm3(sg * att, dmid, TN))
    dgated = mm3(dmid, w_c[0:WA, :], NT)
    late.advance()
    middle.advance()
    early.advance()
    single = triple[:, 0:AP]
    put(ROWS.tabs, mm2r(single, dmid, TN), 4 * AP)
    put(ROWS.tabs, mm2r(single, dgated * att, TN), 2 * AP)
    datt = dgated * sg

    pam = s.pam[...].reshape(NM, WA)
    blocks = jnp.where(head_mask(WA, AP), mm3(pam, datt, TN), 0.0)
    put(ROWS.tabs, jnp.sum(blocks.reshape(HEADS, AP, WA), axis=0))
    rest.advance()
    s.dpam[...] = mm2(datt, s.vb[...], NT).reshape(BS, NI, WA)
    for b in range(NB):
        key_mask = s.sites[b : b + 1, :]
        s.dbias[b] = jnp.zeros((64, length), F32)

        def attention_back(q):
            together = jnp.zeros((64, length), F32)
            for part in range(TOGETHER):
                bs = b * NS + q * TOGETHER + part
                code = letter_codes(bs)
                wide = [spread(p.astype(F32)).astype(BF16) for p in split2(s.dpam[bs])]
                raw = mm(jnp.concatenate(wide, axis=0), code)
                dweight = raw[0:64] + raw[64:128]
                weight = s.prob[bs]
                inner = jnp.sum(weight * dweight, axis=-1, keepdims=True)
                dscore = jnp.where(key_mask > 0, weight * (dweight - inner), 0.0)
                together = together + dscore
                back = mm(jnp.concatenate(split2(dscore), axis=0), code, NT)
                s.da[bs] = gather_heads(back[0:64] + back[64:128])
            s.dbias[b] += together

        for part in range(2):
            count = NS // TOGETHER // 2
            pl.loop(part * count, (part + 1) * count)(attention_back)
            for group in (early, middle, late, rest):
                group.advance()

    put(ROWS.score, mm2r(single, s.da[...].reshape(NM, WA), TN))
    for b in range(NB):
        for i in range(NI):
            part = jnp.concatenate(
                [s.dbias[b, h * NI + i : h * NI + i + 1, :] for h in range(HEADS)], axis=0
            )
            s.dtab[b * NI + i] = mm(
                jnp.concatenate(split2(part), axis=0), codes(b * NI + i), NT
            )
    s.grad[ROWS.bias : ROWS.bias + 8, :] = jnp.sum(
        s.dtab[...].reshape(2 * BI, 8, RP), axis=0
    )

    lane1 = iota((1, 128), 1)
    s.grad[small + 7 : small + 8, :] = jnp.where(lane1 < BINS, dbias_dist, colsum(dlog))
    s.grad[small + 8 : small + 9, :] = jnp.where(
        lane1 == 0, msa_sum, jnp.where(lane1 == 1, dist_sum, 0.0)
    )
    aux[...] = jnp.where(iota((8, 128), 1) == 0, masked, inv_dist)

    last = bases[4]
    piece = (bases[5] - last) // rows

    def mine(p):
        return pl.ds(pl.multiple_of(last + p * piece, 8), piece)

    def spot(p):
        return gfin.at[pl.ds(pl.multiple_of(p * piece, 8), piece)]

    s.fr[me_r] = s.grad[mine(me_r), :]
    flight = exchange(ROW, SUM_ROW, lambda p: s.grad.at[mine(p)], lambda p: s.fr.at[p])
    for group in (middle, late, rest):
        group.advance()
    finish(flight)
    summed = s.fr[0]
    for r in range(1, rows):
        summed = summed + s.fr[r]
    s.fp[...] = summed
    s.fc[me_c] = summed
    flight = exchange(COL, SHARE_COL, lambda p: s.fp, lambda p: s.fc.at[p])
    for group in (middle, late, rest):
        group.advance()
    finish(flight)
    summed = s.fc[0]
    for c in range(1, cols):
        summed = summed + s.fc[c]
    gfin[pl.ds(pl.multiple_of(me_r * piece, 8), piece), :] = summed
    flight = exchange(ROW, SHARE_ROW, lambda p: spot(me_r), spot)
    while min(group.stage for group in (early, middle, late, rest)) < 8:
        for group in (early, middle, late, rest):
            if group.stage < 8:
                group.advance()
    finish(flight)


def post_kernel(rows, cols, *refs):
    gbig, grest, gfin, tout, aux = refs[:5]
    weights, far_moments = refs[5:11], refs[11:23]
    far, loss_out, size_out = refs[23:41], refs[41], refs[42]
    new, moments = refs[43:61], refs[61:73]
    lk, wrel, g_a, g_small, g_rel, store_sem, load_sem = refs[73:]
    loads = [
        pltpu.make_async_copy(source, near, load_sem.at[place])
        for place, (source, near) in enumerate(zip(far_moments, moments))
    ]
    for place in (2, 8, 1, 7, 3, 9, 4, 10, 0, 6, 5, 11):
        loads[place].start()
    means, squares = moments[0:6], moments[6:12]
    lookup, w_a, w_c, w_r, w_p, scal = weights
    ROWS, bases = layout(rows, cols)

    def big(begin, count):
        part = gbig[begin // 8 : (begin + count) // 8].astype(F32)
        return part.reshape(count, 128)

    def exact(begin, count):
        if begin >= bases[4]:
            return gfin[begin - bases[4] : begin - bases[4] + count, :]
        return grest[begin - bases[3] : begin - bases[3] + count, :]

    lk[...] = jnp.zeros((AP, WA), F32)
    lk[0:LETTERS, :] = lookup[...]
    wrel[...] = jnp.zeros((RP, WP), F32)
    wrel[0:NREL, :] = w_r[UP : UP + NREL, :]

    def table(begin):
        return jnp.concatenate([exact(begin, AP), exact(begin + AP, AP)], axis=1)

    dscore = table(ROWS.score)
    dvalue, dgate, dstart = [table(ROWS.tabs + 2 * AP * place) for place in range(3)]
    mapped = tout[...]
    t_q = mapped[:, 0:WA] * HEAD ** (-0.5)
    t_k = mapped[:, WA : 2 * WA].astype(BF16).astype(F32)
    t_g = jax.nn.sigmoid(mapped[:, 3 * WA :])
    square = head_mask(WA, AP)
    key_block = jnp.where(square, jnp.concatenate([t_k] * HEADS, axis=0), 0.0).astype(BF16)
    dq = mm2(dscore, key_block) * HEAD ** (-0.5)
    dk = jnp.where(square, mm3(dscore, t_q, TN), 0.0)
    dk = jnp.sum(dk.reshape(HEADS, AP, WA), axis=0)
    dg = dgate * (t_g * (1.0 - t_g))
    dmapped = jnp.concatenate([dq, dk, dvalue, dg], axis=1)
    unit0, scale0 = norm(lk[...])
    gain_row = scal[0:WA].reshape(1, WA)
    g_a[...] = mm3(dmapped, unit0 * gain_row, TN)
    dnormed = mm3(dmapped, w_a[0 : 4 * WA, :])
    dgain_row = colsum(dnormed * unit0)
    g_lookup = dstart + norm_back(dnormed * gain_row, unit0, scale0)

    unit_r, scale_r = norm(wrel[...])
    gain_rel = scal[768:896].reshape(1, WP)
    dtable = exact(ROWS.bias, 8)
    g_bias = mm3(dtable, unit_r * gain_rel)
    dnormed = mm3(dtable, w_p[768:776, :], TN)
    dgain_rel = colsum(dnormed * unit_r)
    g_rel[...] = exact(ROWS.rel, 72) + norm_back(
        dnormed * gain_rel, unit_r, scale_r
    )[0:72]

    base = ROWS.small
    g_small[0:WA] = dgain_row.reshape(WA)
    for place, row in ((256, 0), (384, 1), (512, 2), (640, 3), (896, 4), (1024, 5), (1152, 6)):
        g_small[place : place + 128] = exact(base + row, 1).reshape(128)
    g_small[768:896] = dgain_rel.reshape(128)
    lane = iota((1, 128), 1)
    tail = jnp.where(lane < 87, exact(base + 7, 1), 0.0)
    g_small[1280:1408] = tail.reshape(128)

    rel_row = iota((72, 128), 0)
    squares_sum = jnp.zeros((1, 1), F32)
    for begin, count in (
        (ROWS.outer, UP),
        (ROWS.tri, 768),
        (ROWS.back, 2 * UP),
        (ROWS.up, 2 * UP),
        (ROWS.o, 2 * WA),
    ):
        part = big(begin, count)
        squares_sum = squares_sum + total_of(part * part)
    for part in (
        g_a[...],
        g_lookup[0:LETTERS],
        jnp.where(rel_row < NREL, g_rel[...], 0.0),
        g_bias,
        dgain_row,
        exact(base, 7),
        exact(ROWS.eh, 87),
        exact(ROWS.eh + 88, 87),
        exact(ROWS.dist, BINS),
        dgain_rel,
        tail,
    ):
        squares_sum = squares_sum + total_of(part * part)
    size = jnp.sqrt(squares_sum)
    scale = jnp.minimum(1.0, CLIP / size)

    def adam(which, where, grad, factor=scale):
        clipped = grad * factor
        weight = weights[which][where]
        moment = B1 * means[which][where] + (1.0 - B1) * clipped
        second = B2 * squares[which][where] + (1.0 - B2) * clipped * clipped
        step = (moment / (1.0 - B1**STEP)) / (jnp.sqrt(second / (1.0 - B2**STEP)) + ADAM_EPS)
        new[3 * which][where] = weight - RATE * (step + DECAY * weight)
        new[3 * which + 1][where] = moment
        new[3 * which + 2][where] = second

    every = slice(None)
    stores = []

    def leave(which):
        for place in range(3 * which, 3 * which + 3):
            store = pltpu.make_async_copy(new[place], far[place], store_sem.at[place])
            store.start()
            stores.append(store)

    def ready(which):
        loads[which].wait()
        loads[6 + which].wait()

    ready(2)
    for w in range(2):
        half = slice(128 * w, 128 * w + 128)
        adam(2, (slice(0, WA), half), big(ROWS.o + w * WA, WA))
        adam(2, (slice(WA, WA + UP), half), big(ROWS.back + w * UP, UP))
    leave(2)
    ready(1)
    adam(1, (slice(0, 4 * WA), every), g_a[...])
    for w in range(2):
        half = slice(128 * w, 128 * w + 128)
        adam(1, (slice(1024, 2048), half), big(ROWS.up + w * UP, UP))
        adam(1, (slice(2048, 2135), half), exact(ROWS.eh + w * 88, 87))
    leave(1)
    ready(3)
    adam(3, (slice(0, UP), every), big(ROWS.outer, UP))
    adam(3, (slice(UP, UP + NREL), every), g_rel[0:NREL, :])
    leave(3)
    ready(4)
    adam(4, (slice(0, 768), every), big(ROWS.tri, 768))
    adam(4, (slice(768, 776), every), g_bias)
    adam(4, (slice(776, 840), every), exact(ROWS.dist, BINS))
    leave(4)
    ready(0)
    adam(0, (every, every), g_lookup[0:LETTERS])
    leave(0)
    ready(5)
    adam(5, (slice(0, 1367),), g_small[0:1367], scale.reshape(1))
    leave(5)

    sums = exact(base + 8, 1)
    loss = sums[:, 0:1] / aux[0:1, 0:1] + sums[:, 1:2] * aux[0:1, 1:2]
    loss_out[0] = loss[0, 0]
    size_out[0] = size[0, 0]
    for store in stores:
        store.wait()


def vmem():
    return pl.BlockSpec(memory_space=pltpu.VMEM)


def per_device(rows, cols, *arrays):
    letters, truth, concealed, existing, ordinals, observed, bins = arrays[:7]

    def turned(group):
        return [w.T if place in (1, 4) else w for place, w in enumerate(group)]

    weights, means, squares = turned(arrays[7:13]), turned(arrays[13:19]), turned(arrays[19:25])
    plan = scratch_plan(rows, cols)
    bases = layout(rows, cols)[1]
    far = pl.BlockSpec(memory_space=pltpu.HBM)
    summed = pl.pallas_call(
        functools.partial(main_kernel, rows, cols, tuple(plan)),
        out_shape=(
            jax.ShapeDtypeStruct((bases[3] // 8, 8, 128), BF16),
            jax.ShapeDtypeStruct((bases[4] - bases[3], 128), F32),
            jax.ShapeDtypeStruct((bases[5] - bases[4], 128), F32),
            jax.ShapeDtypeStruct((AP, 4 * WA), F32),
            jax.ShapeDtypeStruct((8, 128), F32),
        ),
        in_specs=[far] * OPERANDS,
        out_specs=tuple([vmem()] * 5),
        scratch_shapes=[pltpu.VMEM(dims, kind) for dims, kind in plan.values()]
        + [
            pltpu.SemaphoreType.DMA((rows - 1,)),
            pltpu.SemaphoreType.DMA((PHASES, rows - 1)),
            pltpu.SemaphoreType.DMA((cols - 1,)),
            pltpu.SemaphoreType.DMA((PHASES - 1, cols - 1)),
            pltpu.SemaphoreType.DMA((4, 2, max(rows, cols) // 2 - 1)),
            pltpu.SemaphoreType.DMA((4, 2, rows + cols)),
            pltpu.SemaphoreType.DMA((OPERANDS,)),
        ],
        compiler_params=pltpu.CompilerParams(
            collective_id=0, has_side_effects=True, vmem_limit_bytes=MAIN_VMEM
        ),
    )(
        *[
            pltpu.with_memory_space_constraint(value, pltpu.HBM)
            for value in (
                jnp.swapaxes(letters, 1, 2),
                jnp.swapaxes(truth, 1, 2),
                jnp.swapaxes(concealed, 1, 2),
                existing,
                ordinals,
                observed,
                bins,
                *weights,
            )
        ]
    )

    shapes = []
    for w in weights:
        shapes += [jax.ShapeDtypeStruct(w.shape, F32)] * 3
    one = jax.ShapeDtypeStruct((1,), F32)
    scalar = pl.BlockSpec(memory_space=pltpu.SMEM)
    result = pl.pallas_call(
        functools.partial(post_kernel, rows, cols),
        out_shape=tuple(shapes) + (one, one),
        in_specs=[vmem()] * 11 + [far] * 12,
        out_specs=tuple([far] * 18) + (scalar, scalar),
        scratch_shapes=[pltpu.VMEM(shape.shape, F32) for shape in shapes]
        + [pltpu.VMEM(value.shape, F32) for value in (*means, *squares)]
        + [
            pltpu.VMEM((AP, WA), F32),
            pltpu.VMEM((RP, WP), F32),
            pltpu.VMEM((4 * WA, WA), F32),
            pltpu.VMEM((1408,), F32),
            pltpu.VMEM((72, 128), F32),
            pltpu.SemaphoreType.DMA((18,)),
            pltpu.SemaphoreType.DMA((12,)),
        ],
        compiler_params=pltpu.CompilerParams(vmem_limit_bytes=POST_VMEM),
    )(
        *summed,
        *weights,
        *[pltpu.with_memory_space_constraint(value, pltpu.HBM) for value in (*means, *squares)],
    )
    outs = [result[18].reshape(()), result[19].reshape(())]
    for place, value in enumerate(result[:18]):
        outs.append(value.T if place // 3 in (1, 4) else value)
    return tuple(outs)


def solution(mesh):
    rows, cols = mesh.shape[ROW], mesh.shape[COL]
    placed = (
        (P(None, COL, ROW),) * 3 + (P(),) * 3 + (P(None, ROW, COL),) + (P(),) * 18
    )
    return jax.shard_map(
        functools.partial(per_device, rows, cols),
        mesh=mesh,
        in_specs=placed,
        out_specs=(P(),) * 20,
        check_vma=False,
    )
```

```python
import functools
from types import SimpleNamespace

import jax
import jax.numpy as jnp
from jax import lax
from jax.experimental import pallas as pl
from jax.experimental.pallas import tpu as pltpu
from jax.sharding import PartitionSpec as P

F32, BF16 = jnp.float32, jnp.bfloat16
MESH = pl.DeviceIdType.MESH
ROW, COL = "row", "col"
CORE, X, Y, Z = "core", "x", "y", "z"
WA, WP, WO, LETTERS, BINS, REACH, HEADS, HEAD = 256, 128, 32, 23, 64, 32, 8, 32
UP = 1024
NREL = 2 * REACH + 1
AP = 32
TR = 24
RP = 128
EPS = 1e-05
NB, NS, NI, NJ = 2, 16, 8, 16
NM = NB * NS * NI
NP = NB * NI * NJ
BS = NB * NS
BI = NB * NI
DS = WO * NS
TOGETHER = 4
CLIP, RATE, B1, B2, STEP, ADAM_EPS, DECAY = 0.02, 0.05, 0.9, 0.999, 4, 1e-08, 0.01

MAIN_VMEM, POST_VMEM = 44 * 2**20, 30 * 2**20

NN = (((1,), (0,)), ((), ()))
NT = (((1,), (1,)), ((), ()))
TN = (((0,), (0,)), ((), ()))

GROUPS = (
    dict(outer=WO * WO, tri=5 * WP, out=WP),
    dict(up=2 * UP, o=2 * WA),
    dict(back=2 * UP),
    dict(eh=176, tabs=6 * TR, dist=BINS, rel=72, small=16),
    dict(score=2 * TR, bias=8),
)
BF16_GROUPS = 2
BF16_SUM = 1


def layout(rows, cols):
    places, bases, begin = {}, [], 0
    for number, group in enumerate(GROUPS):
        bases.append(begin)
        for name, count in group.items():
            places[name] = begin
            begin += count
        size = 8 * rows if number + 1 == len(GROUPS) else 16 * rows * cols
        begin = bases[-1] - (bases[-1] - begin) // size * size
    return SimpleNamespace(**places), bases + [begin]


def mm(a, b, dims=NN):
    return lax.dot_general(a, b, dims, preferred_element_type=F32)


def split2(x):
    high = x.astype(BF16)
    return high, (x - high.astype(F32)).astype(BF16)


def split3(x):
    high = x.astype(BF16)
    rest = x - high.astype(F32)
    middle = rest.astype(BF16)
    return high, middle, (rest - middle.astype(F32)).astype(BF16)


def mm3(a, b, dims=NN):
    ah, al = split2(a)
    bh, bl = split2(b)
    return mm(ah, bh, dims) + (mm(al, bh, dims) + mm(ah, bl, dims))


def mm6(a, b, dims=NN):
    ah, am, al = split3(a)
    bh, bm, bl = split3(b)
    low = mm(al, bh, dims) + (mm(am, bm, dims) + mm(ah, bl, dims))
    return mm(ah, bh, dims) + ((mm(am, bh, dims) + mm(ah, bm, dims)) + low)


def mm2(a, exact, dims=NN):
    ah, al = split2(a)
    return mm(ah, exact, dims) + mm(al, exact, dims)


def mm2r(exact, b, dims=NN):
    bh, bl = split2(b)
    return mm(exact, bh, dims) + mm(exact, bl, dims)


def mm3r(exact, b, dims=NN):
    bh, bm, bl = split3(b)
    return mm(exact, bh, dims) + (mm(exact, bm, dims) + mm(exact, bl, dims))


def norm(x):
    centred = x - jnp.mean(x, axis=-1, keepdims=True)
    scale = lax.rsqrt(jnp.mean(centred * centred, axis=-1, keepdims=True) + EPS)
    return centred * scale, scale


def norm_back(grad, unit, scale):
    return scale * (
        grad
        - jnp.mean(grad, axis=-1, keepdims=True)
        - unit * jnp.mean(grad * unit, axis=-1, keepdims=True)
    )


def iota(shape, axis):
    return lax.broadcasted_iota(jnp.int32, shape, axis)


def head_mask(rows, per_row):
    shape = (rows, WA)
    return iota(shape, 0) // per_row == iota(shape, 1) // HEAD


def colsum(x):
    return jnp.sum(x, axis=0, keepdims=True)


def total_of(x):
    return jnp.sum(jnp.sum(x, axis=1, keepdims=True), axis=0, keepdims=True)


def scratch_plan(rows, cols):
    length = rows * NI
    bases = layout(rows, cols)[1]
    final = bases[5] - bases[4]
    return dict(
        lk=((AP, WA), F32),
        weh=((128, WA), F32),
        wbd=((128, WP), F32),
        seqw=((NM, 1), F32),
        lmask=((NM, 1), F32),
        truth=((NM, 1), F32),
        target=((NP, 1), F32),
        pmask=((NP, 1), F32),
        offset=((NP, 1), F32),
        codes=((BI, length), F32),
        sites=((8, length), F32),
        wrel=((RP, WP), F32),
        tail=((8, 128), F32),
        kb=((WA, WA), BF16),
        vb=((WA, WA), BF16),
        amat=((BS, NI, WA), F32),
        pam=((BS, NI, WA), F32),
        hm=((64, WA), F32),
        letx=((128, length), F32),
        biash=((NB, 64, length), F32),
        prob=((BS, 64, length), F32),
        sg=((NM, WA), F32),
        att=((NM, WA), F32),
        xh1=((NM, WA), F32),
        r1=((NM, 1), F32),
        hid=((NM, UP), F32),
        rep=((NM, WA), F32),
        xh2=((NM, WA), F32),
        r2=((NM, 1), F32),
        dlog=((NM, 128), F32),
        left3=((NM, 96), BF16),
        mhi=((BI, DS, WP), BF16),
        mlo=((BI, DS, WP), BF16),
        rall=((NB, length, DS), BF16),
        prep=((NP, WP), F32),
        xh3=((NP, WP), F32),
        r3=((NP, 1), F32),
        proj=((NP, 5 * WP), F32),
        le=((BI * NJ, WP), F32),
        re=((NB * length * NJ, WP), F32),
        dm=((BI * length, WP), F32),
        gl=((BI, NJ, WP), F32),
        dr=((length, DS), F32),
        dmid=((NM, WA), F32),
        dbias=((NB, 64, length), F32),
        da=((BS, NI, WA), F32),
        dpam=((BS, NI, WA), F32),
        dtab=((BI, 16, RP), F32),
        dn=((NM, WA), F32),
        sum8=((8, WA), F32),
        grad=((bases[5], 128), F32),
        lets=((8, 128), F32),
        letr=((rows, 8, 128), F32),
        cnts=((8, 128), F32),
        cntr=((cols, 8, 128), F32),
        rs=((NB, NI, DS), BF16),
        rr=((rows, NB, NI, DS), BF16),
        os=((cols, BI, NJ, WP), BF16),
        orr=((cols, BI, NJ, WP), BF16),
        er=((rows, NB, NI, NJ, WP), BF16),
        ts=((cols, BI, NJ, WP), BF16),
        tr=((cols, BI, NJ, WP), BF16),
        ds=((BI, NJ, WP), BF16),
        dsr=((cols, BI, NJ, WP), BF16),
        gs=((rows, NB, NI, NJ, WP), BF16),
        ga=((rows // 2, NB, NI, NJ, WP), BF16),
        gh=((rows // 2 - 1, NB, NI, NJ, WP), BF16),
        gz=((rows // 2 - 1, NB, NI, NJ, WP), BF16),
        qs=((BI, NJ, WP), BF16),
        qr=((cols, BI, NJ, WP), BF16),
        us=((rows, NB, NI, DS), BF16),
        ur=((rows, NB, NI, DS), BF16),
        arx=((bases[4], 128), F32),
        lows=(((bases[2] - bases[1]) // 8, 8, 128), BF16),
        lowr=(((bases[2] - bases[1]) // 8, 8, 128), BF16),
        fr=((rows, final // rows, 128), F32),
        fp=((final // rows, 128), F32),
        fc=((cols, final // rows, 128), F32),
        letters=((NB, NI, NS), jnp.int32),
        truths=((NB, NI, NS), jnp.int32),
        concealed=((NB, NI, NS), jnp.int32),
        existing=((NB, cols * NS), jnp.int32),
        ordinals=((NB, length), jnp.int32),
        observed=((NB, length), jnp.int32),
        targets=((NB, NI, NJ), jnp.int32),
        lookup=((LETTERS, WA), F32),
        w_a=((2135, WA), F32),
        w_c=((WA + UP, WA), F32),
        w_r=((UP + NREL, WP), F32),
        w_p=((840, WP), F32),
        scal=((1367,), F32),
    )


OPERANDS = 13


LET, RIGHT, EDGE, GEDGE, GRIGHT, SUM_ROW, SHARE_ROW = range(7)
CNT, OUTER, TRI, GMIX, GOUTER, SHARE_COL = range(6)
PHASES = 7


def main_kernel(rows, cols, names, *refs):
    operands = refs[:OPERANDS]
    gbig, grest, gfin, tout, aux = refs[OPERANDS : OPERANDS + 5]
    s = SimpleNamespace(**dict(zip(names, refs[OPERANDS + 5 : -7])))
    row_send, row_recv, col_send, col_recv, sum_send, sum_recv, load_sem = refs[-7:]
    held = refs[OPERANDS + 5 : -7][-OPERANDS:]
    loads = [
        pltpu.make_async_copy(far, near, load_sem.at[place])
        for place, (far, near) in enumerate(zip(operands, held))
    ]
    for load in loads:
        load.start()
    letters, truths, hidden_sites, existing, ordinals, observed, targets = held[:7]
    lookup, w_a, w_c, w_r, w_p, scal = held[7:]
    ROWS, bases = layout(rows, cols)
    length = rows * NI
    me_r, me_c = lax.axis_index(ROW), lax.axis_index(COL)

    barrier = pltpu.get_barrier_semaphore()
    for step in range(1, rows):
        pl.semaphore_signal(
            barrier,
            inc=1,
            device_id={ROW: lax.rem(me_r + step, rows), COL: me_c},
            device_id_type=MESH,
        )
    for step in range(1, cols):
        pl.semaphore_signal(
            barrier,
            inc=1,
            device_id={ROW: me_r, COL: lax.rem(me_c + step, cols)},
            device_id_type=MESH,
        )
    def exchange(along, phase, source, target):
        if along == ROW:
            count, me, number = rows, me_r, phase
            send, recv = row_send, row_recv
        else:
            count, me, number = cols, me_c, phase
            send, recv = col_send, col_recv
        copies = []
        for step in range(1, count):
            peer = lax.rem(me + step, count)
            origin = lax.rem(me + (count - step), count)
            where = (
                {ROW: peer, COL: me_c} if along == ROW else {ROW: me_r, COL: peer}
            )
            out = pltpu.make_async_remote_copy(
                src_ref=source(peer),
                dst_ref=target(me),
                send_sem=send.at[step - 1],
                recv_sem=recv.at[number, step - 1],
                device_id=where,
                device_id_type=MESH,
            )
            out.start()
            arriving = pltpu.make_async_remote_copy(
                src_ref=source(peer),
                dst_ref=target(origin),
                send_sem=send.at[step - 1],
                recv_sem=recv.at[number, step - 1],
                device_id=where,
                device_id_type=MESH,
            )
            copies.append((out, arriving))
        return copies

    def finish(copies):
        for out, arriving in copies:
            out.wait_send()
            arriving.wait_recv()

    for load in loads[:7]:
        load.wait()
    here = existing[...].astype(F32)
    sites = observed[...].astype(F32)
    numbers = ordinals[...].astype(F32)

    def by_protein(values, count, each):
        wide = (count, values.shape[1])
        return jnp.where(iota(wide, 0) // each == 0, values[0:1], values[1:2])

    def at_lane(values, lanes):
        return jnp.sum(jnp.where(iota(values.shape, 1) == lanes, values, 0.0), axis=1, keepdims=True)

    row_m, row_p = iota((NM, 1), 0), iota((NP, 1), 0)
    seq_m, res_m = (row_m // NI) % NS, row_m % NI
    spread_m = jnp.where(
        iota((NM, BI), 1) == (iota((NM, BI), 0) // (NI * NS)) * NI + iota((NM, BI), 0) % NI, 1.0, 0.0
    ).astype(BF16)
    spread_p = jnp.where(iota((NP, BI), 1) == iota((NP, BI), 0) // NJ, 1.0, 0.0).astype(BF16)

    def column_m(values):
        wide = mm(spread_m, values[...].reshape(BI, NS).astype(F32).astype(BF16))
        return at_lane(wide, seq_m)

    seq_weight = at_lane(by_protein(here, NM, NI * NS), me_c * NS + seq_m)
    letter = column_m(letters)
    loss_mask = column_m(hidden_sites) * seq_weight
    s.seqw[...] = seq_weight
    s.lmask[...] = loss_mask
    s.truth[...] = column_m(truths)
    s.target[...] = at_lane(
        mm(spread_p, targets[...].reshape(BI, NJ).astype(F32).astype(BF16)), row_p % NJ
    )

    me_y, me_z = me_r % 2, me_r // 2
    lines = rows // 2

    def row_copy(source, target, slot, send_slot, place_z, place_y):
        return pltpu.make_async_remote_copy(
            src_ref=source,
            dst_ref=target,
            send_sem=row_send.at[send_slot],
            recv_sem=row_recv.at[slot],
            device_id={ROW: place_z * 2 + place_y, COL: me_c},
            device_id_type=MESH,
        )

    def gather_lines(phase, blocks):
        own = blocks.at[me_r]
        out = [row_copy(own, own, (phase, 0), 0, me_z, 1 - me_y)]
        arriving = []
        for step in range(1, lines):
            out.append(
                row_copy(own, own, (phase, step), step, lax.rem(me_z + step, lines), me_y)
            )
        for copy in out:
            copy.start()
        for step in range(1, lines):
            place = lax.rem(me_z + (lines - step), lines) * 2
            block = blocks.at[place + me_y]
            row_copy(own, block, (phase, step), step, me_z, me_y).wait_recv()
            slot = lines - 1 + step
            out.append(row_copy(block, block, (phase, slot), slot, me_z, 1 - me_y))
            out[-1].start()
            arriving.append((blocks.at[place + 1 - me_y], slot))
        arriving.append((blocks.at[me_z * 2 + 1 - me_y], 0))
        for block, slot in arriving:
            row_copy(own, block, (phase, slot), 0, me_z, 1 - me_y).wait_recv()
        for copy in out:
            copy.wait_send()

    def start_scatter(phase, blocks, across):
        out = []
        for step in (*range(1, lines), 0):
            place = lax.rem(me_z + step, lines)
            out.append(
                row_copy(
                    blocks.at[place * 2 + 1 - me_y],
                    across.at[place],
                    (phase, step),
                    step,
                    me_z,
                    1 - me_y,
                )
            )
            out[-1].start()
        return out

    def finish_scatter(phase, out, blocks, across, halves, along):
        for step in (*range(1, lines), 0):
            place = lax.rem(me_z + step, lines)
            here = across.at[place]
            row_copy(here, here, (phase, step), step, me_z, 1 - me_y).wait_recv()
            both = blocks[place * 2 + me_y].astype(F32) + across[place].astype(F32)
            if step == 0:
                break
            halves[step - 1] = both.astype(BF16)
            slot = lines - 1 + step
            out.append(
                row_copy(halves.at[step - 1], along.at[step - 1], (phase, slot), slot, place, me_y)
            )
            out[-1].start()
        for step in range(1, lines):
            slot = lines - 1 + step
            here = along.at[step - 1]
            row_copy(here, here, (phase, slot), slot, me_z, me_y).wait_recv()
            both = both + along[step - 1].astype(F32)
        for copy in out:
            copy.wait_send()
        return both

    s.lets[...] = jnp.where(
        (iota((NI, 128), 0) == 0) & (iota((NI, 128), 1) == BS), total_of(loss_mask), 0.0
    )
    for b in range(NB):
        s.lets[:, b * NS : (b + 1) * NS] = letters[b].astype(F32)
    s.letr[me_r] = s.lets[...]
    first, second = me_r * NI + (row_p // NJ) % NI, me_c * NJ + row_p % NJ
    sites_p = by_protein(sites, NP, NI * NJ)
    numbers_p = by_protein(numbers, NP, NI * NJ)
    s.pmask[...] = at_lane(sites_p, first) * at_lane(sites_p, second)
    s.offset[...] = (
        jnp.clip(at_lane(numbers_p, first) - at_lane(numbers_p, second), -REACH, REACH) + REACH
    )
    numbers_b = by_protein(numbers, BI, NI)
    own = at_lane(numbers_b, me_r * NI + iota((BI, 1), 0) % NI)
    s.codes[...] = jnp.clip(own - numbers_b, -REACH, REACH) + REACH
    s.sites[...] = jnp.zeros((8, length), F32)
    s.sites[0:NB, :] = sites
    inv_all = 1.0 / (jnp.sum(here, axis=1, keepdims=True) + 1.0)
    inv_count = [inv_all[b : b + 1] for b in range(NB)]
    per_protein = jnp.sum(sites, axis=1, keepdims=True)
    inv_dist = 1.0 / jnp.maximum(colsum(per_protein * per_protein), 1.0)

    for load in loads[7:]:
        load.wait()

    def gain(begin, width):
        return scal[begin : begin + width].reshape(1, width)

    gain_row, gain_trans, gain_outer = gain(0, WA), gain(256, WA), gain(512, WA)
    gain_rel, gain_pair, gain_mixed = gain(768, WP), gain(896, WP), gain(1024, WP)
    bias_outer = gain(1152, WP)
    s.lk[...] = jnp.zeros((AP, WA), F32)
    s.lk[0:LETTERS, :] = lookup[...]
    s.weh[...] = jnp.zeros((128, WA), F32)
    s.weh[0:87, :] = w_a[2048:2135, :]
    s.wbd[...] = jnp.zeros((128, WP), F32)
    s.wbd[0:72, :] = w_p[768:840, :]
    s.wrel[...] = jnp.zeros((RP, WP), F32)
    s.wrel[0:NREL, :] = w_r[UP : UP + NREL, :]
    s.tail[...] = jnp.zeros((8, 128), F32)
    s.tail[0:1, 0:87] = scal[1280:1367].reshape(1, 87)

    table = s.lk[...]
    unit0, _ = norm(table)
    mapped = mm6(unit0 * gain_row, w_a[0 : 4 * WA, :], NT)
    tout[...] = mapped
    pl.semaphore_wait(barrier, rows + cols - 2)
    flight = exchange(ROW, LET, lambda p: s.lets, lambda p: s.letr.at[p])
    t_q = mapped[:, 0:WA] * HEAD ** (-0.5)
    t_k = mapped[:, WA : 2 * WA].astype(BF16).astype(F32)
    t_v = mapped[:, 2 * WA : 3 * WA].astype(BF16).astype(F32)
    t_g = jax.nn.sigmoid(mapped[:, 3 * WA :])
    square = head_mask(WA, AP)
    key_block = jnp.where(square, jnp.concatenate([t_k] * HEADS, axis=0), 0.0).astype(BF16)
    s.vb[...] = jnp.where(square, jnp.concatenate([t_v] * HEADS, axis=0), 0.0).astype(BF16)
    stacked = mm(jnp.concatenate(split3(t_q), axis=0), key_block, NT)
    score_table = stacked[0:AP] + (stacked[AP : 2 * AP] + stacked[2 * AP :])
    s.hm[...] = jnp.where(head_mask(64, NI), 1.0, 0.0)

    letter = letter.astype(jnp.int32)
    triple = jnp.where(
        (iota((NM, 3 * AP), 1) % AP) == letter, 1.0, 0.0
    ).astype(BF16)

    def chosen(values):
        return mm(triple, jnp.concatenate(split3(values), axis=0))

    s.amat[...] = chosen(score_table).reshape(BS, NI, WA)
    start = chosen(table)
    s.sg[...] = chosen(t_g)

    unit_r, _ = norm(s.wrel[...])
    bias_table = mm3(s.wbd[0:8, :], unit_r * gain_rel, NT)
    bias_parts = jnp.concatenate(split3(bias_table), axis=0)

    def codes(index):
        return jnp.where(
            iota((RP, length), 0) == s.codes[index : index + 1, :].astype(jnp.int32), 1.0, 0.0
        ).astype(BF16)

    for b in range(NB):
        for i in range(NI):
            part = mm(bias_parts, codes(b * NI + i))
            part = part[0:8] + (part[8:16] + part[16:24])
            for h in range(HEADS):
                s.biash[b, h * NI + i : h * NI + i + 1, :] = part[h : h + 1, :]

    finish(flight)
    letters_all = s.letr[...].reshape(length, 128).T
    s.letx[...] = letters_all
    s.cnts[...] = jnp.broadcast_to(
        jnp.sum(letters_all[BS : BS + 1, :], axis=1, keepdims=True), (8, 128)
    )
    s.cntr[me_c] = s.cnts[...]
    count_flight = exchange(COL, CNT, lambda p: s.cnts, lambda p: s.cntr.at[p])

    def letter_codes(bs):
        row = s.letx[pl.ds(bs, 1), :].astype(jnp.int32)
        one = jnp.where(iota((AP, length), 0) == row, 1.0, 0.0)
        return jnp.concatenate([one] * HEADS, axis=0).astype(BF16)

    def spread(value):
        wide = jnp.broadcast_to(value[None], (HEADS, NI, WA)).reshape(64, WA)
        return wide * s.hm[...]

    def gather_heads(value):
        return jnp.sum((value * s.hm[...]).reshape(HEADS, NI, WA), axis=0)

    for b in range(NB):
        key_mask = s.sites[b : b + 1, :]

        @pl.loop(0, NS // TOGETHER)
        def _(q):
            for part in range(TOGETHER):
                bs = b * NS + q * TOGETHER + part
                code = letter_codes(bs)
                wide = [spread(p.astype(F32)).astype(BF16) for p in split2(s.amat[bs])]
                raw = mm(jnp.concatenate(wide, axis=0), code)
                scores = (raw[0:64] + raw[64:128]) + s.biash[b]
                scores = jnp.where(key_mask > 0, scores, -1000000000.0)
                power = jnp.exp(scores - jnp.max(scores, axis=-1, keepdims=True))
                weight = power / jnp.sum(power, axis=-1, keepdims=True)
                s.prob[bs] = weight
                picked = mm(jnp.concatenate(split2(weight), axis=0), code, NT)
                s.pam[bs] = gather_heads(picked[0:64] + picked[64:128])

    att = mm2(s.pam[...].reshape(NM, WA), s.vb[...])
    s.att[...] = att
    mid = start + mm3(s.sg[...] * att, w_c[0:WA, :])
    unit1, scale1 = norm(mid)
    s.xh1[...] = unit1
    s.r1[...] = scale1
    hidden = jnp.maximum(mm3(unit1 * gain_trans, w_a[4 * WA : 4 * WA + UP, :], NT), 0.0)
    s.hid[...] = hidden
    rep = mid + mm3(hidden, w_c[WA:, :])
    s.rep[...] = rep
    unit2, scale2 = norm(rep)
    s.xh2[...] = unit2
    s.r2[...] = scale2
    seq_weight = s.seqw[...]
    lane = iota((NM, 128), 1)
    edges = mm3(unit2 * gain_outer, s.weh[...], NT) * seq_weight

    right = jnp.where((lane >= 32) & (lane < 64), edges, 0.0).astype(BF16)
    spot = iota((128, DS), 0)
    repeat = jnp.where(spot - 32 == iota((128, DS), 1) // NS, 1.0, 0.0)
    repeat = jnp.where((spot >= 32) & (spot < 64), repeat, 0.0).astype(BF16)
    wide = mm(right, repeat)
    own_seq = (iota((NM, DS), 0) // NI) % NS == iota((NM, DS), 1) % NS
    wide = jnp.sum(jnp.where(own_seq, wide, 0.0).reshape(NB, NS, NI, DS), axis=1)
    s.rs[...] = wide.astype(BF16)
    s.rr[me_r] = s.rs[...]
    flight = exchange(ROW, RIGHT, lambda p: s.rs, lambda p: s.rr.at[p])

    finish(count_flight)
    masked = jnp.maximum(jnp.sum(s.cntr[...], axis=0)[0:1, 0:1], 1.0)
    logits = mm3(rep, s.weh[...], NT) + s.tail[0:1, :]
    valid = (lane >= 64) & (lane < 64 + LETTERS)
    top = jnp.max(jnp.where(valid, logits, -3e38), axis=-1, keepdims=True)
    power = jnp.where(valid, jnp.exp(jnp.where(valid, logits, top) - top), 0.0)
    whole = jnp.sum(power, axis=-1, keepdims=True)
    truth = lane - 64 == s.truth[...].astype(jnp.int32)
    truth = truth & valid
    picked = jnp.sum(jnp.where(truth, logits, 0.0), axis=-1, keepdims=True)
    loss_mask = s.lmask[...]
    msa_sum = colsum((jnp.log(whole) + top - picked) * loss_mask)
    s.dlog[...] = (power / whole - jnp.where(truth, 1.0, 0.0)) * (loss_mask / masked)

    order_to = (iota((NM, NM), 0) // (NI * NS) == iota((NM, NM), 1) // (NI * NS)) & (
        (iota((NM, NM), 0) // NS) % NI == iota((NM, NM), 1) % NI
    )
    order_to = order_to & (iota((NM, NM), 0) % NS == (iota((NM, NM), 1) // NI) % NS)
    order = jnp.where(order_to, 1.0, 0.0).astype(BF16)
    left = mm3r(order, jnp.where(lane < 32, edges, 0.0))
    high, low = split2(left)
    high32, low32 = high.astype(F32), low.astype(F32)
    left3 = high32 + pltpu.roll(low32, 32, 1) + pltpu.roll(high32, 64, 1)
    s.left3[...] = left3[:, 0:96].astype(BF16)

    def outer_weight(d):
        return w_r[pl.ds(d, WO, stride=WO), :]

    for pair in range(WO // 2):
        both = jnp.concatenate([outer_weight(2 * pair), outer_weight(2 * pair + 1)], axis=1)
        wh, wl = split2(both)
        made = mm(s.left3[...], jnp.concatenate([wh, wh, wl], axis=0))
        for half in range(2):
            d = 2 * pair + half
            mh, ml = split2(made[:, half * WP : (half + 1) * WP].reshape(BI, NS, WP))
            s.mhi[:, d * NS : (d + 1) * NS, :] = mh
            s.mlo[:, d * NS : (d + 1) * NS, :] = ml

    finish(flight)
    for b in range(NB):
        s.rall[b] = s.rr[:, b].astype(F32).reshape(length, DS).astype(BF16)
    for b in range(NB):

        @pl.loop(0, NI)
        def _(i):
            bi = b * NI + i
            block = mm(s.rall[b], s.mhi[bi]) + mm(s.rall[b], s.mlo[bi])
            block = block * inv_count[b]
            for c in range(cols):
                s.os[c, bi] = block[c * NJ : (c + 1) * NJ].astype(BF16)

    s.orr[me_c] = s.os[me_c]
    finish(exchange(COL, OUTER, lambda p: s.os.at[p], lambda p: s.orr.at[p]))

    pair_lane = iota((NP, 128), 1)
    offset = s.offset[...].astype(jnp.int32)
    pair_codes = jnp.where(pair_lane == offset, 1.0, 0.0).astype(BF16)
    outer = s.orr[0].astype(F32)
    for c in range(1, cols):
        outer = outer + s.orr[c].astype(F32)
    pair_rep = (mm3r(pair_codes, s.wrel[...]) + outer.reshape(NP, WP)) + bias_outer
    s.prep[...] = pair_rep
    unit3, scale3 = norm(pair_rep)
    s.xh3[...] = unit3
    s.r3[...] = scale3
    proj = mm3(unit3 * gain_pair, w_p[0 : 5 * WP, :], NT)
    pair_mask = s.pmask[...]
    sig1 = jax.nn.sigmoid(proj[:, WP : 2 * WP])
    sig2 = jax.nn.sigmoid(proj[:, 3 * WP : 4 * WP])
    sig3 = jax.nn.sigmoid(proj[:, 4 * WP :])
    s.proj[:, 0 : WP] = proj[:, 0:WP]
    s.proj[:, WP : 2 * WP] = sig1
    s.proj[:, 2 * WP : 3 * WP] = proj[:, 2 * WP : 3 * WP]
    s.proj[:, 3 * WP : 4 * WP] = sig2
    s.proj[:, 4 * WP :] = sig3
    s.le[...] = sig1 * proj[:, 0:WP] * pair_mask
    right_edge = (sig2 * proj[:, 2 * WP : 3 * WP] * pair_mask).astype(BF16)
    s.er[me_r] = right_edge.reshape(NB, NI, NJ, WP)
    gather_lines(EDGE, s.er)
    for b in range(NB):
        for r in range(rows):
            begin = (b * length + r * NI) * NJ
            s.re[begin : begin + NI * NJ, :] = (
                s.er[r, b].astype(F32).reshape(NI * NJ, WP)
            )

    for b in range(NB):

        @pl.loop(0, NI)
        def _(i):
            bi = b * NI + i
            for c in range(cols):
                block = jnp.zeros((NJ, WP), F32)
                for k in range(NJ):
                    other = s.re[pl.ds((b * length + c * NJ) * NJ + k, NJ, stride=NJ), :]
                    block = block + s.le[pl.ds(bi * NJ + k, 1), :] * other
                s.ts[c, bi] = block.astype(BF16)

    s.tr[me_c] = s.ts[me_c]
    finish(exchange(COL, TRI, lambda p: s.ts.at[p], lambda p: s.tr.at[p]))

    mixed = s.tr[0].astype(F32)
    for c in range(1, cols):
        mixed = mixed + s.tr[c].astype(F32)
    unit4, scale4 = norm(mixed.reshape(NP, WP))
    w_out = w_p[5 * WP : 6 * WP, :]
    moved = mm3(unit4 * gain_mixed, w_out, NT)
    sig3 = s.proj[:, 4 * WP :]
    pair_out = s.prep[...] + sig3 * moved
    bins = mm3(pair_out, s.wbd[...], NT) + pltpu.roll(
        jnp.where(iota((8, 128), 1) < BINS, s.tail[...], 0.0), 8, 1
    )[0:1]
    valid = (pair_lane >= 8) & (pair_lane < 8 + BINS)
    top = jnp.max(jnp.where(valid, bins, -3e38), axis=-1, keepdims=True)
    power = jnp.where(valid, jnp.exp(jnp.where(valid, bins, top) - top), 0.0)
    whole = jnp.sum(power, axis=-1, keepdims=True)
    truth = (pair_lane - 8 == s.target[...].astype(jnp.int32)) & valid
    picked = jnp.sum(jnp.where(truth, bins, 0.0), axis=-1, keepdims=True)
    dist_sum = colsum((jnp.log(whole) + top - picked) * pair_mask)
    dbins = (power / whole - jnp.where(truth, 1.0, 0.0)) * (pair_mask * inv_dist)

    def put(place, value, skip=0):
        base = place + skip
        height, width = value.shape
        for w in range(width // 128):
            s.grad[base + w * height : base + (w + 1) * height, :] = value[
                :, w * 128 : (w + 1) * 128
            ]

    sizes = {CORE: 2, X: cols // 2, Y: 2, Z: rows // 2}
    places = {CORE: me_c % 2, X: me_c // 2, Y: me_r % 2, Z: me_r // 2}

    def line_peer(axis, place):
        if axis == CORE:
            return {ROW: me_r, COL: me_c // 2 * 2 + place}
        if axis == X:
            return {ROW: me_r, COL: place * 2 + me_c % 2}
        if axis == Y:
            return {ROW: me_r // 2 * 2 + place, COL: me_c}
        return {ROW: place * 2 + me_r % 2, COL: me_c}

    class Sum:
        def __init__(self, number):
            self.number = number
            self.stage = -1
            self.used = [0, 0]
            base, size = bases[number] // 8, (bases[number + 1] - bases[number]) // 8
            self.parts = []
            for half in range(2):
                order = (CORE, X, Y, Z) if half == 0 else (CORE, Y, X, Z)
                begin = base + half * (size // 2)
                self.parts.append(SimpleNamespace(order=order, at=begin, size=size // 2, rx=begin))
            self.flight = []

        def copies(self, part, half, axis, source, target, arrive):
            count = sizes[axis]
            for step in range(1, count):
                peer = lax.rem(places[axis] + step, count)
                origin = lax.rem(places[axis] + (count - step), count)
                used = self.used[half]
                self.used[half] += 1
                both = []
                for end in (target(peer, step), arrive(origin, step)):
                    both.append(
                        pltpu.make_async_remote_copy(
                            src_ref=source(peer, step),
                            dst_ref=end,
                            send_sem=sum_send.at[self.number, half, step - 1],
                            recv_sem=sum_recv.at[self.number, half, used],
                            device_id=line_peer(axis, peer),
                            device_id_type=MESH,
                        )
                    )
                both[0].start()
                self.flight.append(both)

        def advance(self):
            finish(self.flight)
            self.flight = []
            if 0 <= self.stage < 4:
                for part in self.parts:
                    self.add(part)
            self.stage += 1
            if self.stage == 4:
                for part in self.parts:
                    self.store(part)
            if self.stage < 4:
                for half, part in enumerate(self.parts):
                    self.start_sum(part, half)
            elif self.stage < 8:
                for half, part in enumerate(self.parts):
                    self.start_share(part, half)

        def start_sum(self, part, half):
            axis = part.order[self.stage]
            small = part.size // sizes[axis]
            part.small, part.axis = small, axis

            low = self.number == BF16_SUM
            for step in range(1, sizes[axis] if low else 1):
                peer = lax.rem(places[axis] + step, sizes[axis])
                value = s.grad[rows_at(part.at + peer * small, small), :]
                slot = part.rx - bases[BF16_SUM] // 8 + (step - 1) * small
                s.lows[slot : slot + small] = value.reshape(small, 8, 128).astype(BF16)

            def source(peer, step):
                if low:
                    return low_spot(s.lows, step)
                return s.grad.at[rows_at(part.at + peer * small, small)]

            def low_spot(buffer, step):
                slot = part.rx - bases[BF16_SUM] // 8 + (step - 1) * small
                return buffer.at[pl.ds(slot, small)]

            def target(place, step):
                if low:
                    return low_spot(s.lowr, step)
                return s.arx.at[pl.ds((part.rx + (step - 1) * small) * 8, small * 8)]

            self.copies(part, half, axis, source, target, target)

        def add(self, part):
            mine = rows_at(part.at + places[part.axis] * part.small, part.small)
            value = s.grad[mine, :]
            for step in range(1, sizes[part.axis]):
                begin = part.rx + (step - 1) * part.small
                if self.number == BF16_SUM:
                    begin = begin - bases[BF16_SUM] // 8
                    other = s.lowr[begin : begin + part.small].astype(F32)
                    value = value + other.reshape(part.small * 8, 128)
                else:
                    value = value + s.arx[begin * 8 : (begin + part.small) * 8, :]
            s.grad[mine, :] = value
            part.at = part.at + places[part.axis] * part.small
            part.rx += (sizes[part.axis] - 1) * part.small
            part.size = part.small

        def store(self, part):
            value = s.grad[rows_at(part.at, part.size), :]
            if self.number < BF16_GROUPS:
                gbig[pl.ds(part.at, part.size)] = value.reshape(part.size, 8, 128).astype(BF16)
            else:
                grest[rows_at(part.at - bases[2] // 8, part.size), :] = value

        def start_share(self, part, half):
            axis = part.order[7 - self.stage]
            size, here = part.size, part.at
            first = here - places[axis] * size

            def spot(place, step):
                at = first + place * size
                if self.number < BF16_GROUPS:
                    return gbig.at[pl.ds(at, size)]
                return grest.at[rows_at(at - bases[2] // 8, size)]

            self.copies(
                part,
                half,
                axis,
                lambda peer, step: spot(places[axis], 0),
                lambda peer, step: spot(places[axis], step),
                spot,
            )
            part.at, part.size = first, size * sizes[axis]

    def rows_at(unit, count):
        return pl.ds(pl.multiple_of(unit * 8, 8), count * 8)

    early, late, middle, rest = [Sum(number) for number in range(4)]

    def column_products(name, place):
        s.sum8[...] = jnp.zeros((8, WA), F32)

        @pl.loop(0, NM // 32)
        def _(q):
            some = pl.ds(pl.multiple_of(q * 32, 32), 32)
            product = s.dn[some, :] * name[some, :]
            s.sum8[...] += jnp.sum(product.reshape(4, 8, WA), axis=0)

        whole = colsum(s.sum8[...])
        for half in range(2):
            s.grad[small + place + half : small + place + half + 1, :] = whole[
                :, 128 * half : 128 * half + 128
            ]

    for begin, end in (
        (ROWS.out + WP, bases[1]),
        (ROWS.o + 2 * WA, bases[2]),
        (ROWS.small, bases[4]),
        (ROWS.bias, bases[5]),
    ):
        if end > begin:
            s.grad[begin:end, :] = jnp.zeros((end - begin, 128), F32)
    small = ROWS.small
    put(ROWS.dist, mm3(dbins, pair_out, TN)[8 : 8 + BINS])
    dbias_dist = pltpu.roll(jnp.broadcast_to(colsum(dbins), (8, 128)), 120, 1)[0:1]
    dout = mm3(dbins, s.wbd[...])
    dgate = dout * moved * (sig3 * (1.0 - sig3))
    dmoved = dout * sig3
    put(ROWS.out, mm3(dmoved, unit4 * gain_mixed, TN))
    dnormed = mm3(dmoved, w_out)
    s.grad[small + 5 : small + 6, :] = colsum(dnormed * unit4)
    dmixed = norm_back(dnormed * gain_mixed, unit4, scale4)
    s.ds[...] = dmixed.astype(BF16).reshape(BI, NJ, WP)
    s.dsr[me_c] = s.ds[...]
    finish(exchange(COL, GMIX, lambda p: s.ds, lambda p: s.dsr.at[p]))
    for bi in range(BI):
        for c in range(cols):
            begin = bi * length + c * NJ
            s.dm[begin : begin + NJ, :] = s.dsr[c, bi].astype(F32)

    for b in range(NB):

        @pl.loop(0, rows)
        def _(r):
            for q in range(NI):
                block = jnp.zeros((NJ, WP), F32)
                for i in range(NI):
                    bi = b * NI + i
                    block = block + (
                        s.dm[pl.ds(bi * length + r * NI + q, 1), :]
                        * s.le[bi * NJ : (bi + 1) * NJ, :]
                    )
                s.gs[r, b, q] = block.astype(BF16)

    flight = start_scatter(GEDGE, s.gs, s.ga)
    for b in range(NB):

        @pl.loop(0, NI)
        def _(i):
            bi = b * NI + i
            block = jnp.zeros((NJ, WP), F32)
            for j in range(length):
                begin = (b * length + j) * NJ
                block = block + (
                    s.dm[pl.ds(bi * length + j, 1), :] * s.re[begin : begin + NJ, :]
                )
            s.gl[bi] = block

    dright = finish_scatter(GEDGE, flight, s.gs, s.ga, s.gh, s.gz)
    dright = dright.reshape(NP, WP) * pair_mask
    dleft = s.gl[...].reshape(NP, WP) * pair_mask
    p1, sig1 = s.proj[:, 0:WP], s.proj[:, WP : 2 * WP]
    p2, sig2 = s.proj[:, 2 * WP : 3 * WP], s.proj[:, 3 * WP : 4 * WP]
    dproj = jnp.concatenate(
        [
            dleft * sig1,
            dleft * p1 * (sig1 * (1.0 - sig1)),
            dright * sig2,
            dright * p2 * (sig2 * (1.0 - sig2)),
            dgate,
        ],
        axis=1,
    )
    unit3 = s.xh3[...]
    put(ROWS.tri, mm3(dproj, unit3 * gain_pair, TN))
    dnormed = mm3(dproj, w_p[0 : 5 * WP, :])
    s.grad[small + 4 : small + 5, :] = colsum(dnormed * unit3)
    drep = dout + norm_back(dnormed * gain_pair, unit3, s.r3[...])
    s.grad[small + 6 : small + 7, :] = colsum(drep)
    s.grad[ROWS.rel : ROWS.rel + 72, :] = mm2r(pair_codes, drep, TN)[0:72]
    s.qs[...] = drep.astype(BF16).reshape(BI, NJ, WP)
    s.qr[me_c] = s.qs[...]
    finish(exchange(COL, GOUTER, lambda p: s.qs, lambda p: s.qr.at[p]))

    for b in range(NB):
        turned = s.rall[b].astype(F32).T.astype(BF16)
        s.dr[...] = jnp.zeros((length, DS), F32)

        @pl.loop(0, NI)
        def _(i):
            bi = b * NI + i
            block = jnp.concatenate([s.qr[c, bi] for c in range(cols)], axis=0)
            s.dr[...] += mm(block, s.mhi[bi], NT) + mm(block, s.mlo[bi], NT)
            mh, ml = split2(mm(turned, block) * inv_count[b])
            s.mhi[bi] = mh
            s.mlo[bi] = ml

        for r in range(rows):
            s.us[r, b] = (s.dr[r * NI : (r + 1) * NI, :] * inv_count[b]).astype(BF16)
    s.ur[me_r] = s.us[me_r]
    flight = exchange(ROW, GRIGHT, lambda p: s.us.at[p], lambda p: s.ur.at[p])

    left3 = s.left3[...].astype(F32).T.astype(BF16)
    left_both, left_high = left3[0:64], left3[0:32]
    dleft = jnp.zeros((NM, WO), F32)
    for pair in range(WO // 2):
        two = (2 * pair, 2 * pair + 1)
        wh, wl = split2(jnp.concatenate([outer_weight(d) for d in two], axis=1))

        def both_of(ref):
            return jnp.concatenate(
                [ref[:, d * NS : (d + 1) * NS, :].reshape(NM, WP) for d in two], axis=1
            )

        mh, ml = both_of(s.mhi), both_of(s.mlo)
        dleft = dleft + (mm(mh, wh, NT) + (mm(ml, wh, NT) + mm(mh, wl, NT)))
        made = mm(left_both, mh)
        made = made[0:32] + made[32:64] + mm(left_high, ml)
        for half in range(2):
            s.grad[pl.ds(ROWS.outer + two[half], WO, stride=WO), :] = made[
                :, half * WP : (half + 1) * WP
            ]
    early.advance()
    dleft = mm3r(order, dleft, TN)

    finish(flight)
    dright = s.ur[0].astype(F32)
    for r in range(1, rows):
        dright = dright + s.ur[r].astype(F32)
    wide = jnp.broadcast_to(dright[:, None], (NB, NS, NI, DS)).reshape(NM, DS)
    dedges = mm2(jnp.where(own_seq, wide, 0.0), repeat, NT)
    dedges = (dedges + jnp.concatenate([dleft, jnp.zeros((NM, 96), F32)], axis=1)) * seq_weight
    unit2, rep = s.xh2[...], s.rep[...]
    dlog = s.dlog[...]
    put(ROWS.eh, (mm3(dedges, unit2 * gain_outer, TN) + mm3(dlog, rep, TN))[0:88])
    s.dn[...] = mm3(dedges, s.weh[...])
    dnormed = s.dn[...]
    column_products(s.xh2, 2)
    drep = mm3(dlog, s.weh[...]) + norm_back(dnormed * gain_outer, unit2, s.r2[...])
    early.advance()
    hidden = s.hid[...]
    put(ROWS.back, mm3(hidden, drep, TN))
    middle.advance()
    early.advance()
    dhidden = jnp.where(hidden > 0, mm3(drep, w_c[WA:, :], NT), 0.0)
    unit1 = s.xh1[...]
    put(ROWS.up, mm3(dhidden, unit1 * gain_trans, TN))
    s.dn[...] = mm3(dhidden, w_a[4 * WA : 4 * WA + UP, :])
    dnormed = s.dn[...]
    column_products(s.xh1, 0)
    dmid = drep + norm_back(dnormed * gain_trans, unit1, s.r1[...])
    sg, att = s.sg[...], s.att[...]
    put(ROWS.o, mm3(sg * att, dmid, TN))
    dgated = mm3(dmid, w_c[0:WA, :], NT)
    late.advance()
    middle.advance()
    early.advance()
    single = triple[:, 0:AP]
    put(ROWS.tabs, mm2r(single, dmid, TN)[0:TR], 4 * TR)
    put(ROWS.tabs, mm2r(single, dgated * att, TN)[0:TR], 2 * TR)
    datt = dgated * sg

    pam = s.pam[...].reshape(NM, WA)
    blocks = jnp.where(head_mask(WA, AP), mm3(pam, datt, TN), 0.0)
    put(ROWS.tabs, jnp.sum(blocks.reshape(HEADS, AP, WA), axis=0)[0:TR])
    lane1 = iota((1, 128), 1)
    s.grad[small + 7 : small + 8, :] = jnp.where(lane1 < BINS, dbias_dist, colsum(dlog))
    s.grad[small + 8 : small + 9, :] = jnp.where(
        lane1 == 0, msa_sum, jnp.where(lane1 == 1, dist_sum, 0.0)
    )
    rest.advance()
    s.dpam[...] = mm2(datt, s.vb[...], NT).reshape(BS, NI, WA)
    for b in range(NB):
        key_mask = s.sites[b : b + 1, :]
        s.dbias[b] = jnp.zeros((64, length), F32)

        def attention_back(q):
            together = jnp.zeros((64, length), F32)
            for part in range(TOGETHER):
                bs = b * NS + q * TOGETHER + part
                code = letter_codes(bs)
                wide = [spread(p.astype(F32)).astype(BF16) for p in split2(s.dpam[bs])]
                raw = mm(jnp.concatenate(wide, axis=0), code)
                dweight = raw[0:64] + raw[64:128]
                weight = s.prob[bs]
                inner = jnp.sum(weight * dweight, axis=-1, keepdims=True)
                dscore = jnp.where(key_mask > 0, weight * (dweight - inner), 0.0)
                together = together + dscore
                back = mm(jnp.concatenate(split2(dscore), axis=0), code, NT)
                s.da[bs] = gather_heads(back[0:64] + back[64:128])
            s.dbias[b] += together

        for part in range(2):
            count = NS // TOGETHER // 2
            pl.loop(part * count, (part + 1) * count)(attention_back)
            for group in (early, middle, late, rest):
                group.advance()

    put(ROWS.score, mm2r(single, s.da[...].reshape(NM, WA), TN)[0:TR])
    for b in range(NB):
        for i in range(NI):
            part = jnp.concatenate(
                [s.dbias[b, h * NI + i : h * NI + i + 1, :] for h in range(HEADS)], axis=0
            )
            s.dtab[b * NI + i] = mm(
                jnp.concatenate(split2(part), axis=0), codes(b * NI + i), NT
            )
    s.grad[ROWS.bias : ROWS.bias + 8, :] = jnp.sum(
        s.dtab[...].reshape(2 * BI, 8, RP), axis=0
    )

    aux[...] = jnp.where(iota((8, 128), 1) == 0, masked, inv_dist)

    last = bases[4]
    piece = (bases[5] - last) // rows

    def mine(p):
        return pl.ds(pl.multiple_of(last + p * piece, 8), piece)

    def spot(p):
        return gfin.at[pl.ds(pl.multiple_of(p * piece, 8), piece)]

    s.fr[me_r] = s.grad[mine(me_r), :]
    flight = exchange(ROW, SUM_ROW, lambda p: s.grad.at[mine(p)], lambda p: s.fr.at[p])
    for group in (middle, late, rest):
        group.advance()
    finish(flight)
    summed = s.fr[0]
    for r in range(1, rows):
        summed = summed + s.fr[r]
    s.fp[...] = summed
    s.fc[me_c] = summed
    flight = exchange(COL, SHARE_COL, lambda p: s.fp, lambda p: s.fc.at[p])
    for group in (middle, late, rest):
        group.advance()
    finish(flight)
    summed = s.fc[0]
    for c in range(1, cols):
        summed = summed + s.fc[c]
    gfin[pl.ds(pl.multiple_of(me_r * piece, 8), piece), :] = summed
    flight = exchange(ROW, SHARE_ROW, lambda p: spot(me_r), spot)
    while min(group.stage for group in (early, middle, late, rest)) < 8:
        for group in (early, middle, late, rest):
            if group.stage < 8:
                group.advance()
    finish(flight)


def post_kernel(rows, cols, *refs):
    gbig, grest, gfin, tout, aux = refs[:5]
    weights, far_moments = refs[5:11], refs[11:23]
    far, loss_out, size_out = refs[23:41], refs[41], refs[42]
    new, moments = refs[43:61], refs[61:73]
    lk, wrel, g_a, g_small, g_rel, store_sem, load_sem = refs[73:]
    loads = [
        pltpu.make_async_copy(source, near, load_sem.at[place])
        for place, (source, near) in enumerate(zip(far_moments, moments))
    ]
    for place in (2, 8, 1, 7, 3, 9, 4, 10, 0, 6, 5, 11):
        loads[place].start()
    means, squares = moments[0:6], moments[6:12]
    lookup, w_a, w_c, w_r, w_p, scal = weights
    ROWS, bases = layout(rows, cols)

    def big(begin, count):
        part = gbig[begin // 8 : (begin + count) // 8].astype(F32)
        return part.reshape(count, 128)

    def exact(begin, count):
        if begin >= bases[4]:
            return gfin[begin - bases[4] : begin - bases[4] + count, :]
        return grest[begin - bases[2] : begin - bases[2] + count, :]

    lk[...] = jnp.zeros((AP, WA), F32)
    lk[0:LETTERS, :] = lookup[...]
    wrel[...] = jnp.zeros((RP, WP), F32)
    wrel[0:NREL, :] = w_r[UP : UP + NREL, :]

    def table(begin):
        both = jnp.concatenate([exact(begin, TR), exact(begin + TR, TR)], axis=1)
        return jnp.concatenate([both, jnp.zeros((AP - TR, WA), F32)], axis=0)

    dscore = table(ROWS.score)
    dvalue, dgate, dstart = [table(ROWS.tabs + 2 * TR * place) for place in range(3)]
    mapped = tout[...]
    t_q = mapped[:, 0:WA] * HEAD ** (-0.5)
    t_k = mapped[:, WA : 2 * WA].astype(BF16).astype(F32)
    t_g = jax.nn.sigmoid(mapped[:, 3 * WA :])
    square = head_mask(WA, AP)
    key_block = jnp.where(square, jnp.concatenate([t_k] * HEADS, axis=0), 0.0).astype(BF16)
    dq = mm2(dscore, key_block) * HEAD ** (-0.5)
    dk = jnp.where(square, mm3(dscore, t_q, TN), 0.0)
    dk = jnp.sum(dk.reshape(HEADS, AP, WA), axis=0)
    dg = dgate * (t_g * (1.0 - t_g))
    dmapped = jnp.concatenate([dq, dk, dvalue, dg], axis=1)
    unit0, scale0 = norm(lk[...])
    gain_row = scal[0:WA].reshape(1, WA)
    g_a[...] = mm3(dmapped, unit0 * gain_row, TN)
    dnormed = mm3(dmapped, w_a[0 : 4 * WA, :])
    dgain_row = colsum(dnormed * unit0)
    g_lookup = dstart + norm_back(dnormed * gain_row, unit0, scale0)

    unit_r, scale_r = norm(wrel[...])
    gain_rel = scal[768:896].reshape(1, WP)
    dtable = exact(ROWS.bias, 8)
    g_bias = mm3(dtable, unit_r * gain_rel)
    dnormed = mm3(dtable, w_p[768:776, :], TN)
    dgain_rel = colsum(dnormed * unit_r)
    g_rel[...] = exact(ROWS.rel, 72) + norm_back(
        dnormed * gain_rel, unit_r, scale_r
    )[0:72]

    base = ROWS.small
    g_small[0:WA] = dgain_row.reshape(WA)
    for place, row in ((256, 0), (384, 1), (512, 2), (640, 3), (896, 4), (1024, 5), (1152, 6)):
        g_small[place : place + 128] = exact(base + row, 1).reshape(128)
    g_small[768:896] = dgain_rel.reshape(128)
    lane = iota((1, 128), 1)
    tail = jnp.where(lane < 87, exact(base + 7, 1), 0.0)
    g_small[1280:1408] = tail.reshape(128)

    rel_row = iota((72, 128), 0)
    squares_sum = jnp.zeros((1, 1), F32)
    for begin, count in (
        (ROWS.outer, UP),
        (ROWS.tri, 768),
        (ROWS.up, 2 * UP),
        (ROWS.o, 2 * WA),
    ):
        part = big(begin, count)
        squares_sum = squares_sum + total_of(part * part)
    for part in (
        g_a[...],
        g_lookup[0:LETTERS],
        jnp.where(rel_row < NREL, g_rel[...], 0.0),
        g_bias,
        dgain_row,
        exact(ROWS.back, 2 * UP),
        exact(base, 7),
        exact(ROWS.eh, 87),
        exact(ROWS.eh + 88, 87),
        exact(ROWS.dist, BINS),
        dgain_rel,
        tail,
    ):
        squares_sum = squares_sum + total_of(part * part)
    size = jnp.sqrt(squares_sum)
    scale = jnp.minimum(1.0, CLIP / size)

    def adam(which, where, grad, factor=scale):
        clipped = grad * factor
        weight = weights[which][where]
        moment = B1 * means[which][where] + (1.0 - B1) * clipped
        second = B2 * squares[which][where] + (1.0 - B2) * clipped * clipped
        level = second * (1.0 / (1.0 - B2**STEP))
        step = (moment * (1.0 / (1.0 - B1**STEP))) / (level * lax.rsqrt(level) + ADAM_EPS)
        new[3 * which][where] = weight - RATE * (step + DECAY * weight)
        new[3 * which + 1][where] = moment
        new[3 * which + 2][where] = second

    every = slice(None)
    stores = []

    def leave(which):
        for place in range(3 * which, 3 * which + 3):
            store = pltpu.make_async_copy(new[place], far[place], store_sem.at[place])
            store.start()
            stores.append(store)

    def ready(which):
        loads[which].wait()
        loads[6 + which].wait()

    ready(2)
    for w in range(2):
        half = slice(128 * w, 128 * w + 128)
        adam(2, (slice(0, WA), half), big(ROWS.o + w * WA, WA))
        adam(2, (slice(WA, WA + UP), half), exact(ROWS.back + w * UP, UP))
    leave(2)
    ready(1)
    adam(1, (slice(0, 4 * WA), every), g_a[...])
    for w in range(2):
        half = slice(128 * w, 128 * w + 128)
        adam(1, (slice(1024, 2048), half), big(ROWS.up + w * UP, UP))
        adam(1, (slice(2048, 2135), half), exact(ROWS.eh + w * 88, 87))
    leave(1)
    ready(3)
    adam(3, (slice(0, UP), every), big(ROWS.outer, UP))
    adam(3, (slice(UP, UP + NREL), every), g_rel[0:NREL, :])
    leave(3)
    ready(4)
    adam(4, (slice(0, 768), every), big(ROWS.tri, 768))
    adam(4, (slice(768, 776), every), g_bias)
    adam(4, (slice(776, 840), every), exact(ROWS.dist, BINS))
    leave(4)
    ready(0)
    adam(0, (every, every), g_lookup[0:LETTERS])
    leave(0)
    ready(5)
    adam(5, (slice(0, 1367),), g_small[0:1367], scale.reshape(1))
    leave(5)

    sums = exact(base + 8, 1)
    loss = sums[:, 0:1] / aux[0:1, 0:1] + sums[:, 1:2] * aux[0:1, 1:2]
    loss_out[0] = loss[0, 0]
    size_out[0] = size[0, 0]
    for store in stores:
        store.wait()


def vmem():
    return pl.BlockSpec(memory_space=pltpu.VMEM)


def per_device(rows, cols, *arrays):
    letters, truth, concealed, existing, ordinals, observed, bins = arrays[:7]

    def turned(group):
        return [w.T if place in (1, 4) else w for place, w in enumerate(group)]

    weights, means, squares = turned(arrays[7:13]), turned(arrays[13:19]), turned(arrays[19:25])
    plan = scratch_plan(rows, cols)
    bases = layout(rows, cols)[1]
    far = pl.BlockSpec(memory_space=pltpu.HBM)
    summed = pl.pallas_call(
        functools.partial(main_kernel, rows, cols, tuple(plan)),
        out_shape=(
            jax.ShapeDtypeStruct((bases[2] // 8, 8, 128), BF16),
            jax.ShapeDtypeStruct((bases[4] - bases[2], 128), F32),
            jax.ShapeDtypeStruct((bases[5] - bases[4], 128), F32),
            jax.ShapeDtypeStruct((AP, 4 * WA), F32),
            jax.ShapeDtypeStruct((8, 128), F32),
        ),
        in_specs=[far] * OPERANDS,
        out_specs=tuple([vmem()] * 5),
        scratch_shapes=[pltpu.VMEM(dims, kind) for dims, kind in plan.values()]
        + [
            pltpu.SemaphoreType.DMA((rows - 1,)),
            pltpu.SemaphoreType.DMA((PHASES, rows - 1)),
            pltpu.SemaphoreType.DMA((cols - 1,)),
            pltpu.SemaphoreType.DMA((PHASES - 1, cols - 1)),
            pltpu.SemaphoreType.DMA((4, 2, max(rows, cols) // 2 - 1)),
            pltpu.SemaphoreType.DMA((4, 2, rows + cols)),
            pltpu.SemaphoreType.DMA((OPERANDS,)),
        ],
        compiler_params=pltpu.CompilerParams(
            collective_id=0, has_side_effects=True, vmem_limit_bytes=MAIN_VMEM
        ),
    )(
        *[
            pltpu.with_memory_space_constraint(value, pltpu.HBM)
            for value in (
                jnp.swapaxes(letters, 1, 2),
                jnp.swapaxes(truth, 1, 2),
                jnp.swapaxes(concealed, 1, 2),
                existing,
                ordinals,
                observed,
                bins,
                *weights,
            )
        ]
    )

    shapes = []
    for w in weights:
        shapes += [jax.ShapeDtypeStruct(w.shape, F32)] * 3
    one = jax.ShapeDtypeStruct((1,), F32)
    scalar = pl.BlockSpec(memory_space=pltpu.SMEM)
    result = pl.pallas_call(
        functools.partial(post_kernel, rows, cols),
        out_shape=tuple(shapes) + (one, one),
        in_specs=[vmem()] * 11 + [far] * 12,
        out_specs=tuple([far] * 18) + (scalar, scalar),
        scratch_shapes=[pltpu.VMEM(shape.shape, F32) for shape in shapes]
        + [pltpu.VMEM(value.shape, F32) for value in (*means, *squares)]
        + [
            pltpu.VMEM((AP, WA), F32),
            pltpu.VMEM((RP, WP), F32),
            pltpu.VMEM((4 * WA, WA), F32),
            pltpu.VMEM((1408,), F32),
            pltpu.VMEM((72, 128), F32),
            pltpu.SemaphoreType.DMA((18,)),
            pltpu.SemaphoreType.DMA((12,)),
        ],
        compiler_params=pltpu.CompilerParams(vmem_limit_bytes=POST_VMEM),
    )(
        *summed,
        *weights,
        *[pltpu.with_memory_space_constraint(value, pltpu.HBM) for value in (*means, *squares)],
    )
    outs = [result[18].reshape(()), result[19].reshape(())]
    for place, value in enumerate(result[:18]):
        outs.append(value.T if place // 3 in (1, 4) else value)
    return tuple(outs)


def solution(mesh):
    rows, cols = mesh.shape[ROW], mesh.shape[COL]
    placed = (
        (P(None, COL, ROW),) * 3 + (P(),) * 3 + (P(None, ROW, COL),) + (P(),) * 18
    )
    return jax.shard_map(
        functools.partial(per_device, rows, cols),
        mesh=mesh,
        in_specs=placed,
        out_specs=(P(),) * 20,
        check_vma=False,
    )
```

```python
import functools
from types import SimpleNamespace

import jax
import jax.numpy as jnp
from jax import lax
from jax.experimental import pallas as pl
from jax.experimental.pallas import tpu as pltpu
from jax.sharding import PartitionSpec as P

F32, BF16 = jnp.float32, jnp.bfloat16
MESH = pl.DeviceIdType.MESH
ROW, COL, QUAD = "row", "col", "quad"
CORE, X, Y, Z = "core", "x", "y", "z"
WA, WP, WO, LETTERS, BINS, REACH, HEADS, HEAD = 256, 128, 32, 23, 64, 32, 8, 32
UP = 1024
NREL = 2 * REACH + 1
AP = 32
TR = 24
RP = 128
EPS = 1e-05
NB, NS, NI, NJ = 2, 16, 8, 16
NM = NB * NS * NI
NP = 2 * NI * NJ
BS = NB * NS
BI = NB * NI
DS = WO * NS
TOGETHER = 4
CLIP, RATE, B1, B2, STEP, ADAM_EPS, DECAY = 0.02, 0.05, 0.9, 0.999, 4, 1e-08, 0.01

MAIN_VMEM, POST_VMEM = 44 * 2**20, 30 * 2**20

NN = (((1,), (0,)), ((), ()))
NT = (((1,), (1,)), ((), ()))
TN = (((0,), (0,)), ((), ()))

GROUPS = (
    dict(up=2 * UP, o=2 * WA),
    dict(outer=WO * WO, tri=5 * WP, out=WP),
    dict(back=2 * UP),
    dict(eh=176, tabs=6 * TR, dist=BINS, rel=72, small=16),
    dict(score=2 * TR, bias=8),
)
BF16_GROUPS = 1
BF16_SUM = 0


def layout(rows, cols):
    places, bases, begin = {}, [], 0
    for number, group in enumerate(GROUPS):
        bases.append(begin)
        for name, count in group.items():
            places[name] = begin
            begin += count
        size = 8 * cols * 2 if number + 1 == len(GROUPS) else 16 * rows * cols
        begin = bases[-1] - (bases[-1] - begin) // size * size
    return SimpleNamespace(**places), bases + [begin]


def mm(a, b, dims=NN):
    return lax.dot_general(a, b, dims, preferred_element_type=F32)


def split2(x):
    high = x.astype(BF16)
    return high, (x - high.astype(F32)).astype(BF16)


def split3(x):
    high = x.astype(BF16)
    rest = x - high.astype(F32)
    middle = rest.astype(BF16)
    return high, middle, (rest - middle.astype(F32)).astype(BF16)


def mm3(a, b, dims=NN):
    ah, al = split2(a)
    bh, bl = split2(b)
    return mm(ah, bh, dims) + (mm(al, bh, dims) + mm(ah, bl, dims))


def mm6(a, b, dims=NN):
    ah, am, al = split3(a)
    bh, bm, bl = split3(b)
    low = mm(al, bh, dims) + (mm(am, bm, dims) + mm(ah, bl, dims))
    return mm(ah, bh, dims) + ((mm(am, bh, dims) + mm(ah, bm, dims)) + low)


def mm2(a, exact, dims=NN):
    ah, al = split2(a)
    return mm(ah, exact, dims) + mm(al, exact, dims)


def mm2r(exact, b, dims=NN):
    bh, bl = split2(b)
    return mm(exact, bh, dims) + mm(exact, bl, dims)


def mm3r(exact, b, dims=NN):
    bh, bm, bl = split3(b)
    return mm(exact, bh, dims) + (mm(exact, bm, dims) + mm(exact, bl, dims))


def norm(x):
    centred = x - jnp.mean(x, axis=-1, keepdims=True)
    scale = lax.rsqrt(jnp.mean(centred * centred, axis=-1, keepdims=True) + EPS)
    return centred * scale, scale


def norm_back(grad, unit, scale):
    return scale * (
        grad
        - jnp.mean(grad, axis=-1, keepdims=True)
        - unit * jnp.mean(grad * unit, axis=-1, keepdims=True)
    )


def iota(shape, axis):
    return lax.broadcasted_iota(jnp.int32, shape, axis)


def head_mask(rows, per_row):
    shape = (rows, WA)
    return iota(shape, 0) // per_row == iota(shape, 1) // HEAD


def colsum(x):
    return jnp.sum(x, axis=0, keepdims=True)


def total_of(x):
    return jnp.sum(jnp.sum(x, axis=1, keepdims=True), axis=0, keepdims=True)


def scratch_plan(rows, cols):
    length = rows * NI
    bases = layout(rows, cols)[1]
    final = bases[5] - bases[4]
    return dict(
        lk=((AP, WA), F32),
        weh=((128, WA), F32),
        wbd=((128, WP), F32),
        seqw=((NM, 1), F32),
        lmask=((NM, 1), F32),
        truth=((NM, 1), F32),
        pmask=((NP, 1), F32),
        offset=((NP, 1), F32),
        codes=((BI, length), F32),
        sites=((8, length), F32),
        wrel=((RP, WP), F32),
        tail=((8, 128), F32),
        kb=((WA, WA), BF16),
        vb=((WA, WA), BF16),
        amat=((BS, NI, WA), F32),
        pam=((BS, NI, WA), F32),
        hm=((64, WA), F32),
        letx=((128, length), F32),
        biash=((NB, 64, length), F32),
        prob=((BS, 64, length), F32),
        sg=((NM, WA), F32),
        att=((NM, WA), F32),
        xh1=((NM, WA), F32),
        r1=((NM, 1), F32),
        hid=((NM, UP), F32),
        rep=((NM, WA), F32),
        xh2=((NM, WA), F32),
        r2=((NM, 1), F32),
        dlog=((NM, 128), F32),
        left3=((NB, NI * NS, 128), BF16),
        mhi=((BI, DS, WP), BF16),
        mlo=((BI, DS, WP), BF16),
        rall=((length, DS), BF16),
        prep=((NP, WP), F32),
        xh3=((NP, WP), F32),
        r3=((NP, 1), F32),
        proj=((NP, 5 * WP), F32),
        le=((BI * NJ, WP), F32),
        re=((length * NJ, WP), F32),
        dm=((BI * length, WP), F32),
        gl=((BI, NJ, WP), F32),
        dr=((length, DS), F32),
        dmid=((NM, WA), F32),
        dbias=((NB, 64, length), F32),
        da=((BS, NI, WA), F32),
        dpam=((BS, NI, WA), F32),
        dtab=((BI, 16, RP), F32),
        dn=((NM, WA), F32),
        sum8=((8, WA), F32),
        grad=((bases[5], 128), F32),
        lets=((8, 128), F32),
        letr=((rows, 8, 128), F32),
        cnts=((8, 128), F32),
        cntr=((cols, 8, 128), F32),
        rs=((NB, NI, DS), BF16),
        rr=((rows, NI, DS), BF16),
        lr=((2, NI * NS, 128), BF16),
        tgr=((2, NI, NJ), jnp.int32),
        os=((cols, BI, NJ, WP), BF16),
        orr=((cols, BI, NJ, WP), BF16),
        er=((rows // 2, BI, NJ, WP), BF16),
        ts=((cols, BI, NJ, WP), BF16),
        tr=((cols, BI, NJ, WP), BF16),
        ds=((BI, NJ, WP), BF16),
        dsr=((cols, BI, NJ, WP), BF16),
        gs=((rows // 2, BI, NJ, WP), BF16),
        gr=((rows // 2, BI, NJ, WP), BF16),
        qs=((BI, NJ, WP), BF16),
        qr=((cols, BI, NJ, WP), BF16),
        us=((rows, NI, DS), BF16),
        ur=((rows, NI, DS), BF16),
        dl=((2, NI * NS, 128), BF16),
        dlr=((NB, NI * NS, 128), BF16),
        arx=((bases[4], 128), F32),
        lows=((bases[1] // 8, 8, 128), BF16),
        lowr=((bases[1] // 8, 8, 128), BF16),
        fc=((cols, final // cols, 128), F32),
        fp=((final // cols, 128), F32),
        fr=((rows, final // cols, 128), F32),
        letters=((NB, NI, NS), jnp.int32),
        truths=((NB, NI, NS), jnp.int32),
        concealed=((NB, NI, NS), jnp.int32),
        existing=((NB, cols * NS), jnp.int32),
        ordinals=((NB, length), jnp.int32),
        observed=((NB, length), jnp.int32),
        targets=((NB, NI, NJ), jnp.int32),
        lookup=((LETTERS, WA), F32),
        w_a=((2135, WA), F32),
        w_c=((WA + UP, WA), F32),
        w_r=((UP + NREL, WP), F32),
        w_p=((840, WP), F32),
        scal=((1367,), F32),
    )


OPERANDS = 13


LET, RIGHT, EDGE, GEDGE, GRIGHT, SUM_ROW = range(6)
CNT, OUTER, TRI, GMIX, GOUTER, SUM_COL, SHARE_COL = range(7)
PHASES = 7


def main_kernel(rows, cols, names, *refs):
    operands = refs[:OPERANDS]
    gbig, grest, gfin, tout, aux = refs[OPERANDS : OPERANDS + 5]
    s = SimpleNamespace(**dict(zip(names, refs[OPERANDS + 5 : -8])))
    row_send, row_recv, col_send, col_recv, pair_sem, sum_send, sum_recv, load_sem = refs[-8:]
    held = refs[OPERANDS + 5 : -8][-OPERANDS:]
    loads = [
        pltpu.make_async_copy(far, near, load_sem.at[place])
        for place, (far, near) in enumerate(zip(operands, held))
    ]
    for load in loads:
        load.start()
    letters, truths, hidden_sites, existing, ordinals, observed, targets = held[:7]
    lookup, w_a, w_c, w_r, w_p, scal = held[7:]
    ROWS, bases = layout(rows, cols)
    length = rows * NI
    me_r, me_c = lax.axis_index(ROW), lax.axis_index(COL)

    barrier = pltpu.get_barrier_semaphore()
    for step in range(1, rows):
        pl.semaphore_signal(
            barrier,
            inc=1,
            device_id={ROW: lax.rem(me_r + step, rows), COL: me_c},
            device_id_type=MESH,
        )
    for step in range(1, cols):
        pl.semaphore_signal(
            barrier,
            inc=1,
            device_id={ROW: me_r, COL: lax.rem(me_c + step, cols)},
            device_id_type=MESH,
        )
    quads = rows // 2
    side, quad = me_r // quads, me_r % quads

    def to_partner(number, source, target):
        return pltpu.make_async_remote_copy(
            src_ref=source,
            dst_ref=target,
            send_sem=pair_sem.at[number, 0],
            recv_sem=pair_sem.at[number, 1],
            device_id={ROW: (1 - side) * quads + quad, COL: me_c},
            device_id_type=MESH,
        )

    def swap(number, source, target):
        out = to_partner(number, source.at[1 - side], target.at[side])
        out.start()
        return out, to_partner(number, source.at[1 - side], target.at[1 - side])

    def exchange(along, phase, source, target):
        if along == ROW:
            count, me, number = rows, me_r, phase
            send, recv = row_send, row_recv
        elif along == QUAD:
            count, me, number = quads, quad, phase
            send, recv = row_send, row_recv
        else:
            count, me, number = cols, me_c, phase
            send, recv = col_send, col_recv
        copies = []
        for step in range(1, count):
            peer = lax.rem(me + step, count)
            origin = lax.rem(me + (count - step), count)
            where = {ROW: me_r, COL: peer}
            if along == ROW:
                where = {ROW: peer, COL: me_c}
            elif along == QUAD:
                where = {ROW: side * quads + peer, COL: me_c}
            out = pltpu.make_async_remote_copy(
                src_ref=source(peer),
                dst_ref=target(me),
                send_sem=send.at[step - 1],
                recv_sem=recv.at[number, step - 1],
                device_id=where,
                device_id_type=MESH,
            )
            out.start()
            arriving = pltpu.make_async_remote_copy(
                src_ref=source(peer),
                dst_ref=target(origin),
                send_sem=send.at[step - 1],
                recv_sem=recv.at[number, step - 1],
                device_id=where,
                device_id_type=MESH,
            )
            copies.append((out, arriving))
        return copies

    def finish(copies):
        for out, arriving in copies:
            out.wait_send()
            arriving.wait_recv()

    for load in loads[:7]:
        load.wait()
    here = existing[...].astype(F32)
    sites = observed[...].astype(F32)
    numbers = ordinals[...].astype(F32)

    def by_protein(values, count, each):
        wide = (count, values.shape[1])
        return jnp.where(iota(wide, 0) // each == 0, values[0:1], values[1:2])

    def at_lane(values, lanes):
        return jnp.sum(jnp.where(iota(values.shape, 1) == lanes, values, 0.0), axis=1, keepdims=True)

    row_m, row_p = iota((NM, 1), 0), iota((NP, 1), 0)
    seq_m, res_m = (row_m // NI) % NS, row_m % NI
    spread_m = jnp.where(
        iota((NM, BI), 1) == (iota((NM, BI), 0) // (NI * NS)) * NI + iota((NM, BI), 0) % NI, 1.0, 0.0
    ).astype(BF16)

    def column_m(values):
        wide = mm(spread_m, values[...].reshape(BI, NS).astype(F32).astype(BF16))
        return at_lane(wide, seq_m)

    seq_weight = at_lane(by_protein(here, NM, NI * NS), me_c * NS + seq_m)
    letter = column_m(letters)
    loss_mask = column_m(hidden_sites) * seq_weight
    s.seqw[...] = seq_weight
    s.lmask[...] = loss_mask
    s.truth[...] = column_m(truths)
    s.tgr[side] = targets[side]

    s.lets[...] = jnp.where(
        (iota((NI, 128), 0) == 0) & (iota((NI, 128), 1) == BS), total_of(loss_mask), 0.0
    )
    for b in range(NB):
        s.lets[:, b * NS : (b + 1) * NS] = letters[b].astype(F32)
    s.letr[me_r] = s.lets[...]
    near = row_p // NJ
    first = (quad + quads * (near // NI)) * NI + near % NI
    second = me_c * NJ + row_p % NJ

    def of_side(values):
        return jnp.where(side == 0, values[0:1], values[1:2])

    sites_p = jnp.broadcast_to(of_side(sites), (NP, length))
    numbers_p = jnp.broadcast_to(of_side(numbers), (NP, length))
    s.pmask[...] = at_lane(sites_p, first) * at_lane(sites_p, second)
    s.offset[...] = (
        jnp.clip(at_lane(numbers_p, first) - at_lane(numbers_p, second), -REACH, REACH) + REACH
    )
    numbers_b = by_protein(numbers, BI, NI)
    own = at_lane(numbers_b, me_r * NI + iota((BI, 1), 0) % NI)
    s.codes[...] = jnp.clip(own - numbers_b, -REACH, REACH) + REACH
    s.sites[...] = jnp.zeros((8, length), F32)
    s.sites[0:NB, :] = sites
    inv_all = 1.0 / (jnp.sum(here, axis=1, keepdims=True) + 1.0)
    inv_count = of_side(inv_all)
    per_protein = jnp.sum(sites, axis=1, keepdims=True)
    inv_dist = 1.0 / jnp.maximum(colsum(per_protein * per_protein), 1.0)

    for load in loads[7:]:
        load.wait()

    def gain(begin, width):
        return scal[begin : begin + width].reshape(1, width)

    gain_row, gain_trans, gain_outer = gain(0, WA), gain(256, WA), gain(512, WA)
    gain_rel, gain_pair, gain_mixed = gain(768, WP), gain(896, WP), gain(1024, WP)
    bias_outer = gain(1152, WP)
    s.lk[...] = jnp.zeros((AP, WA), F32)
    s.lk[0:LETTERS, :] = lookup[...]
    s.weh[...] = jnp.zeros((128, WA), F32)
    s.weh[0:87, :] = w_a[2048:2135, :]
    s.wbd[...] = jnp.zeros((128, WP), F32)
    s.wbd[0:72, :] = w_p[768:840, :]
    s.wrel[...] = jnp.zeros((RP, WP), F32)
    s.wrel[0:NREL, :] = w_r[UP : UP + NREL, :]
    s.tail[...] = jnp.zeros((8, 128), F32)
    s.tail[0:1, 0:87] = scal[1280:1367].reshape(1, 87)

    table = s.lk[...]
    unit0, _ = norm(table)
    mapped = mm6(unit0 * gain_row, w_a[0 : 4 * WA, :], NT)
    tout[...] = mapped
    pl.semaphore_wait(barrier, rows + cols - 2)
    flight = exchange(ROW, LET, lambda p: s.lets, lambda p: s.letr.at[p])
    flight.append(swap(0, targets, s.tgr))
    t_q = mapped[:, 0:WA] * HEAD ** (-0.5)
    t_k = mapped[:, WA : 2 * WA].astype(BF16).astype(F32)
    t_v = mapped[:, 2 * WA : 3 * WA].astype(BF16).astype(F32)
    t_g = jax.nn.sigmoid(mapped[:, 3 * WA :])
    square = head_mask(WA, AP)
    key_block = jnp.where(square, jnp.concatenate([t_k] * HEADS, axis=0), 0.0).astype(BF16)
    s.vb[...] = jnp.where(square, jnp.concatenate([t_v] * HEADS, axis=0), 0.0).astype(BF16)
    stacked = mm(jnp.concatenate(split3(t_q), axis=0), key_block, NT)
    score_table = stacked[0:AP] + (stacked[AP : 2 * AP] + stacked[2 * AP :])
    s.hm[...] = jnp.where(head_mask(64, NI), 1.0, 0.0)

    letter = letter.astype(jnp.int32)
    triple = jnp.where(
        (iota((NM, 3 * AP), 1) % AP) == letter, 1.0, 0.0
    ).astype(BF16)

    def chosen(values):
        return mm(triple, jnp.concatenate(split3(values), axis=0))

    s.amat[...] = chosen(score_table).reshape(BS, NI, WA)
    start = chosen(table)
    s.sg[...] = chosen(t_g)

    unit_r, _ = norm(s.wrel[...])
    bias_table = mm3(s.wbd[0:8, :], unit_r * gain_rel, NT)
    bias_parts = jnp.concatenate(split3(bias_table), axis=0)

    def codes(index):
        return jnp.where(
            iota((RP, length), 0) == s.codes[index : index + 1, :].astype(jnp.int32), 1.0, 0.0
        ).astype(BF16)

    for b in range(NB):
        for i in range(NI):
            part = mm(bias_parts, codes(b * NI + i))
            part = part[0:8] + (part[8:16] + part[16:24])
            for h in range(HEADS):
                s.biash[b, h * NI + i : h * NI + i + 1, :] = part[h : h + 1, :]

    finish(flight)
    letters_all = s.letr[...].reshape(length, 128).T
    s.letx[...] = letters_all
    s.cnts[...] = jnp.broadcast_to(
        jnp.sum(letters_all[BS : BS + 1, :], axis=1, keepdims=True), (8, 128)
    )
    s.cntr[me_c] = s.cnts[...]
    count_flight = exchange(COL, CNT, lambda p: s.cnts, lambda p: s.cntr.at[p])

    def letter_codes(bs):
        row = s.letx[pl.ds(bs, 1), :].astype(jnp.int32)
        one = jnp.where(iota((AP, length), 0) == row, 1.0, 0.0)
        return jnp.concatenate([one] * HEADS, axis=0).astype(BF16)

    def spread(value):
        wide = jnp.broadcast_to(value[None], (HEADS, NI, WA)).reshape(64, WA)
        return wide * s.hm[...]

    def gather_heads(value):
        return jnp.sum((value * s.hm[...]).reshape(HEADS, NI, WA), axis=0)

    for b in range(NB):
        key_mask = s.sites[b : b + 1, :]

        @pl.loop(0, NS // TOGETHER)
        def _(q):
            for part in range(TOGETHER):
                bs = b * NS + q * TOGETHER + part
                code = letter_codes(bs)
                wide = [spread(p.astype(F32)).astype(BF16) for p in split2(s.amat[bs])]
                raw = mm(jnp.concatenate(wide, axis=0), code)
                scores = (raw[0:64] + raw[64:128]) + s.biash[b]
                scores = jnp.where(key_mask > 0, scores, -1000000000.0)
                power = jnp.exp(scores - jnp.max(scores, axis=-1, keepdims=True))
                weight = power / jnp.sum(power, axis=-1, keepdims=True)
                s.prob[bs] = weight
                picked = mm(jnp.concatenate(split2(weight), axis=0), code, NT)
                s.pam[bs] = gather_heads(picked[0:64] + picked[64:128])

    att = mm2(s.pam[...].reshape(NM, WA), s.vb[...])
    s.att[...] = att
    mid = start + mm3(s.sg[...] * att, w_c[0:WA, :])
    unit1, scale1 = norm(mid)
    s.xh1[...] = unit1
    s.r1[...] = scale1
    hidden = jnp.maximum(mm3(unit1 * gain_trans, w_a[4 * WA : 4 * WA + UP, :], NT), 0.0)
    s.hid[...] = hidden
    rep = mid + mm3(hidden, w_c[WA:, :])
    s.rep[...] = rep
    unit2, scale2 = norm(rep)
    s.xh2[...] = unit2
    s.r2[...] = scale2
    seq_weight = s.seqw[...]
    lane = iota((NM, 128), 1)
    edges = mm3(unit2 * gain_outer, s.weh[...], NT) * seq_weight

    right = jnp.where((lane >= 32) & (lane < 64), edges, 0.0).astype(BF16)
    spot = iota((128, DS), 0)
    repeat = jnp.where(spot - 32 == iota((128, DS), 1) // NS, 1.0, 0.0)
    repeat = jnp.where((spot >= 32) & (spot < 64), repeat, 0.0).astype(BF16)
    wide = mm(right, repeat)
    own_seq = (iota((NM, DS), 0) // NI) % NS == iota((NM, DS), 1) % NS
    wide = jnp.sum(jnp.where(own_seq, wide, 0.0).reshape(NB, NS, NI, DS), axis=1)
    s.rs[...] = wide.astype(BF16)
    s.rr[me_r] = s.rs[side]
    flight = exchange(ROW, RIGHT, lambda p: s.rs.at[p // quads], lambda p: s.rr.at[p])

    order_to = (iota((NM, NM), 0) // (NI * NS) == iota((NM, NM), 1) // (NI * NS)) & (
        (iota((NM, NM), 0) // NS) % NI == iota((NM, NM), 1) % NI
    )
    order_to = order_to & (iota((NM, NM), 0) % NS == (iota((NM, NM), 1) // NI) % NS)
    order = jnp.where(order_to, 1.0, 0.0).astype(BF16)
    left = mm3r(order, jnp.where(lane < 32, edges, 0.0))
    high, low = split2(left)
    high32, low32 = high.astype(F32), low.astype(F32)
    left3 = high32 + pltpu.roll(low32, 32, 1) + pltpu.roll(high32, 64, 1)
    s.left3[...] = left3.astype(BF16).reshape(NB, NI * NS, 128)
    s.lr[side] = s.left3[side]
    flight.append(swap(1, s.left3, s.lr))

    finish(count_flight)
    masked = jnp.maximum(jnp.sum(s.cntr[...], axis=0)[0:1, 0:1], 1.0)
    logits = mm3(rep, s.weh[...], NT) + s.tail[0:1, :]
    valid = (lane >= 64) & (lane < 64 + LETTERS)
    top = jnp.max(jnp.where(valid, logits, -3e38), axis=-1, keepdims=True)
    power = jnp.where(valid, jnp.exp(jnp.where(valid, logits, top) - top), 0.0)
    whole = jnp.sum(power, axis=-1, keepdims=True)
    truth = lane - 64 == s.truth[...].astype(jnp.int32)
    truth = truth & valid
    picked = jnp.sum(jnp.where(truth, logits, 0.0), axis=-1, keepdims=True)
    loss_mask = s.lmask[...]
    msa_sum = colsum((jnp.log(whole) + top - picked) * loss_mask)
    s.dlog[...] = (power / whole - jnp.where(truth, 1.0, 0.0)) * (loss_mask / masked)

    def outer_weight(d):
        return w_r[pl.ds(d, WO, stride=WO), :]

    def expand(block):
        for pair in range(WO // 2):
            both = jnp.concatenate([outer_weight(2 * pair), outer_weight(2 * pair + 1)], axis=1)
            wh, wl = split2(both)
            made = mm(s.lr[block][:, 0:96], jnp.concatenate([wh, wh, wl], axis=0))
            for half in range(2):
                d = 2 * pair + half
                mh, ml = split2(made[:, half * WP : (half + 1) * WP].reshape(NI, NS, WP))
                s.mhi[pl.ds(block * NI, NI), d * NS : (d + 1) * NS, :] = mh
                s.mlo[pl.ds(block * NI, NI), d * NS : (d + 1) * NS, :] = ml

    expand(side)
    finish(flight)
    expand(1 - side)
    s.rall[...] = s.rr[...].astype(F32).reshape(length, DS).astype(BF16)

    @pl.loop(0, BI)
    def _(i):
        block = mm(s.rall[...], s.mhi[i]) + mm(s.rall[...], s.mlo[i])
        block = block * inv_count
        for c in range(cols):
            s.os[c, i] = block[c * NJ : (c + 1) * NJ].astype(BF16)

    s.orr[me_c] = s.os[me_c]
    finish(exchange(COL, OUTER, lambda p: s.os.at[p], lambda p: s.orr.at[p]))

    pair_lane = iota((NP, 128), 1)
    offset = s.offset[...].astype(jnp.int32)
    pair_codes = jnp.where(pair_lane == offset, 1.0, 0.0).astype(BF16)
    outer = s.orr[0].astype(F32)
    for c in range(1, cols):
        outer = outer + s.orr[c].astype(F32)
    pair_rep = (mm3r(pair_codes, s.wrel[...]) + outer.reshape(NP, WP)) + bias_outer
    s.prep[...] = pair_rep
    unit3, scale3 = norm(pair_rep)
    s.xh3[...] = unit3
    s.r3[...] = scale3
    proj = mm3(unit3 * gain_pair, w_p[0 : 5 * WP, :], NT)
    pair_mask = s.pmask[...]
    sig1 = jax.nn.sigmoid(proj[:, WP : 2 * WP])
    sig2 = jax.nn.sigmoid(proj[:, 3 * WP : 4 * WP])
    sig3 = jax.nn.sigmoid(proj[:, 4 * WP :])
    s.proj[:, 0 : WP] = proj[:, 0:WP]
    s.proj[:, WP : 2 * WP] = sig1
    s.proj[:, 2 * WP : 3 * WP] = proj[:, 2 * WP : 3 * WP]
    s.proj[:, 3 * WP : 4 * WP] = sig2
    s.proj[:, 4 * WP :] = sig3
    s.le[...] = sig1 * proj[:, 0:WP] * pair_mask
    right_edge = (sig2 * proj[:, 2 * WP : 3 * WP] * pair_mask).astype(BF16)
    s.er[quad] = right_edge.reshape(BI, NJ, WP)
    finish(exchange(QUAD, EDGE, lambda p: s.er.at[quad], lambda p: s.er.at[p]))
    for q in range(quads):
        for block in range(2):
            begin = (q + quads * block) * NI * NJ
            s.re[begin : begin + NI * NJ, :] = (
                s.er[q, block * NI : (block + 1) * NI].astype(F32).reshape(NI * NJ, WP)
            )

    @pl.loop(0, BI)
    def _(i):
        for c in range(cols):
            block = jnp.zeros((NJ, WP), F32)
            for k in range(NJ):
                other = s.re[pl.ds(c * NJ * NJ + k, NJ, stride=NJ), :]
                block = block + s.le[pl.ds(i * NJ + k, 1), :] * other
            s.ts[c, i] = block.astype(BF16)

    s.tr[me_c] = s.ts[me_c]
    finish(exchange(COL, TRI, lambda p: s.ts.at[p], lambda p: s.tr.at[p]))

    mixed = s.tr[0].astype(F32)
    for c in range(1, cols):
        mixed = mixed + s.tr[c].astype(F32)
    unit4, scale4 = norm(mixed.reshape(NP, WP))
    w_out = w_p[5 * WP : 6 * WP, :]
    moved = mm3(unit4 * gain_mixed, w_out, NT)
    sig3 = s.proj[:, 4 * WP :]
    pair_out = s.prep[...] + sig3 * moved
    bins = mm3(pair_out, s.wbd[...], NT) + pltpu.roll(
        jnp.where(iota((8, 128), 1) < BINS, s.tail[...], 0.0), 8, 1
    )[0:1]
    valid = (pair_lane >= 8) & (pair_lane < 8 + BINS)
    top = jnp.max(jnp.where(valid, bins, -3e38), axis=-1, keepdims=True)
    power = jnp.where(valid, jnp.exp(jnp.where(valid, bins, top) - top), 0.0)
    whole = jnp.sum(power, axis=-1, keepdims=True)
    spread_p = jnp.where(iota((NP, BI), 1) == iota((NP, BI), 0) // NJ, 1.0, 0.0).astype(BF16)
    target = at_lane(
        mm(spread_p, s.tgr[...].reshape(BI, NJ).astype(F32).astype(BF16)), row_p % NJ
    )
    truth = (pair_lane - 8 == target.astype(jnp.int32)) & valid
    picked = jnp.sum(jnp.where(truth, bins, 0.0), axis=-1, keepdims=True)
    dist_sum = colsum((jnp.log(whole) + top - picked) * pair_mask)
    dbins = (power / whole - jnp.where(truth, 1.0, 0.0)) * (pair_mask * inv_dist)

    def put(place, value, skip=0):
        base = place + skip
        height, width = value.shape
        for w in range(width // 128):
            s.grad[base + w * height : base + (w + 1) * height, :] = value[
                :, w * 128 : (w + 1) * 128
            ]

    sizes = {CORE: 2, X: cols // 2, Y: 2, Z: rows // 2}
    places = {CORE: me_c % 2, X: me_c // 2, Y: me_r % 2, Z: me_r // 2}

    def line_peer(axis, place):
        if axis == CORE:
            return {ROW: me_r, COL: me_c // 2 * 2 + place}
        if axis == X:
            return {ROW: me_r, COL: place * 2 + me_c % 2}
        if axis == Y:
            return {ROW: me_r // 2 * 2 + place, COL: me_c}
        return {ROW: place * 2 + me_r % 2, COL: me_c}

    class Sum:
        def __init__(self, number):
            self.number = number
            self.stage = -1
            self.used = [0, 0]
            base, size = bases[number] // 8, (bases[number + 1] - bases[number]) // 8
            self.parts = []
            for half in range(2):
                order = (CORE, X, Y, Z) if half == 0 else (CORE, Y, X, Z)
                begin = base + half * (size // 2)
                self.parts.append(SimpleNamespace(order=order, at=begin, size=size // 2, rx=begin))
            self.flight = []

        def copies(self, part, half, axis, source, target, arrive):
            count = sizes[axis]
            for step in range(1, count):
                peer = lax.rem(places[axis] + step, count)
                origin = lax.rem(places[axis] + (count - step), count)
                used = self.used[half]
                self.used[half] += 1
                both = []
                for end in (target(peer, step), arrive(origin, step)):
                    both.append(
                        pltpu.make_async_remote_copy(
                            src_ref=source(peer, step),
                            dst_ref=end,
                            send_sem=sum_send.at[self.number, half, step - 1],
                            recv_sem=sum_recv.at[self.number, half, used],
                            device_id=line_peer(axis, peer),
                            device_id_type=MESH,
                        )
                    )
                both[0].start()
                self.flight.append(both)

        def advance(self):
            finish(self.flight)
            self.flight = []
            if 0 <= self.stage < 4:
                for part in self.parts:
                    self.add(part)
            self.stage += 1
            if self.stage == 4:
                for part in self.parts:
                    self.store(part)
            if self.stage < 4:
                for half, part in enumerate(self.parts):
                    self.start_sum(part, half)
            elif self.stage < 8:
                for half, part in enumerate(self.parts):
                    self.start_share(part, half)

        def start_sum(self, part, half):
            axis = part.order[self.stage]
            small = part.size // sizes[axis]
            part.small, part.axis = small, axis

            low = self.number == BF16_SUM
            for step in range(1, sizes[axis] if low else 1):
                peer = lax.rem(places[axis] + step, sizes[axis])
                value = s.grad[rows_at(part.at + peer * small, small), :]
                slot = part.rx - bases[BF16_SUM] // 8 + (step - 1) * small
                s.lows[slot : slot + small] = value.reshape(small, 8, 128).astype(BF16)

            def source(peer, step):
                if low:
                    return low_spot(s.lows, step)
                return s.grad.at[rows_at(part.at + peer * small, small)]

            def low_spot(buffer, step):
                slot = part.rx - bases[BF16_SUM] // 8 + (step - 1) * small
                return buffer.at[pl.ds(slot, small)]

            def target(place, step):
                if low:
                    return low_spot(s.lowr, step)
                return s.arx.at[pl.ds((part.rx + (step - 1) * small) * 8, small * 8)]

            self.copies(part, half, axis, source, target, target)

        def add(self, part):
            mine = rows_at(part.at + places[part.axis] * part.small, part.small)
            value = s.grad[mine, :]
            for step in range(1, sizes[part.axis]):
                begin = part.rx + (step - 1) * part.small
                if self.number == BF16_SUM:
                    begin = begin - bases[BF16_SUM] // 8
                    other = s.lowr[begin : begin + part.small].astype(F32)
                    value = value + other.reshape(part.small * 8, 128)
                else:
                    value = value + s.arx[begin * 8 : (begin + part.small) * 8, :]
            s.grad[mine, :] = value
            part.at = part.at + places[part.axis] * part.small
            part.rx += (sizes[part.axis] - 1) * part.small
            part.size = part.small

        def store(self, part):
            value = s.grad[rows_at(part.at, part.size), :]
            if self.number < BF16_GROUPS:
                gbig[pl.ds(part.at, part.size)] = value.reshape(part.size, 8, 128).astype(BF16)
            else:
                grest[rows_at(part.at - bases[1] // 8, part.size), :] = value

        def start_share(self, part, half):
            axis = part.order[7 - self.stage]
            size, here = part.size, part.at
            first = here - places[axis] * size

            def spot(place, step):
                at = first + place * size
                if self.number < BF16_GROUPS:
                    return gbig.at[pl.ds(at, size)]
                return grest.at[rows_at(at - bases[1] // 8, size)]

            self.copies(
                part,
                half,
                axis,
                lambda peer, step: spot(places[axis], 0),
                lambda peer, step: spot(places[axis], step),
                spot,
            )
            part.at, part.size = first, size * sizes[axis]

    def rows_at(unit, count):
        return pl.ds(pl.multiple_of(unit * 8, 8), count * 8)

    late, early, middle, rest = [Sum(number) for number in range(4)]

    def column_products(name, place):
        s.sum8[...] = jnp.zeros((8, WA), F32)

        @pl.loop(0, NM // 32)
        def _(q):
            some = pl.ds(pl.multiple_of(q * 32, 32), 32)
            product = s.dn[some, :] * name[some, :]
            s.sum8[...] += jnp.sum(product.reshape(4, 8, WA), axis=0)

        whole = colsum(s.sum8[...])
        for half in range(2):
            s.grad[small + place + half : small + place + half + 1, :] = whole[
                :, 128 * half : 128 * half + 128
            ]

    for begin, end in (
        (ROWS.o + 2 * WA, bases[1]),
        (ROWS.out + WP, bases[2]),
        (ROWS.small, bases[4]),
        (ROWS.bias, bases[5]),
    ):
        if end > begin:
            s.grad[begin:end, :] = jnp.zeros((end - begin, 128), F32)
    small = ROWS.small
    put(ROWS.dist, mm3(dbins, pair_out, TN)[8 : 8 + BINS])
    dbias_dist = pltpu.roll(jnp.broadcast_to(colsum(dbins), (8, 128)), 120, 1)[0:1]
    dout = mm3(dbins, s.wbd[...])
    dgate = dout * moved * (sig3 * (1.0 - sig3))
    dmoved = dout * sig3
    put(ROWS.out, mm3(dmoved, unit4 * gain_mixed, TN))
    dnormed = mm3(dmoved, w_out)
    s.grad[small + 5 : small + 6, :] = colsum(dnormed * unit4)
    dmixed = norm_back(dnormed * gain_mixed, unit4, scale4)
    s.ds[...] = dmixed.astype(BF16).reshape(BI, NJ, WP)
    s.dsr[me_c] = s.ds[...]
    finish(exchange(COL, GMIX, lambda p: s.ds, lambda p: s.dsr.at[p]))
    for bi in range(BI):
        for c in range(cols):
            begin = bi * length + c * NJ
            s.dm[begin : begin + NJ, :] = s.dsr[c, bi].astype(F32)

    @pl.loop(0, quads)
    def _(q):
        for place in range(BI):
            j = (q + quads * (place // NI)) * NI + place % NI
            block = jnp.zeros((NJ, WP), F32)
            for i in range(BI):
                block = block + (
                    s.dm[pl.ds(i * length + j, 1), :] * s.le[i * NJ : (i + 1) * NJ, :]
                )
            s.gs[q, place] = block.astype(BF16)

    s.gr[quad] = s.gs[quad]
    flight = exchange(QUAD, GEDGE, lambda p: s.gs.at[p], lambda p: s.gr.at[p])

    @pl.loop(0, BI)
    def _(i):
        block = jnp.zeros((NJ, WP), F32)
        for j in range(length):
            block = block + (
                s.dm[pl.ds(i * length + j, 1), :] * s.re[j * NJ : (j + 1) * NJ, :]
            )
        s.gl[i] = block

    finish(flight)
    dright = s.gr[0].astype(F32)
    for q in range(1, quads):
        dright = dright + s.gr[q].astype(F32)
    dright = dright.reshape(NP, WP) * pair_mask
    dleft = s.gl[...].reshape(NP, WP) * pair_mask
    p1, sig1 = s.proj[:, 0:WP], s.proj[:, WP : 2 * WP]
    p2, sig2 = s.proj[:, 2 * WP : 3 * WP], s.proj[:, 3 * WP : 4 * WP]
    dproj = jnp.concatenate(
        [
            dleft * sig1,
            dleft * p1 * (sig1 * (1.0 - sig1)),
            dright * sig2,
            dright * p2 * (sig2 * (1.0 - sig2)),
            dgate,
        ],
        axis=1,
    )
    unit3 = s.xh3[...]
    put(ROWS.tri, mm3(dproj, unit3 * gain_pair, TN))
    dnormed = mm3(dproj, w_p[0 : 5 * WP, :])
    s.grad[small + 4 : small + 5, :] = colsum(dnormed * unit3)
    drep = dout + norm_back(dnormed * gain_pair, unit3, s.r3[...])
    s.grad[small + 6 : small + 7, :] = colsum(drep)
    s.grad[ROWS.rel : ROWS.rel + 72, :] = mm2r(pair_codes, drep, TN)[0:72]
    s.qs[...] = drep.astype(BF16).reshape(BI, NJ, WP)
    s.qr[me_c] = s.qs[...]
    finish(exchange(COL, GOUTER, lambda p: s.qs, lambda p: s.qr.at[p]))

    turned = s.rall[...].astype(F32).T.astype(BF16)
    s.dr[...] = jnp.zeros((length, DS), F32)

    @pl.loop(0, BI)
    def _(i):
        block = jnp.concatenate([s.qr[c, i] for c in range(cols)], axis=0)
        s.dr[...] += mm(block, s.mhi[i], NT) + mm(block, s.mlo[i], NT)
        mh, ml = split2(mm(turned, block) * inv_count)
        s.mhi[i] = mh
        s.mlo[i] = ml

    for r in range(rows):
        s.us[r] = (s.dr[r * NI : (r + 1) * NI, :] * inv_count).astype(BF16)
    s.ur[me_r] = s.us[me_r]
    flight = exchange(ROW, GRIGHT, lambda p: s.us.at[p], lambda p: s.ur.at[p])

    def pair_weight(pair):
        return split2(
            jnp.concatenate([outer_weight(2 * pair), outer_weight(2 * pair + 1)], axis=1)
        )

    def pair_of(ref, pair):
        return jnp.concatenate(
            [
                ref[:, d * NS : (d + 1) * NS, :].reshape(NM, WP)
                for d in (2 * pair, 2 * pair + 1)
            ],
            axis=1,
        )

    dleft = jnp.zeros((NM, WO), F32)
    for pair in range(WO // 2):
        wh, wl = pair_weight(pair)
        mh, ml = pair_of(s.mhi, pair), pair_of(s.mlo, pair)
        dleft = dleft + (mm(mh, wh, NT) + (mm(ml, wh, NT) + mm(mh, wl, NT)))
    high, low = split2(jnp.concatenate([dleft, jnp.zeros((NM, 96), F32)], axis=1))
    both = high.astype(F32) + pltpu.roll(low.astype(F32), 32, 1)
    s.dl[...] = both.astype(BF16).reshape(2, NI * NS, 128)
    s.dlr[side] = s.dl[side]
    flight.append(swap(2, s.dl, s.dlr))
    left3 = s.lr[...].astype(F32).reshape(NM, 128).T.astype(BF16)
    left_both, left_high = left3[0:64], left3[0:32]
    for pair in range(WO // 2):
        mh, ml = pair_of(s.mhi, pair), pair_of(s.mlo, pair)
        made = mm(left_both, mh)
        made = made[0:32] + made[32:64] + mm(left_high, ml)
        for half in range(2):
            s.grad[pl.ds(ROWS.outer + 2 * pair + half, WO, stride=WO), :] = made[
                :, half * WP : (half + 1) * WP
            ]
    early.advance()

    finish(flight)
    both = s.dlr[...].astype(F32).reshape(NM, 128)
    both = jnp.where(lane < 32, both + pltpu.roll(both, 96, 1), 0.0)
    dleft = mm3r(order, both, TN)
    dright = []
    for b in range(NB):
        some = s.ur[b * quads].astype(F32)
        for q in range(1, quads):
            some = some + s.ur[b * quads + q].astype(F32)
        dright.append(some)
    dright = jnp.stack(dright)
    wide = jnp.broadcast_to(dright[:, None], (NB, NS, NI, DS)).reshape(NM, DS)
    dedges = mm2(jnp.where(own_seq, wide, 0.0), repeat, NT)
    dedges = (dedges + dleft) * seq_weight
    unit2, rep = s.xh2[...], s.rep[...]
    dlog = s.dlog[...]
    put(ROWS.eh, (mm3(dedges, unit2 * gain_outer, TN) + mm3(dlog, rep, TN))[0:88])
    s.dn[...] = mm3(dedges, s.weh[...])
    dnormed = s.dn[...]
    column_products(s.xh2, 2)
    drep = mm3(dlog, s.weh[...]) + norm_back(dnormed * gain_outer, unit2, s.r2[...])
    early.advance()
    hidden = s.hid[...]
    put(ROWS.back, mm3(hidden, drep, TN))
    middle.advance()
    early.advance()
    dhidden = jnp.where(hidden > 0, mm3(drep, w_c[WA:, :], NT), 0.0)
    unit1 = s.xh1[...]
    put(ROWS.up, mm3(dhidden, unit1 * gain_trans, TN))
    s.dn[...] = mm3(dhidden, w_a[4 * WA : 4 * WA + UP, :])
    dnormed = s.dn[...]
    column_products(s.xh1, 0)
    dmid = drep + norm_back(dnormed * gain_trans, unit1, s.r1[...])
    sg, att = s.sg[...], s.att[...]
    put(ROWS.o, mm3(sg * att, dmid, TN))
    dgated = mm3(dmid, w_c[0:WA, :], NT)
    late.advance()
    middle.advance()
    early.advance()
    single = triple[:, 0:AP]
    put(ROWS.tabs, mm2r(single, dmid, TN)[0:TR], 4 * TR)
    put(ROWS.tabs, mm2r(single, dgated * att, TN)[0:TR], 2 * TR)
    datt = dgated * sg

    pam = s.pam[...].reshape(NM, WA)
    blocks = jnp.where(head_mask(WA, AP), mm3(pam, datt, TN), 0.0)
    put(ROWS.tabs, jnp.sum(blocks.reshape(HEADS, AP, WA), axis=0)[0:TR])
    lane1 = iota((1, 128), 1)
    s.grad[small + 7 : small + 8, :] = jnp.where(lane1 < BINS, dbias_dist, colsum(dlog))
    s.grad[small + 8 : small + 9, :] = jnp.where(
        lane1 == 0, msa_sum, jnp.where(lane1 == 1, dist_sum, 0.0)
    )
    rest.advance()
    s.dpam[...] = mm2(datt, s.vb[...], NT).reshape(BS, NI, WA)
    for b in range(NB):
        key_mask = s.sites[b : b + 1, :]
        s.dbias[b] = jnp.zeros((64, length), F32)

        def attention_back(q):
            together = jnp.zeros((64, length), F32)
            for part in range(TOGETHER):
                bs = b * NS + q * TOGETHER + part
                code = letter_codes(bs)
                wide = [spread(p.astype(F32)).astype(BF16) for p in split2(s.dpam[bs])]
                raw = mm(jnp.concatenate(wide, axis=0), code)
                dweight = raw[0:64] + raw[64:128]
                weight = s.prob[bs]
                inner = jnp.sum(weight * dweight, axis=-1, keepdims=True)
                dscore = jnp.where(key_mask > 0, weight * (dweight - inner), 0.0)
                together = together + dscore
                back = mm(jnp.concatenate(split2(dscore), axis=0), code, NT)
                s.da[bs] = gather_heads(back[0:64] + back[64:128])
            s.dbias[b] += together

        for part in range(2):
            count = NS // TOGETHER // 2
            pl.loop(part * count, (part + 1) * count)(attention_back)
            for group in (early, middle, late, rest):
                group.advance()

    put(ROWS.score, mm2r(single, s.da[...].reshape(NM, WA), TN)[0:TR])
    for b in range(NB):
        for i in range(NI):
            part = jnp.concatenate(
                [s.dbias[b, h * NI + i : h * NI + i + 1, :] for h in range(HEADS)], axis=0
            )
            s.dtab[b * NI + i] = mm(
                jnp.concatenate(split2(part), axis=0), codes(b * NI + i), NT
            )
    s.grad[ROWS.bias : ROWS.bias + 8, :] = jnp.sum(
        s.dtab[...].reshape(2 * BI, 8, RP), axis=0
    )

    aux[...] = jnp.where(iota((8, 128), 1) == 0, masked, inv_dist)

    last = bases[4]
    piece = (bases[5] - last) // cols

    def mine(p):
        return pl.ds(pl.multiple_of(last + p * piece, 8), piece)

    def spot(p):
        return gfin.at[pl.ds(pl.multiple_of(p * piece, 8), piece)]

    s.fc[me_c] = s.grad[mine(me_c), :]
    flight = exchange(COL, SUM_COL, lambda p: s.grad.at[mine(p)], lambda p: s.fc.at[p])
    finish(flight)
    summed = s.fc[0]
    for c in range(1, cols):
        summed = summed + s.fc[c]
    s.fp[...] = summed
    s.fr[me_r] = summed
    flight = exchange(ROW, SUM_ROW, lambda p: s.fp, lambda p: s.fr.at[p])
    for group in (early, middle, late, rest):
        group.advance()
    finish(flight)
    summed = s.fr[0]
    for r in range(1, rows):
        summed = summed + s.fr[r]
    gfin[pl.ds(pl.multiple_of(me_c * piece, 8), piece), :] = summed
    flight = exchange(COL, SHARE_COL, lambda p: spot(me_c), spot)
    while min(group.stage for group in (early, middle, late, rest)) < 8:
        for group in (early, middle, late, rest):
            if group.stage < 8:
                group.advance()
    finish(flight)


def post_kernel(rows, cols, *refs):
    gbig, grest, gfin, tout, aux = refs[:5]
    weights, far_moments = refs[5:11], refs[11:23]
    far, loss_out, size_out = refs[23:41], refs[41], refs[42]
    new, moments = refs[43:61], refs[61:73]
    lk, wrel, g_a, g_small, g_rel, store_sem, load_sem = refs[73:]
    loads = [
        pltpu.make_async_copy(source, near, load_sem.at[place])
        for place, (source, near) in enumerate(zip(far_moments, moments))
    ]
    for place in (2, 8, 1, 7, 3, 9, 4, 10, 0, 6, 5, 11):
        loads[place].start()
    means, squares = moments[0:6], moments[6:12]
    lookup, w_a, w_c, w_r, w_p, scal = weights
    ROWS, bases = layout(rows, cols)

    def big(begin, count):
        part = gbig[begin // 8 : (begin + count) // 8].astype(F32)
        return part.reshape(count, 128)

    def exact(begin, count):
        if begin >= bases[4]:
            return gfin[begin - bases[4] : begin - bases[4] + count, :]
        return grest[begin - bases[1] : begin - bases[1] + count, :]

    lk[...] = jnp.zeros((AP, WA), F32)
    lk[0:LETTERS, :] = lookup[...]
    wrel[...] = jnp.zeros((RP, WP), F32)
    wrel[0:NREL, :] = w_r[UP : UP + NREL, :]

    def table(begin):
        both = jnp.concatenate([exact(begin, TR), exact(begin + TR, TR)], axis=1)
        return jnp.concatenate([both, jnp.zeros((AP - TR, WA), F32)], axis=0)

    dscore = table(ROWS.score)
    dvalue, dgate, dstart = [table(ROWS.tabs + 2 * TR * place) for place in range(3)]
    mapped = tout[...]
    t_q = mapped[:, 0:WA] * HEAD ** (-0.5)
    t_k = mapped[:, WA : 2 * WA].astype(BF16).astype(F32)
    t_g = jax.nn.sigmoid(mapped[:, 3 * WA :])
    square = head_mask(WA, AP)
    key_block = jnp.where(square, jnp.concatenate([t_k] * HEADS, axis=0), 0.0).astype(BF16)
    dq = mm2(dscore, key_block) * HEAD ** (-0.5)
    dk = jnp.where(square, mm3(dscore, t_q, TN), 0.0)
    dk = jnp.sum(dk.reshape(HEADS, AP, WA), axis=0)
    dg = dgate * (t_g * (1.0 - t_g))
    dmapped = jnp.concatenate([dq, dk, dvalue, dg], axis=1)
    unit0, scale0 = norm(lk[...])
    gain_row = scal[0:WA].reshape(1, WA)
    g_a[...] = mm3(dmapped, unit0 * gain_row, TN)
    dnormed = mm3(dmapped, w_a[0 : 4 * WA, :])
    dgain_row = colsum(dnormed * unit0)
    g_lookup = dstart + norm_back(dnormed * gain_row, unit0, scale0)

    unit_r, scale_r = norm(wrel[...])
    gain_rel = scal[768:896].reshape(1, WP)
    dtable = exact(ROWS.bias, 8)
    g_bias = mm3(dtable, unit_r * gain_rel)
    dnormed = mm3(dtable, w_p[768:776, :], TN)
    dgain_rel = colsum(dnormed * unit_r)
    g_rel[...] = exact(ROWS.rel, 72) + norm_back(
        dnormed * gain_rel, unit_r, scale_r
    )[0:72]

    base = ROWS.small
    g_small[0:WA] = dgain_row.reshape(WA)
    for place, row in ((256, 0), (384, 1), (512, 2), (640, 3), (896, 4), (1024, 5), (1152, 6)):
        g_small[place : place + 128] = exact(base + row, 1).reshape(128)
    g_small[768:896] = dgain_rel.reshape(128)
    lane = iota((1, 128), 1)
    tail = jnp.where(lane < 87, exact(base + 7, 1), 0.0)
    g_small[1280:1408] = tail.reshape(128)

    rel_row = iota((72, 128), 0)
    squares_sum = jnp.zeros((1, 1), F32)
    for begin, count in (
        (ROWS.up, 2 * UP),
        (ROWS.o, 2 * WA),
    ):
        part = big(begin, count)
        squares_sum = squares_sum + total_of(part * part)
    for part in (
        g_a[...],
        g_lookup[0:LETTERS],
        jnp.where(rel_row < NREL, g_rel[...], 0.0),
        g_bias,
        dgain_row,
        exact(ROWS.outer, UP),
        exact(ROWS.tri, 768),
        exact(ROWS.back, 2 * UP),
        exact(base, 7),
        exact(ROWS.eh, 87),
        exact(ROWS.eh + 88, 87),
        exact(ROWS.dist, BINS),
        dgain_rel,
        tail,
    ):
        squares_sum = squares_sum + total_of(part * part)
    size = jnp.sqrt(squares_sum)
    scale = jnp.minimum(1.0, CLIP / size)

    def adam(which, where, grad, factor=scale):
        clipped = grad * factor
        weight = weights[which][where]
        moment = B1 * means[which][where] + (1.0 - B1) * clipped
        second = B2 * squares[which][where] + (1.0 - B2) * clipped * clipped
        level = second * (1.0 / (1.0 - B2**STEP))
        step = (moment * (1.0 / (1.0 - B1**STEP))) / (level * lax.rsqrt(level) + ADAM_EPS)
        new[3 * which][where] = weight - RATE * (step + DECAY * weight)
        new[3 * which + 1][where] = moment
        new[3 * which + 2][where] = second

    every = slice(None)
    stores = []

    def leave(which):
        for place in range(3 * which, 3 * which + 3):
            store = pltpu.make_async_copy(new[place], far[place], store_sem.at[place])
            store.start()
            stores.append(store)

    def ready(which):
        loads[which].wait()
        loads[6 + which].wait()

    ready(2)
    for w in range(2):
        half = slice(128 * w, 128 * w + 128)
        adam(2, (slice(0, WA), half), big(ROWS.o + w * WA, WA))
        adam(2, (slice(WA, WA + UP), half), exact(ROWS.back + w * UP, UP))
    leave(2)
    ready(1)
    adam(1, (slice(0, 4 * WA), every), g_a[...])
    for w in range(2):
        half = slice(128 * w, 128 * w + 128)
        adam(1, (slice(1024, 2048), half), big(ROWS.up + w * UP, UP))
        adam(1, (slice(2048, 2135), half), exact(ROWS.eh + w * 88, 87))
    leave(1)
    ready(3)
    adam(3, (slice(0, UP), every), exact(ROWS.outer, UP))
    adam(3, (slice(UP, UP + NREL), every), g_rel[0:NREL, :])
    leave(3)
    ready(4)
    adam(4, (slice(0, 768), every), exact(ROWS.tri, 768))
    adam(4, (slice(768, 776), every), g_bias)
    adam(4, (slice(776, 840), every), exact(ROWS.dist, BINS))
    leave(4)
    ready(0)
    adam(0, (every, every), g_lookup[0:LETTERS])
    leave(0)
    ready(5)
    adam(5, (slice(0, 1367),), g_small[0:1367], scale.reshape(1))
    leave(5)

    sums = exact(base + 8, 1)
    loss = sums[:, 0:1] / aux[0:1, 0:1] + sums[:, 1:2] * aux[0:1, 1:2]
    loss_out[0] = loss[0, 0]
    size_out[0] = size[0, 0]
    for store in stores:
        store.wait()


def vmem():
    return pl.BlockSpec(memory_space=pltpu.VMEM)


def per_device(rows, cols, *arrays):
    letters, truth, concealed, existing, ordinals, observed, bins = arrays[:7]

    def turned(group):
        return [w.T if place in (1, 4) else w for place, w in enumerate(group)]

    weights, means, squares = turned(arrays[7:13]), turned(arrays[13:19]), turned(arrays[19:25])
    plan = scratch_plan(rows, cols)
    bases = layout(rows, cols)[1]
    far = pl.BlockSpec(memory_space=pltpu.HBM)
    summed = pl.pallas_call(
        functools.partial(main_kernel, rows, cols, tuple(plan)),
        out_shape=(
            jax.ShapeDtypeStruct((bases[1] // 8, 8, 128), BF16),
            jax.ShapeDtypeStruct((bases[4] - bases[1], 128), F32),
            jax.ShapeDtypeStruct((bases[5] - bases[4], 128), F32),
            jax.ShapeDtypeStruct((AP, 4 * WA), F32),
            jax.ShapeDtypeStruct((8, 128), F32),
        ),
        in_specs=[far] * OPERANDS,
        out_specs=tuple([vmem()] * 5),
        scratch_shapes=[pltpu.VMEM(dims, kind) for dims, kind in plan.values()]
        + [
            pltpu.SemaphoreType.DMA((rows - 1,)),
            pltpu.SemaphoreType.DMA((PHASES - 1, rows - 1)),
            pltpu.SemaphoreType.DMA((cols - 1,)),
            pltpu.SemaphoreType.DMA((PHASES, cols - 1)),
            pltpu.SemaphoreType.DMA((3, 2)),
            pltpu.SemaphoreType.DMA((4, 2, max(rows, cols) // 2 - 1)),
            pltpu.SemaphoreType.DMA((4, 2, rows + cols)),
            pltpu.SemaphoreType.DMA((OPERANDS,)),
        ],
        compiler_params=pltpu.CompilerParams(
            collective_id=0, has_side_effects=True, vmem_limit_bytes=MAIN_VMEM
        ),
    )(
        *[
            pltpu.with_memory_space_constraint(value, pltpu.HBM)
            for value in (
                jnp.swapaxes(letters, 1, 2),
                jnp.swapaxes(truth, 1, 2),
                jnp.swapaxes(concealed, 1, 2),
                existing,
                ordinals,
                observed,
                bins,
                *weights,
            )
        ]
    )

    shapes = []
    for w in weights:
        shapes += [jax.ShapeDtypeStruct(w.shape, F32)] * 3
    one = jax.ShapeDtypeStruct((1,), F32)
    scalar = pl.BlockSpec(memory_space=pltpu.SMEM)
    result = pl.pallas_call(
        functools.partial(post_kernel, rows, cols),
        out_shape=tuple(shapes) + (one, one),
        in_specs=[vmem()] * 11 + [far] * 12,
        out_specs=tuple([far] * 18) + (scalar, scalar),
        scratch_shapes=[pltpu.VMEM(shape.shape, F32) for shape in shapes]
        + [pltpu.VMEM(value.shape, F32) for value in (*means, *squares)]
        + [
            pltpu.VMEM((AP, WA), F32),
            pltpu.VMEM((RP, WP), F32),
            pltpu.VMEM((4 * WA, WA), F32),
            pltpu.VMEM((1408,), F32),
            pltpu.VMEM((72, 128), F32),
            pltpu.SemaphoreType.DMA((18,)),
            pltpu.SemaphoreType.DMA((12,)),
        ],
        compiler_params=pltpu.CompilerParams(vmem_limit_bytes=POST_VMEM),
    )(
        *summed,
        *weights,
        *[pltpu.with_memory_space_constraint(value, pltpu.HBM) for value in (*means, *squares)],
    )
    outs = [result[18].reshape(()), result[19].reshape(())]
    for place, value in enumerate(result[:18]):
        outs.append(value.T if place // 3 in (1, 4) else value)
    return tuple(outs)


def solution(mesh):
    rows, cols = mesh.shape[ROW], mesh.shape[COL]
    placed = (
        (P(None, COL, ROW),) * 3 + (P(),) * 3 + (P(None, ROW, COL),) + (P(),) * 18
    )
    return jax.shard_map(
        functools.partial(per_device, rows, cols),
        mesh=mesh,
        in_specs=placed,
        out_specs=(P(),) * 20,
        check_vma=False,
    )
```

```python
import functools
from types import SimpleNamespace

import jax
import jax.numpy as jnp
from jax import lax
from jax.experimental import pallas as pl
from jax.experimental.pallas import tpu as pltpu
from jax.sharding import PartitionSpec as P

F32, BF16 = jnp.float32, jnp.bfloat16
MESH = pl.DeviceIdType.MESH
ROW, COL, QUAD = "row", "col", "quad"
CORE, PLANE, Z = "core", "plane", "z"
WA, WP, WO, LETTERS, BINS, REACH, HEADS, HEAD = 256, 128, 32, 23, 64, 32, 8, 32
UP = 1024
NREL = 2 * REACH + 1
AP = 32
TR = 24
RP = 128
EPS = 1e-05
NB, NS, NI, NJ = 2, 16, 8, 16
NM = NB * NS * NI
NP = 2 * NI * NJ
BS = NB * NS
BI = NB * NI
DS = WO * NS
TOGETHER = 4
CLIP, RATE, B1, B2, STEP, ADAM_EPS, DECAY = 0.02, 0.05, 0.9, 0.999, 4, 1e-08, 0.01

MAIN_VMEM, POST_VMEM = 44 * 2**20, 30 * 2**20

NN = (((1,), (0,)), ((), ()))
NT = (((1,), (1,)), ((), ()))
TN = (((0,), (0,)), ((), ()))

GROUPS = (
    dict(up=2 * UP),
    dict(tri=5 * WP, out=WP, o=2 * WA),
    dict(back=UP),
    dict(back2=UP),
    dict(outer=WO * WO),
    dict(eh=176, tabs=6 * TR, dist=BINS, rel=72, small=16),
    dict(score=2 * TR, bias=8),
)
LAST = len(GROUPS) - 1
LOW_SUM = 2
LOW_SHARE = 4
REST = 5


def layout(rows, cols):
    places, bases, begin = {}, [], 0
    for number, group in enumerate(GROUPS):
        bases.append(begin)
        for name, count in group.items():
            places[name] = begin
            begin += count
        size = 16 * cols if number == LAST else 8 * rows * cols
        begin = bases[-1] - (bases[-1] - begin) // size * size
    return SimpleNamespace(**places), bases + [begin]


def mm(a, b, dims=NN):
    return lax.dot_general(a, b, dims, preferred_element_type=F32)


def split2(x):
    high = x.astype(BF16)
    return high, (x - high.astype(F32)).astype(BF16)


def split3(x):
    high = x.astype(BF16)
    rest = x - high.astype(F32)
    middle = rest.astype(BF16)
    return high, middle, (rest - middle.astype(F32)).astype(BF16)


def mm3(a, b, dims=NN):
    ah, al = split2(a)
    bh, bl = split2(b)
    return mm(ah, bh, dims) + (mm(al, bh, dims) + mm(ah, bl, dims))


def mm6(a, b, dims=NN):
    ah, am, al = split3(a)
    bh, bm, bl = split3(b)
    low = mm(al, bh, dims) + (mm(am, bm, dims) + mm(ah, bl, dims))
    return mm(ah, bh, dims) + ((mm(am, bh, dims) + mm(ah, bm, dims)) + low)


def mm2(a, exact, dims=NN):
    ah, al = split2(a)
    return mm(ah, exact, dims) + mm(al, exact, dims)


def mm2r(exact, b, dims=NN):
    bh, bl = split2(b)
    return mm(exact, bh, dims) + mm(exact, bl, dims)


def mm3r(exact, b, dims=NN):
    bh, bm, bl = split3(b)
    return mm(exact, bh, dims) + (mm(exact, bm, dims) + mm(exact, bl, dims))


def norm(x):
    centred = x - jnp.mean(x, axis=-1, keepdims=True)
    scale = lax.rsqrt(jnp.mean(centred * centred, axis=-1, keepdims=True) + EPS)
    return centred * scale, scale


def norm_back(grad, unit, scale):
    return scale * (
        grad
        - jnp.mean(grad, axis=-1, keepdims=True)
        - unit * jnp.mean(grad * unit, axis=-1, keepdims=True)
    )


def iota(shape, axis):
    return lax.broadcasted_iota(jnp.int32, shape, axis)


def head_mask(rows, per_row):
    shape = (rows, WA)
    return iota(shape, 0) // per_row == iota(shape, 1) // HEAD


def colsum(x):
    return jnp.sum(x, axis=0, keepdims=True)


def total_of(x):
    return jnp.sum(jnp.sum(x, axis=1, keepdims=True), axis=0, keepdims=True)


def scratch_plan(rows, cols):
    length = rows * NI
    bases = layout(rows, cols)[1]
    final = bases[-1] - bases[LAST]
    lines = rows // 2
    return dict(
        lk=((AP, WA), F32),
        weh=((128, WA), F32),
        wbd=((128, WP), F32),
        seqw=((NM, 1), F32),
        lmask=((NM, 1), F32),
        truth=((NM, 1), F32),
        pmask=((NP, 1), F32),
        offset=((NP, 1), F32),
        codes=((BI, length), F32),
        sites=((8, length), F32),
        wrel=((RP, WP), F32),
        tail=((8, 128), F32),
        kb=((WA, WA), BF16),
        vb=((WA, WA), BF16),
        amat=((BS, NI, WA), F32),
        pam=((BS, NI, WA), F32),
        hm=((64, WA), F32),
        letx=((128, length), F32),
        biash=((NB, 64, length), F32),
        prob=((BS, 64, length), F32),
        sg=((NM, WA), F32),
        att=((NM, WA), F32),
        xh1=((NM, WA), F32),
        r1=((NM, 1), F32),
        hid=((NM, UP), F32),
        rep=((NM, WA), F32),
        xh2=((NM, WA), F32),
        r2=((NM, 1), F32),
        dlog=((NM, 128), F32),
        left3=((NB, NI * NS, 128), BF16),
        mhi=((BI, DS, WP), BF16),
        mlo=((BI, DS, WP), BF16),
        rall=((length, DS), BF16),
        prep=((NP, WP), F32),
        xh3=((NP, WP), F32),
        r3=((NP, 1), F32),
        proj=((NP, 5 * WP), F32),
        le=((BI * NJ, WP), F32),
        re=((length * NJ, WP), F32),
        dm=((BI * length, WP), F32),
        gl=((BI, NJ, WP), F32),
        dr=((length, DS), F32),
        dmid=((NM, WA), F32),
        dbias=((NB, 64, length), F32),
        da=((BS, NI, WA), F32),
        dpam=((BS, NI, WA), F32),
        dtab=((BI, 16, RP), F32),
        dn=((NM, WA), F32),
        sum8=((8, WA), F32),
        grad=((bases[-1], 128), F32),
        lets=((8, 128), F32),
        letr=((rows, 8, 128), F32),
        cnts=((8, 128), F32),
        cntr=((cols, 8, 128), F32),
        rs=((NB, NI, DS), BF16),
        rr=((rows, NI, DS), BF16),
        lr=((2, NI * NS, 128), BF16),
        tgr=((2, NI, NJ), jnp.int32),
        os=((cols, BI, NJ, WP), BF16),
        orr=((cols, BI, NJ, WP), BF16),
        er=((rows // 2, BI, NJ, WP), BF16),
        ts=((cols, BI, NJ, WP), BF16),
        tr=((cols, BI, NJ, WP), BF16),
        ds=((BI, NJ, WP), BF16),
        dsr=((cols, BI, NJ, WP), BF16),
        gs=((rows // 2, BI, NJ, WP), BF16),
        gr=((rows // 2, BI, NJ, WP), BF16),
        qs=((BI, NJ, WP), BF16),
        qr=((cols, BI, NJ, WP), BF16),
        us=((rows, NI, DS), BF16),
        ur=((rows, NI, DS), BF16),
        dl=((2, NI * NS, 128), BF16),
        dlr=((NB, NI * NS, 128), BF16),
        arx=((bases[LAST], 128), F32),
        lows=((bases[LOW_SUM] // 8, 8, 128), BF16),
        lowr=((bases[LOW_SUM] // 8, 8, 128), BF16),
        zlow=((lines, bases[LOW_SUM] // 16 // cols, 8, 128), BF16),
        zrest=((lines, (bases[LAST] - bases[REST]) // 2 // cols, 128), F32),
        fc=((cols, final // cols, 128), F32),
        fp=((final // cols, 128), F32),
        fr=((rows, final // cols, 128), F32),
        letters=((NB, NI, NS), jnp.int32),
        truths=((NB, NI, NS), jnp.int32),
        concealed=((NB, NI, NS), jnp.int32),
        existing=((NB, cols * NS), jnp.int32),
        ordinals=((NB, length), jnp.int32),
        observed=((NB, length), jnp.int32),
        targets=((NB, NI, NJ), jnp.int32),
        lookup=((LETTERS, WA), F32),
        w_a=((2135, WA), F32),
        w_c=((WA + UP, WA), F32),
        w_r=((UP + NREL, WP), F32),
        w_p=((840, WP), F32),
        scal=((1367,), F32),
    )


OPERANDS = 13


LET, RIGHT, EDGE, GEDGE, GRIGHT, SUM_ROW = range(6)
CNT, OUTER, TRI, GMIX, GOUTER, SUM_COL, SHARE_COL = range(7)
PHASES = 7


def main_kernel(rows, cols, names, *refs):
    operands = refs[:OPERANDS]
    gbig, grest, gfin, tout, aux = refs[OPERANDS : OPERANDS + 5]
    s = SimpleNamespace(**dict(zip(names, refs[OPERANDS + 5 : -8])))
    row_send, row_recv, col_send, col_recv, pair_sem, sum_send, sum_recv, load_sem = refs[-8:]
    held = refs[OPERANDS + 5 : -8][-OPERANDS:]
    loads = [
        pltpu.make_async_copy(far, near, load_sem.at[place])
        for place, (far, near) in enumerate(zip(operands, held))
    ]
    for load in loads:
        load.start()
    letters, truths, hidden_sites, existing, ordinals, observed, targets = held[:7]
    lookup, w_a, w_c, w_r, w_p, scal = held[7:]
    ROWS, bases = layout(rows, cols)
    length = rows * NI
    me_r, me_c = lax.axis_index(ROW), lax.axis_index(COL)

    barrier = pltpu.get_barrier_semaphore()
    for step in range(1, rows):
        pl.semaphore_signal(
            barrier,
            inc=1,
            device_id={ROW: lax.rem(me_r + step, rows), COL: me_c},
            device_id_type=MESH,
        )
    for step in range(1, cols):
        pl.semaphore_signal(
            barrier,
            inc=1,
            device_id={ROW: me_r, COL: lax.rem(me_c + step, cols)},
            device_id_type=MESH,
        )
    quads = rows // 2
    side, quad = me_r // quads, me_r % quads

    def to_partner(number, source, target):
        return pltpu.make_async_remote_copy(
            src_ref=source,
            dst_ref=target,
            send_sem=pair_sem.at[number, 0],
            recv_sem=pair_sem.at[number, 1],
            device_id={ROW: (1 - side) * quads + quad, COL: me_c},
            device_id_type=MESH,
        )

    def swap(number, source, target):
        out = to_partner(number, source.at[1 - side], target.at[side])
        out.start()
        return out, to_partner(number, source.at[1 - side], target.at[1 - side])

    def exchange(along, phase, source, target):
        if along == ROW:
            count, me, number = rows, me_r, phase
            send, recv = row_send, row_recv
        elif along == QUAD:
            count, me, number = quads, quad, phase
            send, recv = row_send, row_recv
        else:
            count, me, number = cols, me_c, phase
            send, recv = col_send, col_recv
        copies = []
        for step in range(1, count):
            peer = lax.rem(me + step, count)
            origin = lax.rem(me + (count - step), count)
            where = {ROW: me_r, COL: peer}
            if along == ROW:
                where = {ROW: peer, COL: me_c}
            elif along == QUAD:
                where = {ROW: side * quads + peer, COL: me_c}
            out = pltpu.make_async_remote_copy(
                src_ref=source(peer),
                dst_ref=target(me),
                send_sem=send.at[step - 1],
                recv_sem=recv.at[number, step - 1],
                device_id=where,
                device_id_type=MESH,
            )
            out.start()
            arriving = pltpu.make_async_remote_copy(
                src_ref=source(peer),
                dst_ref=target(origin),
                send_sem=send.at[step - 1],
                recv_sem=recv.at[number, step - 1],
                device_id=where,
                device_id_type=MESH,
            )
            copies.append((out, arriving))
        return copies

    def finish(copies):
        for out, arriving in copies:
            out.wait_send()
            arriving.wait_recv()

    for load in loads[:7]:
        load.wait()
    here = existing[...].astype(F32)
    sites = observed[...].astype(F32)
    numbers = ordinals[...].astype(F32)

    def by_protein(values, count, each):
        wide = (count, values.shape[1])
        return jnp.where(iota(wide, 0) // each == 0, values[0:1], values[1:2])

    def at_lane(values, lanes):
        return jnp.sum(jnp.where(iota(values.shape, 1) == lanes, values, 0.0), axis=1, keepdims=True)

    row_m, row_p = iota((NM, 1), 0), iota((NP, 1), 0)
    seq_m, res_m = (row_m // NI) % NS, row_m % NI
    spread_m = jnp.where(
        iota((NM, BI), 1) == (iota((NM, BI), 0) // (NI * NS)) * NI + iota((NM, BI), 0) % NI, 1.0, 0.0
    ).astype(BF16)

    def column_m(values):
        wide = mm(spread_m, values[...].reshape(BI, NS).astype(F32).astype(BF16))
        return at_lane(wide, seq_m)

    seq_weight = at_lane(by_protein(here, NM, NI * NS), me_c * NS + seq_m)
    letter = column_m(letters)
    loss_mask = column_m(hidden_sites) * seq_weight
    s.seqw[...] = seq_weight
    s.lmask[...] = loss_mask
    s.truth[...] = column_m(truths)
    s.tgr[side] = targets[side]

    s.lets[...] = jnp.where(
        (iota((NI, 128), 0) == 0) & (iota((NI, 128), 1) == BS), total_of(loss_mask), 0.0
    )
    for b in range(NB):
        s.lets[:, b * NS : (b + 1) * NS] = letters[b].astype(F32)
    s.letr[me_r] = s.lets[...]
    near = row_p // NJ
    first = (quad + quads * (near // NI)) * NI + near % NI
    second = me_c * NJ + row_p % NJ

    def of_side(values):
        return jnp.where(side == 0, values[0:1], values[1:2])

    sites_p = jnp.broadcast_to(of_side(sites), (NP, length))
    numbers_p = jnp.broadcast_to(of_side(numbers), (NP, length))
    s.pmask[...] = at_lane(sites_p, first) * at_lane(sites_p, second)
    s.offset[...] = (
        jnp.clip(at_lane(numbers_p, first) - at_lane(numbers_p, second), -REACH, REACH) + REACH
    )
    numbers_b = by_protein(numbers, BI, NI)
    own = at_lane(numbers_b, me_r * NI + iota((BI, 1), 0) % NI)
    s.codes[...] = jnp.clip(own - numbers_b, -REACH, REACH) + REACH
    s.sites[...] = jnp.zeros((8, length), F32)
    s.sites[0:NB, :] = sites
    inv_all = 1.0 / (jnp.sum(here, axis=1, keepdims=True) + 1.0)
    inv_count = of_side(inv_all)
    per_protein = jnp.sum(sites, axis=1, keepdims=True)
    inv_dist = 1.0 / jnp.maximum(colsum(per_protein * per_protein), 1.0)

    for load in loads[7:]:
        load.wait()

    def gain(begin, width):
        return scal[begin : begin + width].reshape(1, width)

    gain_row, gain_trans, gain_outer = gain(0, WA), gain(256, WA), gain(512, WA)
    gain_rel, gain_pair, gain_mixed = gain(768, WP), gain(896, WP), gain(1024, WP)
    bias_outer = gain(1152, WP)
    s.lk[...] = jnp.zeros((AP, WA), F32)
    s.lk[0:LETTERS, :] = lookup[...]
    s.weh[...] = jnp.zeros((128, WA), F32)
    s.weh[0:87, :] = w_a[2048:2135, :]
    s.wbd[...] = jnp.zeros((128, WP), F32)
    s.wbd[0:72, :] = w_p[768:840, :]
    s.wrel[...] = jnp.zeros((RP, WP), F32)
    s.wrel[0:NREL, :] = w_r[UP : UP + NREL, :]
    s.tail[...] = jnp.zeros((8, 128), F32)
    s.tail[0:1, 0:87] = scal[1280:1367].reshape(1, 87)

    table = s.lk[...]
    unit0, _ = norm(table)
    mapped = mm6(unit0 * gain_row, w_a[0 : 4 * WA, :], NT)
    tout[...] = mapped
    pl.semaphore_wait(barrier, rows + cols - 2)
    flight = exchange(ROW, LET, lambda p: s.lets, lambda p: s.letr.at[p])
    flight.append(swap(0, targets, s.tgr))
    t_q = mapped[:, 0:WA] * HEAD ** (-0.5)
    t_k = mapped[:, WA : 2 * WA].astype(BF16).astype(F32)
    t_v = mapped[:, 2 * WA : 3 * WA].astype(BF16).astype(F32)
    t_g = jax.nn.sigmoid(mapped[:, 3 * WA :])
    square = head_mask(WA, AP)
    key_block = jnp.where(square, jnp.concatenate([t_k] * HEADS, axis=0), 0.0).astype(BF16)
    s.vb[...] = jnp.where(square, jnp.concatenate([t_v] * HEADS, axis=0), 0.0).astype(BF16)
    stacked = mm(jnp.concatenate(split3(t_q), axis=0), key_block, NT)
    score_table = stacked[0:AP] + (stacked[AP : 2 * AP] + stacked[2 * AP :])
    s.hm[...] = jnp.where(head_mask(64, NI), 1.0, 0.0)

    letter = letter.astype(jnp.int32)
    triple = jnp.where(
        (iota((NM, 3 * AP), 1) % AP) == letter, 1.0, 0.0
    ).astype(BF16)

    def chosen(values):
        return mm(triple, jnp.concatenate(split3(values), axis=0))

    s.amat[...] = chosen(score_table).reshape(BS, NI, WA)
    start = chosen(table)
    s.sg[...] = chosen(t_g)

    unit_r, _ = norm(s.wrel[...])
    bias_table = mm3(s.wbd[0:8, :], unit_r * gain_rel, NT)
    bias_parts = jnp.concatenate(split3(bias_table), axis=0)

    def codes(index):
        return jnp.where(
            iota((RP, length), 0) == s.codes[index : index + 1, :].astype(jnp.int32), 1.0, 0.0
        ).astype(BF16)

    for b in range(NB):
        for i in range(NI):
            part = mm(bias_parts, codes(b * NI + i))
            part = part[0:8] + (part[8:16] + part[16:24])
            for h in range(HEADS):
                s.biash[b, h * NI + i : h * NI + i + 1, :] = part[h : h + 1, :]

    finish(flight)
    letters_all = s.letr[...].reshape(length, 128).T
    s.letx[...] = letters_all
    s.cnts[...] = jnp.broadcast_to(
        jnp.sum(letters_all[BS : BS + 1, :], axis=1, keepdims=True), (8, 128)
    )
    s.cntr[me_c] = s.cnts[...]
    count_flight = exchange(COL, CNT, lambda p: s.cnts, lambda p: s.cntr.at[p])

    def letter_codes(bs):
        row = s.letx[pl.ds(bs, 1), :].astype(jnp.int32)
        one = jnp.where(iota((AP, length), 0) == row, 1.0, 0.0)
        return jnp.concatenate([one] * HEADS, axis=0).astype(BF16)

    def spread(value):
        wide = jnp.broadcast_to(value[None], (HEADS, NI, WA)).reshape(64, WA)
        return wide * s.hm[...]

    def gather_heads(value):
        return jnp.sum((value * s.hm[...]).reshape(HEADS, NI, WA), axis=0)

    for b in range(NB):
        key_mask = s.sites[b : b + 1, :]

        @pl.loop(0, NS // TOGETHER)
        def _(q):
            for part in range(TOGETHER):
                bs = b * NS + q * TOGETHER + part
                code = letter_codes(bs)
                wide = [spread(p.astype(F32)).astype(BF16) for p in split2(s.amat[bs])]
                raw = mm(jnp.concatenate(wide, axis=0), code)
                scores = (raw[0:64] + raw[64:128]) + s.biash[b]
                scores = jnp.where(key_mask > 0, scores, -1000000000.0)
                power = jnp.exp(scores - jnp.max(scores, axis=-1, keepdims=True))
                weight = power / jnp.sum(power, axis=-1, keepdims=True)
                s.prob[bs] = weight
                picked = mm(jnp.concatenate(split2(weight), axis=0), code, NT)
                s.pam[bs] = gather_heads(picked[0:64] + picked[64:128])

    att = mm2(s.pam[...].reshape(NM, WA), s.vb[...])
    s.att[...] = att
    mid = start + mm3(s.sg[...] * att, w_c[0:WA, :])
    unit1, scale1 = norm(mid)
    s.xh1[...] = unit1
    s.r1[...] = scale1
    hidden = jnp.maximum(mm3(unit1 * gain_trans, w_a[4 * WA : 4 * WA + UP, :], NT), 0.0)
    s.hid[...] = hidden
    rep = mid + mm3(hidden, w_c[WA:, :])
    s.rep[...] = rep
    unit2, scale2 = norm(rep)
    s.xh2[...] = unit2
    s.r2[...] = scale2
    seq_weight = s.seqw[...]
    lane = iota((NM, 128), 1)
    edges = mm3(unit2 * gain_outer, s.weh[...], NT) * seq_weight

    right = jnp.where((lane >= 32) & (lane < 64), edges, 0.0).astype(BF16)
    spot = iota((128, DS), 0)
    repeat = jnp.where(spot - 32 == iota((128, DS), 1) // NS, 1.0, 0.0)
    repeat = jnp.where((spot >= 32) & (spot < 64), repeat, 0.0).astype(BF16)
    wide = mm(right, repeat)
    own_seq = (iota((NM, DS), 0) // NI) % NS == iota((NM, DS), 1) % NS
    wide = jnp.sum(jnp.where(own_seq, wide, 0.0).reshape(NB, NS, NI, DS), axis=1)
    s.rs[...] = wide.astype(BF16)
    s.rr[me_r] = s.rs[side]
    flight = exchange(ROW, RIGHT, lambda p: s.rs.at[p // quads], lambda p: s.rr.at[p])

    order_to = (iota((NM, NM), 0) // (NI * NS) == iota((NM, NM), 1) // (NI * NS)) & (
        (iota((NM, NM), 0) // NS) % NI == iota((NM, NM), 1) % NI
    )
    order_to = order_to & (iota((NM, NM), 0) % NS == (iota((NM, NM), 1) // NI) % NS)
    order = jnp.where(order_to, 1.0, 0.0).astype(BF16)
    left = mm3r(order, jnp.where(lane < 32, edges, 0.0))
    high, low = split2(left)
    high32, low32 = high.astype(F32), low.astype(F32)
    left3 = high32 + pltpu.roll(low32, 32, 1) + pltpu.roll(high32, 64, 1)
    s.left3[...] = left3.astype(BF16).reshape(NB, NI * NS, 128)
    s.lr[side] = s.left3[side]
    flight.append(swap(1, s.left3, s.lr))

    finish(count_flight)
    masked = jnp.maximum(jnp.sum(s.cntr[...], axis=0)[0:1, 0:1], 1.0)
    logits = mm3(rep, s.weh[...], NT) + s.tail[0:1, :]
    valid = (lane >= 64) & (lane < 64 + LETTERS)
    top = jnp.max(jnp.where(valid, logits, -3e38), axis=-1, keepdims=True)
    power = jnp.where(valid, jnp.exp(jnp.where(valid, logits, top) - top), 0.0)
    whole = jnp.sum(power, axis=-1, keepdims=True)
    truth = lane - 64 == s.truth[...].astype(jnp.int32)
    truth = truth & valid
    picked = jnp.sum(jnp.where(truth, logits, 0.0), axis=-1, keepdims=True)
    loss_mask = s.lmask[...]
    msa_sum = colsum((jnp.log(whole) + top - picked) * loss_mask)
    s.dlog[...] = (power / whole - jnp.where(truth, 1.0, 0.0)) * (loss_mask / masked)

    def outer_weight(d):
        return w_r[pl.ds(d, WO, stride=WO), :]

    def expand(block):
        for pair in range(WO // 2):
            both = jnp.concatenate([outer_weight(2 * pair), outer_weight(2 * pair + 1)], axis=1)
            wh, wl = split2(both)
            made = mm(s.lr[block][:, 0:96], jnp.concatenate([wh, wh, wl], axis=0))
            for half in range(2):
                d = 2 * pair + half
                mh, ml = split2(made[:, half * WP : (half + 1) * WP].reshape(NI, NS, WP))
                s.mhi[pl.ds(block * NI, NI), d * NS : (d + 1) * NS, :] = mh
                s.mlo[pl.ds(block * NI, NI), d * NS : (d + 1) * NS, :] = ml

    expand(side)
    finish(flight)
    expand(1 - side)
    s.rall[...] = s.rr[...].astype(F32).reshape(length, DS).astype(BF16)

    @pl.loop(0, BI)
    def _(i):
        block = mm(s.rall[...], s.mhi[i]) + mm(s.rall[...], s.mlo[i])
        block = block * inv_count
        for c in range(cols):
            s.os[c, i] = block[c * NJ : (c + 1) * NJ].astype(BF16)

    s.orr[me_c] = s.os[me_c]
    finish(exchange(COL, OUTER, lambda p: s.os.at[p], lambda p: s.orr.at[p]))

    pair_lane = iota((NP, 128), 1)
    offset = s.offset[...].astype(jnp.int32)
    pair_codes = jnp.where(pair_lane == offset, 1.0, 0.0).astype(BF16)
    outer = s.orr[0].astype(F32)
    for c in range(1, cols):
        outer = outer + s.orr[c].astype(F32)
    pair_rep = (mm3r(pair_codes, s.wrel[...]) + outer.reshape(NP, WP)) + bias_outer
    s.prep[...] = pair_rep
    unit3, scale3 = norm(pair_rep)
    s.xh3[...] = unit3
    s.r3[...] = scale3
    proj = mm3(unit3 * gain_pair, w_p[0 : 5 * WP, :], NT)
    pair_mask = s.pmask[...]
    sig1 = jax.nn.sigmoid(proj[:, WP : 2 * WP])
    sig2 = jax.nn.sigmoid(proj[:, 3 * WP : 4 * WP])
    sig3 = jax.nn.sigmoid(proj[:, 4 * WP :])
    s.proj[:, 0 : WP] = proj[:, 0:WP]
    s.proj[:, WP : 2 * WP] = sig1
    s.proj[:, 2 * WP : 3 * WP] = proj[:, 2 * WP : 3 * WP]
    s.proj[:, 3 * WP : 4 * WP] = sig2
    s.proj[:, 4 * WP :] = sig3
    s.le[...] = sig1 * proj[:, 0:WP] * pair_mask
    right_edge = (sig2 * proj[:, 2 * WP : 3 * WP] * pair_mask).astype(BF16)
    s.er[quad] = right_edge.reshape(BI, NJ, WP)
    finish(exchange(QUAD, EDGE, lambda p: s.er.at[quad], lambda p: s.er.at[p]))
    for q in range(quads):
        for block in range(2):
            begin = (q + quads * block) * NI * NJ
            s.re[begin : begin + NI * NJ, :] = (
                s.er[q, block * NI : (block + 1) * NI].astype(F32).reshape(NI * NJ, WP)
            )

    @pl.loop(0, BI)
    def _(i):
        for c in range(cols):
            block = jnp.zeros((NJ, WP), F32)
            for k in range(NJ):
                other = s.re[pl.ds(c * NJ * NJ + k, NJ, stride=NJ), :]
                block = block + s.le[pl.ds(i * NJ + k, 1), :] * other
            s.ts[c, i] = block.astype(BF16)

    s.tr[me_c] = s.ts[me_c]
    finish(exchange(COL, TRI, lambda p: s.ts.at[p], lambda p: s.tr.at[p]))

    mixed = s.tr[0].astype(F32)
    for c in range(1, cols):
        mixed = mixed + s.tr[c].astype(F32)
    unit4, scale4 = norm(mixed.reshape(NP, WP))
    w_out = w_p[5 * WP : 6 * WP, :]
    moved = mm3(unit4 * gain_mixed, w_out, NT)
    sig3 = s.proj[:, 4 * WP :]
    pair_out = s.prep[...] + sig3 * moved
    bins = mm3(pair_out, s.wbd[...], NT) + pltpu.roll(
        jnp.where(iota((8, 128), 1) < BINS, s.tail[...], 0.0), 8, 1
    )[0:1]
    valid = (pair_lane >= 8) & (pair_lane < 8 + BINS)
    top = jnp.max(jnp.where(valid, bins, -3e38), axis=-1, keepdims=True)
    power = jnp.where(valid, jnp.exp(jnp.where(valid, bins, top) - top), 0.0)
    whole = jnp.sum(power, axis=-1, keepdims=True)
    spread_p = jnp.where(iota((NP, BI), 1) == iota((NP, BI), 0) // NJ, 1.0, 0.0).astype(BF16)
    target = at_lane(
        mm(spread_p, s.tgr[...].reshape(BI, NJ).astype(F32).astype(BF16)), row_p % NJ
    )
    truth = (pair_lane - 8 == target.astype(jnp.int32)) & valid
    picked = jnp.sum(jnp.where(truth, bins, 0.0), axis=-1, keepdims=True)
    dist_sum = colsum((jnp.log(whole) + top - picked) * pair_mask)
    dbins = (power / whole - jnp.where(truth, 1.0, 0.0)) * (pair_mask * inv_dist)

    def put(place, value, skip=0):
        base = place + skip
        height, width = value.shape
        for w in range(width // 128):
            s.grad[base + w * height : base + (w + 1) * height, :] = value[
                :, w * 128 : (w + 1) * 128
            ]

    planes, lines = cols, rows // 2
    sizes = {CORE: 2, PLANE: planes, Z: lines}
    places = {CORE: me_c % 2, PLANE: me_c // 2 * 2 + me_r % 2, Z: me_r // 2}

    def line_peer(axis, place):
        if axis == CORE:
            return {ROW: me_r, COL: me_c // 2 * 2 + place}
        if axis == PLANE:
            return {ROW: me_r // 2 * 2 + place % 2, COL: place // 2 * 2 + me_c % 2}
        return {ROW: place * 2 + me_r % 2, COL: me_c}

    def rows_at(unit, count):
        return pl.ds(pl.multiple_of(unit * 8, 8), count * 8)

    class Sum:
        def __init__(self, number):
            self.number = number
            self.begin = bases[number] // 8
            self.at, self.size = self.begin, (bases[number + 1] - bases[number]) // 8
            self.rx = self.begin
            self.low_sum, self.low_share = number < LOW_SUM, number < LOW_SHARE
            self.once = self.low_sum or number == REST
            down = [(self.reduce, CORE), (self.reduce, PLANE)]
            along = [(self.all_to_all, Z)] if self.once else [(self.reduce, Z), (self.share, Z)]
            self.stages = down + along + [(self.share, PLANE), (self.share, CORE)]
            self.flight, self.after, self.used, self.stored = [], None, 0, False

        @property
        def done(self):
            return not self.stages and self.after is None

        def copies(self, axis, source, target):
            count = sizes[axis]
            for step in range(1, count):
                peer = lax.rem(places[axis] + step, count)
                origin = lax.rem(places[axis] + (count - step), count)
                both = []
                for end in (target(places[axis], step), target(origin, step)):
                    both.append(
                        pltpu.make_async_remote_copy(
                            src_ref=source(peer, step),
                            dst_ref=end,
                            send_sem=sum_send.at[self.number, step - 1],
                            recv_sem=sum_recv.at[self.number, self.used],
                            device_id=line_peer(axis, peer),
                            device_id_type=MESH,
                        )
                    )
                self.used += 1
                both[0].start()
                self.flight.append(both)

        def advance(self):
            finish(self.flight)
            self.flight = []
            if self.after is not None:
                self.after()
                self.after = None
            if self.stages:
                stage, axis = self.stages.pop(0)
                stage(axis)

        def reduce(self, axis):
            count = sizes[axis]
            small = self.size // count
            rx = self.rx

            def slot(buffer, step):
                if self.low_sum:
                    return buffer.at[pl.ds(rx + (step - 1) * small, small)]
                return buffer.at[pl.ds((rx + (step - 1) * small) * 8, small * 8)]

            if self.low_sum:
                for step in range(1, count):
                    peer = lax.rem(places[axis] + step, count)
                    value = s.grad[rows_at(self.at + peer * small, small), :]
                    slot(s.lows, step)[...] = value.reshape(small, 8, 128).astype(BF16)

            def source(peer, step):
                if self.low_sum:
                    return slot(s.lows, step)
                return s.grad.at[rows_at(self.at + peer * small, small)]

            near = s.lowr if self.low_sum else s.arx
            self.copies(axis, source, lambda place, step: slot(near, step))

            def add():
                self.at = self.at + places[axis] * small
                self.size = small
                mine = rows_at(self.at, small)
                value = s.grad[mine, :]
                for step in range(1, count):
                    other = slot(near, step)[...].astype(F32)
                    value = value + other.reshape(small * 8, 128)
                s.grad[mine, :] = value

            self.after = add
            self.rx = rx + (count - 1) * small

        def all_to_all(self, axis):
            mine = rows_at(self.at, self.size)
            if self.low_sum:
                part = pl.ds(self.begin // (2 * planes), self.size)
                value = s.grad[mine, :].reshape(self.size, 8, 128)
                s.zlow[places[axis], part] = value.astype(BF16)

                def slot(place, step=0):
                    return s.zlow.at[place, part]
            else:
                s.zrest[places[axis]] = s.grad[mine, :]

                def slot(place, step=0):
                    return s.zrest.at[place]

            self.copies(axis, lambda peer, step: slot(places[axis]), slot)

            def add():
                value = slot(0)[...].astype(F32)
                for place in range(1, sizes[axis]):
                    value = value + slot(place)[...].astype(F32)
                s.grad[mine, :] = value.reshape(self.size * 8, 128)

            self.after = add

        def spot(self, at, size):
            if self.low_share:
                return gbig.at[pl.ds(at, size)]
            return grest.at[rows_at(at - bases[LOW_SHARE] // 8, size)]

        def share(self, axis):
            if not self.stored:
                self.stored = True
                value = s.grad[rows_at(self.at, self.size), :]
                if self.low_share:
                    value = value.reshape(self.size, 8, 128).astype(BF16)
                self.spot(self.at, self.size)[...] = value
            size = self.size
            first = self.at - places[axis] * size
            self.copies(
                axis,
                lambda peer, step: self.spot(first + places[axis] * size, size),
                lambda place, step: self.spot(first + place * size, size),
            )
            self.at, self.size = first, size * sizes[axis]

    up, thin, back, back2, early, rest = [Sum(number) for number in range(LAST)]

    def column_products(name, place):
        s.sum8[...] = jnp.zeros((8, WA), F32)

        @pl.loop(0, NM // 32)
        def _(q):
            some = pl.ds(pl.multiple_of(q * 32, 32), 32)
            product = s.dn[some, :] * name[some, :]
            s.sum8[...] += jnp.sum(product.reshape(4, 8, WA), axis=0)

        whole = colsum(s.sum8[...])
        for half in range(2):
            s.grad[small + place + half : small + place + half + 1, :] = whole[
                :, 128 * half : 128 * half + 128
            ]

    for begin, end in (
        (ROWS.o + 2 * WA, bases[2]),
        (ROWS.small, bases[LAST]),
        (ROWS.bias, bases[-1]),
    ):
        if end > begin:
            s.grad[begin:end, :] = jnp.zeros((end - begin, 128), F32)
    small = ROWS.small
    put(ROWS.dist, mm3(dbins, pair_out, TN)[8 : 8 + BINS])
    dbias_dist = pltpu.roll(jnp.broadcast_to(colsum(dbins), (8, 128)), 120, 1)[0:1]
    dout = mm3(dbins, s.wbd[...])
    dgate = dout * moved * (sig3 * (1.0 - sig3))
    dmoved = dout * sig3
    put(ROWS.out, mm3(dmoved, unit4 * gain_mixed, TN))
    dnormed = mm3(dmoved, w_out)
    s.grad[small + 5 : small + 6, :] = colsum(dnormed * unit4)
    dmixed = norm_back(dnormed * gain_mixed, unit4, scale4)
    s.ds[...] = dmixed.astype(BF16).reshape(BI, NJ, WP)
    s.dsr[me_c] = s.ds[...]
    finish(exchange(COL, GMIX, lambda p: s.ds, lambda p: s.dsr.at[p]))
    for bi in range(BI):
        for c in range(cols):
            begin = bi * length + c * NJ
            s.dm[begin : begin + NJ, :] = s.dsr[c, bi].astype(F32)

    @pl.loop(0, quads)
    def _(q):
        for place in range(BI):
            j = (q + quads * (place // NI)) * NI + place % NI
            block = jnp.zeros((NJ, WP), F32)
            for i in range(BI):
                block = block + (
                    s.dm[pl.ds(i * length + j, 1), :] * s.le[i * NJ : (i + 1) * NJ, :]
                )
            s.gs[q, place] = block.astype(BF16)

    s.gr[quad] = s.gs[quad]
    flight = exchange(QUAD, GEDGE, lambda p: s.gs.at[p], lambda p: s.gr.at[p])

    @pl.loop(0, BI)
    def _(i):
        block = jnp.zeros((NJ, WP), F32)
        for j in range(length):
            block = block + (
                s.dm[pl.ds(i * length + j, 1), :] * s.re[j * NJ : (j + 1) * NJ, :]
            )
        s.gl[i] = block

    finish(flight)
    dright = s.gr[0].astype(F32)
    for q in range(1, quads):
        dright = dright + s.gr[q].astype(F32)
    dright = dright.reshape(NP, WP) * pair_mask
    dleft = s.gl[...].reshape(NP, WP) * pair_mask
    p1, sig1 = s.proj[:, 0:WP], s.proj[:, WP : 2 * WP]
    p2, sig2 = s.proj[:, 2 * WP : 3 * WP], s.proj[:, 3 * WP : 4 * WP]
    dproj = jnp.concatenate(
        [
            dleft * sig1,
            dleft * p1 * (sig1 * (1.0 - sig1)),
            dright * sig2,
            dright * p2 * (sig2 * (1.0 - sig2)),
            dgate,
        ],
        axis=1,
    )
    unit3 = s.xh3[...]
    put(ROWS.tri, mm3(dproj, unit3 * gain_pair, TN))
    dnormed = mm3(dproj, w_p[0 : 5 * WP, :])
    s.grad[small + 4 : small + 5, :] = colsum(dnormed * unit3)
    drep = dout + norm_back(dnormed * gain_pair, unit3, s.r3[...])
    s.grad[small + 6 : small + 7, :] = colsum(drep)
    s.grad[ROWS.rel : ROWS.rel + 72, :] = mm2r(pair_codes, drep, TN)[0:72]
    s.qs[...] = drep.astype(BF16).reshape(BI, NJ, WP)
    s.qr[me_c] = s.qs[...]
    finish(exchange(COL, GOUTER, lambda p: s.qs, lambda p: s.qr.at[p]))

    turned = s.rall[...].astype(F32).T.astype(BF16)
    s.dr[...] = jnp.zeros((length, DS), F32)

    @pl.loop(0, BI)
    def _(i):
        block = jnp.concatenate([s.qr[c, i] for c in range(cols)], axis=0)
        s.dr[...] += mm(block, s.mhi[i], NT) + mm(block, s.mlo[i], NT)
        mh, ml = split2(mm(turned, block) * inv_count)
        s.mhi[i] = mh
        s.mlo[i] = ml

    for r in range(rows):
        s.us[r] = (s.dr[r * NI : (r + 1) * NI, :] * inv_count).astype(BF16)
    s.ur[me_r] = s.us[me_r]
    flight = exchange(ROW, GRIGHT, lambda p: s.us.at[p], lambda p: s.ur.at[p])

    def pair_weight(pair):
        return split2(
            jnp.concatenate([outer_weight(2 * pair), outer_weight(2 * pair + 1)], axis=1)
        )

    def pair_of(ref, pair):
        return jnp.concatenate(
            [
                ref[:, d * NS : (d + 1) * NS, :].reshape(NM, WP)
                for d in (2 * pair, 2 * pair + 1)
            ],
            axis=1,
        )

    dleft = jnp.zeros((NM, WO), F32)
    for pair in range(WO // 2):
        wh, wl = pair_weight(pair)
        mh, ml = pair_of(s.mhi, pair), pair_of(s.mlo, pair)
        dleft = dleft + (mm(mh, wh, NT) + (mm(ml, wh, NT) + mm(mh, wl, NT)))
    high, low = split2(jnp.concatenate([dleft, jnp.zeros((NM, 96), F32)], axis=1))
    both = high.astype(F32) + pltpu.roll(low.astype(F32), 32, 1)
    s.dl[...] = both.astype(BF16).reshape(2, NI * NS, 128)
    s.dlr[side] = s.dl[side]
    flight.append(swap(2, s.dl, s.dlr))
    left3 = s.lr[...].astype(F32).reshape(NM, 128).T.astype(BF16)
    left_both, left_high = left3[0:64], left3[0:32]
    for pair in range(WO // 2):
        mh, ml = pair_of(s.mhi, pair), pair_of(s.mlo, pair)
        made = mm(left_both, mh)
        made = made[0:32] + made[32:64] + mm(left_high, ml)
        for half in range(2):
            s.grad[pl.ds(ROWS.outer + 2 * pair + half, WO, stride=WO), :] = made[
                :, half * WP : (half + 1) * WP
            ]
    early.advance()

    finish(flight)
    both = s.dlr[...].astype(F32).reshape(NM, 128)
    both = jnp.where(lane < 32, both + pltpu.roll(both, 96, 1), 0.0)
    dleft = mm3r(order, both, TN)
    dright = []
    for b in range(NB):
        some = s.ur[b * quads].astype(F32)
        for q in range(1, quads):
            some = some + s.ur[b * quads + q].astype(F32)
        dright.append(some)
    dright = jnp.stack(dright)
    wide = jnp.broadcast_to(dright[:, None], (NB, NS, NI, DS)).reshape(NM, DS)
    dedges = mm2(jnp.where(own_seq, wide, 0.0), repeat, NT)
    dedges = (dedges + dleft) * seq_weight
    unit2, rep = s.xh2[...], s.rep[...]
    dlog = s.dlog[...]
    put(ROWS.eh, (mm3(dedges, unit2 * gain_outer, TN) + mm3(dlog, rep, TN))[0:88])
    s.dn[...] = mm3(dedges, s.weh[...])
    dnormed = s.dn[...]
    column_products(s.xh2, 2)
    drep = mm3(dlog, s.weh[...]) + norm_back(dnormed * gain_outer, unit2, s.r2[...])
    early.advance()
    hidden = s.hid[...]
    dhidden = jnp.where(hidden > 0, mm3(drep, w_c[WA:, :], NT), 0.0)
    unit1 = s.xh1[...]
    put(ROWS.up, mm3(dhidden, unit1 * gain_trans, TN))
    up.advance()
    put(ROWS.back, mm3(hidden, drep, TN))
    back.advance()
    back2.advance()
    up.advance()
    s.dn[...] = mm3(dhidden, w_a[4 * WA : 4 * WA + UP, :])
    dnormed = s.dn[...]
    column_products(s.xh1, 0)
    dmid = drep + norm_back(dnormed * gain_trans, unit1, s.r1[...])
    sg, att = s.sg[...], s.att[...]
    put(ROWS.o, mm3(sg * att, dmid, TN))
    dgated = mm3(dmid, w_c[0:WA, :], NT)
    thin.advance()
    back.advance()
    back2.advance()
    single = triple[:, 0:AP]
    put(ROWS.tabs, mm2r(single, dmid, TN)[0:TR], 4 * TR)
    put(ROWS.tabs, mm2r(single, dgated * att, TN)[0:TR], 2 * TR)
    datt = dgated * sg

    pam = s.pam[...].reshape(NM, WA)
    blocks = jnp.where(head_mask(WA, AP), mm3(pam, datt, TN), 0.0)
    put(ROWS.tabs, jnp.sum(blocks.reshape(HEADS, AP, WA), axis=0)[0:TR])
    lane1 = iota((1, 128), 1)
    s.grad[small + 7 : small + 8, :] = jnp.where(lane1 < BINS, dbias_dist, colsum(dlog))
    s.grad[small + 8 : small + 9, :] = jnp.where(
        lane1 == 0, msa_sum, jnp.where(lane1 == 1, dist_sum, 0.0)
    )
    rest.advance()
    thin.advance()
    early.advance()
    s.dpam[...] = mm2(datt, s.vb[...], NT).reshape(BS, NI, WA)
    for b in range(NB):
        key_mask = s.sites[b : b + 1, :]
        s.dbias[b] = jnp.zeros((64, length), F32)

        def attention_back(q):
            together = jnp.zeros((64, length), F32)
            for part in range(TOGETHER):
                bs = b * NS + q * TOGETHER + part
                code = letter_codes(bs)
                wide = [spread(p.astype(F32)).astype(BF16) for p in split2(s.dpam[bs])]
                raw = mm(jnp.concatenate(wide, axis=0), code)
                dweight = raw[0:64] + raw[64:128]
                weight = s.prob[bs]
                inner = jnp.sum(weight * dweight, axis=-1, keepdims=True)
                dscore = jnp.where(key_mask > 0, weight * (dweight - inner), 0.0)
                together = together + dscore
                back = mm(jnp.concatenate(split2(dscore), axis=0), code, NT)
                s.da[bs] = gather_heads(back[0:64] + back[64:128])
            s.dbias[b] += together

        for part in range(2):
            count = NS // TOGETHER // 2
            pl.loop(part * count, (part + 1) * count)(attention_back)
            for group in ((rest,), (up,), (back, back2), (thin, early))[2 * b + part]:
                group.advance()

    put(ROWS.score, mm2r(single, s.da[...].reshape(NM, WA), TN)[0:TR])
    for b in range(NB):
        for i in range(NI):
            part = jnp.concatenate(
                [s.dbias[b, h * NI + i : h * NI + i + 1, :] for h in range(HEADS)], axis=0
            )
            s.dtab[b * NI + i] = mm(
                jnp.concatenate(split2(part), axis=0), codes(b * NI + i), NT
            )
    s.grad[ROWS.bias : ROWS.bias + 8, :] = jnp.sum(
        s.dtab[...].reshape(2 * BI, 8, RP), axis=0
    )

    aux[...] = jnp.where(iota((8, 128), 1) == 0, masked, inv_dist)

    last = bases[LAST]
    piece = (bases[-1] - last) // cols

    def mine(p):
        return pl.ds(pl.multiple_of(last + p * piece, 8), piece)

    def spot(p):
        return gfin.at[pl.ds(pl.multiple_of(p * piece, 8), piece)]

    s.fc[me_c] = s.grad[mine(me_c), :]
    flight = exchange(COL, SUM_COL, lambda p: s.grad.at[mine(p)], lambda p: s.fc.at[p])
    rest.advance()
    finish(flight)
    summed = s.fc[0]
    for c in range(1, cols):
        summed = summed + s.fc[c]
    s.fp[...] = summed
    s.fr[me_r] = summed
    flight = exchange(ROW, SUM_ROW, lambda p: s.fp, lambda p: s.fr.at[p])
    for group in (back, back2, early, up):
        group.advance()
    finish(flight)
    summed = s.fr[0]
    for r in range(1, rows):
        summed = summed + s.fr[r]
    gfin[pl.ds(pl.multiple_of(me_c * piece, 8), piece), :] = summed
    flight = exchange(COL, SHARE_COL, lambda p: spot(me_c), spot)
    for group in (thin, rest, early, back, back2, up, thin, rest):
        group.advance()
    finish(flight)
    while not all(group.done and not group.flight for group in (early, up, thin, rest, back, back2)):
        for group in (early, up, thin, rest, back, back2):
            group.advance()


def post_kernel(rows, cols, *refs):
    gbig, grest, gfin, tout, aux = refs[:5]
    weights, far_moments = refs[5:11], refs[11:23]
    far, loss_out, size_out = refs[23:41], refs[41], refs[42]
    new, moments = refs[43:61], refs[61:73]
    lk, wrel, g_a, g_small, g_rel, store_sem, load_sem = refs[73:]
    loads = [
        pltpu.make_async_copy(source, near, load_sem.at[place])
        for place, (source, near) in enumerate(zip(far_moments, moments))
    ]
    for place in (2, 8, 1, 7, 3, 9, 4, 10, 0, 6, 5, 11):
        loads[place].start()
    means, squares = moments[0:6], moments[6:12]
    lookup, w_a, w_c, w_r, w_p, scal = weights
    ROWS, bases = layout(rows, cols)

    def big(begin, count):
        part = gbig[begin // 8 : (begin + count) // 8].astype(F32)
        return part.reshape(count, 128)

    def exact(begin, count):
        if begin >= bases[LAST]:
            return gfin[begin - bases[LAST] : begin - bases[LAST] + count, :]
        return grest[begin - bases[LOW_SHARE] : begin - bases[LOW_SHARE] + count, :]

    lk[...] = jnp.zeros((AP, WA), F32)
    lk[0:LETTERS, :] = lookup[...]
    wrel[...] = jnp.zeros((RP, WP), F32)
    wrel[0:NREL, :] = w_r[UP : UP + NREL, :]

    def table(begin):
        both = jnp.concatenate([exact(begin, TR), exact(begin + TR, TR)], axis=1)
        return jnp.concatenate([both, jnp.zeros((AP - TR, WA), F32)], axis=0)

    dscore = table(ROWS.score)
    dvalue, dgate, dstart = [table(ROWS.tabs + 2 * TR * place) for place in range(3)]
    mapped = tout[...]
    t_q = mapped[:, 0:WA] * HEAD ** (-0.5)
    t_k = mapped[:, WA : 2 * WA].astype(BF16).astype(F32)
    t_g = jax.nn.sigmoid(mapped[:, 3 * WA :])
    square = head_mask(WA, AP)
    key_block = jnp.where(square, jnp.concatenate([t_k] * HEADS, axis=0), 0.0).astype(BF16)
    dq = mm2(dscore, key_block) * HEAD ** (-0.5)
    dk = jnp.where(square, mm3(dscore, t_q, TN), 0.0)
    dk = jnp.sum(dk.reshape(HEADS, AP, WA), axis=0)
    dg = dgate * (t_g * (1.0 - t_g))
    dmapped = jnp.concatenate([dq, dk, dvalue, dg], axis=1)
    unit0, scale0 = norm(lk[...])
    gain_row = scal[0:WA].reshape(1, WA)
    g_a[...] = mm3(dmapped, unit0 * gain_row, TN)
    dnormed = mm3(dmapped, w_a[0 : 4 * WA, :])
    dgain_row = colsum(dnormed * unit0)
    g_lookup = dstart + norm_back(dnormed * gain_row, unit0, scale0)

    unit_r, scale_r = norm(wrel[...])
    gain_rel = scal[768:896].reshape(1, WP)
    dtable = exact(ROWS.bias, 8)
    g_bias = mm3(dtable, unit_r * gain_rel)
    dnormed = mm3(dtable, w_p[768:776, :], TN)
    dgain_rel = colsum(dnormed * unit_r)
    g_rel[...] = exact(ROWS.rel, 72) + norm_back(
        dnormed * gain_rel, unit_r, scale_r
    )[0:72]

    base = ROWS.small
    g_small[0:WA] = dgain_row.reshape(WA)
    for place, row in ((256, 0), (384, 1), (512, 2), (640, 3), (896, 4), (1024, 5), (1152, 6)):
        g_small[place : place + 128] = exact(base + row, 1).reshape(128)
    g_small[768:896] = dgain_rel.reshape(128)
    lane = iota((1, 128), 1)
    tail = jnp.where(lane < 87, exact(base + 7, 1), 0.0)
    g_small[1280:1408] = tail.reshape(128)

    rel_row = iota((72, 128), 0)
    squares_sum = jnp.zeros((1, 1), F32)
    for begin, count in (
        (ROWS.up, 2 * UP),
        (ROWS.tri, 768),
        (ROWS.o, 2 * WA),
        (ROWS.back, 2 * UP),
    ):
        part = big(begin, count)
        squares_sum = squares_sum + total_of(part * part)
    for part in (
        g_a[...],
        g_lookup[0:LETTERS],
        jnp.where(rel_row < NREL, g_rel[...], 0.0),
        g_bias,
        dgain_row,
        exact(ROWS.outer, UP),
        exact(base, 7),
        exact(ROWS.eh, 87),
        exact(ROWS.eh + 88, 87),
        exact(ROWS.dist, BINS),
        dgain_rel,
        tail,
    ):
        squares_sum = squares_sum + total_of(part * part)
    size = jnp.sqrt(squares_sum)
    scale = jnp.minimum(1.0, CLIP / size)

    def adam(which, where, grad, factor=scale):
        clipped = grad * factor
        weight = weights[which][where]
        moment = B1 * means[which][where] + (1.0 - B1) * clipped
        second = B2 * squares[which][where] + (1.0 - B2) * clipped * clipped
        level = second * (1.0 / (1.0 - B2**STEP))
        step = (moment * (1.0 / (1.0 - B1**STEP))) / (level * lax.rsqrt(level) + ADAM_EPS)
        new[3 * which][where] = weight - RATE * (step + DECAY * weight)
        new[3 * which + 1][where] = moment
        new[3 * which + 2][where] = second

    every = slice(None)
    stores = []

    def leave(which):
        for place in range(3 * which, 3 * which + 3):
            store = pltpu.make_async_copy(new[place], far[place], store_sem.at[place])
            store.start()
            stores.append(store)

    def ready(which):
        loads[which].wait()
        loads[6 + which].wait()

    ready(2)
    for w in range(2):
        half = slice(128 * w, 128 * w + 128)
        adam(2, (slice(0, WA), half), big(ROWS.o + w * WA, WA))
        adam(2, (slice(WA, WA + UP), half), big(ROWS.back + w * UP, UP))
    leave(2)
    ready(1)
    adam(1, (slice(0, 4 * WA), every), g_a[...])
    for w in range(2):
        half = slice(128 * w, 128 * w + 128)
        adam(1, (slice(1024, 2048), half), big(ROWS.up + w * UP, UP))
        adam(1, (slice(2048, 2135), half), exact(ROWS.eh + w * 88, 87))
    leave(1)
    ready(3)
    adam(3, (slice(0, UP), every), exact(ROWS.outer, UP))
    adam(3, (slice(UP, UP + NREL), every), g_rel[0:NREL, :])
    leave(3)
    ready(4)
    adam(4, (slice(0, 768), every), big(ROWS.tri, 768))
    adam(4, (slice(768, 776), every), g_bias)
    adam(4, (slice(776, 840), every), exact(ROWS.dist, BINS))
    leave(4)
    ready(0)
    adam(0, (every, every), g_lookup[0:LETTERS])
    leave(0)
    ready(5)
    adam(5, (slice(0, 1367),), g_small[0:1367], scale.reshape(1))
    leave(5)

    sums = exact(base + 8, 1)
    loss = sums[:, 0:1] / aux[0:1, 0:1] + sums[:, 1:2] * aux[0:1, 1:2]
    loss_out[0] = loss[0, 0]
    size_out[0] = size[0, 0]
    for store in stores:
        store.wait()


def vmem():
    return pl.BlockSpec(memory_space=pltpu.VMEM)


def per_device(rows, cols, *arrays):
    letters, truth, concealed, existing, ordinals, observed, bins = arrays[:7]

    def turned(group):
        return [w.T if place in (1, 4) else w for place, w in enumerate(group)]

    weights, means, squares = turned(arrays[7:13]), turned(arrays[13:19]), turned(arrays[19:25])
    plan = scratch_plan(rows, cols)
    bases = layout(rows, cols)[1]
    far = pl.BlockSpec(memory_space=pltpu.HBM)
    summed = pl.pallas_call(
        functools.partial(main_kernel, rows, cols, tuple(plan)),
        out_shape=(
            jax.ShapeDtypeStruct((bases[LOW_SHARE] // 8, 8, 128), BF16),
            jax.ShapeDtypeStruct((bases[LAST] - bases[LOW_SHARE], 128), F32),
            jax.ShapeDtypeStruct((bases[-1] - bases[LAST], 128), F32),
            jax.ShapeDtypeStruct((AP, 4 * WA), F32),
            jax.ShapeDtypeStruct((8, 128), F32),
        ),
        in_specs=[far] * OPERANDS,
        out_specs=tuple([vmem()] * 5),
        scratch_shapes=[pltpu.VMEM(dims, kind) for dims, kind in plan.values()]
        + [
            pltpu.SemaphoreType.DMA((rows - 1,)),
            pltpu.SemaphoreType.DMA((PHASES - 1, rows - 1)),
            pltpu.SemaphoreType.DMA((cols - 1,)),
            pltpu.SemaphoreType.DMA((PHASES, cols - 1)),
            pltpu.SemaphoreType.DMA((3, 2)),
            pltpu.SemaphoreType.DMA((LAST, max(rows // 2, cols) - 1)),
            pltpu.SemaphoreType.DMA((LAST, 2 * cols + rows - 2)),
            pltpu.SemaphoreType.DMA((OPERANDS,)),
        ],
        compiler_params=pltpu.CompilerParams(
            collective_id=0, has_side_effects=True, vmem_limit_bytes=MAIN_VMEM
        ),
    )(
        *[
            pltpu.with_memory_space_constraint(value, pltpu.HBM)
            for value in (
                jnp.swapaxes(letters, 1, 2),
                jnp.swapaxes(truth, 1, 2),
                jnp.swapaxes(concealed, 1, 2),
                existing,
                ordinals,
                observed,
                bins,
                *weights,
            )
        ]
    )

    shapes = []
    for w in weights:
        shapes += [jax.ShapeDtypeStruct(w.shape, F32)] * 3
    one = jax.ShapeDtypeStruct((1,), F32)
    scalar = pl.BlockSpec(memory_space=pltpu.SMEM)
    result = pl.pallas_call(
        functools.partial(post_kernel, rows, cols),
        out_shape=tuple(shapes) + (one, one),
        in_specs=[vmem()] * 11 + [far] * 12,
        out_specs=tuple([far] * 18) + (scalar, scalar),
        scratch_shapes=[pltpu.VMEM(shape.shape, F32) for shape in shapes]
        + [pltpu.VMEM(value.shape, F32) for value in (*means, *squares)]
        + [
            pltpu.VMEM((AP, WA), F32),
            pltpu.VMEM((RP, WP), F32),
            pltpu.VMEM((4 * WA, WA), F32),
            pltpu.VMEM((1408,), F32),
            pltpu.VMEM((72, 128), F32),
            pltpu.SemaphoreType.DMA((18,)),
            pltpu.SemaphoreType.DMA((12,)),
        ],
        compiler_params=pltpu.CompilerParams(vmem_limit_bytes=POST_VMEM),
    )(
        *summed,
        *weights,
        *[pltpu.with_memory_space_constraint(value, pltpu.HBM) for value in (*means, *squares)],
    )
    outs = [result[18].reshape(()), result[19].reshape(())]
    for place, value in enumerate(result[:18]):
        outs.append(value.T if place // 3 in (1, 4) else value)
    return tuple(outs)


def solution(mesh):
    rows, cols = mesh.shape[ROW], mesh.shape[COL]
    placed = (
        (P(None, COL, ROW),) * 3 + (P(),) * 3 + (P(None, ROW, COL),) + (P(),) * 18
    )
    return jax.shard_map(
        functools.partial(per_device, rows, cols),
        mesh=mesh,
        in_specs=placed,
        out_specs=(P(),) * 20,
        check_vma=False,
    )
```

```python
import functools
from types import SimpleNamespace

import jax
import jax.numpy as jnp
from jax import lax
from jax.experimental import pallas as pl
from jax.experimental.pallas import tpu as pltpu
from jax.sharding import PartitionSpec as P

F32, BF16 = jnp.float32, jnp.bfloat16
MESH = pl.DeviceIdType.MESH
ROW, COL, QUAD = "row", "col", "quad"
CORE, PLANE, Z = "core", "plane", "z"
WA, WP, WO, LETTERS, BINS, REACH, HEADS, HEAD = 256, 128, 32, 23, 64, 32, 8, 32
UP = 1024
NREL = 2 * REACH + 1
AP = 32
TR = 24
RP = 128
EPS = 1e-05
NB, NS, NI, NJ = 2, 16, 8, 16
NM = NB * NS * NI
NP = 2 * NI * NJ
BS = NB * NS
BI = NB * NI
DS = WO * NS
TOGETHER = 4
CLIP, RATE, B1, B2, STEP, ADAM_EPS, DECAY = 0.02, 0.05, 0.9, 0.999, 4, 1e-08, 0.01

MAIN_VMEM, POST_VMEM = 44 * 2**20, 30 * 2**20

NN = (((1,), (0,)), ((), ()))
NT = (((1,), (1,)), ((), ()))
TN = (((0,), (0,)), ((), ()))

GROUPS = (
    dict(up=2 * UP),
    dict(tri=5 * WP, out=WP, o=2 * WA),
    dict(back=UP),
    dict(back2=UP),
    dict(outer=WO * WO),
    dict(eh=176, tabs=6 * TR, dist=BINS, rel=72, small=16),
    dict(score=2 * TR, bias=8),
)
LAST = len(GROUPS) - 1
LOW_SUM = 2
LOW_SHARE = 4


def layout(rows, cols):
    places, bases, begin = {}, [], 0
    for number, group in enumerate(GROUPS):
        bases.append(begin)
        for name, count in group.items():
            places[name] = begin
            begin += count
        size = 16 * cols if number == LAST else 8 * rows * cols
        begin = bases[-1] - (bases[-1] - begin) // size * size
    return SimpleNamespace(**places), bases + [begin]


def mm(a, b, dims=NN):
    return lax.dot_general(a, b, dims, preferred_element_type=F32)


def split2(x):
    high = x.astype(BF16)
    return high, (x - high.astype(F32)).astype(BF16)


def split3(x):
    high = x.astype(BF16)
    rest = x - high.astype(F32)
    middle = rest.astype(BF16)
    return high, middle, (rest - middle.astype(F32)).astype(BF16)


def mm3(a, b, dims=NN):
    ah, al = split2(a)
    bh, bl = split2(b)
    return mm(ah, bh, dims) + (mm(al, bh, dims) + mm(ah, bl, dims))


def mm6(a, b, dims=NN):
    ah, am, al = split3(a)
    bh, bm, bl = split3(b)
    low = mm(al, bh, dims) + (mm(am, bm, dims) + mm(ah, bl, dims))
    return mm(ah, bh, dims) + ((mm(am, bh, dims) + mm(ah, bm, dims)) + low)


def mm2(a, exact, dims=NN):
    ah, al = split2(a)
    return mm(ah, exact, dims) + mm(al, exact, dims)


def mm2r(exact, b, dims=NN):
    bh, bl = split2(b)
    return mm(exact, bh, dims) + mm(exact, bl, dims)


def mm3r(exact, b, dims=NN):
    bh, bm, bl = split3(b)
    return mm(exact, bh, dims) + (mm(exact, bm, dims) + mm(exact, bl, dims))


def norm(x):
    centred = x - jnp.mean(x, axis=-1, keepdims=True)
    scale = lax.rsqrt(jnp.mean(centred * centred, axis=-1, keepdims=True) + EPS)
    return centred * scale, scale


def norm_back(grad, unit, scale):
    return scale * (
        grad
        - jnp.mean(grad, axis=-1, keepdims=True)
        - unit * jnp.mean(grad * unit, axis=-1, keepdims=True)
    )


def iota(shape, axis):
    return lax.broadcasted_iota(jnp.int32, shape, axis)


def head_mask(rows, per_row):
    shape = (rows, WA)
    return iota(shape, 0) // per_row == iota(shape, 1) // HEAD


def colsum(x):
    return jnp.sum(x, axis=0, keepdims=True)


def total_of(x):
    return jnp.sum(jnp.sum(x, axis=1, keepdims=True), axis=0, keepdims=True)


def scratch_plan(rows, cols):
    length = rows * NI
    bases = layout(rows, cols)[1]
    final = bases[-1] - bases[LAST]
    return dict(
        lk=((AP, WA), F32),
        weh=((128, WA), F32),
        wbd=((128, WP), F32),
        seqw=((NM, 1), F32),
        lmask=((NM, 1), F32),
        truth=((NM, 1), F32),
        pmask=((NP, 1), F32),
        offset=((NP, 1), F32),
        codes=((BI, length), F32),
        sites=((8, length), F32),
        wrel=((RP, WP), F32),
        tail=((8, 128), F32),
        kb=((WA, WA), BF16),
        vb=((WA, WA), BF16),
        amat=((BS, NI, WA), F32),
        pam=((BS, NI, WA), F32),
        hm=((64, WA), F32),
        letx=((128, length), F32),
        biash=((NB, 64, length), F32),
        prob=((BS, 64, length), F32),
        sg=((NM, WA), F32),
        att=((NM, WA), F32),
        xh1=((NM, WA), F32),
        r1=((NM, 1), F32),
        hid=((NM, UP), F32),
        rep=((NM, WA), F32),
        xh2=((NM, WA), F32),
        r2=((NM, 1), F32),
        dlog=((NM, 128), F32),
        left3=((NB, NI * NS, 128), BF16),
        mhi=((BI, DS, WP), BF16),
        mlo=((BI, DS, WP), BF16),
        rall=((length, DS), BF16),
        prep=((NP, WP), F32),
        xh3=((NP, WP), F32),
        r3=((NP, 1), F32),
        proj=((NP, 5 * WP), F32),
        le=((BI * NJ, WP), F32),
        re=((length * NJ, WP), F32),
        dm=((BI * length, WP), F32),
        gl=((BI, NJ, WP), F32),
        dr=((length, DS), F32),
        dmid=((NM, WA), F32),
        dbias=((NB, 64, length), F32),
        da=((BS, NI, WA), F32),
        dpam=((BS, NI, WA), F32),
        dtab=((BI, 16, RP), F32),
        dn=((NM, WA), F32),
        sum8=((8, WA), F32),
        grad=((bases[-1], 128), F32),
        lets=((8, 128), F32),
        letr=((rows, 8, 128), F32),
        cnts=((8, 128), F32),
        cntr=((cols, 8, 128), F32),
        rs=((NB, NI, DS), BF16),
        rr=((rows, NI, DS), BF16),
        lr=((2, NI * NS, 128), BF16),
        tgr=((2, NI, NJ), jnp.int32),
        os=((cols, BI, NJ, WP), BF16),
        orr=((cols, BI, NJ, WP), BF16),
        er=((rows // 2, BI, NJ, WP), BF16),
        ts=((cols, BI, NJ, WP), BF16),
        tr=((cols, BI, NJ, WP), BF16),
        ds=((BI, NJ, WP), BF16),
        dsr=((cols, BI, NJ, WP), BF16),
        gs=((rows // 2, BI, NJ, WP), BF16),
        gr=((rows // 2, BI, NJ, WP), BF16),
        qs=((BI, NJ, WP), BF16),
        qr=((cols, BI, NJ, WP), BF16),
        us=((rows, NI, DS), BF16),
        ur=((rows, NI, DS), BF16),
        dl=((2, NI * NS, 128), BF16),
        dlr=((NB, NI * NS, 128), BF16),
        arx=((bases[LAST], 128), F32),
        lows=((bases[LOW_SUM] // 8, 8, 128), BF16),
        lowr=((bases[LOW_SUM] // 8, 8, 128), BF16),
        fc=((cols, final // cols, 128), F32),
        fp=((final // cols, 128), F32),
        fr=((rows, final // cols, 128), F32),
        letters=((NB, NI, NS), jnp.int32),
        truths=((NB, NI, NS), jnp.int32),
        concealed=((NB, NI, NS), jnp.int32),
        existing=((NB, cols * NS), jnp.int32),
        ordinals=((NB, length), jnp.int32),
        observed=((NB, length), jnp.int32),
        targets=((NB, NI, NJ), jnp.int32),
        lookup=((LETTERS, WA), F32),
        w_a=((2135, WA), F32),
        w_c=((WA + UP, WA), F32),
        w_r=((UP + NREL, WP), F32),
        w_p=((840, WP), F32),
        scal=((1367,), F32),
    )


OPERANDS = 13


LET, RIGHT, EDGE, GEDGE, GRIGHT, SUM_ROW = range(6)
CNT, OUTER, TRI, GMIX, GOUTER, SUM_COL, SHARE_COL = range(7)
PHASES = 7


def main_kernel(rows, cols, names, *refs):
    operands = refs[:OPERANDS]
    gbig, grest, gfin, tout, aux = refs[OPERANDS : OPERANDS + 5]
    s = SimpleNamespace(**dict(zip(names, refs[OPERANDS + 5 : -8])))
    row_send, row_recv, col_send, col_recv, pair_sem, sum_send, sum_recv, load_sem = refs[-8:]
    held = refs[OPERANDS + 5 : -8][-OPERANDS:]
    loads = [
        pltpu.make_async_copy(far, near, load_sem.at[place])
        for place, (far, near) in enumerate(zip(operands, held))
    ]
    for load in loads:
        load.start()
    letters, truths, hidden_sites, existing, ordinals, observed, targets = held[:7]
    lookup, w_a, w_c, w_r, w_p, scal = held[7:]
    ROWS, bases = layout(rows, cols)
    length = rows * NI
    me_r, me_c = lax.axis_index(ROW), lax.axis_index(COL)

    barrier = pltpu.get_barrier_semaphore()
    for step in range(1, rows):
        pl.semaphore_signal(
            barrier,
            inc=1,
            device_id={ROW: lax.rem(me_r + step, rows), COL: me_c},
            device_id_type=MESH,
        )
    for step in range(1, cols):
        pl.semaphore_signal(
            barrier,
            inc=1,
            device_id={ROW: me_r, COL: lax.rem(me_c + step, cols)},
            device_id_type=MESH,
        )
    quads = rows // 2
    side, quad = me_r // quads, me_r % quads

    def to_partner(number, source, target):
        return pltpu.make_async_remote_copy(
            src_ref=source,
            dst_ref=target,
            send_sem=pair_sem.at[number, 0],
            recv_sem=pair_sem.at[number, 1],
            device_id={ROW: (1 - side) * quads + quad, COL: me_c},
            device_id_type=MESH,
        )

    def swap(number, source, target):
        out = to_partner(number, source.at[1 - side], target.at[side])
        out.start()
        return out, to_partner(number, source.at[1 - side], target.at[1 - side])

    def exchange(along, phase, source, target):
        if along == ROW:
            count, me, number = rows, me_r, phase
            send, recv = row_send, row_recv
        elif along == QUAD:
            count, me, number = quads, quad, phase
            send, recv = row_send, row_recv
        else:
            count, me, number = cols, me_c, phase
            send, recv = col_send, col_recv
        copies = []
        for step in range(1, count):
            peer = lax.rem(me + step, count)
            origin = lax.rem(me + (count - step), count)
            where = {ROW: me_r, COL: peer}
            if along == ROW:
                where = {ROW: peer, COL: me_c}
            elif along == QUAD:
                where = {ROW: side * quads + peer, COL: me_c}
            out = pltpu.make_async_remote_copy(
                src_ref=source(peer),
                dst_ref=target(me),
                send_sem=send.at[step - 1],
                recv_sem=recv.at[number, step - 1],
                device_id=where,
                device_id_type=MESH,
            )
            out.start()
            arriving = pltpu.make_async_remote_copy(
                src_ref=source(peer),
                dst_ref=target(origin),
                send_sem=send.at[step - 1],
                recv_sem=recv.at[number, step - 1],
                device_id=where,
                device_id_type=MESH,
            )
            copies.append((out, arriving))
        return copies

    def finish(copies):
        for out, arriving in copies:
            out.wait_send()
            arriving.wait_recv()

    for load in loads[:7]:
        load.wait()
    here = existing[...].astype(F32)
    sites = observed[...].astype(F32)
    numbers = ordinals[...].astype(F32)

    def by_protein(values, count, each):
        wide = (count, values.shape[1])
        return jnp.where(iota(wide, 0) // each == 0, values[0:1], values[1:2])

    def at_lane(values, lanes):
        return jnp.sum(jnp.where(iota(values.shape, 1) == lanes, values, 0.0), axis=1, keepdims=True)

    row_m, row_p = iota((NM, 1), 0), iota((NP, 1), 0)
    seq_m, res_m = (row_m // NI) % NS, row_m % NI
    spread_m = jnp.where(
        iota((NM, BI), 1) == (iota((NM, BI), 0) // (NI * NS)) * NI + iota((NM, BI), 0) % NI, 1.0, 0.0
    ).astype(BF16)

    def column_m(values):
        wide = mm(spread_m, values[...].reshape(BI, NS).astype(F32).astype(BF16))
        return at_lane(wide, seq_m)

    seq_weight = at_lane(by_protein(here, NM, NI * NS), me_c * NS + seq_m)
    letter = column_m(letters)
    loss_mask = column_m(hidden_sites) * seq_weight
    s.seqw[...] = seq_weight
    s.lmask[...] = loss_mask
    s.truth[...] = column_m(truths)
    s.tgr[side] = targets[side]

    s.lets[...] = jnp.where(
        (iota((NI, 128), 0) == 0) & (iota((NI, 128), 1) == BS), total_of(loss_mask), 0.0
    )
    for b in range(NB):
        s.lets[:, b * NS : (b + 1) * NS] = letters[b].astype(F32)
    s.letr[me_r] = s.lets[...]
    near = row_p // NJ
    first = (quad + quads * (near // NI)) * NI + near % NI
    second = me_c * NJ + row_p % NJ

    def of_side(values):
        return jnp.where(side == 0, values[0:1], values[1:2])

    sites_p = jnp.broadcast_to(of_side(sites), (NP, length))
    numbers_p = jnp.broadcast_to(of_side(numbers), (NP, length))
    s.pmask[...] = at_lane(sites_p, first) * at_lane(sites_p, second)
    s.offset[...] = (
        jnp.clip(at_lane(numbers_p, first) - at_lane(numbers_p, second), -REACH, REACH) + REACH
    )
    numbers_b = by_protein(numbers, BI, NI)
    own = at_lane(numbers_b, me_r * NI + iota((BI, 1), 0) % NI)
    s.codes[...] = jnp.clip(own - numbers_b, -REACH, REACH) + REACH
    s.sites[...] = jnp.zeros((8, length), F32)
    s.sites[0:NB, :] = sites
    inv_all = 1.0 / (jnp.sum(here, axis=1, keepdims=True) + 1.0)
    inv_count = of_side(inv_all)
    per_protein = jnp.sum(sites, axis=1, keepdims=True)
    inv_dist = 1.0 / jnp.maximum(colsum(per_protein * per_protein), 1.0)

    for load in loads[7:]:
        load.wait()

    def gain(begin, width):
        return scal[begin : begin + width].reshape(1, width)

    gain_row, gain_trans, gain_outer = gain(0, WA), gain(256, WA), gain(512, WA)
    gain_rel, gain_pair, gain_mixed = gain(768, WP), gain(896, WP), gain(1024, WP)
    bias_outer = gain(1152, WP)
    s.lk[...] = jnp.zeros((AP, WA), F32)
    s.lk[0:LETTERS, :] = lookup[...]
    s.weh[...] = jnp.zeros((128, WA), F32)
    s.weh[0:87, :] = w_a[2048:2135, :]
    s.wbd[...] = jnp.zeros((128, WP), F32)
    s.wbd[0:72, :] = w_p[768:840, :]
    s.wrel[...] = jnp.zeros((RP, WP), F32)
    s.wrel[0:NREL, :] = w_r[UP : UP + NREL, :]
    s.tail[...] = jnp.zeros((8, 128), F32)
    s.tail[0:1, 0:87] = scal[1280:1367].reshape(1, 87)

    table = s.lk[...]
    unit0, _ = norm(table)
    mapped = mm6(unit0 * gain_row, w_a[0 : 4 * WA, :], NT)
    tout[...] = mapped
    pl.semaphore_wait(barrier, rows + cols - 2)
    flight = exchange(ROW, LET, lambda p: s.lets, lambda p: s.letr.at[p])
    flight.append(swap(0, targets, s.tgr))
    t_q = mapped[:, 0:WA] * HEAD ** (-0.5)
    t_k = mapped[:, WA : 2 * WA].astype(BF16).astype(F32)
    t_v = mapped[:, 2 * WA : 3 * WA].astype(BF16).astype(F32)
    t_g = jax.nn.sigmoid(mapped[:, 3 * WA :])
    square = head_mask(WA, AP)
    key_block = jnp.where(square, jnp.concatenate([t_k] * HEADS, axis=0), 0.0).astype(BF16)
    s.vb[...] = jnp.where(square, jnp.concatenate([t_v] * HEADS, axis=0), 0.0).astype(BF16)
    stacked = mm(jnp.concatenate(split3(t_q), axis=0), key_block, NT)
    score_table = stacked[0:AP] + (stacked[AP : 2 * AP] + stacked[2 * AP :])
    s.hm[...] = jnp.where(head_mask(64, NI), 1.0, 0.0)

    letter = letter.astype(jnp.int32)
    triple = jnp.where(
        (iota((NM, 3 * AP), 1) % AP) == letter, 1.0, 0.0
    ).astype(BF16)

    def chosen(values):
        return mm(triple, jnp.concatenate(split3(values), axis=0))

    s.amat[...] = chosen(score_table).reshape(BS, NI, WA)
    start = chosen(table)
    s.sg[...] = chosen(t_g)

    unit_r, _ = norm(s.wrel[...])
    bias_table = mm3(s.wbd[0:8, :], unit_r * gain_rel, NT)
    bias_parts = jnp.concatenate(split3(bias_table), axis=0)

    def codes(index):
        return jnp.where(
            iota((RP, length), 0) == s.codes[index : index + 1, :].astype(jnp.int32), 1.0, 0.0
        ).astype(BF16)

    for b in range(NB):
        for i in range(NI):
            part = mm(bias_parts, codes(b * NI + i))
            part = part[0:8] + (part[8:16] + part[16:24])
            for h in range(HEADS):
                s.biash[b, h * NI + i : h * NI + i + 1, :] = part[h : h + 1, :]

    finish(flight)
    letters_all = s.letr[...].reshape(length, 128).T
    s.letx[...] = letters_all
    s.cnts[...] = jnp.broadcast_to(
        jnp.sum(letters_all[BS : BS + 1, :], axis=1, keepdims=True), (8, 128)
    )
    s.cntr[me_c] = s.cnts[...]
    count_flight = exchange(COL, CNT, lambda p: s.cnts, lambda p: s.cntr.at[p])

    def letter_codes(bs):
        row = s.letx[pl.ds(bs, 1), :].astype(jnp.int32)
        one = jnp.where(iota((AP, length), 0) == row, 1.0, 0.0)
        return jnp.concatenate([one] * HEADS, axis=0).astype(BF16)

    def spread(value):
        wide = jnp.broadcast_to(value[None], (HEADS, NI, WA)).reshape(64, WA)
        return wide * s.hm[...]

    def gather_heads(value):
        return jnp.sum((value * s.hm[...]).reshape(HEADS, NI, WA), axis=0)

    for b in range(NB):
        key_mask = s.sites[b : b + 1, :]

        @pl.loop(0, NS // TOGETHER)
        def _(q):
            for part in range(TOGETHER):
                bs = b * NS + q * TOGETHER + part
                code = letter_codes(bs)
                wide = [spread(p.astype(F32)).astype(BF16) for p in split2(s.amat[bs])]
                raw = mm(jnp.concatenate(wide, axis=0), code)
                scores = (raw[0:64] + raw[64:128]) + s.biash[b]
                scores = jnp.where(key_mask > 0, scores, -1000000000.0)
                power = jnp.exp(scores - jnp.max(scores, axis=-1, keepdims=True))
                weight = power / jnp.sum(power, axis=-1, keepdims=True)
                s.prob[bs] = weight
                picked = mm(jnp.concatenate(split2(weight), axis=0), code, NT)
                s.pam[bs] = gather_heads(picked[0:64] + picked[64:128])

    att = mm2(s.pam[...].reshape(NM, WA), s.vb[...])
    s.att[...] = att
    mid = start + mm3(s.sg[...] * att, w_c[0:WA, :])
    unit1, scale1 = norm(mid)
    s.xh1[...] = unit1
    s.r1[...] = scale1
    hidden = jnp.maximum(mm3(unit1 * gain_trans, w_a[4 * WA : 4 * WA + UP, :], NT), 0.0)
    s.hid[...] = hidden
    rep = mid + mm3(hidden, w_c[WA:, :])
    s.rep[...] = rep
    unit2, scale2 = norm(rep)
    s.xh2[...] = unit2
    s.r2[...] = scale2
    seq_weight = s.seqw[...]
    lane = iota((NM, 128), 1)
    edges = mm3(unit2 * gain_outer, s.weh[...], NT) * seq_weight

    right = jnp.where((lane >= 32) & (lane < 64), edges, 0.0).astype(BF16)
    spot = iota((128, DS), 0)
    repeat = jnp.where(spot - 32 == iota((128, DS), 1) // NS, 1.0, 0.0)
    repeat = jnp.where((spot >= 32) & (spot < 64), repeat, 0.0).astype(BF16)
    wide = mm(right, repeat)
    own_seq = (iota((NM, DS), 0) // NI) % NS == iota((NM, DS), 1) % NS
    wide = jnp.sum(jnp.where(own_seq, wide, 0.0).reshape(NB, NS, NI, DS), axis=1)
    s.rs[...] = wide.astype(BF16)
    s.rr[me_r] = s.rs[side]
    flight = exchange(ROW, RIGHT, lambda p: s.rs.at[p // quads], lambda p: s.rr.at[p])

    order_to = (iota((NM, NM), 0) // (NI * NS) == iota((NM, NM), 1) // (NI * NS)) & (
        (iota((NM, NM), 0) // NS) % NI == iota((NM, NM), 1) % NI
    )
    order_to = order_to & (iota((NM, NM), 0) % NS == (iota((NM, NM), 1) // NI) % NS)
    order = jnp.where(order_to, 1.0, 0.0).astype(BF16)
    left = mm3r(order, jnp.where(lane < 32, edges, 0.0))
    high, low = split2(left)
    high32, low32 = high.astype(F32), low.astype(F32)
    left3 = high32 + pltpu.roll(low32, 32, 1) + pltpu.roll(high32, 64, 1)
    s.left3[...] = left3.astype(BF16).reshape(NB, NI * NS, 128)
    s.lr[side] = s.left3[side]
    flight.append(swap(1, s.left3, s.lr))

    finish(count_flight)
    masked = jnp.maximum(jnp.sum(s.cntr[...], axis=0)[0:1, 0:1], 1.0)
    logits = mm3(rep, s.weh[...], NT) + s.tail[0:1, :]
    valid = (lane >= 64) & (lane < 64 + LETTERS)
    top = jnp.max(jnp.where(valid, logits, -3e38), axis=-1, keepdims=True)
    power = jnp.where(valid, jnp.exp(jnp.where(valid, logits, top) - top), 0.0)
    whole = jnp.sum(power, axis=-1, keepdims=True)
    truth = lane - 64 == s.truth[...].astype(jnp.int32)
    truth = truth & valid
    picked = jnp.sum(jnp.where(truth, logits, 0.0), axis=-1, keepdims=True)
    loss_mask = s.lmask[...]
    msa_sum = colsum((jnp.log(whole) + top - picked) * loss_mask)
    s.dlog[...] = (power / whole - jnp.where(truth, 1.0, 0.0)) * (loss_mask / masked)

    def outer_weight(d):
        return w_r[pl.ds(d, WO, stride=WO), :]

    def expand(block):
        for pair in range(WO // 2):
            both = jnp.concatenate([outer_weight(2 * pair), outer_weight(2 * pair + 1)], axis=1)
            wh, wl = split2(both)
            made = mm(s.lr[block][:, 0:96], jnp.concatenate([wh, wh, wl], axis=0))
            for half in range(2):
                d = 2 * pair + half
                mh, ml = split2(made[:, half * WP : (half + 1) * WP].reshape(NI, NS, WP))
                s.mhi[pl.ds(block * NI, NI), d * NS : (d + 1) * NS, :] = mh
                s.mlo[pl.ds(block * NI, NI), d * NS : (d + 1) * NS, :] = ml

    expand(side)
    finish(flight)
    expand(1 - side)
    s.rall[...] = s.rr[...].astype(F32).reshape(length, DS).astype(BF16)

    @pl.loop(0, BI)
    def _(i):
        block = mm(s.rall[...], s.mhi[i]) + mm(s.rall[...], s.mlo[i])
        block = block * inv_count
        for c in range(cols):
            s.os[c, i] = block[c * NJ : (c + 1) * NJ].astype(BF16)

    s.orr[me_c] = s.os[me_c]
    finish(exchange(COL, OUTER, lambda p: s.os.at[p], lambda p: s.orr.at[p]))

    pair_lane = iota((NP, 128), 1)
    offset = s.offset[...].astype(jnp.int32)
    pair_codes = jnp.where(pair_lane == offset, 1.0, 0.0).astype(BF16)
    outer = s.orr[0].astype(F32)
    for c in range(1, cols):
        outer = outer + s.orr[c].astype(F32)
    pair_rep = (mm3r(pair_codes, s.wrel[...]) + outer.reshape(NP, WP)) + bias_outer
    s.prep[...] = pair_rep
    unit3, scale3 = norm(pair_rep)
    s.xh3[...] = unit3
    s.r3[...] = scale3
    proj = mm3(unit3 * gain_pair, w_p[0 : 5 * WP, :], NT)
    pair_mask = s.pmask[...]
    sig1 = jax.nn.sigmoid(proj[:, WP : 2 * WP])
    sig2 = jax.nn.sigmoid(proj[:, 3 * WP : 4 * WP])
    sig3 = jax.nn.sigmoid(proj[:, 4 * WP :])
    s.proj[:, 0 : WP] = proj[:, 0:WP]
    s.proj[:, WP : 2 * WP] = sig1
    s.proj[:, 2 * WP : 3 * WP] = proj[:, 2 * WP : 3 * WP]
    s.proj[:, 3 * WP : 4 * WP] = sig2
    s.proj[:, 4 * WP :] = sig3
    s.le[...] = sig1 * proj[:, 0:WP] * pair_mask
    right_edge = (sig2 * proj[:, 2 * WP : 3 * WP] * pair_mask).astype(BF16)
    s.er[quad] = right_edge.reshape(BI, NJ, WP)
    finish(exchange(QUAD, EDGE, lambda p: s.er.at[quad], lambda p: s.er.at[p]))
    for q in range(quads):
        for block in range(2):
            begin = (q + quads * block) * NI * NJ
            s.re[begin : begin + NI * NJ, :] = (
                s.er[q, block * NI : (block + 1) * NI].astype(F32).reshape(NI * NJ, WP)
            )

    @pl.loop(0, BI)
    def _(i):
        for c in range(cols):
            block = jnp.zeros((NJ, WP), F32)
            for k in range(NJ):
                other = s.re[pl.ds(c * NJ * NJ + k, NJ, stride=NJ), :]
                block = block + s.le[pl.ds(i * NJ + k, 1), :] * other
            s.ts[c, i] = block.astype(BF16)

    s.tr[me_c] = s.ts[me_c]
    finish(exchange(COL, TRI, lambda p: s.ts.at[p], lambda p: s.tr.at[p]))

    mixed = s.tr[0].astype(F32)
    for c in range(1, cols):
        mixed = mixed + s.tr[c].astype(F32)
    unit4, scale4 = norm(mixed.reshape(NP, WP))
    w_out = w_p[5 * WP : 6 * WP, :]
    moved = mm3(unit4 * gain_mixed, w_out, NT)
    sig3 = s.proj[:, 4 * WP :]
    pair_out = s.prep[...] + sig3 * moved
    bins = mm3(pair_out, s.wbd[...], NT) + pltpu.roll(
        jnp.where(iota((8, 128), 1) < BINS, s.tail[...], 0.0), 8, 1
    )[0:1]
    valid = (pair_lane >= 8) & (pair_lane < 8 + BINS)
    top = jnp.max(jnp.where(valid, bins, -3e38), axis=-1, keepdims=True)
    power = jnp.where(valid, jnp.exp(jnp.where(valid, bins, top) - top), 0.0)
    whole = jnp.sum(power, axis=-1, keepdims=True)
    spread_p = jnp.where(iota((NP, BI), 1) == iota((NP, BI), 0) // NJ, 1.0, 0.0).astype(BF16)
    target = at_lane(
        mm(spread_p, s.tgr[...].reshape(BI, NJ).astype(F32).astype(BF16)), row_p % NJ
    )
    truth = (pair_lane - 8 == target.astype(jnp.int32)) & valid
    picked = jnp.sum(jnp.where(truth, bins, 0.0), axis=-1, keepdims=True)
    dist_sum = colsum((jnp.log(whole) + top - picked) * pair_mask)
    dbins = (power / whole - jnp.where(truth, 1.0, 0.0)) * (pair_mask * inv_dist)

    def put(place, value, skip=0):
        base = place + skip
        height, width = value.shape
        for w in range(width // 128):
            s.grad[base + w * height : base + (w + 1) * height, :] = value[
                :, w * 128 : (w + 1) * 128
            ]

    planes, lines = cols, rows // 2
    sizes = {CORE: 2, PLANE: planes, Z: lines}
    places = {CORE: me_c % 2, PLANE: me_c // 2 * 2 + me_r % 2, Z: me_r // 2}

    def line_peer(axis, place):
        if axis == CORE:
            return {ROW: me_r, COL: me_c // 2 * 2 + place}
        if axis == PLANE:
            return {ROW: me_r // 2 * 2 + place % 2, COL: place // 2 * 2 + me_c % 2}
        return {ROW: place * 2 + me_r % 2, COL: me_c}

    def rows_at(unit, count):
        return pl.ds(pl.multiple_of(unit * 8, 8), count * 8)

    class Sum:
        def __init__(self, number):
            self.number = number
            self.begin = bases[number] // 8
            self.at, self.size = self.begin, (bases[number + 1] - bases[number]) // 8
            self.rx = self.begin
            self.low_sum, self.low_share = number < LOW_SUM, number < LOW_SHARE
            self.stages = [(self.reduce, axis) for axis in (CORE, PLANE, Z)]
            self.stages += [(self.share, axis) for axis in (Z, PLANE, CORE)]
            self.flight, self.after, self.used, self.stored = [], None, 0, False

        @property
        def done(self):
            return not self.stages and not self.flight

        def copies(self, axis, source, target):
            count = sizes[axis]
            for step in range(1, count):
                peer = lax.rem(places[axis] + step, count)
                origin = lax.rem(places[axis] + (count - step), count)
                both = []
                for end in (target(places[axis], step), target(origin, step)):
                    both.append(
                        pltpu.make_async_remote_copy(
                            src_ref=source(peer, step),
                            dst_ref=end,
                            send_sem=sum_send.at[self.number, step - 1],
                            recv_sem=sum_recv.at[self.number, self.used],
                            device_id=line_peer(axis, peer),
                            device_id_type=MESH,
                        )
                    )
                self.used += 1
                both[0].start()
                self.flight.append(both)

        def advance(self):
            finish(self.flight)
            self.flight = []
            if self.after is not None:
                self.after()
                self.after = None
            if self.stages:
                stage, axis = self.stages.pop(0)
                stage(axis)

        def reduce(self, axis):
            count = sizes[axis]
            small = self.size // count
            rx = self.rx

            def slot(buffer, step):
                if self.low_sum:
                    return buffer.at[pl.ds(rx + (step - 1) * small, small)]
                return buffer.at[pl.ds((rx + (step - 1) * small) * 8, small * 8)]

            if self.low_sum:
                for step in range(1, count):
                    peer = lax.rem(places[axis] + step, count)
                    value = s.grad[rows_at(self.at + peer * small, small), :]
                    slot(s.lows, step)[...] = value.reshape(small, 8, 128).astype(BF16)

            def source(peer, step):
                if self.low_sum:
                    return slot(s.lows, step)
                return s.grad.at[rows_at(self.at + peer * small, small)]

            near = s.lowr if self.low_sum else s.arx
            self.copies(axis, source, lambda place, step: slot(near, step))

            def add():
                self.at = self.at + places[axis] * small
                self.size = small
                mine = rows_at(self.at, small)
                value = s.grad[mine, :]
                for step in range(1, count):
                    other = slot(near, step)[...].astype(F32)
                    value = value + other.reshape(small * 8, 128)
                s.grad[mine, :] = value

            self.after = add
            self.rx = rx + (count - 1) * small

        def spot(self, at, size):
            if self.low_share:
                return gbig.at[pl.ds(at, size)]
            return grest.at[rows_at(at - bases[LOW_SHARE] // 8, size)]

        def share(self, axis):
            if not self.stored:
                self.stored = True
                value = s.grad[rows_at(self.at, self.size), :]
                if self.low_share:
                    value = value.reshape(self.size, 8, 128).astype(BF16)
                self.spot(self.at, self.size)[...] = value
            size = self.size
            first = self.at - places[axis] * size
            self.copies(
                axis,
                lambda peer, step: self.spot(first + places[axis] * size, size),
                lambda place, step: self.spot(first + place * size, size),
            )
            self.at, self.size = first, size * sizes[axis]

    up, thin, back, back2, early, rest = [Sum(number) for number in range(LAST)]

    def turn(*groups):
        for group in groups:
            group.advance()

    def column_products(name, place):
        s.sum8[...] = jnp.zeros((8, WA), F32)

        @pl.loop(0, NM // 32)
        def _(q):
            some = pl.ds(pl.multiple_of(q * 32, 32), 32)
            product = s.dn[some, :] * name[some, :]
            s.sum8[...] += jnp.sum(product.reshape(4, 8, WA), axis=0)

        whole = colsum(s.sum8[...])
        for half in range(2):
            s.grad[small + place + half : small + place + half + 1, :] = whole[
                :, 128 * half : 128 * half + 128
            ]

    for begin, end in (
        (ROWS.o + 2 * WA, bases[2]),
        (ROWS.small, bases[LAST]),
        (ROWS.bias, bases[-1]),
    ):
        if end > begin:
            s.grad[begin:end, :] = jnp.zeros((end - begin, 128), F32)
    small = ROWS.small
    put(ROWS.dist, mm3(dbins, pair_out, TN)[8 : 8 + BINS])
    dbias_dist = pltpu.roll(jnp.broadcast_to(colsum(dbins), (8, 128)), 120, 1)[0:1]
    dout = mm3(dbins, s.wbd[...])
    dgate = dout * moved * (sig3 * (1.0 - sig3))
    dmoved = dout * sig3
    put(ROWS.out, mm3(dmoved, unit4 * gain_mixed, TN))
    dnormed = mm3(dmoved, w_out)
    s.grad[small + 5 : small + 6, :] = colsum(dnormed * unit4)
    dmixed = norm_back(dnormed * gain_mixed, unit4, scale4)
    s.ds[...] = dmixed.astype(BF16).reshape(BI, NJ, WP)
    s.dsr[me_c] = s.ds[...]
    finish(exchange(COL, GMIX, lambda p: s.ds, lambda p: s.dsr.at[p]))
    for bi in range(BI):
        for c in range(cols):
            begin = bi * length + c * NJ
            s.dm[begin : begin + NJ, :] = s.dsr[c, bi].astype(F32)

    @pl.loop(0, quads)
    def _(q):
        for place in range(BI):
            j = (q + quads * (place // NI)) * NI + place % NI
            block = jnp.zeros((NJ, WP), F32)
            for i in range(BI):
                block = block + (
                    s.dm[pl.ds(i * length + j, 1), :] * s.le[i * NJ : (i + 1) * NJ, :]
                )
            s.gs[q, place] = block.astype(BF16)

    s.gr[quad] = s.gs[quad]
    flight = exchange(QUAD, GEDGE, lambda p: s.gs.at[p], lambda p: s.gr.at[p])

    @pl.loop(0, BI)
    def _(i):
        block = jnp.zeros((NJ, WP), F32)
        for j in range(length):
            block = block + (
                s.dm[pl.ds(i * length + j, 1), :] * s.re[j * NJ : (j + 1) * NJ, :]
            )
        s.gl[i] = block

    finish(flight)
    dright = s.gr[0].astype(F32)
    for q in range(1, quads):
        dright = dright + s.gr[q].astype(F32)
    dright = dright.reshape(NP, WP) * pair_mask
    dleft = s.gl[...].reshape(NP, WP) * pair_mask
    p1, sig1 = s.proj[:, 0:WP], s.proj[:, WP : 2 * WP]
    p2, sig2 = s.proj[:, 2 * WP : 3 * WP], s.proj[:, 3 * WP : 4 * WP]
    dproj = jnp.concatenate(
        [
            dleft * sig1,
            dleft * p1 * (sig1 * (1.0 - sig1)),
            dright * sig2,
            dright * p2 * (sig2 * (1.0 - sig2)),
            dgate,
        ],
        axis=1,
    )
    unit3 = s.xh3[...]
    put(ROWS.tri, mm3(dproj, unit3 * gain_pair, TN))
    dnormed = mm3(dproj, w_p[0 : 5 * WP, :])
    s.grad[small + 4 : small + 5, :] = colsum(dnormed * unit3)
    drep = dout + norm_back(dnormed * gain_pair, unit3, s.r3[...])
    s.grad[small + 6 : small + 7, :] = colsum(drep)
    s.grad[ROWS.rel : ROWS.rel + 72, :] = mm2r(pair_codes, drep, TN)[0:72]
    s.qs[...] = drep.astype(BF16).reshape(BI, NJ, WP)
    s.qr[me_c] = s.qs[...]
    finish(exchange(COL, GOUTER, lambda p: s.qs, lambda p: s.qr.at[p]))

    turned = s.rall[...].astype(F32).T.astype(BF16)
    s.dr[...] = jnp.zeros((length, DS), F32)

    @pl.loop(0, BI)
    def _(i):
        block = jnp.concatenate([s.qr[c, i] for c in range(cols)], axis=0)
        s.dr[...] += mm(block, s.mhi[i], NT) + mm(block, s.mlo[i], NT)
        mh, ml = split2(mm(turned, block) * inv_count)
        s.mhi[i] = mh
        s.mlo[i] = ml

    for r in range(rows):
        s.us[r] = (s.dr[r * NI : (r + 1) * NI, :] * inv_count).astype(BF16)
    s.ur[me_r] = s.us[me_r]
    flight = exchange(ROW, GRIGHT, lambda p: s.us.at[p], lambda p: s.ur.at[p])

    def pair_weight(pair):
        return split2(
            jnp.concatenate([outer_weight(2 * pair), outer_weight(2 * pair + 1)], axis=1)
        )

    def pair_of(ref, pair):
        return jnp.concatenate(
            [
                ref[:, d * NS : (d + 1) * NS, :].reshape(NM, WP)
                for d in (2 * pair, 2 * pair + 1)
            ],
            axis=1,
        )

    dleft = jnp.zeros((NM, WO), F32)
    for pair in range(WO // 2):
        wh, wl = pair_weight(pair)
        mh, ml = pair_of(s.mhi, pair), pair_of(s.mlo, pair)
        dleft = dleft + (mm(mh, wh, NT) + (mm(ml, wh, NT) + mm(mh, wl, NT)))
    high, low = split2(jnp.concatenate([dleft, jnp.zeros((NM, 96), F32)], axis=1))
    both = high.astype(F32) + pltpu.roll(low.astype(F32), 32, 1)
    s.dl[...] = both.astype(BF16).reshape(2, NI * NS, 128)
    s.dlr[side] = s.dl[side]
    flight.append(swap(2, s.dl, s.dlr))
    left3 = s.lr[...].astype(F32).reshape(NM, 128).T.astype(BF16)
    left_both, left_high = left3[0:64], left3[0:32]
    for pair in range(WO // 2):
        mh, ml = pair_of(s.mhi, pair), pair_of(s.mlo, pair)
        made = mm(left_both, mh)
        made = made[0:32] + made[32:64] + mm(left_high, ml)
        for half in range(2):
            s.grad[pl.ds(ROWS.outer + 2 * pair + half, WO, stride=WO), :] = made[
                :, half * WP : (half + 1) * WP
            ]
    early.advance()

    finish(flight)
    both = s.dlr[...].astype(F32).reshape(NM, 128)
    both = jnp.where(lane < 32, both + pltpu.roll(both, 96, 1), 0.0)
    dleft = mm3r(order, both, TN)
    dright = []
    for b in range(NB):
        some = s.ur[b * quads].astype(F32)
        for q in range(1, quads):
            some = some + s.ur[b * quads + q].astype(F32)
        dright.append(some)
    dright = jnp.stack(dright)
    wide = jnp.broadcast_to(dright[:, None], (NB, NS, NI, DS)).reshape(NM, DS)
    dedges = mm2(jnp.where(own_seq, wide, 0.0), repeat, NT)
    dedges = (dedges + dleft) * seq_weight
    unit2, rep = s.xh2[...], s.rep[...]
    dlog = s.dlog[...]
    put(ROWS.eh, (mm3(dedges, unit2 * gain_outer, TN) + mm3(dlog, rep, TN))[0:88])
    s.dn[...] = mm3(dedges, s.weh[...])
    dnormed = s.dn[...]
    column_products(s.xh2, 2)
    drep = mm3(dlog, s.weh[...]) + norm_back(dnormed * gain_outer, unit2, s.r2[...])
    early.advance()
    hidden = s.hid[...]
    dhidden = jnp.where(hidden > 0, mm3(drep, w_c[WA:, :], NT), 0.0)
    unit1 = s.xh1[...]
    put(ROWS.up, mm3(dhidden, unit1 * gain_trans, TN))
    up.advance()
    put(ROWS.back, mm3(hidden, drep, TN))
    turn(back, back2, up)
    s.dn[...] = mm3(dhidden, w_a[4 * WA : 4 * WA + UP, :])
    dnormed = s.dn[...]
    column_products(s.xh1, 0)
    dmid = drep + norm_back(dnormed * gain_trans, unit1, s.r1[...])
    sg, att = s.sg[...], s.att[...]
    put(ROWS.o, mm3(sg * att, dmid, TN))
    dgated = mm3(dmid, w_c[0:WA, :], NT)
    turn(thin, back, back2, early)
    single = triple[:, 0:AP]
    put(ROWS.tabs, mm2r(single, dmid, TN)[0:TR], 4 * TR)
    put(ROWS.tabs, mm2r(single, dgated * att, TN)[0:TR], 2 * TR)
    datt = dgated * sg

    pam = s.pam[...].reshape(NM, WA)
    blocks = jnp.where(head_mask(WA, AP), mm3(pam, datt, TN), 0.0)
    put(ROWS.tabs, jnp.sum(blocks.reshape(HEADS, AP, WA), axis=0)[0:TR])
    lane1 = iota((1, 128), 1)
    s.grad[small + 7 : small + 8, :] = jnp.where(lane1 < BINS, dbias_dist, colsum(dlog))
    s.grad[small + 8 : small + 9, :] = jnp.where(
        lane1 == 0, msa_sum, jnp.where(lane1 == 1, dist_sum, 0.0)
    )
    turn(rest, thin)
    s.dpam[...] = mm2(datt, s.vb[...], NT).reshape(BS, NI, WA)
    for b in range(NB):
        key_mask = s.sites[b : b + 1, :]
        s.dbias[b] = jnp.zeros((64, length), F32)

        def attention_back(q):
            together = jnp.zeros((64, length), F32)
            for part in range(TOGETHER):
                bs = b * NS + q * TOGETHER + part
                code = letter_codes(bs)
                wide = [spread(p.astype(F32)).astype(BF16) for p in split2(s.dpam[bs])]
                raw = mm(jnp.concatenate(wide, axis=0), code)
                dweight = raw[0:64] + raw[64:128]
                weight = s.prob[bs]
                inner = jnp.sum(weight * dweight, axis=-1, keepdims=True)
                dscore = jnp.where(key_mask > 0, weight * (dweight - inner), 0.0)
                together = together + dscore
                back = mm(jnp.concatenate(split2(dscore), axis=0), code, NT)
                s.da[bs] = gather_heads(back[0:64] + back[64:128])
            s.dbias[b] += together

        for part in range(2):
            count = NS // TOGETHER // 2
            pl.loop(part * count, (part + 1) * count)(attention_back)
            turn(*((rest, up), (back, early), (back2,), (thin, rest, up))[2 * b + part])

    put(ROWS.score, mm2r(single, s.da[...].reshape(NM, WA), TN)[0:TR])
    for b in range(NB):
        for i in range(NI):
            part = jnp.concatenate(
                [s.dbias[b, h * NI + i : h * NI + i + 1, :] for h in range(HEADS)], axis=0
            )
            s.dtab[b * NI + i] = mm(
                jnp.concatenate(split2(part), axis=0), codes(b * NI + i), NT
            )
    s.grad[ROWS.bias : ROWS.bias + 8, :] = jnp.sum(
        s.dtab[...].reshape(2 * BI, 8, RP), axis=0
    )

    aux[...] = jnp.where(iota((8, 128), 1) == 0, masked, inv_dist)

    last = bases[LAST]
    piece = (bases[-1] - last) // cols

    def mine(p):
        return pl.ds(pl.multiple_of(last + p * piece, 8), piece)

    def spot(p):
        return gfin.at[pl.ds(pl.multiple_of(p * piece, 8), piece)]

    s.fc[me_c] = s.grad[mine(me_c), :]
    flight = exchange(COL, SUM_COL, lambda p: s.grad.at[mine(p)], lambda p: s.fc.at[p])
    turn(back, early)
    finish(flight)
    summed = s.fc[0]
    for c in range(1, cols):
        summed = summed + s.fc[c]
    s.fp[...] = summed
    s.fr[me_r] = summed
    flight = exchange(ROW, SUM_ROW, lambda p: s.fp, lambda p: s.fr.at[p])
    turn(back2, thin, rest, up, back, early)
    finish(flight)
    summed = s.fr[0]
    for r in range(1, rows):
        summed = summed + s.fr[r]
    gfin[pl.ds(pl.multiple_of(me_c * piece, 8), piece), :] = summed
    flight = exchange(COL, SHARE_COL, lambda p: spot(me_c), spot)
    turn(back2, early, thin, rest)
    finish(flight)
    turn(up, back, up, back2, back, back2, thin, rest, thin, rest)
    assert all(group.done for group in (up, thin, back, back2, early, rest))


def post_kernel(rows, cols, *refs):
    gbig, grest, gfin, tout, aux = refs[:5]
    weights, far_moments = refs[5:11], refs[11:23]
    far, loss_out, size_out = refs[23:41], refs[41], refs[42]
    new, moments = refs[43:61], refs[61:73]
    lk, wrel, g_a, g_small, g_rel, store_sem, load_sem = refs[73:]
    loads = [
        pltpu.make_async_copy(source, near, load_sem.at[place])
        for place, (source, near) in enumerate(zip(far_moments, moments))
    ]
    for place in (2, 8, 1, 7, 3, 9, 4, 10, 0, 6, 5, 11):
        loads[place].start()
    means, squares = moments[0:6], moments[6:12]
    lookup, w_a, w_c, w_r, w_p, scal = weights
    ROWS, bases = layout(rows, cols)

    def big(begin, count):
        part = gbig[begin // 8 : (begin + count) // 8].astype(F32)
        return part.reshape(count, 128)

    def exact(begin, count):
        if begin >= bases[LAST]:
            return gfin[begin - bases[LAST] : begin - bases[LAST] + count, :]
        return grest[begin - bases[LOW_SHARE] : begin - bases[LOW_SHARE] + count, :]

    lk[...] = jnp.zeros((AP, WA), F32)
    lk[0:LETTERS, :] = lookup[...]
    wrel[...] = jnp.zeros((RP, WP), F32)
    wrel[0:NREL, :] = w_r[UP : UP + NREL, :]

    def table(begin):
        both = jnp.concatenate([exact(begin, TR), exact(begin + TR, TR)], axis=1)
        return jnp.concatenate([both, jnp.zeros((AP - TR, WA), F32)], axis=0)

    dscore = table(ROWS.score)
    dvalue, dgate, dstart = [table(ROWS.tabs + 2 * TR * place) for place in range(3)]
    mapped = tout[...]
    t_q = mapped[:, 0:WA] * HEAD ** (-0.5)
    t_k = mapped[:, WA : 2 * WA].astype(BF16).astype(F32)
    t_g = jax.nn.sigmoid(mapped[:, 3 * WA :])
    square = head_mask(WA, AP)
    key_block = jnp.where(square, jnp.concatenate([t_k] * HEADS, axis=0), 0.0).astype(BF16)
    dq = mm2(dscore, key_block) * HEAD ** (-0.5)
    dk = jnp.where(square, mm3(dscore, t_q, TN), 0.0)
    dk = jnp.sum(dk.reshape(HEADS, AP, WA), axis=0)
    dg = dgate * (t_g * (1.0 - t_g))
    dmapped = jnp.concatenate([dq, dk, dvalue, dg], axis=1)
    unit0, scale0 = norm(lk[...])
    gain_row = scal[0:WA].reshape(1, WA)
    g_a[...] = mm3(dmapped, unit0 * gain_row, TN)
    dnormed = mm3(dmapped, w_a[0 : 4 * WA, :])
    dgain_row = colsum(dnormed * unit0)
    g_lookup = dstart + norm_back(dnormed * gain_row, unit0, scale0)

    unit_r, scale_r = norm(wrel[...])
    gain_rel = scal[768:896].reshape(1, WP)
    dtable = exact(ROWS.bias, 8)
    g_bias = mm3(dtable, unit_r * gain_rel)
    dnormed = mm3(dtable, w_p[768:776, :], TN)
    dgain_rel = colsum(dnormed * unit_r)
    g_rel[...] = exact(ROWS.rel, 72) + norm_back(
        dnormed * gain_rel, unit_r, scale_r
    )[0:72]

    base = ROWS.small
    g_small[0:WA] = dgain_row.reshape(WA)
    for place, row in ((256, 0), (384, 1), (512, 2), (640, 3), (896, 4), (1024, 5), (1152, 6)):
        g_small[place : place + 128] = exact(base + row, 1).reshape(128)
    g_small[768:896] = dgain_rel.reshape(128)
    lane = iota((1, 128), 1)
    tail = jnp.where(lane < 87, exact(base + 7, 1), 0.0)
    g_small[1280:1408] = tail.reshape(128)

    rel_row = iota((72, 128), 0)
    squares_sum = jnp.zeros((1, 1), F32)
    for begin, count in (
        (ROWS.up, 2 * UP),
        (ROWS.tri, 768),
        (ROWS.o, 2 * WA),
        (ROWS.back, 2 * UP),
    ):
        part = big(begin, count)
        squares_sum = squares_sum + total_of(part * part)
    for part in (
        g_a[...],
        g_lookup[0:LETTERS],
        jnp.where(rel_row < NREL, g_rel[...], 0.0),
        g_bias,
        dgain_row,
        exact(ROWS.outer, UP),
        exact(base, 7),
        exact(ROWS.eh, 87),
        exact(ROWS.eh + 88, 87),
        exact(ROWS.dist, BINS),
        dgain_rel,
        tail,
    ):
        squares_sum = squares_sum + total_of(part * part)
    size = jnp.sqrt(squares_sum)
    scale = jnp.minimum(1.0, CLIP / size)

    def adam(which, where, grad, factor=scale):
        clipped = grad * factor
        weight = weights[which][where]
        moment = B1 * means[which][where] + (1.0 - B1) * clipped
        second = B2 * squares[which][where] + (1.0 - B2) * clipped * clipped
        root = (1.0 - B2**STEP) ** 0.5
        step = (moment * (RATE * root / (1.0 - B1**STEP))) / (
            second * lax.rsqrt(second) + ADAM_EPS * root
        )
        new[3 * which][where] = weight * (1.0 - RATE * DECAY) - step
        new[3 * which + 1][where] = moment
        new[3 * which + 2][where] = second

    every = slice(None)
    stores = []

    def leave(which):
        for place in range(3 * which, 3 * which + 3):
            store = pltpu.make_async_copy(new[place], far[place], store_sem.at[place])
            store.start()
            stores.append(store)

    def ready(which):
        loads[which].wait()
        loads[6 + which].wait()

    ready(2)
    for w in range(2):
        half = slice(128 * w, 128 * w + 128)
        adam(2, (slice(0, WA), half), big(ROWS.o + w * WA, WA))
        adam(2, (slice(WA, WA + UP), half), big(ROWS.back + w * UP, UP))
    leave(2)
    ready(1)
    adam(1, (slice(0, 4 * WA), every), g_a[...])
    for w in range(2):
        half = slice(128 * w, 128 * w + 128)
        adam(1, (slice(1024, 2048), half), big(ROWS.up + w * UP, UP))
        adam(1, (slice(2048, 2135), half), exact(ROWS.eh + w * 88, 87))
    leave(1)
    ready(3)
    adam(3, (slice(0, UP), every), exact(ROWS.outer, UP))
    adam(3, (slice(UP, UP + NREL), every), g_rel[0:NREL, :])
    leave(3)
    ready(4)
    adam(4, (slice(0, 768), every), big(ROWS.tri, 768))
    adam(4, (slice(768, 776), every), g_bias)
    adam(4, (slice(776, 840), every), exact(ROWS.dist, BINS))
    leave(4)
    ready(0)
    adam(0, (every, every), g_lookup[0:LETTERS])
    leave(0)
    ready(5)
    adam(5, (slice(0, 1367),), g_small[0:1367], scale.reshape(1))
    leave(5)

    sums = exact(base + 8, 1)
    loss = sums[:, 0:1] / aux[0:1, 0:1] + sums[:, 1:2] * aux[0:1, 1:2]
    loss_out[0] = loss[0, 0]
    size_out[0] = size[0, 0]
    for store in stores:
        store.wait()


def vmem():
    return pl.BlockSpec(memory_space=pltpu.VMEM)


def per_device(rows, cols, *arrays):
    letters, truth, concealed, existing, ordinals, observed, bins = arrays[:7]

    def turned(group):
        return [w.T if place in (1, 4) else w for place, w in enumerate(group)]

    weights, means, squares = turned(arrays[7:13]), turned(arrays[13:19]), turned(arrays[19:25])
    plan = scratch_plan(rows, cols)
    bases = layout(rows, cols)[1]
    far = pl.BlockSpec(memory_space=pltpu.HBM)
    summed = pl.pallas_call(
        functools.partial(main_kernel, rows, cols, tuple(plan)),
        out_shape=(
            jax.ShapeDtypeStruct((bases[LOW_SHARE] // 8, 8, 128), BF16),
            jax.ShapeDtypeStruct((bases[LAST] - bases[LOW_SHARE], 128), F32),
            jax.ShapeDtypeStruct((bases[-1] - bases[LAST], 128), F32),
            jax.ShapeDtypeStruct((AP, 4 * WA), F32),
            jax.ShapeDtypeStruct((8, 128), F32),
        ),
        in_specs=[far] * OPERANDS,
        out_specs=tuple([vmem()] * 5),
        scratch_shapes=[pltpu.VMEM(dims, kind) for dims, kind in plan.values()]
        + [
            pltpu.SemaphoreType.DMA((rows - 1,)),
            pltpu.SemaphoreType.DMA((PHASES - 1, rows - 1)),
            pltpu.SemaphoreType.DMA((cols - 1,)),
            pltpu.SemaphoreType.DMA((PHASES, cols - 1)),
            pltpu.SemaphoreType.DMA((3, 2)),
            pltpu.SemaphoreType.DMA((LAST, max(rows // 2, cols) - 1)),
            pltpu.SemaphoreType.DMA((LAST, 2 * cols + rows - 2)),
            pltpu.SemaphoreType.DMA((OPERANDS,)),
        ],
        compiler_params=pltpu.CompilerParams(
            collective_id=0, has_side_effects=True, vmem_limit_bytes=MAIN_VMEM
        ),
    )(
        *[
            pltpu.with_memory_space_constraint(value, pltpu.HBM)
            for value in (
                jnp.swapaxes(letters, 1, 2),
                jnp.swapaxes(truth, 1, 2),
                jnp.swapaxes(concealed, 1, 2),
                existing,
                ordinals,
                observed,
                bins,
                *weights,
            )
        ]
    )

    shapes = []
    for w in weights:
        shapes += [jax.ShapeDtypeStruct(w.shape, F32)] * 3
    one = jax.ShapeDtypeStruct((1,), F32)
    scalar = pl.BlockSpec(memory_space=pltpu.SMEM)
    result = pl.pallas_call(
        functools.partial(post_kernel, rows, cols),
        out_shape=tuple(shapes) + (one, one),
        in_specs=[vmem()] * 11 + [far] * 12,
        out_specs=tuple([far] * 18) + (scalar, scalar),
        scratch_shapes=[pltpu.VMEM(shape.shape, F32) for shape in shapes]
        + [pltpu.VMEM(value.shape, F32) for value in (*means, *squares)]
        + [
            pltpu.VMEM((AP, WA), F32),
            pltpu.VMEM((RP, WP), F32),
            pltpu.VMEM((4 * WA, WA), F32),
            pltpu.VMEM((1408,), F32),
            pltpu.VMEM((72, 128), F32),
            pltpu.SemaphoreType.DMA((18,)),
            pltpu.SemaphoreType.DMA((12,)),
        ],
        compiler_params=pltpu.CompilerParams(vmem_limit_bytes=POST_VMEM),
    )(
        *summed,
        *weights,
        *[pltpu.with_memory_space_constraint(value, pltpu.HBM) for value in (*means, *squares)],
    )
    outs = [result[18].reshape(()), result[19].reshape(())]
    for place, value in enumerate(result[:18]):
        outs.append(value.T if place // 3 in (1, 4) else value)
    return tuple(outs)


def solution(mesh):
    rows, cols = mesh.shape[ROW], mesh.shape[COL]
    placed = (
        (P(None, COL, ROW),) * 3 + (P(),) * 3 + (P(None, ROW, COL),) + (P(),) * 18
    )
    return jax.shard_map(
        functools.partial(per_device, rows, cols),
        mesh=mesh,
        in_specs=placed,
        out_specs=(P(),) * 20,
        check_vma=False,
    )
```

```python
import functools
from types import SimpleNamespace

import jax
import jax.numpy as jnp
from jax import lax
from jax.experimental import pallas as pl
from jax.experimental.pallas import tpu as pltpu
from jax.sharding import PartitionSpec as P

F32, BF16 = jnp.float32, jnp.bfloat16
MESH = pl.DeviceIdType.MESH
ROW, COL, QUAD = "row", "col", "quad"
CORE, PLANE, Z = "core", "plane", "z"
WA, WP, WO, LETTERS, BINS, REACH, HEADS, HEAD = 256, 128, 32, 23, 64, 32, 8, 32
UP = 1024
NREL = 2 * REACH + 1
AP = 32
TR = 24
RP = 128
EPS = 1e-05
NB, NS, NI, NJ = 2, 16, 8, 16
NM = NB * NS * NI
NP = 2 * NI * NJ
BS = NB * NS
BI = NB * NI
DS = WO * NS
FORWARD, TOGETHER = 16, 8
CLIP, RATE, B1, B2, STEP, ADAM_EPS, DECAY = 0.02, 0.05, 0.9, 0.999, 4, 1e-08, 0.01

MAIN_VMEM, POST_VMEM = 44 * 2**20, 30 * 2**20

NN = (((1,), (0,)), ((), ()))
NT = (((1,), (1,)), ((), ()))
TN = (((0,), (0,)), ((), ()))

GROUPS = (
    dict(up=2 * UP),
    dict(tri=5 * WP, out=WP, o=2 * WA),
    dict(back=UP),
    dict(back2=UP),
    dict(outer=WO * WO),
    dict(eh=176, tabs=6 * TR, dist=BINS, rel=72, small=16),
    dict(score=2 * TR, bias=8),
)
LAST = len(GROUPS) - 1
LOW_SUM = 2
LOW_SHARE = 4


def layout(rows, cols):
    places, bases, begin = {}, [], 0
    for number, group in enumerate(GROUPS):
        bases.append(begin)
        for name, count in group.items():
            places[name] = begin
            begin += count
        size = 16 * cols if number == LAST else 8 * rows * cols
        begin = bases[-1] - (bases[-1] - begin) // size * size
    return SimpleNamespace(**places), bases + [begin]


def mm(a, b, dims=NN):
    return lax.dot_general(a, b, dims, preferred_element_type=F32)


def split2(x):
    high = x.astype(BF16)
    return high, (x - high.astype(F32)).astype(BF16)


def split3(x):
    high = x.astype(BF16)
    rest = x - high.astype(F32)
    middle = rest.astype(BF16)
    return high, middle, (rest - middle.astype(F32)).astype(BF16)


def mm3(a, b, dims=NN):
    ah, al = split2(a)
    bh, bl = split2(b)
    return mm(ah, bh, dims) + (mm(al, bh, dims) + mm(ah, bl, dims))


def mm6(a, b, dims=NN):
    ah, am, al = split3(a)
    bh, bm, bl = split3(b)
    low = mm(al, bh, dims) + (mm(am, bm, dims) + mm(ah, bl, dims))
    return mm(ah, bh, dims) + ((mm(am, bh, dims) + mm(ah, bm, dims)) + low)


def mm2(a, exact, dims=NN):
    ah, al = split2(a)
    return mm(ah, exact, dims) + mm(al, exact, dims)


def mm2r(exact, b, dims=NN):
    bh, bl = split2(b)
    return mm(exact, bh, dims) + mm(exact, bl, dims)


def mm3r(exact, b, dims=NN):
    bh, bm, bl = split3(b)
    return mm(exact, bh, dims) + (mm(exact, bm, dims) + mm(exact, bl, dims))


def norm(x):
    centred = x - jnp.mean(x, axis=-1, keepdims=True)
    scale = lax.rsqrt(jnp.mean(centred * centred, axis=-1, keepdims=True) + EPS)
    return centred * scale, scale


def norm_back(grad, unit, scale):
    return scale * (
        grad
        - jnp.mean(grad, axis=-1, keepdims=True)
        - unit * jnp.mean(grad * unit, axis=-1, keepdims=True)
    )


def iota(shape, axis):
    return lax.broadcasted_iota(jnp.int32, shape, axis)


def head_mask(rows, per_row):
    shape = (rows, WA)
    return iota(shape, 0) // per_row == iota(shape, 1) // HEAD


def colsum(x):
    return jnp.sum(x, axis=0, keepdims=True)


def total_of(x):
    return jnp.sum(jnp.sum(x, axis=1, keepdims=True), axis=0, keepdims=True)


def scratch_plan(rows, cols):
    length = rows * NI
    bases = layout(rows, cols)[1]
    final = bases[-1] - bases[LAST]
    return dict(
        lk=((AP, WA), F32),
        weh=((128, WA), F32),
        wbd=((128, WP), F32),
        seqw=((NM, 1), F32),
        lmask=((NM, 1), F32),
        truth=((NM, 1), F32),
        pmask=((NP, 1), F32),
        offset=((NP, 1), F32),
        codes=((BI, length), F32),
        sites=((8, length), F32),
        wrel=((RP, WP), F32),
        tail=((8, 128), F32),
        kb=((WA, WA), BF16),
        vb=((WA, WA), BF16),
        amat=((BS, NI, WA), F32),
        pam=((BS, NI, WA), F32),
        hm=((64, WA), F32),
        letx=((128, length), F32),
        biash=((NB, 64, length), F32),
        prob=((BS, 64, length), F32),
        sg=((NM, WA), F32),
        att=((NM, WA), F32),
        xh1=((NM, WA), F32),
        r1=((NM, 1), F32),
        hid=((NM, UP), F32),
        rep=((NM, WA), F32),
        xh2=((NM, WA), F32),
        r2=((NM, 1), F32),
        dlog=((NM, 128), F32),
        left3=((NB, NI * NS, 128), BF16),
        mhi=((BI, DS, WP), BF16),
        mlo=((BI, DS, WP), BF16),
        rall=((length, DS), BF16),
        prep=((NP, WP), F32),
        xh3=((NP, WP), F32),
        r3=((NP, 1), F32),
        proj=((NP, 5 * WP), F32),
        le=((BI * NJ, WP), F32),
        re=((length * NJ, WP), F32),
        dm=((BI * length, WP), F32),
        gl=((BI, NJ, WP), F32),
        dr=((length, DS), F32),
        dmid=((NM, WA), F32),
        dbias=((NB, 64, length), F32),
        da=((BS, NI, WA), F32),
        dpam=((BS, NI, WA), F32),
        dtab=((BI, 16, RP), F32),
        dn=((NM, WA), F32),
        sum8=((8, WA), F32),
        grad=((bases[-1], 128), F32),
        lets=((8, 128), F32),
        letr=((rows, 8, 128), F32),
        cnts=((8, 128), F32),
        cntr=((cols, 8, 128), F32),
        rs=((NB, NI, DS), BF16),
        rr=((rows, NI, DS), BF16),
        lr=((2, NI * NS, 128), BF16),
        tgr=((2, NI, NJ), jnp.int32),
        os=((cols, BI, NJ, WP), BF16),
        orr=((cols, BI, NJ, WP), BF16),
        er=((rows // 2, BI, NJ, WP), BF16),
        ts=((cols, BI, NJ, WP), BF16),
        tr=((cols, BI, NJ, WP), BF16),
        ds=((BI, NJ, WP), BF16),
        dsr=((cols, BI, NJ, WP), BF16),
        gs=((rows // 2, BI, NJ, WP), BF16),
        gr=((rows // 2, BI, NJ, WP), BF16),
        qs=((BI, NJ, WP), BF16),
        qr=((cols, BI, NJ, WP), BF16),
        us=((rows, NI, DS), BF16),
        ur=((rows, NI, DS), BF16),
        dl=((2, NI * NS, 128), BF16),
        dlr=((NB, NI * NS, 128), BF16),
        arx=((bases[LAST], 128), F32),
        lows=((bases[LOW_SUM] // 8, 8, 128), BF16),
        lowr=((bases[LOW_SUM] // 8, 8, 128), BF16),
        fc=((cols, final // cols, 128), F32),
        fp=((final // cols, 128), F32),
        fr=((rows, final // cols, 128), F32),
        letters=((NB, NI, NS), jnp.int32),
        truths=((NB, NI, NS), jnp.int32),
        concealed=((NB, NI, NS), jnp.int32),
        existing=((NB, cols * NS), jnp.int32),
        ordinals=((NB, length), jnp.int32),
        observed=((NB, length), jnp.int32),
        targets=((NB, NI, NJ), jnp.int32),
        lookup=((LETTERS, WA), F32),
        w_a=((2135, WA), F32),
        w_c=((WA + UP, WA), F32),
        w_r=((UP + NREL, WP), F32),
        w_p=((840, WP), F32),
        scal=((1367,), F32),
    )


OPERANDS = 13


LET, RIGHT, EDGE, GEDGE, GRIGHT, SUM_ROW = range(6)
CNT, OUTER, TRI, GMIX, GOUTER, SUM_COL, SHARE_COL = range(7)
PHASES = 7


def main_kernel(rows, cols, names, *refs):
    operands = refs[:OPERANDS]
    gbig, grest, gfin, tout, aux = refs[OPERANDS : OPERANDS + 5]
    s = SimpleNamespace(**dict(zip(names, refs[OPERANDS + 5 : -8])))
    row_send, row_recv, col_send, col_recv, pair_sem, sum_send, sum_recv, load_sem = refs[-8:]
    held = refs[OPERANDS + 5 : -8][-OPERANDS:]
    loads = [
        pltpu.make_async_copy(far, near, load_sem.at[place])
        for place, (far, near) in enumerate(zip(operands, held))
    ]
    for load in loads:
        load.start()
    letters, truths, hidden_sites, existing, ordinals, observed, targets = held[:7]
    lookup, w_a, w_c, w_r, w_p, scal = held[7:]
    ROWS, bases = layout(rows, cols)
    length = rows * NI
    me_r, me_c = lax.axis_index(ROW), lax.axis_index(COL)

    barrier = pltpu.get_barrier_semaphore()
    for step in range(1, rows):
        pl.semaphore_signal(
            barrier,
            inc=1,
            device_id={ROW: lax.rem(me_r + step, rows), COL: me_c},
            device_id_type=MESH,
        )
    for step in range(1, cols):
        pl.semaphore_signal(
            barrier,
            inc=1,
            device_id={ROW: me_r, COL: lax.rem(me_c + step, cols)},
            device_id_type=MESH,
        )
    quads = rows // 2
    side, quad = me_r // quads, me_r % quads

    def to_partner(number, source, target):
        return pltpu.make_async_remote_copy(
            src_ref=source,
            dst_ref=target,
            send_sem=pair_sem.at[number, 0],
            recv_sem=pair_sem.at[number, 1],
            device_id={ROW: (1 - side) * quads + quad, COL: me_c},
            device_id_type=MESH,
        )

    def swap(number, source, target):
        out = to_partner(number, source.at[1 - side], target.at[side])
        out.start()
        return out, to_partner(number, source.at[1 - side], target.at[1 - side])

    def exchange(along, phase, source, target):
        if along == ROW:
            count, me, number = rows, me_r, phase
            send, recv = row_send, row_recv
        elif along == QUAD:
            count, me, number = quads, quad, phase
            send, recv = row_send, row_recv
        else:
            count, me, number = cols, me_c, phase
            send, recv = col_send, col_recv
        copies = []
        for step in range(1, count):
            peer = lax.rem(me + step, count)
            origin = lax.rem(me + (count - step), count)
            where = {ROW: me_r, COL: peer}
            if along == ROW:
                where = {ROW: peer, COL: me_c}
            elif along == QUAD:
                where = {ROW: side * quads + peer, COL: me_c}
            out = pltpu.make_async_remote_copy(
                src_ref=source(peer),
                dst_ref=target(me),
                send_sem=send.at[step - 1],
                recv_sem=recv.at[number, step - 1],
                device_id=where,
                device_id_type=MESH,
            )
            out.start()
            arriving = pltpu.make_async_remote_copy(
                src_ref=source(peer),
                dst_ref=target(origin),
                send_sem=send.at[step - 1],
                recv_sem=recv.at[number, step - 1],
                device_id=where,
                device_id_type=MESH,
            )
            copies.append((out, arriving))
        return copies

    def finish(copies):
        for out, arriving in copies:
            out.wait_send()
            arriving.wait_recv()

    for load in loads[:7]:
        load.wait()
    here = existing[...].astype(F32)
    sites = observed[...].astype(F32)
    numbers = ordinals[...].astype(F32)

    def by_protein(values, count, each):
        wide = (count, values.shape[1])
        return jnp.where(iota(wide, 0) // each == 0, values[0:1], values[1:2])

    def at_lane(values, lanes):
        return jnp.sum(jnp.where(iota(values.shape, 1) == lanes, values, 0.0), axis=1, keepdims=True)

    row_m, row_p = iota((NM, 1), 0), iota((NP, 1), 0)
    seq_m, res_m = (row_m // NI) % NS, row_m % NI
    spread_m = jnp.where(
        iota((NM, BI), 1) == (iota((NM, BI), 0) // (NI * NS)) * NI + iota((NM, BI), 0) % NI, 1.0, 0.0
    ).astype(BF16)

    def column_m(values):
        wide = mm(spread_m, values[...].reshape(BI, NS).astype(F32).astype(BF16))
        return at_lane(wide, seq_m)

    seq_weight = at_lane(by_protein(here, NM, NI * NS), me_c * NS + seq_m)
    letter = column_m(letters)
    loss_mask = column_m(hidden_sites) * seq_weight
    s.seqw[...] = seq_weight
    s.lmask[...] = loss_mask
    s.truth[...] = column_m(truths)
    s.tgr[side] = targets[side]

    s.lets[...] = jnp.where(
        (iota((NI, 128), 0) == 0) & (iota((NI, 128), 1) == BS), total_of(loss_mask), 0.0
    )
    for b in range(NB):
        s.lets[:, b * NS : (b + 1) * NS] = letters[b].astype(F32)
    s.letr[me_r] = s.lets[...]
    pl.semaphore_wait(barrier, rows + cols - 2)
    flight = exchange(ROW, LET, lambda p: s.lets, lambda p: s.letr.at[p])
    flight.append(swap(0, targets, s.tgr))
    near = row_p // NJ
    first = (quad + quads * (near // NI)) * NI + near % NI
    second = me_c * NJ + row_p % NJ

    def of_side(values):
        return jnp.where(side == 0, values[0:1], values[1:2])

    sites_p = jnp.broadcast_to(of_side(sites), (NP, length))
    numbers_p = jnp.broadcast_to(of_side(numbers), (NP, length))
    s.pmask[...] = at_lane(sites_p, first) * at_lane(sites_p, second)
    s.offset[...] = (
        jnp.clip(at_lane(numbers_p, first) - at_lane(numbers_p, second), -REACH, REACH) + REACH
    )
    numbers_b = by_protein(numbers, BI, NI)
    own = at_lane(numbers_b, me_r * NI + iota((BI, 1), 0) % NI)
    s.codes[...] = jnp.clip(own - numbers_b, -REACH, REACH) + REACH
    s.sites[...] = jnp.zeros((8, length), F32)
    s.sites[0:NB, :] = sites
    inv_all = 1.0 / (jnp.sum(here, axis=1, keepdims=True) + 1.0)
    inv_count = of_side(inv_all)
    per_protein = jnp.sum(sites, axis=1, keepdims=True)
    inv_dist = 1.0 / jnp.maximum(colsum(per_protein * per_protein), 1.0)

    for load in loads[7:]:
        load.wait()

    def gain(begin, width):
        return scal[begin : begin + width].reshape(1, width)

    gain_row, gain_trans, gain_outer = gain(0, WA), gain(256, WA), gain(512, WA)
    gain_rel, gain_pair, gain_mixed = gain(768, WP), gain(896, WP), gain(1024, WP)
    bias_outer = gain(1152, WP)
    s.lk[...] = jnp.zeros((AP, WA), F32)
    s.lk[0:LETTERS, :] = lookup[...]
    s.weh[...] = jnp.zeros((128, WA), F32)
    s.weh[0:87, :] = w_a[2048:2135, :]
    s.wbd[...] = jnp.zeros((128, WP), F32)
    s.wbd[0:72, :] = w_p[768:840, :]
    s.wrel[...] = jnp.zeros((RP, WP), F32)
    s.wrel[0:NREL, :] = w_r[UP : UP + NREL, :]
    s.tail[...] = jnp.zeros((8, 128), F32)
    s.tail[0:1, 0:87] = scal[1280:1367].reshape(1, 87)

    table = s.lk[...]
    unit0, _ = norm(table)
    mapped = mm6(unit0 * gain_row, w_a[0 : 4 * WA, :], NT)
    tout[...] = mapped
    t_q = mapped[:, 0:WA] * HEAD ** (-0.5)
    t_k = mapped[:, WA : 2 * WA].astype(BF16).astype(F32)
    t_v = mapped[:, 2 * WA : 3 * WA].astype(BF16).astype(F32)
    t_g = jax.nn.sigmoid(mapped[:, 3 * WA :])
    square = head_mask(WA, AP)
    key_block = jnp.where(square, jnp.concatenate([t_k] * HEADS, axis=0), 0.0).astype(BF16)
    s.vb[...] = jnp.where(square, jnp.concatenate([t_v] * HEADS, axis=0), 0.0).astype(BF16)
    stacked = mm(jnp.concatenate(split3(t_q), axis=0), key_block, NT)
    score_table = stacked[0:AP] + (stacked[AP : 2 * AP] + stacked[2 * AP :])
    s.hm[...] = jnp.where(head_mask(64, NI), 1.0, 0.0)

    letter = letter.astype(jnp.int32)
    triple = jnp.where(
        (iota((NM, 3 * AP), 1) % AP) == letter, 1.0, 0.0
    ).astype(BF16)

    def chosen(values):
        return mm(triple, jnp.concatenate(split3(values), axis=0))

    s.amat[...] = chosen(score_table).reshape(BS, NI, WA)
    start = chosen(table)
    s.sg[...] = chosen(t_g)

    unit_r, _ = norm(s.wrel[...])
    bias_table = mm3(s.wbd[0:8, :], unit_r * gain_rel, NT)
    bias_parts = jnp.concatenate(split3(bias_table), axis=0)

    def codes(index):
        return jnp.where(
            iota((RP, length), 0) == s.codes[index : index + 1, :].astype(jnp.int32), 1.0, 0.0
        ).astype(BF16)

    for b in range(NB):
        for i in range(NI):
            part = mm(bias_parts, codes(b * NI + i))
            part = part[0:8] + (part[8:16] + part[16:24])
            for h in range(HEADS):
                s.biash[b, h * NI + i : h * NI + i + 1, :] = part[h : h + 1, :]

    finish(flight)
    letters_all = s.letr[...].reshape(length, 128).T
    s.letx[...] = letters_all
    s.cnts[...] = jnp.broadcast_to(
        jnp.sum(letters_all[BS : BS + 1, :], axis=1, keepdims=True), (8, 128)
    )
    s.cntr[me_c] = s.cnts[...]
    count_flight = exchange(COL, CNT, lambda p: s.cnts, lambda p: s.cntr.at[p])

    def letter_codes(bs):
        row = s.letx[pl.ds(bs, 1), :].astype(jnp.int32)
        one = jnp.where(iota((AP, length), 0) == row, 1.0, 0.0)
        return jnp.concatenate([one] * HEADS, axis=0).astype(BF16)

    def spread(value):
        wide = jnp.broadcast_to(value[None], (HEADS, NI, WA)).reshape(64, WA)
        return wide * s.hm[...]

    def gather_heads(value):
        return jnp.sum((value * s.hm[...]).reshape(HEADS, NI, WA), axis=0)

    for b in range(NB):
        key_mask = s.sites[b : b + 1, :]

        @pl.loop(0, NS // FORWARD)
        def _(q):
            for part in range(FORWARD):
                bs = b * NS + q * FORWARD + part
                code = letter_codes(bs)
                wide = [spread(p.astype(F32)).astype(BF16) for p in split2(s.amat[bs])]
                raw = mm(jnp.concatenate(wide, axis=0), code)
                scores = (raw[0:64] + raw[64:128]) + s.biash[b]
                scores = jnp.where(key_mask > 0, scores, -1000000000.0)
                power = jnp.exp(scores - jnp.max(scores, axis=-1, keepdims=True))
                weight = power / jnp.sum(power, axis=-1, keepdims=True)
                s.prob[bs] = weight
                picked = mm(jnp.concatenate(split2(weight), axis=0), code, NT)
                s.pam[bs] = gather_heads(picked[0:64] + picked[64:128])

    att = mm2(s.pam[...].reshape(NM, WA), s.vb[...])
    s.att[...] = att
    mid = start + mm3(s.sg[...] * att, w_c[0:WA, :])
    unit1, scale1 = norm(mid)
    s.xh1[...] = unit1
    s.r1[...] = scale1
    hidden = jnp.maximum(mm3(unit1 * gain_trans, w_a[4 * WA : 4 * WA + UP, :], NT), 0.0)
    s.hid[...] = hidden
    rep = mid + mm3(hidden, w_c[WA:, :])
    s.rep[...] = rep
    unit2, scale2 = norm(rep)
    s.xh2[...] = unit2
    s.r2[...] = scale2
    seq_weight = s.seqw[...]
    lane = iota((NM, 128), 1)
    edges = mm3(unit2 * gain_outer, s.weh[...], NT) * seq_weight

    right = jnp.where((lane >= 32) & (lane < 64), edges, 0.0).astype(BF16)
    spot = iota((128, DS), 0)
    repeat = jnp.where(spot - 32 == iota((128, DS), 1) // NS, 1.0, 0.0)
    repeat = jnp.where((spot >= 32) & (spot < 64), repeat, 0.0).astype(BF16)
    wide = mm(right, repeat)
    own_seq = (iota((NM, DS), 0) // NI) % NS == iota((NM, DS), 1) % NS
    wide = jnp.sum(jnp.where(own_seq, wide, 0.0).reshape(NB, NS, NI, DS), axis=1)
    s.rs[...] = wide.astype(BF16)
    s.rr[me_r] = s.rs[side]
    flight = exchange(ROW, RIGHT, lambda p: s.rs.at[p // quads], lambda p: s.rr.at[p])

    order_to = (iota((NM, NM), 0) // (NI * NS) == iota((NM, NM), 1) // (NI * NS)) & (
        (iota((NM, NM), 0) // NS) % NI == iota((NM, NM), 1) % NI
    )
    order_to = order_to & (iota((NM, NM), 0) % NS == (iota((NM, NM), 1) // NI) % NS)
    order = jnp.where(order_to, 1.0, 0.0).astype(BF16)
    left = mm3r(order, jnp.where(lane < 32, edges, 0.0))
    high, low = split2(left)
    high32, low32 = high.astype(F32), low.astype(F32)
    left3 = high32 + pltpu.roll(low32, 32, 1) + pltpu.roll(high32, 64, 1)
    s.left3[...] = left3.astype(BF16).reshape(NB, NI * NS, 128)
    s.lr[side] = s.left3[side]
    flight.append(swap(1, s.left3, s.lr))

    finish(count_flight)
    masked = jnp.maximum(jnp.sum(s.cntr[...], axis=0)[0:1, 0:1], 1.0)
    logits = mm3(rep, s.weh[...], NT) + s.tail[0:1, :]
    valid = (lane >= 64) & (lane < 64 + LETTERS)
    top = jnp.max(jnp.where(valid, logits, -3e38), axis=-1, keepdims=True)
    power = jnp.where(valid, jnp.exp(jnp.where(valid, logits, top) - top), 0.0)
    whole = jnp.sum(power, axis=-1, keepdims=True)
    truth = lane - 64 == s.truth[...].astype(jnp.int32)
    truth = truth & valid
    picked = jnp.sum(jnp.where(truth, logits, 0.0), axis=-1, keepdims=True)
    loss_mask = s.lmask[...]
    msa_sum = colsum((jnp.log(whole) + top - picked) * loss_mask)
    s.dlog[...] = (power / whole - jnp.where(truth, 1.0, 0.0)) * (loss_mask / masked)

    def outer_weight(d):
        return w_r[pl.ds(d, WO, stride=WO), :]

    def expand(block):
        for pair in range(WO // 2):
            both = jnp.concatenate([outer_weight(2 * pair), outer_weight(2 * pair + 1)], axis=1)
            wh, wl = split2(both)
            made = mm(s.lr[block][:, 0:96], jnp.concatenate([wh, wh, wl], axis=0))
            for half in range(2):
                d = 2 * pair + half
                mh, ml = split2(made[:, half * WP : (half + 1) * WP].reshape(NI, NS, WP))
                s.mhi[pl.ds(block * NI, NI), d * NS : (d + 1) * NS, :] = mh
                s.mlo[pl.ds(block * NI, NI), d * NS : (d + 1) * NS, :] = ml

    expand(side)
    finish(flight)
    expand(1 - side)
    s.rall[...] = s.rr[...].astype(F32).reshape(length, DS).astype(BF16)

    @pl.loop(0, BI // TOGETHER)
    def _(q):
        for part in range(TOGETHER):
            i = q * TOGETHER + part
            block = mm(s.rall[...], s.mhi[i]) + mm(s.rall[...], s.mlo[i])
            block = block * inv_count
            for c in range(cols):
                s.os[c, i] = block[c * NJ : (c + 1) * NJ].astype(BF16)

    s.orr[me_c] = s.os[me_c]
    finish(exchange(COL, OUTER, lambda p: s.os.at[p], lambda p: s.orr.at[p]))

    pair_lane = iota((NP, 128), 1)
    offset = s.offset[...].astype(jnp.int32)
    pair_codes = jnp.where(pair_lane == offset, 1.0, 0.0).astype(BF16)
    outer = s.orr[0].astype(F32)
    for c in range(1, cols):
        outer = outer + s.orr[c].astype(F32)
    pair_rep = (mm3r(pair_codes, s.wrel[...]) + outer.reshape(NP, WP)) + bias_outer
    s.prep[...] = pair_rep
    unit3, scale3 = norm(pair_rep)
    s.xh3[...] = unit3
    s.r3[...] = scale3
    proj = mm3(unit3 * gain_pair, w_p[0 : 5 * WP, :], NT)
    pair_mask = s.pmask[...]
    sig1 = jax.nn.sigmoid(proj[:, WP : 2 * WP])
    sig2 = jax.nn.sigmoid(proj[:, 3 * WP : 4 * WP])
    sig3 = jax.nn.sigmoid(proj[:, 4 * WP :])
    s.proj[:, 0 : WP] = proj[:, 0:WP]
    s.proj[:, WP : 2 * WP] = sig1
    s.proj[:, 2 * WP : 3 * WP] = proj[:, 2 * WP : 3 * WP]
    s.proj[:, 3 * WP : 4 * WP] = sig2
    s.proj[:, 4 * WP :] = sig3
    s.le[...] = sig1 * proj[:, 0:WP] * pair_mask
    right_edge = (sig2 * proj[:, 2 * WP : 3 * WP] * pair_mask).astype(BF16)
    s.er[quad] = right_edge.reshape(BI, NJ, WP)
    finish(exchange(QUAD, EDGE, lambda p: s.er.at[quad], lambda p: s.er.at[p]))
    for q in range(quads):
        for block in range(2):
            begin = (q + quads * block) * NI * NJ
            s.re[begin : begin + NI * NJ, :] = (
                s.er[q, block * NI : (block + 1) * NI].astype(F32).reshape(NI * NJ, WP)
            )

    @pl.loop(0, BI)
    def _(i):
        for c in range(cols):
            block = jnp.zeros((NJ, WP), F32)
            for k in range(NJ):
                other = s.re[pl.ds(c * NJ * NJ + k, NJ, stride=NJ), :]
                block = block + s.le[pl.ds(i * NJ + k, 1), :] * other
            s.ts[c, i] = block.astype(BF16)

    s.tr[me_c] = s.ts[me_c]
    finish(exchange(COL, TRI, lambda p: s.ts.at[p], lambda p: s.tr.at[p]))

    mixed = s.tr[0].astype(F32)
    for c in range(1, cols):
        mixed = mixed + s.tr[c].astype(F32)
    unit4, scale4 = norm(mixed.reshape(NP, WP))
    w_out = w_p[5 * WP : 6 * WP, :]
    moved = mm3(unit4 * gain_mixed, w_out, NT)
    sig3 = s.proj[:, 4 * WP :]
    pair_out = s.prep[...] + sig3 * moved
    bins = mm3(pair_out, s.wbd[...], NT) + pltpu.roll(
        jnp.where(iota((8, 128), 1) < BINS, s.tail[...], 0.0), 8, 1
    )[0:1]
    valid = (pair_lane >= 8) & (pair_lane < 8 + BINS)
    top = jnp.max(jnp.where(valid, bins, -3e38), axis=-1, keepdims=True)
    power = jnp.where(valid, jnp.exp(jnp.where(valid, bins, top) - top), 0.0)
    whole = jnp.sum(power, axis=-1, keepdims=True)
    spread_p = jnp.where(iota((NP, BI), 1) == iota((NP, BI), 0) // NJ, 1.0, 0.0).astype(BF16)
    target = at_lane(
        mm(spread_p, s.tgr[...].reshape(BI, NJ).astype(F32).astype(BF16)), row_p % NJ
    )
    truth = (pair_lane - 8 == target.astype(jnp.int32)) & valid
    picked = jnp.sum(jnp.where(truth, bins, 0.0), axis=-1, keepdims=True)
    dist_sum = colsum((jnp.log(whole) + top - picked) * pair_mask)
    dbins = (power / whole - jnp.where(truth, 1.0, 0.0)) * (pair_mask * inv_dist)

    def put(place, value, skip=0):
        base = place + skip
        height, width = value.shape
        for w in range(width // 128):
            s.grad[base + w * height : base + (w + 1) * height, :] = value[
                :, w * 128 : (w + 1) * 128
            ]

    planes, lines = cols, rows // 2
    sizes = {CORE: 2, PLANE: planes, Z: lines}
    places = {CORE: me_c % 2, PLANE: me_c // 2 * 2 + me_r % 2, Z: me_r // 2}

    def line_peer(axis, place):
        if axis == CORE:
            return {ROW: me_r, COL: me_c // 2 * 2 + place}
        if axis == PLANE:
            return {ROW: me_r // 2 * 2 + place % 2, COL: place // 2 * 2 + me_c % 2}
        return {ROW: place * 2 + me_r % 2, COL: me_c}

    def rows_at(unit, count):
        return pl.ds(pl.multiple_of(unit * 8, 8), count * 8)

    class Sum:
        def __init__(self, number):
            self.number = number
            self.begin = bases[number] // 8
            self.at, self.size = self.begin, (bases[number + 1] - bases[number]) // 8
            self.rx = self.begin
            self.low_sum, self.low_share = number < LOW_SUM, number < LOW_SHARE
            self.stages = [(self.reduce, axis) for axis in (CORE, PLANE, Z)]
            self.stages += [(self.share, axis) for axis in (Z, PLANE, CORE)]
            self.flight, self.after, self.used, self.stored = [], None, 0, False

        @property
        def done(self):
            return not self.stages and not self.flight

        def copies(self, axis, source, target):
            count = sizes[axis]
            for step in range(1, count):
                peer = lax.rem(places[axis] + step, count)
                origin = lax.rem(places[axis] + (count - step), count)
                both = []
                for end in (target(places[axis], step), target(origin, step)):
                    both.append(
                        pltpu.make_async_remote_copy(
                            src_ref=source(peer, step),
                            dst_ref=end,
                            send_sem=sum_send.at[self.number, step - 1],
                            recv_sem=sum_recv.at[self.number, self.used],
                            device_id=line_peer(axis, peer),
                            device_id_type=MESH,
                        )
                    )
                self.used += 1
                both[0].start()
                self.flight.append(both)

        def advance(self):
            finish(self.flight)
            self.flight = []
            if self.after is not None:
                self.after()
                self.after = None
            if self.stages:
                stage, axis = self.stages.pop(0)
                stage(axis)

        def reduce(self, axis):
            count = sizes[axis]
            small = self.size // count
            rx = self.rx

            def slot(buffer, step):
                if self.low_sum:
                    return buffer.at[pl.ds(rx + (step - 1) * small, small)]
                return buffer.at[pl.ds((rx + (step - 1) * small) * 8, small * 8)]

            if self.low_sum:
                for step in range(1, count):
                    peer = lax.rem(places[axis] + step, count)
                    value = s.grad[rows_at(self.at + peer * small, small), :]
                    slot(s.lows, step)[...] = value.reshape(small, 8, 128).astype(BF16)

            def source(peer, step):
                if self.low_sum:
                    return slot(s.lows, step)
                return s.grad.at[rows_at(self.at + peer * small, small)]

            near = s.lowr if self.low_sum else s.arx
            self.copies(axis, source, lambda place, step: slot(near, step))

            def add():
                self.at = self.at + places[axis] * small
                self.size = small
                mine = rows_at(self.at, small)
                value = s.grad[mine, :]
                for step in range(1, count):
                    other = slot(near, step)[...].astype(F32)
                    value = value + other.reshape(small * 8, 128)
                s.grad[mine, :] = value

            self.after = add
            self.rx = rx + (count - 1) * small

        def spot(self, at, size):
            if self.low_share:
                return gbig.at[pl.ds(at, size)]
            return grest.at[rows_at(at - bases[LOW_SHARE] // 8, size)]

        def share(self, axis):
            if not self.stored:
                self.stored = True
                value = s.grad[rows_at(self.at, self.size), :]
                if self.low_share:
                    value = value.reshape(self.size, 8, 128).astype(BF16)
                self.spot(self.at, self.size)[...] = value
            size = self.size
            first = self.at - places[axis] * size
            self.copies(
                axis,
                lambda peer, step: self.spot(first + places[axis] * size, size),
                lambda place, step: self.spot(first + place * size, size),
            )
            self.at, self.size = first, size * sizes[axis]

    up, thin, back, back2, early, rest = [Sum(number) for number in range(LAST)]

    def turn(*groups):
        for group in groups:
            group.advance()

    def column_products(name, place):
        s.sum8[...] = jnp.zeros((8, WA), F32)

        @pl.loop(0, NM // 32)
        def _(q):
            some = pl.ds(pl.multiple_of(q * 32, 32), 32)
            product = s.dn[some, :] * name[some, :]
            s.sum8[...] += jnp.sum(product.reshape(4, 8, WA), axis=0)

        whole = colsum(s.sum8[...])
        for half in range(2):
            s.grad[small + place + half : small + place + half + 1, :] = whole[
                :, 128 * half : 128 * half + 128
            ]

    for begin, end in (
        (ROWS.o + 2 * WA, bases[2]),
        (ROWS.small, bases[LAST]),
        (ROWS.bias, bases[-1]),
    ):
        if end > begin:
            s.grad[begin:end, :] = jnp.zeros((end - begin, 128), F32)
    small = ROWS.small
    put(ROWS.dist, mm3(dbins, pair_out, TN)[8 : 8 + BINS])
    dbias_dist = pltpu.roll(jnp.broadcast_to(colsum(dbins), (8, 128)), 120, 1)[0:1]
    dout = mm3(dbins, s.wbd[...])
    dgate = dout * moved * (sig3 * (1.0 - sig3))
    dmoved = dout * sig3
    put(ROWS.out, mm3(dmoved, unit4 * gain_mixed, TN))
    dnormed = mm3(dmoved, w_out)
    s.grad[small + 5 : small + 6, :] = colsum(dnormed * unit4)
    dmixed = norm_back(dnormed * gain_mixed, unit4, scale4)
    s.ds[...] = dmixed.astype(BF16).reshape(BI, NJ, WP)
    s.dsr[me_c] = s.ds[...]
    finish(exchange(COL, GMIX, lambda p: s.ds, lambda p: s.dsr.at[p]))
    for bi in range(BI):
        for c in range(cols):
            begin = bi * length + c * NJ
            s.dm[begin : begin + NJ, :] = s.dsr[c, bi].astype(F32)

    @pl.loop(0, quads)
    def _(q):
        for place in range(BI):
            j = (q + quads * (place // NI)) * NI + place % NI
            block = jnp.zeros((NJ, WP), F32)
            for i in range(BI):
                block = block + (
                    s.dm[pl.ds(i * length + j, 1), :] * s.le[i * NJ : (i + 1) * NJ, :]
                )
            s.gs[q, place] = block.astype(BF16)

    s.gr[quad] = s.gs[quad]
    flight = exchange(QUAD, GEDGE, lambda p: s.gs.at[p], lambda p: s.gr.at[p])

    @pl.loop(0, BI)
    def _(i):
        block = jnp.zeros((NJ, WP), F32)
        for j in range(length):
            block = block + (
                s.dm[pl.ds(i * length + j, 1), :] * s.re[j * NJ : (j + 1) * NJ, :]
            )
        s.gl[i] = block

    finish(flight)
    dright = s.gr[0].astype(F32)
    for q in range(1, quads):
        dright = dright + s.gr[q].astype(F32)
    dright = dright.reshape(NP, WP) * pair_mask
    dleft = s.gl[...].reshape(NP, WP) * pair_mask
    p1, sig1 = s.proj[:, 0:WP], s.proj[:, WP : 2 * WP]
    p2, sig2 = s.proj[:, 2 * WP : 3 * WP], s.proj[:, 3 * WP : 4 * WP]
    dproj = jnp.concatenate(
        [
            dleft * sig1,
            dleft * p1 * (sig1 * (1.0 - sig1)),
            dright * sig2,
            dright * p2 * (sig2 * (1.0 - sig2)),
            dgate,
        ],
        axis=1,
    )
    unit3 = s.xh3[...]
    put(ROWS.tri, mm3(dproj, unit3 * gain_pair, TN))
    dnormed = mm3(dproj, w_p[0 : 5 * WP, :])
    s.grad[small + 4 : small + 5, :] = colsum(dnormed * unit3)
    drep = dout + norm_back(dnormed * gain_pair, unit3, s.r3[...])
    s.grad[small + 6 : small + 7, :] = colsum(drep)
    s.grad[ROWS.rel : ROWS.rel + 72, :] = mm2r(pair_codes, drep, TN)[0:72]
    s.qs[...] = drep.astype(BF16).reshape(BI, NJ, WP)
    s.qr[me_c] = s.qs[...]
    finish(exchange(COL, GOUTER, lambda p: s.qs, lambda p: s.qr.at[p]))

    turned = s.rall[...].astype(F32).T.astype(BF16)
    s.dr[...] = jnp.zeros((length, DS), F32)

    @pl.loop(0, BI // TOGETHER)
    def _(q):
        total = jnp.zeros((length, DS), F32)
        for part in range(TOGETHER):
            i = q * TOGETHER + part
            block = jnp.concatenate([s.qr[c, i] for c in range(cols)], axis=0)
            total = total + (mm(block, s.mhi[i], NT) + mm(block, s.mlo[i], NT))
            mh, ml = split2(mm(turned, block) * inv_count)
            s.mhi[i] = mh
            s.mlo[i] = ml
        s.dr[...] += total

    for r in range(rows):
        s.us[r] = (s.dr[r * NI : (r + 1) * NI, :] * inv_count).astype(BF16)
    s.ur[me_r] = s.us[me_r]
    flight = exchange(ROW, GRIGHT, lambda p: s.us.at[p], lambda p: s.ur.at[p])

    def pair_weight(pair):
        return split2(
            jnp.concatenate([outer_weight(2 * pair), outer_weight(2 * pair + 1)], axis=1)
        )

    def pair_of(ref, pair):
        return jnp.concatenate(
            [
                ref[:, d * NS : (d + 1) * NS, :].reshape(NM, WP)
                for d in (2 * pair, 2 * pair + 1)
            ],
            axis=1,
        )

    dleft = jnp.zeros((NM, WO), F32)
    for pair in range(WO // 2):
        wh, wl = pair_weight(pair)
        mh, ml = pair_of(s.mhi, pair), pair_of(s.mlo, pair)
        dleft = dleft + (mm(mh, wh, NT) + (mm(ml, wh, NT) + mm(mh, wl, NT)))
    high, low = split2(jnp.concatenate([dleft, jnp.zeros((NM, 96), F32)], axis=1))
    both = high.astype(F32) + pltpu.roll(low.astype(F32), 32, 1)
    s.dl[...] = both.astype(BF16).reshape(2, NI * NS, 128)
    s.dlr[side] = s.dl[side]
    flight.append(swap(2, s.dl, s.dlr))
    left3 = s.lr[...].astype(F32).reshape(NM, 128).T.astype(BF16)
    left_both, left_high = left3[0:64], left3[0:32]
    for pair in range(WO // 2):
        mh, ml = pair_of(s.mhi, pair), pair_of(s.mlo, pair)
        made = mm(left_both, mh)
        made = made[0:32] + made[32:64] + mm(left_high, ml)
        for half in range(2):
            s.grad[pl.ds(ROWS.outer + 2 * pair + half, WO, stride=WO), :] = made[
                :, half * WP : (half + 1) * WP
            ]
    early.advance()

    finish(flight)
    both = s.dlr[...].astype(F32).reshape(NM, 128)
    both = jnp.where(lane < 32, both + pltpu.roll(both, 96, 1), 0.0)
    dleft = mm3r(order, both, TN)
    dright = []
    for b in range(NB):
        some = s.ur[b * quads].astype(F32)
        for q in range(1, quads):
            some = some + s.ur[b * quads + q].astype(F32)
        dright.append(some)
    dright = jnp.stack(dright)
    wide = jnp.broadcast_to(dright[:, None], (NB, NS, NI, DS)).reshape(NM, DS)
    dedges = mm2(jnp.where(own_seq, wide, 0.0), repeat, NT)
    dedges = (dedges + dleft) * seq_weight
    unit2, rep = s.xh2[...], s.rep[...]
    dlog = s.dlog[...]
    put(ROWS.eh, (mm3(dedges, unit2 * gain_outer, TN) + mm3(dlog, rep, TN))[0:88])
    s.dn[...] = mm3(dedges, s.weh[...])
    dnormed = s.dn[...]
    column_products(s.xh2, 2)
    drep = mm3(dlog, s.weh[...]) + norm_back(dnormed * gain_outer, unit2, s.r2[...])
    early.advance()
    hidden = s.hid[...]
    dhidden = jnp.where(hidden > 0, mm3(drep, w_c[WA:, :], NT), 0.0)
    unit1 = s.xh1[...]
    put(ROWS.up, mm3(dhidden, unit1 * gain_trans, TN))
    up.advance()
    put(ROWS.back, mm3(hidden, drep, TN))
    turn(back, back2, up)
    s.dn[...] = mm3(dhidden, w_a[4 * WA : 4 * WA + UP, :])
    dnormed = s.dn[...]
    column_products(s.xh1, 0)
    dmid = drep + norm_back(dnormed * gain_trans, unit1, s.r1[...])
    sg, att = s.sg[...], s.att[...]
    put(ROWS.o, mm3(sg * att, dmid, TN))
    dgated = mm3(dmid, w_c[0:WA, :], NT)
    turn(thin, back, back2, early)
    single = triple[:, 0:AP]
    put(ROWS.tabs, mm2r(single, dmid, TN)[0:TR], 4 * TR)
    put(ROWS.tabs, mm2r(single, dgated * att, TN)[0:TR], 2 * TR)
    datt = dgated * sg

    pam = s.pam[...].reshape(NM, WA)
    blocks = jnp.where(head_mask(WA, AP), mm3(pam, datt, TN), 0.0)
    put(ROWS.tabs, jnp.sum(blocks.reshape(HEADS, AP, WA), axis=0)[0:TR])
    lane1 = iota((1, 128), 1)
    s.grad[small + 7 : small + 8, :] = jnp.where(lane1 < BINS, dbias_dist, colsum(dlog))
    s.grad[small + 8 : small + 9, :] = jnp.where(
        lane1 == 0, msa_sum, jnp.where(lane1 == 1, dist_sum, 0.0)
    )
    turn(rest, thin)
    s.dpam[...] = mm2(datt, s.vb[...], NT).reshape(BS, NI, WA)
    for b in range(NB):
        key_mask = s.sites[b : b + 1, :]
        s.dbias[b] = jnp.zeros((64, length), F32)

        def attention_back(q):
            together = jnp.zeros((64, length), F32)
            for part in range(TOGETHER):
                bs = b * NS + q * TOGETHER + part
                code = letter_codes(bs)
                wide = [spread(p.astype(F32)).astype(BF16) for p in split2(s.dpam[bs])]
                raw = mm(jnp.concatenate(wide, axis=0), code)
                dweight = raw[0:64] + raw[64:128]
                weight = s.prob[bs]
                inner = jnp.sum(weight * dweight, axis=-1, keepdims=True)
                dscore = jnp.where(key_mask > 0, weight * (dweight - inner), 0.0)
                together = together + dscore
                back = mm(jnp.concatenate(split2(dscore), axis=0), code, NT)
                s.da[bs] = gather_heads(back[0:64] + back[64:128])
            s.dbias[b] += together

        for part in range(2):
            count = NS // TOGETHER // 2
            pl.loop(part * count, (part + 1) * count)(attention_back)
            turn(*((rest, up), (back, early), (back2,), (thin, rest, up))[2 * b + part])

    put(ROWS.score, mm2r(single, s.da[...].reshape(NM, WA), TN)[0:TR])
    for b in range(NB):
        for i in range(NI):
            part = jnp.concatenate(
                [s.dbias[b, h * NI + i : h * NI + i + 1, :] for h in range(HEADS)], axis=0
            )
            s.dtab[b * NI + i] = mm(
                jnp.concatenate(split2(part), axis=0), codes(b * NI + i), NT
            )
    s.grad[ROWS.bias : ROWS.bias + 8, :] = jnp.sum(
        s.dtab[...].reshape(2 * BI, 8, RP), axis=0
    )

    aux[...] = jnp.where(iota((8, 128), 1) == 0, masked, inv_dist)

    last = bases[LAST]
    piece = (bases[-1] - last) // cols

    def mine(p):
        return pl.ds(pl.multiple_of(last + p * piece, 8), piece)

    def spot(p):
        return gfin.at[pl.ds(pl.multiple_of(p * piece, 8), piece)]

    s.fc[me_c] = s.grad[mine(me_c), :]
    flight = exchange(COL, SUM_COL, lambda p: s.grad.at[mine(p)], lambda p: s.fc.at[p])
    turn(back, early)
    finish(flight)
    summed = s.fc[0]
    for c in range(1, cols):
        summed = summed + s.fc[c]
    s.fp[...] = summed
    s.fr[me_r] = summed
    flight = exchange(ROW, SUM_ROW, lambda p: s.fp, lambda p: s.fr.at[p])
    turn(back2, thin, rest, up, back, early)
    finish(flight)
    summed = s.fr[0]
    for r in range(1, rows):
        summed = summed + s.fr[r]
    gfin[pl.ds(pl.multiple_of(me_c * piece, 8), piece), :] = summed
    flight = exchange(COL, SHARE_COL, lambda p: spot(me_c), spot)
    turn(back2, early, thin, rest)
    finish(flight)
    turn(up, back, up, back2, back, back2, thin, rest, thin, rest)
    assert all(group.done for group in (up, thin, back, back2, early, rest))


def post_kernel(rows, cols, *refs):
    gbig, grest, gfin, tout, aux = refs[:5]
    weights, far_moments = refs[5:11], refs[11:23]
    far, loss_out, size_out = refs[23:41], refs[41], refs[42]
    new, moments = refs[43:61], refs[61:73]
    lk, wrel, g_a, g_small, g_rel, store_sem, load_sem = refs[73:]
    loads = [
        pltpu.make_async_copy(source, near, load_sem.at[place])
        for place, (source, near) in enumerate(zip(far_moments, moments))
    ]
    for place in (2, 8, 1, 7, 3, 9, 4, 10, 0, 6, 5, 11):
        loads[place].start()
    means, squares = moments[0:6], moments[6:12]
    lookup, w_a, w_c, w_r, w_p, scal = weights
    ROWS, bases = layout(rows, cols)

    def big(begin, count):
        part = gbig[begin // 8 : (begin + count) // 8].astype(F32)
        return part.reshape(count, 128)

    def exact(begin, count):
        if begin >= bases[LAST]:
            return gfin[begin - bases[LAST] : begin - bases[LAST] + count, :]
        return grest[begin - bases[LOW_SHARE] : begin - bases[LOW_SHARE] + count, :]

    lk[...] = jnp.zeros((AP, WA), F32)
    lk[0:LETTERS, :] = lookup[...]
    wrel[...] = jnp.zeros((RP, WP), F32)
    wrel[0:NREL, :] = w_r[UP : UP + NREL, :]

    def table(begin):
        both = jnp.concatenate([exact(begin, TR), exact(begin + TR, TR)], axis=1)
        return jnp.concatenate([both, jnp.zeros((AP - TR, WA), F32)], axis=0)

    dscore = table(ROWS.score)
    dvalue, dgate, dstart = [table(ROWS.tabs + 2 * TR * place) for place in range(3)]
    mapped = tout[...]
    t_q = mapped[:, 0:WA] * HEAD ** (-0.5)
    t_k = mapped[:, WA : 2 * WA].astype(BF16).astype(F32)
    t_g = jax.nn.sigmoid(mapped[:, 3 * WA :])
    square = head_mask(WA, AP)
    key_block = jnp.where(square, jnp.concatenate([t_k] * HEADS, axis=0), 0.0).astype(BF16)
    dq = mm2(dscore, key_block) * HEAD ** (-0.5)
    dk = jnp.where(square, mm3(dscore, t_q, TN), 0.0)
    dk = jnp.sum(dk.reshape(HEADS, AP, WA), axis=0)
    dg = dgate * (t_g * (1.0 - t_g))
    dmapped = jnp.concatenate([dq, dk, dvalue, dg], axis=1)
    unit0, scale0 = norm(lk[...])
    gain_row = scal[0:WA].reshape(1, WA)
    g_a[...] = mm3(dmapped, unit0 * gain_row, TN)
    dnormed = mm3(dmapped, w_a[0 : 4 * WA, :])
    dgain_row = colsum(dnormed * unit0)
    g_lookup = dstart + norm_back(dnormed * gain_row, unit0, scale0)

    unit_r, scale_r = norm(wrel[...])
    gain_rel = scal[768:896].reshape(1, WP)
    dtable = exact(ROWS.bias, 8)
    g_bias = mm3(dtable, unit_r * gain_rel)
    dnormed = mm3(dtable, w_p[768:776, :], TN)
    dgain_rel = colsum(dnormed * unit_r)
    g_rel[...] = exact(ROWS.rel, 72) + norm_back(
        dnormed * gain_rel, unit_r, scale_r
    )[0:72]

    base = ROWS.small
    g_small[0:WA] = dgain_row.reshape(WA)
    for place, row in ((256, 0), (384, 1), (512, 2), (640, 3), (896, 4), (1024, 5), (1152, 6)):
        g_small[place : place + 128] = exact(base + row, 1).reshape(128)
    g_small[768:896] = dgain_rel.reshape(128)
    lane = iota((1, 128), 1)
    tail = jnp.where(lane < 87, exact(base + 7, 1), 0.0)
    g_small[1280:1408] = tail.reshape(128)

    rel_row = iota((72, 128), 0)
    squares_sum = jnp.zeros((1, 1), F32)
    for begin, count in (
        (ROWS.up, 2 * UP),
        (ROWS.tri, 768),
        (ROWS.o, 2 * WA),
        (ROWS.back, 2 * UP),
    ):
        part = big(begin, count)
        squares_sum = squares_sum + total_of(part * part)
    for part in (
        g_a[...],
        g_lookup[0:LETTERS],
        jnp.where(rel_row < NREL, g_rel[...], 0.0),
        g_bias,
        dgain_row,
        exact(ROWS.outer, UP),
        exact(base, 7),
        exact(ROWS.eh, 87),
        exact(ROWS.eh + 88, 87),
        exact(ROWS.dist, BINS),
        dgain_rel,
        tail,
    ):
        squares_sum = squares_sum + total_of(part * part)
    size = jnp.sqrt(squares_sum)
    scale = jnp.minimum(1.0, CLIP / size)

    def adam(which, where, grad, factor=scale):
        clipped = grad * factor
        weight = weights[which][where]
        moment = B1 * means[which][where] + (1.0 - B1) * clipped
        second = B2 * squares[which][where] + (1.0 - B2) * clipped * clipped
        root = (1.0 - B2**STEP) ** 0.5
        step = (moment * (RATE * root / (1.0 - B1**STEP))) / (
            second * lax.rsqrt(second) + ADAM_EPS * root
        )
        new[3 * which][where] = weight * (1.0 - RATE * DECAY) - step
        new[3 * which + 1][where] = moment
        new[3 * which + 2][where] = second

    every = slice(None)
    stores = []

    def leave(which):
        for place in range(3 * which, 3 * which + 3):
            store = pltpu.make_async_copy(new[place], far[place], store_sem.at[place])
            store.start()
            stores.append(store)

    def ready(which):
        loads[which].wait()
        loads[6 + which].wait()

    ready(2)
    for w in range(2):
        half = slice(128 * w, 128 * w + 128)
        adam(2, (slice(0, WA), half), big(ROWS.o + w * WA, WA))
        adam(2, (slice(WA, WA + UP), half), big(ROWS.back + w * UP, UP))
    leave(2)
    ready(1)
    adam(1, (slice(0, 4 * WA), every), g_a[...])
    for w in range(2):
        half = slice(128 * w, 128 * w + 128)
        adam(1, (slice(1024, 2048), half), big(ROWS.up + w * UP, UP))
        adam(1, (slice(2048, 2135), half), exact(ROWS.eh + w * 88, 87))
    leave(1)
    ready(3)
    adam(3, (slice(0, UP), every), exact(ROWS.outer, UP))
    adam(3, (slice(UP, UP + NREL), every), g_rel[0:NREL, :])
    leave(3)
    ready(4)
    adam(4, (slice(0, 768), every), big(ROWS.tri, 768))
    adam(4, (slice(768, 776), every), g_bias)
    adam(4, (slice(776, 840), every), exact(ROWS.dist, BINS))
    leave(4)
    ready(0)
    adam(0, (every, every), g_lookup[0:LETTERS])
    leave(0)
    ready(5)
    adam(5, (slice(0, 1367),), g_small[0:1367], scale.reshape(1))
    leave(5)

    sums = exact(base + 8, 1)
    loss = sums[:, 0:1] / aux[0:1, 0:1] + sums[:, 1:2] * aux[0:1, 1:2]
    loss_out[0] = loss[0, 0]
    size_out[0] = size[0, 0]
    for store in stores:
        store.wait()


def vmem():
    return pl.BlockSpec(memory_space=pltpu.VMEM)


def per_device(rows, cols, *arrays):
    letters, truth, concealed, existing, ordinals, observed, bins = arrays[:7]

    def turned(group):
        return [w.T if place in (1, 4) else w for place, w in enumerate(group)]

    weights, means, squares = turned(arrays[7:13]), turned(arrays[13:19]), turned(arrays[19:25])
    plan = scratch_plan(rows, cols)
    bases = layout(rows, cols)[1]
    far = pl.BlockSpec(memory_space=pltpu.HBM)
    summed = pl.pallas_call(
        functools.partial(main_kernel, rows, cols, tuple(plan)),
        out_shape=(
            jax.ShapeDtypeStruct((bases[LOW_SHARE] // 8, 8, 128), BF16),
            jax.ShapeDtypeStruct((bases[LAST] - bases[LOW_SHARE], 128), F32),
            jax.ShapeDtypeStruct((bases[-1] - bases[LAST], 128), F32),
            jax.ShapeDtypeStruct((AP, 4 * WA), F32),
            jax.ShapeDtypeStruct((8, 128), F32),
        ),
        in_specs=[far] * OPERANDS,
        out_specs=tuple([vmem()] * 5),
        scratch_shapes=[pltpu.VMEM(dims, kind) for dims, kind in plan.values()]
        + [
            pltpu.SemaphoreType.DMA((rows - 1,)),
            pltpu.SemaphoreType.DMA((PHASES - 1, rows - 1)),
            pltpu.SemaphoreType.DMA((cols - 1,)),
            pltpu.SemaphoreType.DMA((PHASES, cols - 1)),
            pltpu.SemaphoreType.DMA((3, 2)),
            pltpu.SemaphoreType.DMA((LAST, max(rows // 2, cols) - 1)),
            pltpu.SemaphoreType.DMA((LAST, 2 * cols + rows - 2)),
            pltpu.SemaphoreType.DMA((OPERANDS,)),
        ],
        compiler_params=pltpu.CompilerParams(
            collective_id=0, has_side_effects=True, vmem_limit_bytes=MAIN_VMEM
        ),
    )(
        *[
            pltpu.with_memory_space_constraint(value, pltpu.HBM)
            for value in (
                jnp.swapaxes(letters, 1, 2),
                jnp.swapaxes(truth, 1, 2),
                jnp.swapaxes(concealed, 1, 2),
                existing,
                ordinals,
                observed,
                bins,
                *weights,
            )
        ]
    )

    shapes = []
    for w in weights:
        shapes += [jax.ShapeDtypeStruct(w.shape, F32)] * 3
    one = jax.ShapeDtypeStruct((1,), F32)
    scalar = pl.BlockSpec(memory_space=pltpu.SMEM)
    result = pl.pallas_call(
        functools.partial(post_kernel, rows, cols),
        out_shape=tuple(shapes) + (one, one),
        in_specs=[vmem()] * 11 + [far] * 12,
        out_specs=tuple([far] * 18) + (scalar, scalar),
        scratch_shapes=[pltpu.VMEM(shape.shape, F32) for shape in shapes]
        + [pltpu.VMEM(value.shape, F32) for value in (*means, *squares)]
        + [
            pltpu.VMEM((AP, WA), F32),
            pltpu.VMEM((RP, WP), F32),
            pltpu.VMEM((4 * WA, WA), F32),
            pltpu.VMEM((1408,), F32),
            pltpu.VMEM((72, 128), F32),
            pltpu.SemaphoreType.DMA((18,)),
            pltpu.SemaphoreType.DMA((12,)),
        ],
        compiler_params=pltpu.CompilerParams(vmem_limit_bytes=POST_VMEM),
    )(
        *summed,
        *weights,
        *[pltpu.with_memory_space_constraint(value, pltpu.HBM) for value in (*means, *squares)],
    )
    outs = [result[18].reshape(()), result[19].reshape(())]
    for place, value in enumerate(result[:18]):
        outs.append(value.T if place // 3 in (1, 4) else value)
    return tuple(outs)


def solution(mesh):
    rows, cols = mesh.shape[ROW], mesh.shape[COL]
    placed = (
        (P(None, COL, ROW),) * 3 + (P(),) * 3 + (P(None, ROW, COL),) + (P(),) * 18
    )
    return jax.shard_map(
        functools.partial(per_device, rows, cols),
        mesh=mesh,
        in_specs=placed,
        out_specs=(P(),) * 20,
        check_vma=False,
    )
```

```python
import functools
from types import SimpleNamespace

import jax
import jax.numpy as jnp
from jax import lax
from jax.experimental import pallas as pl
from jax.experimental.pallas import tpu as pltpu
from jax.sharding import PartitionSpec as P

F32, BF16 = jnp.float32, jnp.bfloat16
MESH = pl.DeviceIdType.MESH
ROW, COL, QUAD = "row", "col", "quad"
CORE, PLANE, Z = "core", "plane", "z"
WA, WP, WO, LETTERS, BINS, REACH, HEADS, HEAD = 256, 128, 32, 23, 64, 32, 8, 32
UP = 1024
NREL = 2 * REACH + 1
AP = 32
TR = 24
RP = 128
EPS = 1e-05
NB, NS, NI, NJ = 2, 16, 8, 16
NM = NB * NS * NI
NP = 2 * NI * NJ
BS = NB * NS
BI = NB * NI
DS = WO * NS
FORWARD, TOGETHER = 16, 8
CLIP, RATE, B1, B2, STEP, ADAM_EPS, DECAY = 0.02, 0.05, 0.9, 0.999, 4, 1e-08, 0.01

MAIN_VMEM, POST_VMEM = 44 * 2**20, 30 * 2**20

NN = (((1,), (0,)), ((), ()))
NT = (((1,), (1,)), ((), ()))
TN = (((0,), (0,)), ((), ()))

GROUPS = (
    dict(up=2 * UP),
    dict(tri=5 * WP, out=WP, o=2 * WA),
    dict(back=UP),
    dict(back2=UP),
    dict(outer=WO * WO),
    dict(eh=176, tabs=6 * TR, dist=BINS, rel=72, small=16),
    dict(score=2 * TR, bias=8),
)
LAST = len(GROUPS) - 1
LOW_SUM = 2
LOW_SHARE = 4


def layout(rows, cols):
    places, bases, begin = {}, [], 0
    for number, group in enumerate(GROUPS):
        bases.append(begin)
        for name, count in group.items():
            places[name] = begin
            begin += count
        size = 16 * cols if number == LAST else 8 * rows * cols
        begin = bases[-1] - (bases[-1] - begin) // size * size
    return SimpleNamespace(**places), bases + [begin]


def mm(a, b, dims=NN):
    return lax.dot_general(a, b, dims, preferred_element_type=F32)


def split2(x):
    high = x.astype(BF16)
    return high, (x - high.astype(F32)).astype(BF16)


def split3(x):
    high = x.astype(BF16)
    rest = x - high.astype(F32)
    middle = rest.astype(BF16)
    return high, middle, (rest - middle.astype(F32)).astype(BF16)


def mm3(a, b, dims=NN):
    ah, al = split2(a)
    bh, bl = split2(b)
    return mm(ah, bh, dims) + (mm(al, bh, dims) + mm(ah, bl, dims))


def mm6(a, b, dims=NN):
    ah, am, al = split3(a)
    bh, bm, bl = split3(b)
    low = mm(al, bh, dims) + (mm(am, bm, dims) + mm(ah, bl, dims))
    return mm(ah, bh, dims) + ((mm(am, bh, dims) + mm(ah, bm, dims)) + low)


def mm2(a, exact, dims=NN):
    ah, al = split2(a)
    return mm(ah, exact, dims) + mm(al, exact, dims)


def mm2r(exact, b, dims=NN):
    bh, bl = split2(b)
    return mm(exact, bh, dims) + mm(exact, bl, dims)


def mm3r(exact, b, dims=NN):
    bh, bm, bl = split3(b)
    return mm(exact, bh, dims) + (mm(exact, bm, dims) + mm(exact, bl, dims))


def norm(x):
    centred = x - jnp.mean(x, axis=-1, keepdims=True)
    scale = lax.rsqrt(jnp.mean(centred * centred, axis=-1, keepdims=True) + EPS)
    return centred * scale, scale


def norm_back(grad, unit, scale):
    return scale * (
        grad
        - jnp.mean(grad, axis=-1, keepdims=True)
        - unit * jnp.mean(grad * unit, axis=-1, keepdims=True)
    )


def iota(shape, axis):
    return lax.broadcasted_iota(jnp.int32, shape, axis)


def head_mask(rows, per_row):
    shape = (rows, WA)
    return iota(shape, 0) // per_row == iota(shape, 1) // HEAD


def colsum(x):
    return jnp.sum(x, axis=0, keepdims=True)


def total_of(x):
    return jnp.sum(jnp.sum(x, axis=1, keepdims=True), axis=0, keepdims=True)


def scratch_plan(rows, cols):
    length = rows * NI
    bases = layout(rows, cols)[1]
    final = bases[-1] - bases[LAST]
    return dict(
        lk=((AP, WA), F32),
        weh=((128, WA), F32),
        wbd=((128, WP), F32),
        seqw=((NM, 1), F32),
        lmask=((NM, 1), F32),
        truth=((NM, 1), F32),
        pmask=((NP, 1), F32),
        offset=((NP, 1), F32),
        codes=((BI, length), F32),
        sites=((8, length), F32),
        wrel=((RP, WP), F32),
        tail=((8, 128), F32),
        kb=((WA, WA), BF16),
        vb=((WA, WA), BF16),
        amat=((BS, NI, WA), F32),
        pam=((BS, NI, WA), F32),
        hm=((64, WA), F32),
        letx=((128, length), F32),
        biash=((NB, 64, length), F32),
        prob=((BS, 64, length), F32),
        sg=((NM, WA), F32),
        att=((NM, WA), F32),
        xh1=((NM, WA), F32),
        r1=((NM, 1), F32),
        hid=((NM, UP), F32),
        rep=((NM, WA), F32),
        xh2=((NM, WA), F32),
        r2=((NM, 1), F32),
        dlog=((NM, 128), F32),
        left3=((NB, NI * NS, 128), BF16),
        mhi=((BI, DS, WP), BF16),
        mlo=((BI, DS, WP), BF16),
        rall=((length, DS), BF16),
        prep=((NP, WP), F32),
        xh3=((NP, WP), F32),
        r3=((NP, 1), F32),
        proj=((NP, 5 * WP), F32),
        le=((BI * NJ, WP), F32),
        re=((length * NJ, WP), F32),
        dm=((BI * length, WP), F32),
        gl=((BI, NJ, WP), F32),
        dr=((length, DS), F32),
        dmid=((NM, WA), F32),
        dbias=((NB, 64, length), F32),
        da=((BS, NI, WA), F32),
        dpam=((BS, NI, WA), F32),
        dtab=((BI, 16, RP), F32),
        dn=((NM, WA), F32),
        sum8=((8, WA), F32),
        grad=((bases[-1], 128), F32),
        lets=((8, 128), F32),
        letr=((rows, 8, 128), F32),
        cnts=((8, 128), F32),
        cntr=((cols, 8, 128), F32),
        rs=((NB, NI, DS), BF16),
        rr=((rows, NI, DS), BF16),
        lr=((2, NI * NS, 128), BF16),
        tgr=((2, NI, NJ), jnp.int32),
        os=((cols, BI, NJ, WP), BF16),
        orr=((cols, BI, NJ, WP), BF16),
        er=((rows // 2, BI, NJ, WP), BF16),
        ts=((cols, BI, NJ, WP), BF16),
        tr=((cols, BI, NJ, WP), BF16),
        ds=((BI, NJ, WP), BF16),
        dsr=((cols, BI, NJ, WP), BF16),
        gs=((rows // 2, BI, NJ, WP), BF16),
        gr=((rows // 2, BI, NJ, WP), BF16),
        qs=((BI, NJ, WP), BF16),
        qr=((cols, BI, NJ, WP), BF16),
        us=((rows, NI, DS), BF16),
        ur=((rows, NI, DS), BF16),
        dl=((2, NI * NS, 128), BF16),
        dlr=((NB, NI * NS, 128), BF16),
        arx=((bases[LAST], 128), F32),
        lows=((bases[LOW_SUM] // 8, 8, 128), BF16),
        lowr=((bases[LOW_SUM] // 8, 8, 128), BF16),
        fc=((cols, final // cols, 128), F32),
        fp=((final // cols, 128), F32),
        fr=((rows, final // cols, 128), F32),
        letters=((NB, NI, NS), jnp.int32),
        truths=((NB, NI, NS), jnp.int32),
        concealed=((NB, NI, NS), jnp.int32),
        existing=((NB, cols * NS), jnp.int32),
        ordinals=((NB, length), jnp.int32),
        observed=((NB, length), jnp.int32),
        targets=((NB, NI, NJ), jnp.int32),
        lookup=((LETTERS, WA), F32),
        w_a=((2135, WA), F32),
        w_c=((WA + UP, WA), F32),
        w_r=((UP + NREL, WP), F32),
        w_p=((840, WP), F32),
        scal=((1367,), F32),
    )


OPERANDS = 13


LET, RIGHT, EDGE, GEDGE, GRIGHT, SUM_ROW = range(6)
CNT, OUTER, TRI, GMIX, GOUTER, SUM_COL, SHARE_COL = range(7)
PHASES = 7


def main_kernel(rows, cols, names, *refs):
    operands = refs[:OPERANDS]
    gbig, grest, gfin, tout, aux = refs[OPERANDS : OPERANDS + 5]
    s = SimpleNamespace(**dict(zip(names, refs[OPERANDS + 5 : -8])))
    row_send, row_recv, col_send, col_recv, pair_sem, sum_send, sum_recv, load_sem = refs[-8:]
    held = refs[OPERANDS + 5 : -8][-OPERANDS:]
    loads = [
        pltpu.make_async_copy(far, near, load_sem.at[place])
        for place, (far, near) in enumerate(zip(operands, held))
    ]
    for load in loads:
        load.start()
    letters, truths, hidden_sites, existing, ordinals, observed, targets = held[:7]
    lookup, w_a, w_c, w_r, w_p, scal = held[7:]
    ROWS, bases = layout(rows, cols)
    length = rows * NI
    me_r, me_c = lax.axis_index(ROW), lax.axis_index(COL)

    barrier = pltpu.get_barrier_semaphore()
    for step in range(1, rows):
        pl.semaphore_signal(
            barrier,
            inc=1,
            device_id={ROW: lax.rem(me_r + step, rows), COL: me_c},
            device_id_type=MESH,
        )
    for step in range(1, cols):
        pl.semaphore_signal(
            barrier,
            inc=1,
            device_id={ROW: me_r, COL: lax.rem(me_c + step, cols)},
            device_id_type=MESH,
        )
    quads = rows // 2
    side, quad = me_r // quads, me_r % quads

    def to_partner(number, source, target):
        return pltpu.make_async_remote_copy(
            src_ref=source,
            dst_ref=target,
            send_sem=pair_sem.at[number, 0],
            recv_sem=pair_sem.at[number, 1],
            device_id={ROW: (1 - side) * quads + quad, COL: me_c},
            device_id_type=MESH,
        )

    def swap(number, source, target):
        out = to_partner(number, source.at[1 - side], target.at[side])
        out.start()
        return out, to_partner(number, source.at[1 - side], target.at[1 - side])

    def exchange(along, phase, source, target):
        if along == ROW:
            count, me, number = rows, me_r, phase
            send, recv = row_send, row_recv
        elif along == QUAD:
            count, me, number = quads, quad, phase
            send, recv = row_send, row_recv
        else:
            count, me, number = cols, me_c, phase
            send, recv = col_send, col_recv
        copies = []
        for step in range(1, count):
            peer = lax.rem(me + step, count)
            origin = lax.rem(me + (count - step), count)
            where = {ROW: me_r, COL: peer}
            if along == ROW:
                where = {ROW: peer, COL: me_c}
            elif along == QUAD:
                where = {ROW: side * quads + peer, COL: me_c}
            out = pltpu.make_async_remote_copy(
                src_ref=source(peer),
                dst_ref=target(me),
                send_sem=send.at[step - 1],
                recv_sem=recv.at[number, step - 1],
                device_id=where,
                device_id_type=MESH,
            )
            out.start()
            arriving = pltpu.make_async_remote_copy(
                src_ref=source(peer),
                dst_ref=target(origin),
                send_sem=send.at[step - 1],
                recv_sem=recv.at[number, step - 1],
                device_id=where,
                device_id_type=MESH,
            )
            copies.append((out, arriving))
        return copies

    def finish(copies):
        for out, arriving in copies:
            out.wait_send()
            arriving.wait_recv()

    for load in loads[:7]:
        load.wait()
    here = existing[...].astype(F32)
    sites = observed[...].astype(F32)
    numbers = ordinals[...].astype(F32)

    def by_protein(values, count, each):
        wide = (count, values.shape[1])
        return jnp.where(iota(wide, 0) // each == 0, values[0:1], values[1:2])

    def at_lane(values, lanes):
        return jnp.sum(jnp.where(iota(values.shape, 1) == lanes, values, 0.0), axis=1, keepdims=True)

    row_m, row_p = iota((NM, 1), 0), iota((NP, 1), 0)
    seq_m, res_m = (row_m // NI) % NS, row_m % NI
    spread_m = jnp.where(
        iota((NM, BI), 1) == (iota((NM, BI), 0) // (NI * NS)) * NI + iota((NM, BI), 0) % NI, 1.0, 0.0
    ).astype(BF16)

    def column_m(values):
        wide = mm(spread_m, values[...].reshape(BI, NS).astype(F32).astype(BF16))
        return at_lane(wide, seq_m)

    seq_weight = at_lane(by_protein(here, NM, NI * NS), me_c * NS + seq_m)
    letter = column_m(letters)
    loss_mask = column_m(hidden_sites) * seq_weight
    s.seqw[...] = seq_weight
    s.lmask[...] = loss_mask
    s.truth[...] = column_m(truths)
    s.tgr[side] = targets[side]

    s.lets[...] = jnp.where(
        (iota((NI, 128), 0) == 0) & (iota((NI, 128), 1) == BS), total_of(loss_mask), 0.0
    )
    for b in range(NB):
        s.lets[:, b * NS : (b + 1) * NS] = letters[b].astype(F32)
    s.letr[me_r] = s.lets[...]
    pl.semaphore_wait(barrier, rows + cols - 2)
    flight = exchange(ROW, LET, lambda p: s.lets, lambda p: s.letr.at[p])
    flight.append(swap(0, targets, s.tgr))
    near = row_p // NJ
    first = (quad + quads * (near // NI)) * NI + near % NI
    second = me_c * NJ + row_p % NJ

    def of_side(values):
        return jnp.where(side == 0, values[0:1], values[1:2])

    sites_p = jnp.broadcast_to(of_side(sites), (NP, length))
    numbers_p = jnp.broadcast_to(of_side(numbers), (NP, length))
    s.pmask[...] = at_lane(sites_p, first) * at_lane(sites_p, second)
    s.offset[...] = (
        jnp.clip(at_lane(numbers_p, first) - at_lane(numbers_p, second), -REACH, REACH) + REACH
    )
    numbers_b = by_protein(numbers, BI, NI)
    own = at_lane(numbers_b, me_r * NI + iota((BI, 1), 0) % NI)
    s.codes[...] = jnp.clip(own - numbers_b, -REACH, REACH) + REACH
    s.sites[...] = jnp.zeros((8, length), F32)
    s.sites[0:NB, :] = sites
    inv_all = 1.0 / (jnp.sum(here, axis=1, keepdims=True) + 1.0)
    inv_count = of_side(inv_all)
    per_protein = jnp.sum(sites, axis=1, keepdims=True)
    inv_dist = 1.0 / jnp.maximum(colsum(per_protein * per_protein), 1.0)

    for load in loads[7:]:
        load.wait()

    def gain(begin, width):
        return scal[begin : begin + width].reshape(1, width)

    gain_row, gain_trans, gain_outer = gain(0, WA), gain(256, WA), gain(512, WA)
    gain_rel, gain_pair, gain_mixed = gain(768, WP), gain(896, WP), gain(1024, WP)
    bias_outer = gain(1152, WP)
    s.lk[...] = jnp.zeros((AP, WA), F32)
    s.lk[0:LETTERS, :] = lookup[...]
    s.weh[...] = jnp.zeros((128, WA), F32)
    s.weh[0:87, :] = w_a[2048:2135, :]
    s.wbd[...] = jnp.zeros((128, WP), F32)
    s.wbd[0:72, :] = w_p[768:840, :]
    s.wrel[...] = jnp.zeros((RP, WP), F32)
    s.wrel[0:NREL, :] = w_r[UP : UP + NREL, :]
    s.tail[...] = jnp.zeros((8, 128), F32)
    s.tail[0:1, 0:87] = scal[1280:1367].reshape(1, 87)

    table = s.lk[...]
    unit0, _ = norm(table)
    mapped = mm6(unit0 * gain_row, w_a[0 : 4 * WA, :], NT)
    tout[...] = mapped
    t_q = mapped[:, 0:WA] * HEAD ** (-0.5)
    t_k = mapped[:, WA : 2 * WA].astype(BF16).astype(F32)
    t_v = mapped[:, 2 * WA : 3 * WA].astype(BF16).astype(F32)
    t_g = jax.nn.sigmoid(mapped[:, 3 * WA :])
    square = head_mask(WA, AP)
    key_block = jnp.where(square, jnp.concatenate([t_k] * HEADS, axis=0), 0.0).astype(BF16)
    s.vb[...] = jnp.where(square, jnp.concatenate([t_v] * HEADS, axis=0), 0.0).astype(BF16)
    stacked = mm(jnp.concatenate(split3(t_q), axis=0), key_block, NT)
    score_table = stacked[0:AP] + (stacked[AP : 2 * AP] + stacked[2 * AP :])
    s.hm[...] = jnp.where(head_mask(64, NI), 1.0, 0.0)

    letter = letter.astype(jnp.int32)
    triple = jnp.where(
        (iota((NM, 3 * AP), 1) % AP) == letter, 1.0, 0.0
    ).astype(BF16)

    def chosen(values):
        return mm(triple, jnp.concatenate(split3(values), axis=0))

    s.amat[...] = chosen(score_table).reshape(BS, NI, WA)
    start = chosen(table)
    s.sg[...] = chosen(t_g)

    unit_r, _ = norm(s.wrel[...])
    bias_table = mm3(s.wbd[0:8, :], unit_r * gain_rel, NT)
    bias_parts = jnp.concatenate(split3(bias_table), axis=0)

    def codes(index):
        return jnp.where(
            iota((RP, length), 0) == s.codes[index : index + 1, :].astype(jnp.int32), 1.0, 0.0
        ).astype(BF16)

    for b in range(NB):
        for i in range(NI):
            part = mm(bias_parts, codes(b * NI + i))
            part = part[0:8] + (part[8:16] + part[16:24])
            for h in range(HEADS):
                s.biash[b, h * NI + i : h * NI + i + 1, :] = part[h : h + 1, :]

    finish(flight)
    letters_all = s.letr[...].reshape(length, 128).T
    s.letx[...] = letters_all
    s.cnts[...] = jnp.broadcast_to(
        jnp.sum(letters_all[BS : BS + 1, :], axis=1, keepdims=True), (8, 128)
    )
    s.cntr[me_c] = s.cnts[...]
    count_flight = exchange(COL, CNT, lambda p: s.cnts, lambda p: s.cntr.at[p])

    def letter_codes(bs):
        row = s.letx[pl.ds(bs, 1), :].astype(jnp.int32)
        one = jnp.where(iota((AP, length), 0) == row, 1.0, 0.0)
        return jnp.concatenate([one] * HEADS, axis=0).astype(BF16)

    def spread(value):
        wide = jnp.broadcast_to(value[None], (HEADS, NI, WA)).reshape(64, WA)
        return wide * s.hm[...]

    def gather_heads(value):
        return jnp.sum((value * s.hm[...]).reshape(HEADS, NI, WA), axis=0)

    for b in range(NB):
        key_mask = s.sites[b : b + 1, :]

        @pl.loop(0, NS // FORWARD)
        def _(q):
            for part in range(FORWARD):
                bs = b * NS + q * FORWARD + part
                code = letter_codes(bs)
                wide = [spread(p.astype(F32)).astype(BF16) for p in split2(s.amat[bs])]
                raw = mm(jnp.concatenate(wide, axis=0), code)
                scores = (raw[0:64] + raw[64:128]) + s.biash[b]
                scores = jnp.where(key_mask > 0, scores, -1000000000.0)
                power = jnp.exp(scores - jnp.max(scores, axis=-1, keepdims=True))
                weight = power / jnp.sum(power, axis=-1, keepdims=True)
                s.prob[bs] = weight
                picked = mm(jnp.concatenate(split2(weight), axis=0), code, NT)
                s.pam[bs] = gather_heads(picked[0:64] + picked[64:128])

    att = mm2(s.pam[...].reshape(NM, WA), s.vb[...])
    s.att[...] = att
    mid = start + mm3(s.sg[...] * att, w_c[0:WA, :])
    unit1, scale1 = norm(mid)
    s.xh1[...] = unit1
    s.r1[...] = scale1
    hidden = jnp.maximum(mm3(unit1 * gain_trans, w_a[4 * WA : 4 * WA + UP, :], NT), 0.0)
    s.hid[...] = hidden
    rep = mid + mm3(hidden, w_c[WA:, :])
    s.rep[...] = rep
    unit2, scale2 = norm(rep)
    s.xh2[...] = unit2
    s.r2[...] = scale2
    seq_weight = s.seqw[...]
    lane = iota((NM, 128), 1)
    edges = mm3(unit2 * gain_outer, s.weh[...], NT) * seq_weight

    right = jnp.where((lane >= 32) & (lane < 64), edges, 0.0).astype(BF16)
    spot = iota((128, DS), 0)
    repeat = jnp.where(spot - 32 == iota((128, DS), 1) // NS, 1.0, 0.0)
    repeat = jnp.where((spot >= 32) & (spot < 64), repeat, 0.0).astype(BF16)
    wide = mm(right, repeat)
    own_seq = (iota((NM, DS), 0) // NI) % NS == iota((NM, DS), 1) % NS
    wide = jnp.sum(jnp.where(own_seq, wide, 0.0).reshape(NB, NS, NI, DS), axis=1)
    s.rs[...] = wide.astype(BF16)
    s.rr[me_r] = s.rs[side]
    flight = exchange(ROW, RIGHT, lambda p: s.rs.at[p // quads], lambda p: s.rr.at[p])

    order_to = (iota((NM, NM), 0) // (NI * NS) == iota((NM, NM), 1) // (NI * NS)) & (
        (iota((NM, NM), 0) // NS) % NI == iota((NM, NM), 1) % NI
    )
    order_to = order_to & (iota((NM, NM), 0) % NS == (iota((NM, NM), 1) // NI) % NS)
    order = jnp.where(order_to, 1.0, 0.0).astype(BF16)
    left = mm3r(order, jnp.where(lane < 32, edges, 0.0))
    high, low = split2(left)
    high32, low32 = high.astype(F32), low.astype(F32)
    left3 = high32 + pltpu.roll(low32, 32, 1) + pltpu.roll(high32, 64, 1)
    s.left3[...] = left3.astype(BF16).reshape(NB, NI * NS, 128)
    s.lr[side] = s.left3[side]
    flight.append(swap(1, s.left3, s.lr))

    finish(count_flight)
    masked = jnp.maximum(jnp.sum(s.cntr[...], axis=0)[0:1, 0:1], 1.0)
    logits = mm3(rep, s.weh[...], NT) + s.tail[0:1, :]
    valid = (lane >= 64) & (lane < 64 + LETTERS)
    top = jnp.max(jnp.where(valid, logits, -3e38), axis=-1, keepdims=True)
    power = jnp.where(valid, jnp.exp(jnp.where(valid, logits, top) - top), 0.0)
    whole = jnp.sum(power, axis=-1, keepdims=True)
    truth = lane - 64 == s.truth[...].astype(jnp.int32)
    truth = truth & valid
    picked = jnp.sum(jnp.where(truth, logits, 0.0), axis=-1, keepdims=True)
    loss_mask = s.lmask[...]
    msa_sum = colsum((jnp.log(whole) + top - picked) * loss_mask)
    s.dlog[...] = (power / whole - jnp.where(truth, 1.0, 0.0)) * (loss_mask / masked)

    def outer_weight(d):
        return w_r[pl.ds(d, WO, stride=WO), :]

    def expand(block):
        for pair in range(WO // 2):
            both = jnp.concatenate([outer_weight(2 * pair), outer_weight(2 * pair + 1)], axis=1)
            wh, wl = split2(both)
            made = mm(s.lr[block][:, 0:96], jnp.concatenate([wh, wh, wl], axis=0))
            for half in range(2):
                d = 2 * pair + half
                mh, ml = split2(made[:, half * WP : (half + 1) * WP].reshape(NI, NS, WP))
                s.mhi[pl.ds(block * NI, NI), d * NS : (d + 1) * NS, :] = mh
                s.mlo[pl.ds(block * NI, NI), d * NS : (d + 1) * NS, :] = ml

    expand(side)
    finish(flight)
    expand(1 - side)
    s.rall[...] = s.rr[...].astype(F32).reshape(length, DS).astype(BF16)

    @pl.loop(0, BI // TOGETHER)
    def _(q):
        for part in range(TOGETHER):
            i = q * TOGETHER + part
            block = mm(s.rall[...], s.mhi[i]) + mm(s.rall[...], s.mlo[i])
            block = block * inv_count
            for c in range(cols):
                s.os[c, i] = block[c * NJ : (c + 1) * NJ].astype(BF16)

    s.orr[me_c] = s.os[me_c]
    finish(exchange(COL, OUTER, lambda p: s.os.at[p], lambda p: s.orr.at[p]))

    pair_lane = iota((NP, 128), 1)
    offset = s.offset[...].astype(jnp.int32)
    pair_codes = jnp.where(pair_lane == offset, 1.0, 0.0).astype(BF16)
    outer = s.orr[0].astype(F32)
    for c in range(1, cols):
        outer = outer + s.orr[c].astype(F32)
    pair_rep = (mm3r(pair_codes, s.wrel[...]) + outer.reshape(NP, WP)) + bias_outer
    s.prep[...] = pair_rep
    unit3, scale3 = norm(pair_rep)
    s.xh3[...] = unit3
    s.r3[...] = scale3
    proj = mm3(unit3 * gain_pair, w_p[0 : 5 * WP, :], NT)
    pair_mask = s.pmask[...]
    sig1 = jax.nn.sigmoid(proj[:, WP : 2 * WP])
    sig2 = jax.nn.sigmoid(proj[:, 3 * WP : 4 * WP])
    sig3 = jax.nn.sigmoid(proj[:, 4 * WP :])
    s.proj[:, 0 : WP] = proj[:, 0:WP]
    s.proj[:, WP : 2 * WP] = sig1
    s.proj[:, 2 * WP : 3 * WP] = proj[:, 2 * WP : 3 * WP]
    s.proj[:, 3 * WP : 4 * WP] = sig2
    s.proj[:, 4 * WP :] = sig3
    s.le[...] = sig1 * proj[:, 0:WP] * pair_mask
    right_edge = (sig2 * proj[:, 2 * WP : 3 * WP] * pair_mask).astype(BF16)
    s.er[quad] = right_edge.reshape(BI, NJ, WP)
    finish(exchange(QUAD, EDGE, lambda p: s.er.at[quad], lambda p: s.er.at[p]))
    for q in range(quads):
        for block in range(2):
            begin = (q + quads * block) * NI * NJ
            s.re[begin : begin + NI * NJ, :] = (
                s.er[q, block * NI : (block + 1) * NI].astype(F32).reshape(NI * NJ, WP)
            )

    @pl.loop(0, BI // 4)
    def _(q):
        for c in range(cols):
            blocks = [jnp.zeros((NJ, WP), F32)] * 4
            for k in range(NJ):
                other = s.re[pl.ds(c * NJ * NJ + k, NJ, stride=NJ), :]
                for part in range(4):
                    near = s.le[pl.ds((q * 4 + part) * NJ + k, 1), :]
                    blocks[part] = blocks[part] + near * other
            for part in range(4):
                s.ts[c, q * 4 + part] = blocks[part].astype(BF16)

    s.tr[me_c] = s.ts[me_c]
    finish(exchange(COL, TRI, lambda p: s.ts.at[p], lambda p: s.tr.at[p]))

    mixed = s.tr[0].astype(F32)
    for c in range(1, cols):
        mixed = mixed + s.tr[c].astype(F32)
    unit4, scale4 = norm(mixed.reshape(NP, WP))
    w_out = w_p[5 * WP : 6 * WP, :]
    moved = mm3(unit4 * gain_mixed, w_out, NT)
    sig3 = s.proj[:, 4 * WP :]
    pair_out = s.prep[...] + sig3 * moved
    bins = mm3(pair_out, s.wbd[...], NT) + pltpu.roll(
        jnp.where(iota((8, 128), 1) < BINS, s.tail[...], 0.0), 8, 1
    )[0:1]
    valid = (pair_lane >= 8) & (pair_lane < 8 + BINS)
    top = jnp.max(jnp.where(valid, bins, -3e38), axis=-1, keepdims=True)
    power = jnp.where(valid, jnp.exp(jnp.where(valid, bins, top) - top), 0.0)
    whole = jnp.sum(power, axis=-1, keepdims=True)
    spread_p = jnp.where(iota((NP, BI), 1) == iota((NP, BI), 0) // NJ, 1.0, 0.0).astype(BF16)
    target = at_lane(
        mm(spread_p, s.tgr[...].reshape(BI, NJ).astype(F32).astype(BF16)), row_p % NJ
    )
    truth = (pair_lane - 8 == target.astype(jnp.int32)) & valid
    picked = jnp.sum(jnp.where(truth, bins, 0.0), axis=-1, keepdims=True)
    dist_sum = colsum((jnp.log(whole) + top - picked) * pair_mask)
    dbins = (power / whole - jnp.where(truth, 1.0, 0.0)) * (pair_mask * inv_dist)

    def put(place, value, skip=0):
        base = place + skip
        height, width = value.shape
        for w in range(width // 128):
            s.grad[base + w * height : base + (w + 1) * height, :] = value[
                :, w * 128 : (w + 1) * 128
            ]

    planes, lines = cols, rows // 2
    sizes = {CORE: 2, PLANE: planes, Z: lines}
    places = {CORE: me_c % 2, PLANE: me_c // 2 * 2 + me_r % 2, Z: me_r // 2}

    def line_peer(axis, place):
        if axis == CORE:
            return {ROW: me_r, COL: me_c // 2 * 2 + place}
        if axis == PLANE:
            return {ROW: me_r // 2 * 2 + place % 2, COL: place // 2 * 2 + me_c % 2}
        return {ROW: place * 2 + me_r % 2, COL: me_c}

    def rows_at(unit, count):
        return pl.ds(pl.multiple_of(unit * 8, 8), count * 8)

    class Sum:
        def __init__(self, number):
            self.number = number
            self.begin = bases[number] // 8
            self.at, self.size = self.begin, (bases[number + 1] - bases[number]) // 8
            self.rx = self.begin
            self.low_sum, self.low_share = number < LOW_SUM, number < LOW_SHARE
            self.stages = [(self.reduce, axis) for axis in (CORE, PLANE, Z)]
            self.stages += [(self.share, axis) for axis in (Z, PLANE, CORE)]
            self.flight, self.after, self.used, self.stored = [], None, 0, False

        @property
        def done(self):
            return not self.stages and not self.flight

        def copies(self, axis, source, target):
            count = sizes[axis]
            for step in range(1, count):
                peer = lax.rem(places[axis] + step, count)
                origin = lax.rem(places[axis] + (count - step), count)
                both = []
                for end in (target(places[axis], step), target(origin, step)):
                    both.append(
                        pltpu.make_async_remote_copy(
                            src_ref=source(peer, step),
                            dst_ref=end,
                            send_sem=sum_send.at[self.number, step - 1],
                            recv_sem=sum_recv.at[self.number, self.used],
                            device_id=line_peer(axis, peer),
                            device_id_type=MESH,
                        )
                    )
                self.used += 1
                both[0].start()
                self.flight.append(both)

        def advance(self):
            finish(self.flight)
            self.flight = []
            if self.after is not None:
                self.after()
                self.after = None
            if self.stages:
                stage, axis = self.stages.pop(0)
                stage(axis)

        def reduce(self, axis):
            count = sizes[axis]
            small = self.size // count
            rx = self.rx

            def slot(buffer, step):
                if self.low_sum:
                    return buffer.at[pl.ds(rx + (step - 1) * small, small)]
                return buffer.at[pl.ds((rx + (step - 1) * small) * 8, small * 8)]

            if self.low_sum:
                for step in range(1, count):
                    peer = lax.rem(places[axis] + step, count)
                    value = s.grad[rows_at(self.at + peer * small, small), :]
                    slot(s.lows, step)[...] = value.reshape(small, 8, 128).astype(BF16)

            def source(peer, step):
                if self.low_sum:
                    return slot(s.lows, step)
                return s.grad.at[rows_at(self.at + peer * small, small)]

            near = s.lowr if self.low_sum else s.arx
            self.copies(axis, source, lambda place, step: slot(near, step))

            def add():
                self.at = self.at + places[axis] * small
                self.size = small
                mine = rows_at(self.at, small)
                value = s.grad[mine, :]
                for step in range(1, count):
                    other = slot(near, step)[...].astype(F32)
                    value = value + other.reshape(small * 8, 128)
                s.grad[mine, :] = value

            self.after = add
            self.rx = rx + (count - 1) * small

        def spot(self, at, size):
            if self.low_share:
                return gbig.at[pl.ds(at, size)]
            return grest.at[rows_at(at - bases[LOW_SHARE] // 8, size)]

        def share(self, axis):
            if not self.stored:
                self.stored = True
                value = s.grad[rows_at(self.at, self.size), :]
                if self.low_share:
                    value = value.reshape(self.size, 8, 128).astype(BF16)
                self.spot(self.at, self.size)[...] = value
            size = self.size
            first = self.at - places[axis] * size
            self.copies(
                axis,
                lambda peer, step: self.spot(first + places[axis] * size, size),
                lambda place, step: self.spot(first + place * size, size),
            )
            self.at, self.size = first, size * sizes[axis]

    up, thin, back, back2, early, rest = [Sum(number) for number in range(LAST)]

    def turn(*groups):
        for group in groups:
            group.advance()

    def column_products(name, place):
        s.sum8[...] = jnp.zeros((8, WA), F32)

        @pl.loop(0, NM // 32)
        def _(q):
            some = pl.ds(pl.multiple_of(q * 32, 32), 32)
            product = s.dn[some, :] * name[some, :]
            s.sum8[...] += jnp.sum(product.reshape(4, 8, WA), axis=0)

        whole = colsum(s.sum8[...])
        for half in range(2):
            s.grad[small + place + half : small + place + half + 1, :] = whole[
                :, 128 * half : 128 * half + 128
            ]

    for begin, end in (
        (ROWS.o + 2 * WA, bases[2]),
        (ROWS.small, bases[LAST]),
        (ROWS.bias, bases[-1]),
    ):
        if end > begin:
            s.grad[begin:end, :] = jnp.zeros((end - begin, 128), F32)
    small = ROWS.small
    put(ROWS.dist, mm3(dbins, pair_out, TN)[8 : 8 + BINS])
    dbias_dist = pltpu.roll(jnp.broadcast_to(colsum(dbins), (8, 128)), 120, 1)[0:1]
    dout = mm3(dbins, s.wbd[...])
    dgate = dout * moved * (sig3 * (1.0 - sig3))
    dmoved = dout * sig3
    put(ROWS.out, mm3(dmoved, unit4 * gain_mixed, TN))
    dnormed = mm3(dmoved, w_out)
    s.grad[small + 5 : small + 6, :] = colsum(dnormed * unit4)
    dmixed = norm_back(dnormed * gain_mixed, unit4, scale4)
    s.ds[...] = dmixed.astype(BF16).reshape(BI, NJ, WP)
    s.dsr[me_c] = s.ds[...]
    finish(exchange(COL, GMIX, lambda p: s.ds, lambda p: s.dsr.at[p]))
    for bi in range(BI):
        for c in range(cols):
            begin = bi * length + c * NJ
            s.dm[begin : begin + NJ, :] = s.dsr[c, bi].astype(F32)

    @pl.loop(0, quads)
    def _(q):
        for begin in range(0, BI, 4):
            blocks = [jnp.zeros((NJ, WP), F32)] * 4
            first_j = (q + quads * (begin // NI)) * NI + begin % NI
            for i in range(BI):
                other = s.le[i * NJ : (i + 1) * NJ, :]
                for part in range(4):
                    near = s.dm[pl.ds(i * length + first_j + part, 1), :]
                    blocks[part] = blocks[part] + near * other
            for part in range(4):
                s.gs[q, begin + part] = blocks[part].astype(BF16)

    s.gr[quad] = s.gs[quad]
    flight = exchange(QUAD, GEDGE, lambda p: s.gs.at[p], lambda p: s.gr.at[p])

    @pl.loop(0, BI // 4)
    def _(q):
        blocks = [jnp.zeros((NJ, WP), F32)] * 4
        for j in range(length):
            other = s.re[j * NJ : (j + 1) * NJ, :]
            for part in range(4):
                near = s.dm[pl.ds((q * 4 + part) * length + j, 1), :]
                blocks[part] = blocks[part] + near * other
        for part in range(4):
            s.gl[q * 4 + part] = blocks[part]

    finish(flight)
    dright = s.gr[0].astype(F32)
    for q in range(1, quads):
        dright = dright + s.gr[q].astype(F32)
    dright = dright.reshape(NP, WP) * pair_mask
    dleft = s.gl[...].reshape(NP, WP) * pair_mask
    p1, sig1 = s.proj[:, 0:WP], s.proj[:, WP : 2 * WP]
    p2, sig2 = s.proj[:, 2 * WP : 3 * WP], s.proj[:, 3 * WP : 4 * WP]
    dproj = jnp.concatenate(
        [
            dleft * sig1,
            dleft * p1 * (sig1 * (1.0 - sig1)),
            dright * sig2,
            dright * p2 * (sig2 * (1.0 - sig2)),
            dgate,
        ],
        axis=1,
    )
    unit3 = s.xh3[...]
    put(ROWS.tri, mm3(dproj, unit3 * gain_pair, TN))
    dnormed = mm3(dproj, w_p[0 : 5 * WP, :])
    s.grad[small + 4 : small + 5, :] = colsum(dnormed * unit3)
    drep = dout + norm_back(dnormed * gain_pair, unit3, s.r3[...])
    s.grad[small + 6 : small + 7, :] = colsum(drep)
    s.grad[ROWS.rel : ROWS.rel + 72, :] = mm2r(pair_codes, drep, TN)[0:72]
    s.qs[...] = drep.astype(BF16).reshape(BI, NJ, WP)
    s.qr[me_c] = s.qs[...]
    finish(exchange(COL, GOUTER, lambda p: s.qs, lambda p: s.qr.at[p]))

    turned = s.rall[...].astype(F32).T.astype(BF16)
    s.dr[...] = jnp.zeros((length, DS), F32)

    @pl.loop(0, BI // TOGETHER)
    def _(q):
        total = jnp.zeros((length, DS), F32)
        for part in range(TOGETHER):
            i = q * TOGETHER + part
            block = jnp.concatenate([s.qr[c, i] for c in range(cols)], axis=0)
            total = total + (mm(block, s.mhi[i], NT) + mm(block, s.mlo[i], NT))
            mh, ml = split2(mm(turned, block) * inv_count)
            s.mhi[i] = mh
            s.mlo[i] = ml
        s.dr[...] += total

    for r in range(rows):
        s.us[r] = (s.dr[r * NI : (r + 1) * NI, :] * inv_count).astype(BF16)
    s.ur[me_r] = s.us[me_r]
    flight = exchange(ROW, GRIGHT, lambda p: s.us.at[p], lambda p: s.ur.at[p])

    def pair_weight(pair):
        return split2(
            jnp.concatenate([outer_weight(2 * pair), outer_weight(2 * pair + 1)], axis=1)
        )

    def pair_of(ref, pair):
        return jnp.concatenate(
            [
                ref[:, d * NS : (d + 1) * NS, :].reshape(NM, WP)
                for d in (2 * pair, 2 * pair + 1)
            ],
            axis=1,
        )

    dleft = jnp.zeros((NM, WO), F32)
    for pair in range(WO // 2):
        wh, wl = pair_weight(pair)
        mh, ml = pair_of(s.mhi, pair), pair_of(s.mlo, pair)
        dleft = dleft + (mm(mh, wh, NT) + (mm(ml, wh, NT) + mm(mh, wl, NT)))
    high, low = split2(jnp.concatenate([dleft, jnp.zeros((NM, 96), F32)], axis=1))
    both = high.astype(F32) + pltpu.roll(low.astype(F32), 32, 1)
    s.dl[...] = both.astype(BF16).reshape(2, NI * NS, 128)
    s.dlr[side] = s.dl[side]
    flight.append(swap(2, s.dl, s.dlr))
    left3 = s.lr[...].astype(F32).reshape(NM, 128).T.astype(BF16)
    left_both, left_high = left3[0:64], left3[0:32]
    for pair in range(WO // 2):
        mh, ml = pair_of(s.mhi, pair), pair_of(s.mlo, pair)
        made = mm(left_both, mh)
        made = made[0:32] + made[32:64] + mm(left_high, ml)
        for half in range(2):
            s.grad[pl.ds(ROWS.outer + 2 * pair + half, WO, stride=WO), :] = made[
                :, half * WP : (half + 1) * WP
            ]
    early.advance()

    finish(flight)
    both = s.dlr[...].astype(F32).reshape(NM, 128)
    both = jnp.where(lane < 32, both + pltpu.roll(both, 96, 1), 0.0)
    dleft = mm3r(order, both, TN)
    dright = []
    for b in range(NB):
        some = s.ur[b * quads].astype(F32)
        for q in range(1, quads):
            some = some + s.ur[b * quads + q].astype(F32)
        dright.append(some)
    dright = jnp.stack(dright)
    wide = jnp.broadcast_to(dright[:, None], (NB, NS, NI, DS)).reshape(NM, DS)
    dedges = mm2(jnp.where(own_seq, wide, 0.0), repeat, NT)
    dedges = (dedges + dleft) * seq_weight
    unit2, rep = s.xh2[...], s.rep[...]
    dlog = s.dlog[...]
    put(ROWS.eh, (mm3(dedges, unit2 * gain_outer, TN) + mm3(dlog, rep, TN))[0:88])
    s.dn[...] = mm3(dedges, s.weh[...])
    dnormed = s.dn[...]
    column_products(s.xh2, 2)
    drep = mm3(dlog, s.weh[...]) + norm_back(dnormed * gain_outer, unit2, s.r2[...])
    early.advance()
    hidden = s.hid[...]
    dhidden = jnp.where(hidden > 0, mm3(drep, w_c[WA:, :], NT), 0.0)
    unit1 = s.xh1[...]
    put(ROWS.up, mm3(dhidden, unit1 * gain_trans, TN))
    up.advance()
    put(ROWS.back, mm3(hidden, drep, TN))
    turn(back, back2, up)
    s.dn[...] = mm3(dhidden, w_a[4 * WA : 4 * WA + UP, :])
    dnormed = s.dn[...]
    column_products(s.xh1, 0)
    dmid = drep + norm_back(dnormed * gain_trans, unit1, s.r1[...])
    sg, att = s.sg[...], s.att[...]
    put(ROWS.o, mm3(sg * att, dmid, TN))
    dgated = mm3(dmid, w_c[0:WA, :], NT)
    turn(thin, back, back2, early)
    single = triple[:, 0:AP]
    put(ROWS.tabs, mm2r(single, dmid, TN)[0:TR], 4 * TR)
    put(ROWS.tabs, mm2r(single, dgated * att, TN)[0:TR], 2 * TR)
    datt = dgated * sg

    pam = s.pam[...].reshape(NM, WA)
    blocks = jnp.where(head_mask(WA, AP), mm3(pam, datt, TN), 0.0)
    put(ROWS.tabs, jnp.sum(blocks.reshape(HEADS, AP, WA), axis=0)[0:TR])
    lane1 = iota((1, 128), 1)
    s.grad[small + 7 : small + 8, :] = jnp.where(lane1 < BINS, dbias_dist, colsum(dlog))
    s.grad[small + 8 : small + 9, :] = jnp.where(
        lane1 == 0, msa_sum, jnp.where(lane1 == 1, dist_sum, 0.0)
    )
    turn(rest, thin)
    s.dpam[...] = mm2(datt, s.vb[...], NT).reshape(BS, NI, WA)
    for b in range(NB):
        key_mask = s.sites[b : b + 1, :]
        s.dbias[b] = jnp.zeros((64, length), F32)

        def attention_back(q):
            together = jnp.zeros((64, length), F32)
            for part in range(TOGETHER):
                bs = b * NS + q * TOGETHER + part
                code = letter_codes(bs)
                wide = [spread(p.astype(F32)).astype(BF16) for p in split2(s.dpam[bs])]
                raw = mm(jnp.concatenate(wide, axis=0), code)
                dweight = raw[0:64] + raw[64:128]
                weight = s.prob[bs]
                inner = jnp.sum(weight * dweight, axis=-1, keepdims=True)
                dscore = jnp.where(key_mask > 0, weight * (dweight - inner), 0.0)
                together = together + dscore
                back = mm(jnp.concatenate(split2(dscore), axis=0), code, NT)
                s.da[bs] = gather_heads(back[0:64] + back[64:128])
            s.dbias[b] += together

        for part in range(2):
            count = NS // TOGETHER // 2
            pl.loop(part * count, (part + 1) * count)(attention_back)
            turn(*((rest, up), (back, early), (back2,), (thin, rest, up))[2 * b + part])

    put(ROWS.score, mm2r(single, s.da[...].reshape(NM, WA), TN)[0:TR])
    for b in range(NB):
        for i in range(NI):
            part = jnp.concatenate(
                [s.dbias[b, h * NI + i : h * NI + i + 1, :] for h in range(HEADS)], axis=0
            )
            s.dtab[b * NI + i] = mm(
                jnp.concatenate(split2(part), axis=0), codes(b * NI + i), NT
            )
    s.grad[ROWS.bias : ROWS.bias + 8, :] = jnp.sum(
        s.dtab[...].reshape(2 * BI, 8, RP), axis=0
    )

    aux[...] = jnp.where(iota((8, 128), 1) == 0, masked, inv_dist)

    last = bases[LAST]
    piece = (bases[-1] - last) // cols

    def mine(p):
        return pl.ds(pl.multiple_of(last + p * piece, 8), piece)

    def spot(p):
        return gfin.at[pl.ds(pl.multiple_of(p * piece, 8), piece)]

    s.fc[me_c] = s.grad[mine(me_c), :]
    flight = exchange(COL, SUM_COL, lambda p: s.grad.at[mine(p)], lambda p: s.fc.at[p])
    turn(back, early)
    finish(flight)
    summed = s.fc[0]
    for c in range(1, cols):
        summed = summed + s.fc[c]
    s.fp[...] = summed
    s.fr[me_r] = summed
    flight = exchange(ROW, SUM_ROW, lambda p: s.fp, lambda p: s.fr.at[p])
    turn(back2, thin, rest, up, back, early)
    finish(flight)
    summed = s.fr[0]
    for r in range(1, rows):
        summed = summed + s.fr[r]
    gfin[pl.ds(pl.multiple_of(me_c * piece, 8), piece), :] = summed
    flight = exchange(COL, SHARE_COL, lambda p: spot(me_c), spot)
    turn(back2, early, thin, rest)
    finish(flight)
    turn(up, back, up, back2, back, back2, thin, rest, thin, rest)
    assert all(group.done for group in (up, thin, back, back2, early, rest))


def post_kernel(rows, cols, *refs):
    gbig, grest, gfin, tout, aux = refs[:5]
    weights, far_moments = refs[5:11], refs[11:23]
    far, loss_out, size_out = refs[23:41], refs[41], refs[42]
    new, moments = refs[43:61], refs[61:73]
    lk, wrel, g_a, g_small, g_rel, store_sem, load_sem = refs[73:]
    loads = [
        pltpu.make_async_copy(source, near, load_sem.at[place])
        for place, (source, near) in enumerate(zip(far_moments, moments))
    ]
    for place in (2, 8, 1, 7, 3, 9, 4, 10, 0, 6, 5, 11):
        loads[place].start()
    means, squares = moments[0:6], moments[6:12]
    lookup, w_a, w_c, w_r, w_p, scal = weights
    ROWS, bases = layout(rows, cols)

    def big(begin, count):
        part = gbig[begin // 8 : (begin + count) // 8].astype(F32)
        return part.reshape(count, 128)

    def exact(begin, count):
        if begin >= bases[LAST]:
            return gfin[begin - bases[LAST] : begin - bases[LAST] + count, :]
        return grest[begin - bases[LOW_SHARE] : begin - bases[LOW_SHARE] + count, :]

    lk[...] = jnp.zeros((AP, WA), F32)
    lk[0:LETTERS, :] = lookup[...]
    wrel[...] = jnp.zeros((RP, WP), F32)
    wrel[0:NREL, :] = w_r[UP : UP + NREL, :]

    def table(begin):
        both = jnp.concatenate([exact(begin, TR), exact(begin + TR, TR)], axis=1)
        return jnp.concatenate([both, jnp.zeros((AP - TR, WA), F32)], axis=0)

    dscore = table(ROWS.score)
    dvalue, dgate, dstart = [table(ROWS.tabs + 2 * TR * place) for place in range(3)]
    mapped = tout[...]
    t_q = mapped[:, 0:WA] * HEAD ** (-0.5)
    t_k = mapped[:, WA : 2 * WA].astype(BF16).astype(F32)
    t_g = jax.nn.sigmoid(mapped[:, 3 * WA :])
    square = head_mask(WA, AP)
    key_block = jnp.where(square, jnp.concatenate([t_k] * HEADS, axis=0), 0.0).astype(BF16)
    dq = mm2(dscore, key_block) * HEAD ** (-0.5)
    dk = jnp.where(square, mm3(dscore, t_q, TN), 0.0)
    dk = jnp.sum(dk.reshape(HEADS, AP, WA), axis=0)
    dg = dgate * (t_g * (1.0 - t_g))
    dmapped = jnp.concatenate([dq, dk, dvalue, dg], axis=1)
    unit0, scale0 = norm(lk[...])
    gain_row = scal[0:WA].reshape(1, WA)
    g_a[...] = mm3(dmapped, unit0 * gain_row, TN)
    dnormed = mm3(dmapped, w_a[0 : 4 * WA, :])
    dgain_row = colsum(dnormed * unit0)
    g_lookup = dstart + norm_back(dnormed * gain_row, unit0, scale0)

    unit_r, scale_r = norm(wrel[...])
    gain_rel = scal[768:896].reshape(1, WP)
    dtable = exact(ROWS.bias, 8)
    g_bias = mm3(dtable, unit_r * gain_rel)
    dnormed = mm3(dtable, w_p[768:776, :], TN)
    dgain_rel = colsum(dnormed * unit_r)
    g_rel[...] = exact(ROWS.rel, 72) + norm_back(
        dnormed * gain_rel, unit_r, scale_r
    )[0:72]

    base = ROWS.small
    g_small[0:WA] = dgain_row.reshape(WA)
    for place, row in ((256, 0), (384, 1), (512, 2), (640, 3), (896, 4), (1024, 5), (1152, 6)):
        g_small[place : place + 128] = exact(base + row, 1).reshape(128)
    g_small[768:896] = dgain_rel.reshape(128)
    lane = iota((1, 128), 1)
    tail = jnp.where(lane < 87, exact(base + 7, 1), 0.0)
    g_small[1280:1408] = tail.reshape(128)

    rel_row = iota((72, 128), 0)
    squares_sum = jnp.zeros((1, 1), F32)
    for begin, count in (
        (ROWS.up, 2 * UP),
        (ROWS.tri, 768),
        (ROWS.o, 2 * WA),
        (ROWS.back, 2 * UP),
    ):
        part = big(begin, count)
        squares_sum = squares_sum + total_of(part * part)
    for part in (
        g_a[...],
        g_lookup[0:LETTERS],
        jnp.where(rel_row < NREL, g_rel[...], 0.0),
        g_bias,
        dgain_row,
        exact(ROWS.outer, UP),
        exact(base, 7),
        exact(ROWS.eh, 87),
        exact(ROWS.eh + 88, 87),
        exact(ROWS.dist, BINS),
        dgain_rel,
        tail,
    ):
        squares_sum = squares_sum + total_of(part * part)
    size = jnp.sqrt(squares_sum)
    scale = jnp.minimum(1.0, CLIP / size)

    def adam(which, where, grad, factor=scale):
        clipped = grad * factor
        weight = weights[which][where]
        moment = B1 * means[which][where] + (1.0 - B1) * clipped
        second = B2 * squares[which][where] + (1.0 - B2) * clipped * clipped
        root = (1.0 - B2**STEP) ** 0.5
        step = (moment * (RATE * root / (1.0 - B1**STEP))) / (
            second * lax.rsqrt(second) + ADAM_EPS * root
        )
        new[3 * which][where] = weight * (1.0 - RATE * DECAY) - step
        new[3 * which + 1][where] = moment
        new[3 * which + 2][where] = second

    every = slice(None)
    stores = []

    def leave(which):
        for place in range(3 * which, 3 * which + 3):
            store = pltpu.make_async_copy(new[place], far[place], store_sem.at[place])
            store.start()
            stores.append(store)

    def ready(which):
        loads[which].wait()
        loads[6 + which].wait()

    ready(2)
    for w in range(2):
        half = slice(128 * w, 128 * w + 128)
        adam(2, (slice(0, WA), half), big(ROWS.o + w * WA, WA))
        adam(2, (slice(WA, WA + UP), half), big(ROWS.back + w * UP, UP))
    leave(2)
    ready(1)
    adam(1, (slice(0, 4 * WA), every), g_a[...])
    for w in range(2):
        half = slice(128 * w, 128 * w + 128)
        adam(1, (slice(1024, 2048), half), big(ROWS.up + w * UP, UP))
        adam(1, (slice(2048, 2135), half), exact(ROWS.eh + w * 88, 87))
    leave(1)
    ready(3)
    adam(3, (slice(0, UP), every), exact(ROWS.outer, UP))
    adam(3, (slice(UP, UP + NREL), every), g_rel[0:NREL, :])
    leave(3)
    ready(4)
    adam(4, (slice(0, 768), every), big(ROWS.tri, 768))
    adam(4, (slice(768, 776), every), g_bias)
    adam(4, (slice(776, 840), every), exact(ROWS.dist, BINS))
    leave(4)
    ready(0)
    adam(0, (every, every), g_lookup[0:LETTERS])
    leave(0)
    ready(5)
    adam(5, (slice(0, 1367),), g_small[0:1367], scale.reshape(1))
    leave(5)

    sums = exact(base + 8, 1)
    loss = sums[:, 0:1] / aux[0:1, 0:1] + sums[:, 1:2] * aux[0:1, 1:2]
    loss_out[0] = loss[0, 0]
    size_out[0] = size[0, 0]
    for store in stores:
        store.wait()


def vmem():
    return pl.BlockSpec(memory_space=pltpu.VMEM)


def per_device(rows, cols, *arrays):
    letters, truth, concealed, existing, ordinals, observed, bins = arrays[:7]

    def turned(group):
        return [w.T if place in (1, 4) else w for place, w in enumerate(group)]

    weights, means, squares = turned(arrays[7:13]), turned(arrays[13:19]), turned(arrays[19:25])
    plan = scratch_plan(rows, cols)
    bases = layout(rows, cols)[1]
    far = pl.BlockSpec(memory_space=pltpu.HBM)
    summed = pl.pallas_call(
        functools.partial(main_kernel, rows, cols, tuple(plan)),
        out_shape=(
            jax.ShapeDtypeStruct((bases[LOW_SHARE] // 8, 8, 128), BF16),
            jax.ShapeDtypeStruct((bases[LAST] - bases[LOW_SHARE], 128), F32),
            jax.ShapeDtypeStruct((bases[-1] - bases[LAST], 128), F32),
            jax.ShapeDtypeStruct((AP, 4 * WA), F32),
            jax.ShapeDtypeStruct((8, 128), F32),
        ),
        in_specs=[far] * OPERANDS,
        out_specs=tuple([vmem()] * 5),
        scratch_shapes=[pltpu.VMEM(dims, kind) for dims, kind in plan.values()]
        + [
            pltpu.SemaphoreType.DMA((rows - 1,)),
            pltpu.SemaphoreType.DMA((PHASES - 1, rows - 1)),
            pltpu.SemaphoreType.DMA((cols - 1,)),
            pltpu.SemaphoreType.DMA((PHASES, cols - 1)),
            pltpu.SemaphoreType.DMA((3, 2)),
            pltpu.SemaphoreType.DMA((LAST, max(rows // 2, cols) - 1)),
            pltpu.SemaphoreType.DMA((LAST, 2 * cols + rows - 2)),
            pltpu.SemaphoreType.DMA((OPERANDS,)),
        ],
        compiler_params=pltpu.CompilerParams(
            collective_id=0, has_side_effects=True, vmem_limit_bytes=MAIN_VMEM
        ),
    )(
        *[
            pltpu.with_memory_space_constraint(value, pltpu.HBM)
            for value in (
                jnp.swapaxes(letters, 1, 2),
                jnp.swapaxes(truth, 1, 2),
                jnp.swapaxes(concealed, 1, 2),
                existing,
                ordinals,
                observed,
                bins,
                *weights,
            )
        ]
    )

    shapes = []
    for w in weights:
        shapes += [jax.ShapeDtypeStruct(w.shape, F32)] * 3
    one = jax.ShapeDtypeStruct((1,), F32)
    scalar = pl.BlockSpec(memory_space=pltpu.SMEM)
    result = pl.pallas_call(
        functools.partial(post_kernel, rows, cols),
        out_shape=tuple(shapes) + (one, one),
        in_specs=[vmem()] * 11 + [far] * 12,
        out_specs=tuple([far] * 18) + (scalar, scalar),
        scratch_shapes=[pltpu.VMEM(shape.shape, F32) for shape in shapes]
        + [pltpu.VMEM(value.shape, F32) for value in (*means, *squares)]
        + [
            pltpu.VMEM((AP, WA), F32),
            pltpu.VMEM((RP, WP), F32),
            pltpu.VMEM((4 * WA, WA), F32),
            pltpu.VMEM((1408,), F32),
            pltpu.VMEM((72, 128), F32),
            pltpu.SemaphoreType.DMA((18,)),
            pltpu.SemaphoreType.DMA((12,)),
        ],
        compiler_params=pltpu.CompilerParams(vmem_limit_bytes=POST_VMEM),
    )(
        *summed,
        *weights,
        *[pltpu.with_memory_space_constraint(value, pltpu.HBM) for value in (*means, *squares)],
    )
    outs = [result[18].reshape(()), result[19].reshape(())]
    for place, value in enumerate(result[:18]):
        outs.append(value.T if place // 3 in (1, 4) else value)
    return tuple(outs)


def solution(mesh):
    rows, cols = mesh.shape[ROW], mesh.shape[COL]
    placed = (
        (P(None, COL, ROW),) * 3 + (P(),) * 3 + (P(None, ROW, COL),) + (P(),) * 18
    )
    return jax.shard_map(
        functools.partial(per_device, rows, cols),
        mesh=mesh,
        in_specs=placed,
        out_specs=(P(),) * 20,
        check_vma=False,
    )
```
